32 devices in a mesh: depth: 8 (over y, x, core), inline: 4 (over z).
Axes of the slice: x: 2, y: 2, z: 4, core: 2. Of those that a mesh axis runs over, the one named last changes fastest.
Arguments:
- control: float32 [32, 32, 16, 128], P(None, 'depth', 'inline'), may hold values from -6 to 6
- filter_coeffs: float32 [4, 32, 32], P(None, None, 'depth'), may hold values from 0 to 1, as said below
- conv_kernels: float32 [8, 4, 4, 5, 5], replicated, may hold values from -0.625 to 0.625
- channel_order: int32 [32], replicated, may hold values from 0 to 31, each once
- point_cells: int32 [3, 8, 4, 256], P(None, 'depth', 'inline'), may hold values from 0 to 127, as said below
- point_values: float32 [32, 8, 4, 256], P(None, 'depth', 'inline'), may hold values from -6 to 6
- point_weights: float32 [8, 4, 256], P('depth', 'inline'), may hold values from 1 to 10
- orient_cells: int32 [3, 8, 4, 128], P(None, 'depth', 'inline'), may hold values from 0 to 126, as said below
- orient_normals: float32 [3, 32, 8, 4, 128], P(None, None, 'depth', 'inline'), may hold values from -6 to 6
- orient_weights: float32 [8, 4, 128], P('depth', 'inline'), may hold values from 1 to 10
Outputs:
- potential: float32 [32, 32, 16, 128], P(None, 'depth', 'inline')
- gradient: float32 [32, 32, 16, 128], P(None, 'depth', 'inline')
The draws below stay inside these ranges and needn't reach their ends.
Inputs may be any that keep to these rules, and one draw needn't show every extreme that they name: `filter_coeffs`: positive; the four lags of one channel and depth cell sum to less than one. `channel_order`: each channel appears once. `point_cells`: the points of row (d, i) lie in depth cells d * 4 to d * 4 + 3 and inline cells i * 4 to i * 4 + 3; the first point of each row is the last cell of that block along all three dimensions. `orient_cells`: the points of row (d, i) lie in depth cells d * 4 to d * 4 + 2, inline cells i * 4 to i * 4 + 2 and crossline cells 0 to 126; the first point of each row is the last such cell along all three dimensions.
All inputs are finite; a program needn't handle non-finite values.
Results may differ from the reference program's by a relative error of at most 0.0003.
Values sent between devices are 32-bit elements; how exact they have to be, the bound alone decides.
No kernel may reach another device: no remote copies, remote signals or barrier semaphores. Data moves between devices by JAX's collectives and lax.ppermute only.
A program may use at most 128 MiB of HBM per device.

```python
import math
import jax
import jax.numpy as jnp
from jax import lax

POTENTIAL_CHANS = 32
GROUPS = 8
GS = 4
KW = 5
DZ = 4
IL = 4
XL = 128
PTS = 256
OPTS = 128
DEPTH_TOTAL = 32
NY = 16
N_DEPTH = 8
N_INLINE = 4


def draw_filter_coeffs(key, part):
    random_key_sequence = jax.random.split(key, 8)
    slow_share = 0.5
    slow_mask = (jax.random.uniform(random_key_sequence[0], (POTENTIAL_CHANS,)) < slow_share).astype(jnp.float32)
    slow_frac = jax.random.uniform(random_key_sequence[1], (POTENTIAL_CHANS,), minval=0.2, maxval=0.6)
    fast_len = jax.random.uniform(random_key_sequence[2], (POTENTIAL_CHANS,), minval=30.0, maxval=50.0)
    base_rate = slow_mask * (math.log(0.1) * slow_frac / DEPTH_TOTAL) + (1.0 - slow_mask) * (-2.5 / fast_len)
    cell_factor = jax.random.uniform(random_key_sequence[3], (POTENTIAL_CHANS, DEPTH_TOTAL), minval=0.5, maxval=1.5)
    block_factor = jnp.repeat(jax.random.uniform(random_key_sequence[4], (POTENTIAL_CHANS, DEPTH_TOTAL // DZ), minval=0.5, maxval=1.5), DZ, axis=1)
    falloff_factor = jnp.exp(base_rate[:, None] * cell_factor * block_factor)
    spike_position = jax.random.randint(random_key_sequence[5], (2,), 0, DEPTH_TOTAL)
    location_index = jnp.arange(DEPTH_TOTAL, dtype=jnp.int32)
    spike_match = jnp.any(location_index[:, None] == spike_position[None, :], axis=1).astype(jnp.float32)[None, :]
    spike_retained = jax.random.uniform(random_key_sequence[6], (POTENTIAL_CHANS, DEPTH_TOTAL), minval=0.65, maxval=0.8)
    falloff_factor = falloff_factor * (1.0 - spike_match + spike_match * spike_retained)
    shares = jax.random.uniform(random_key_sequence[7], (4, POTENTIAL_CHANS, DEPTH_TOTAL), minval=0.2, maxval=1.0)
    shares = shares / jnp.sum(shares, axis=0, keepdims=True)
    return (falloff_factor[None, :, :] * shares).astype(jnp.float32)


def block_cells(key, span_depth, span_inline, span_cross, count):
    random_key_sequence = jax.random.split(key, 3)
    blocks_depth = DEPTH_TOTAL // DZ
    blocks_inline = NY // IL
    shape = (blocks_depth, blocks_inline, count)
    first_point = (jnp.arange(count, dtype=jnp.int32) == 0)[None, None, :]
    depth_local = jnp.where(first_point, span_depth - 1, jax.random.randint(random_key_sequence[0], shape, 0, span_depth))
    inline_local = jnp.where(first_point, span_inline - 1, jax.random.randint(random_key_sequence[1], shape, 0, span_inline))
    cross_local = jnp.where(first_point, span_cross - 1, jax.random.randint(random_key_sequence[2], shape, 0, span_cross))
    depth_glob = depth_local + jnp.arange(blocks_depth, dtype=jnp.int32)[:, None, None] * DZ
    inline_glob = inline_local + jnp.arange(blocks_inline, dtype=jnp.int32)[None, :, None] * IL
    return jnp.stack([depth_glob, inline_glob, cross_local], axis=0).astype(jnp.int32)


def draw_point_cells(key, part):
    return block_cells(jax.random.fold_in(key, 5), DZ, IL, XL, PTS)


def draw_orient_cells(key, part):
    return block_cells(jax.random.fold_in(key, 9), DZ - 1, IL - 1, XL - 1, OPTS)


def block_scale(stream_key, shape, shards, least, high):
    loudness = 1.0
    for position, parts in shards:
        draws = jax.random.uniform(jax.random.fold_in(jax.random.fold_in(stream_key, 6), position), (parts,), jnp.float32, least / len(shards), high / len(shards))
        loudness = loudness * jnp.repeat(jnp.exp(draws), shape[position] // parts).reshape((-1,) + (1,) * (len(shape) - 1 - position))
    return loudness


def gaussian(stream_key, dims, deviation, reach, shards=(), kind=jnp.bfloat16):
    array = deviation * jax.random.normal(stream_key, dims, jnp.float32)
    if shards:
        array = array * block_scale(stream_key, dims, shards, -0.22, 0.18)
    return jnp.clip(array, -reach, reach).astype(kind)


def setup_inputs(seed: int = 0) -> dict:
    arg_keys = jax.random.split(jax.random.key(seed), 11)
    control = gaussian(arg_keys[0], (POTENTIAL_CHANS, DEPTH_TOTAL, NY, XL), 1.0, 6.0, ((1, 8), (2, 4)), jnp.float32)
    filter_coeffs = draw_filter_coeffs(jax.random.fold_in(arg_keys[10], 71), 0)
    conv_kernels = gaussian(arg_keys[2], (GROUPS, GS, GS, KW, KW), (GS * KW * KW) ** -0.5, 0.625, (), jnp.float32)
    channel_order = jax.random.permutation(arg_keys[3], POTENTIAL_CHANS).astype(jnp.int32)
    point_cells = draw_point_cells(jax.random.fold_in(arg_keys[10], 71), 0)
    point_values = gaussian(arg_keys[5], (POTENTIAL_CHANS, N_DEPTH, N_INLINE, PTS), 1.0, 6.0, ((1, 8), (2, 4)), jnp.float32)
    point_weights = jnp.clip(jnp.exp(math.log(10.0) - 2.3025851 * jax.random.uniform(arg_keys[6], (N_DEPTH, N_INLINE, PTS), jnp.float32) ** block_scale(arg_keys[6], (N_DEPTH, N_INLINE, PTS), ((0, 8), (1, 4)), -0.2, 0.2)), 1.0, 10.0)
    orient_cells = draw_orient_cells(jax.random.fold_in(arg_keys[10], 71), 0)
    orient_normals = gaussian(arg_keys[8], (3, POTENTIAL_CHANS, N_DEPTH, N_INLINE, OPTS), 1.0, 6.0, ((2, 8), (3, 4)), jnp.float32)
    orient_weights = jnp.clip(jnp.exp(math.log(10.0) - 2.3025851 * jax.random.uniform(arg_keys[9], (N_DEPTH, N_INLINE, OPTS), jnp.float32) ** block_scale(arg_keys[9], (N_DEPTH, N_INLINE, OPTS), ((0, 8), (1, 4)), -0.2, 0.2)), 1.0, 10.0)
    return {"control": control, "filter_coeffs": filter_coeffs, "conv_kernels": conv_kernels, "channel_order": channel_order, "point_cells": point_cells, "point_values": point_values, "point_weights": point_weights, "orient_cells": orient_cells, "orient_normals": orient_normals, "orient_weights": orient_weights}


HIGHEST = lax.Precision.HIGHEST

def mixing(kernels, channel_order):
    groups = kernels.shape[0]
    group_size = kernels.shape[1]
    channels = groups * group_size
    slots = jnp.arange(channels, dtype=jnp.int32)
    chooser = (channel_order[:, None] == slots[None, :]).astype(jnp.float32)
    in_group = (slots[:, None] // group_size == jnp.arange(groups, dtype=jnp.int32)[None, :]).astype(jnp.float32)
    in_place = (slots[:, None] % group_size == jnp.arange(group_size, dtype=jnp.int32)[None, :]).astype(jnp.float32)
    block_mix = jnp.einsum('sg,sa,tg,tb,gabhw->sthw', in_group, in_place, in_group, in_place, kernels, precision=HIGHEST)
    return jnp.einsum('sc,td,sthw->cdhw', chooser, chooser, block_mix, precision=HIGHEST)

def lateral(field, weights):
    return lax.conv_general_dilated(field, weights, (1, 1), ((2, 2), (2, 2)), dimension_numbers=('CNHW', 'OIHW', 'CNHW'), precision=HIGHEST)

def recurse(field, coeffs):
    moved_field = jnp.moveaxis(field, 1, 0)
    moved_coeffs = jnp.moveaxis(coeffs, 2, 0)

    def advance(history, element):
        layer_in, layer_coeff = element
        output = layer_in + lax.optimization_barrier(jnp.sum(layer_coeff[:, :, None] * history, axis=0))
        history = jnp.concatenate([output[None], history[:3]], axis=0)
        return (history, output)
    start_history = jnp.zeros((4, field.shape[0], field.shape[2]), jnp.float32)
    _, outputs = lax.scan(advance, start_history, (moved_field, moved_coeffs))
    return jnp.moveaxis(outputs, 0, 1)

def shifted(coeffs, downward):
    length = coeffs.shape[2]
    stacked = []
    for lag_index in range(4):
        lag = lag_index + 1
        if downward:
            stacked.append(jnp.pad(coeffs[lag_index], ((0, 0), (lag, 0)))[:, :length])
        else:
            stacked.append(jnp.pad(coeffs[lag_index], ((0, 0), (0, lag)))[:, lag:])
    return jnp.stack(stacked, axis=0)

def reference(control, filter_coeffs, conv_kernels, channel_order, point_cells, point_values, point_weights, orient_cells, orient_normals, orient_weights):
    channels, depth_cells, inline_rows, cross_cols = control.shape
    plane_cells = inline_rows * cross_cols
    source = control.reshape(channels, depth_cells, plane_cells)
    scaling = 1.0 - lax.optimization_barrier(jnp.sum(filter_coeffs, axis=0))
    root_scale = jnp.sqrt(scaling)
    filtered = recurse(root_scale[:, :, None] * source, filter_coeffs)
    smoothed = recurse((scaling[:, :, None] * filtered)[:, ::-1], filter_coeffs[:, :, ::-1])[:, ::-1]
    weights = mixing(conv_kernels, channel_order)
    potential = lateral(smoothed.reshape(control.shape), weights)
    flat_field = potential.reshape(channels, -1)
    cells = point_cells.reshape(3, -1)
    flat_index = (cells[0] * inline_rows + cells[1]) * cross_cols + cells[2]
    misfit = (flat_field[:, flat_index] - point_values.reshape(channels, -1)) * point_weights.reshape(-1)[None, :]
    forcing = jnp.zeros_like(flat_field).at[:, flat_index].add(misfit)
    ocells = orient_cells.reshape(3, -1)
    base_cell = (ocells[0] * inline_rows + ocells[1]) * cross_cols + ocells[2]
    normals = orient_normals.reshape(3, channels, -1)
    oweight = orient_weights.reshape(-1)[None, :]
    for component, stride in enumerate((plane_cells, cross_cols, 1)):
        mismatch = flat_field[:, base_cell + stride] - flat_field[:, base_cell] - normals[component]
        weighted = mismatch * oweight
        forcing = forcing.at[:, base_cell + stride].add(weighted)
        forcing = forcing.at[:, base_cell].add(-weighted)
    adjoint_weights = jnp.transpose(weights, (1, 0, 2, 3))[:, :, ::-1, ::-1]
    spread = lateral(forcing.reshape(control.shape), adjoint_weights).reshape(channels, depth_cells, plane_cells)
    adjoint_back = scaling[:, :, None] * recurse(spread, shifted(filter_coeffs, True))
    upper_coeffs = shifted(filter_coeffs, False)
    adjoint_fore = root_scale[:, :, None] * recurse(adjoint_back[:, ::-1], upper_coeffs[:, :, ::-1])[:, ::-1]
    gradient = control + adjoint_fore.reshape(control.shape)
    return (potential, gradient)
```

```python
import jax
import jax.numpy as jnp
from jax import lax
from jax.experimental import pallas as pl
from jax.experimental.pallas import tpu as pltpu
from jax.sharding import PartitionSpec as P

HIGHEST = lax.Precision.HIGHEST


def entering(value, axis, join, neutral, backward):
    count, mine = (lax.axis_size(axis), lax.axis_index(axis))
    pieces = jax.tree.map(lambda part: lax.all_gather(part, axis), value)
    if backward:
        pieces = jax.tree.map(lambda part: part[::-1], pieces)
        mine = count - 1 - mine
    so_far = jax.tree.map(
        lambda part, zero: jnp.full_like(part, 0) + jnp.asarray(zero, part.dtype), value, neutral
    )

    def hop(position, so_far):
        longer = join(so_far, jax.tree.map(lambda part: part[position], pieces))
        return jax.tree.map(lambda new, old: jnp.where(position < mine, new, old), longer, so_far)

    return lax.fori_loop(0, count - 1, hop, so_far)


def extended_2(cells, sides, width):
    for axis, dim in sides:
        count = lax.axis_size(axis)
        ends = count - 1
        head = lax.slice_in_dim(cells, 0, width, axis=dim)
        tail = lax.slice_in_dim(cells, cells.shape[dim] - width, cells.shape[dim], axis=dim)
        cells = jnp.concatenate(
            [
                lax.ppermute(tail, axis, [(i, (i + 1) % count) for i in range(ends)]),
                cells,
                lax.ppermute(head, axis, [((i + 1) % count, i) for i in range(ends)]),
            ],
            axis=dim,
        )
    return cells


def mixing(kernels, channel_order):
    groups = kernels.shape[0]
    group_size = kernels.shape[1]
    channels = groups * group_size
    slots = jnp.arange(channels, dtype=jnp.int32)
    chooser = (channel_order[:, None] == slots[None, :]).astype(jnp.float32)
    in_group = (
        slots[:, None] // group_size == jnp.arange(groups, dtype=jnp.int32)[None, :]
    ).astype(jnp.float32)
    in_place = (
        slots[:, None] % group_size == jnp.arange(group_size, dtype=jnp.int32)[None, :]
    ).astype(jnp.float32)
    block_mix = jnp.einsum(
        "sg,sa,tg,tb,gabhw->sthw",
        in_group,
        in_place,
        in_group,
        in_place,
        kernels,
        precision=HIGHEST,
    )
    return jnp.einsum("sc,td,sthw->cdhw", chooser, chooser, block_mix, precision=HIGHEST)


def padded_conv(padded, weights):
    return lax.conv_general_dilated(
        padded,
        weights,
        (1, 1),
        ((0, 0), (2, 2)),
        dimension_numbers=("CNHW", "OIHW", "CNHW"),
        precision=HIGHEST,
    )


def compose(earlier, later):
    first_map, first_shift = earlier
    second_map, second_shift = later
    joined_map = jnp.einsum("cnij,cnjk->cnik", second_map, first_map, precision=HIGHEST)
    joined_shift = (
        jnp.einsum("cnij,cnjk->cnik", second_map, first_shift, precision=HIGHEST) + second_shift
    )
    return (joined_map, joined_shift)


def build_tiles(coeffs, by_column, block_len):
    lead = coeffs.shape[1:3]
    lag_steps = jnp.arange(1, 5, dtype=jnp.int32)[:, None, None]
    if by_column:
        row_ids = jnp.arange(block_len + 4, dtype=jnp.int32)[None, :, None]
        col_ids = jnp.arange(block_len, dtype=jnp.int32)[None, None, :]
        picker = (row_ids == col_ids + lag_steps).astype(jnp.float32)
        extended = jnp.einsum("lcnk,lzk->cnzk", coeffs, picker, precision=HIGHEST)
        lower_tile = extended[:, :, :block_len, :]
        exit_map = extended[:, :, block_len:, :]
        entry_base = (
            jnp.arange(block_len, dtype=jnp.int32)[:, None]
            == jnp.arange(4, dtype=jnp.int32)[None, :]
        ).astype(jnp.float32)
        entry_map = jnp.broadcast_to(entry_base, lead + (block_len, 4))
    else:
        row_ids = jnp.arange(block_len, dtype=jnp.int32)[None, :, None]
        col_ids = jnp.arange(block_len + 4, dtype=jnp.int32)[None, None, :]
        picker = (col_ids == row_ids - lag_steps + 4).astype(jnp.float32)
        extended = jnp.einsum("lcnz,lzk->cnzk", coeffs, picker, precision=HIGHEST)
        lower_tile = extended[:, :, :, 4:]
        entry_map = extended[:, :, :, :4]
        exit_base = (
            jnp.arange(block_len, dtype=jnp.int32)[None, :]
            == jnp.arange(4, dtype=jnp.int32)[:, None] + block_len - 4
        ).astype(jnp.float32)
        exit_map = jnp.broadcast_to(exit_base, lead + (4, block_len))
    return (lower_tile, entry_map, exit_map)


def sweep_blocks(field, coeffs, by_column, upward, prefix):
    if upward:
        field = field[:, ::-1, ::-1]
        coeffs = coeffs[:, :, ::-1, ::-1]
    block_len = coeffs.shape[3]
    lower_tile, entry_map, exit_map = build_tiles(coeffs, by_column, block_len)
    identity_tile = jnp.eye(block_len, dtype=jnp.float32)
    inverse = identity_tile + lower_tile
    power = lower_tile
    power = jnp.einsum("cnij,cnjk->cnik", power, power, precision=HIGHEST)
    inverse = inverse + jnp.einsum("cnij,cnjk->cnik", inverse, power, precision=HIGHEST)
    reach_map = jnp.einsum("cnzk,cnkj->cnzj", inverse, entry_map, precision=HIGHEST)
    carry_map = jnp.einsum("cniz,cnzj->cnij", exit_map, reach_map, precision=HIGHEST)
    local_part = jnp.einsum("cnzk,cnkm->cnzm", inverse, field, precision=HIGHEST)
    carry_out = jnp.einsum("cniz,cnzm->cnim", exit_map, local_part, precision=HIGHEST)
    incoming = prefix((carry_map, carry_out), upward)
    result = local_part + jnp.einsum("cnzj,cnjm->cnzm", reach_map, incoming, precision=HIGHEST)
    if upward:
        result = result[:, ::-1, ::-1]
    return result


def shards(
    control,
    filter_coeffs,
    conv_kernels,
    channel_order,
    point_cells,
    point_values,
    point_weights,
    orient_cells,
    orient_normals,
    orient_weights,
):
    channels, block_len, inline_rows, cross_cols = control.shape
    plane_cells = inline_rows * cross_cols
    source = control.reshape(channels, block_len, plane_cells)
    coeffs = filter_coeffs[:, :, None, :]

    def to_blocks(field):
        return field[:, None]

    def from_blocks(field):
        return field[:, 0]

    def scaled(field, factor):
        return factor[..., None] * field

    def prefix(maps, upward):
        start = (
            jnp.broadcast_to(jnp.eye(4, dtype=jnp.float32), maps[0].shape),
            jnp.zeros_like(maps[1]),
        )
        return entering(maps, "depth", compose, start, upward)[1]

    scaling = 1.0 - jnp.sum(coeffs, axis=0)
    root_scale = jnp.sqrt(scaling)
    filtered = sweep_blocks(scaled(to_blocks(source), root_scale), coeffs, False, False, prefix)
    smoothed = sweep_blocks(scaled(filtered, scaling), coeffs, False, True, prefix)
    smoothed_field = from_blocks(smoothed).reshape(control.shape)
    weights = mixing(conv_kernels, channel_order)
    smoothed_padded = extended_2(smoothed_field, (("inline", 2),), 2)
    potential = padded_conv(smoothed_padded, weights)
    flat_field = potential.reshape(channels, -1)
    depth_base = lax.axis_index("depth") * block_len
    inline_base = lax.axis_index("inline") * inline_rows
    cells = point_cells.reshape(3, -1)
    flat_index = (
        (cells[0] - depth_base) * inline_rows + cells[1] - inline_base
    ) * cross_cols + cells[2]
    misfit = (
        flat_field[:, flat_index] - point_values.reshape(channels, -1)
    ) * point_weights.reshape(-1)[None, :]
    ocells = orient_cells.reshape(3, -1)
    base_cell = (
        (ocells[0] - depth_base) * inline_rows + ocells[1] - inline_base
    ) * cross_cols + ocells[2]
    normals = orient_normals.reshape(3, channels, -1)
    oweight = orient_weights.reshape(-1)[None, :]
    update_values = [misfit]
    update_cells = [flat_index]
    for component, stride in enumerate((plane_cells, cross_cols, 1)):
        mismatch = flat_field[:, base_cell + stride] - flat_field[:, base_cell] - normals[component]
        weighted = mismatch * oweight
        update_values.append(weighted)
        update_cells.append(base_cell + stride)
        update_values.append(-weighted)
        update_cells.append(base_cell)
    all_values = jnp.concatenate(update_values, axis=1)
    all_cells = jnp.concatenate(update_cells, axis=0)
    adjoint_weights = jnp.transpose(weights, (1, 0, 2, 3))[:, :, ::-1, ::-1]
    forcing = jnp.zeros_like(flat_field).at[:, all_cells].add(all_values)
    forcing_padded = extended_2(forcing.reshape(control.shape), (("inline", 2),), 2)
    spread = padded_conv(forcing_padded, adjoint_weights).reshape(channels, block_len, plane_cells)
    adjoint_back = scaled(sweep_blocks(to_blocks(spread), coeffs, True, False, prefix), scaling)
    adjoint_fore = scaled(sweep_blocks(adjoint_back, coeffs, True, True, prefix), root_scale)
    gradient = control + from_blocks(adjoint_fore).reshape(control.shape)
    return (potential, gradient)


CHUNK = 96
AT_VALUES, AT_NORMALS, AT_COEFFS, AT_MISC = 64, 72, 84, 88


def f32(*shape):
    return jax.ShapeDtypeStruct(shape, jnp.float32)


def in_vmem(count):
    return [pl.BlockSpec(memory_space=pltpu.VMEM) for _ in range(count)]


def lane_index(shape):
    return lax.broadcasted_iota(jnp.int32, shape, len(shape) - 1)


def pack_kernel(
    order, control, coeffs, values, normals, cells, weights, ocells, oweights, out, by_channel
):
    def flat_cell(ref):
        z, y, x = (ref[k, 0] for k in range(3))
        return (((y & 3) * 4 + (z & 3)) * 128 + x).astype(jnp.float32)

    flat, oflat = flat_cell(cells), flat_cell(ocells)
    weight = weights[0]
    misc = jnp.concatenate(
        [flat[:, :128], flat[:, 128:], oflat, weight[:, :128], weight[:, 128:], oweights[0]]
        + [jnp.zeros((2, 128), jnp.float32)],
        axis=0,
    )
    by_channel[...] = jnp.transpose(
        jnp.concatenate([coeffs[...], jnp.zeros((16, 96), jnp.float32)], axis=1)
    )
    for group in range(8):
        out[group, AT_MISC:CHUNK, :] = misc
    for slot in range(32):
        group, c = divmod(slot, 4)
        channel = order[slot]
        plane = control[channel]
        for z in range(4):
            row = z * 16 + c * 4
            out[group, row : row + 4, :] = plane[z * 4 : z * 4 + 4]
        row = AT_VALUES + 2 * c
        out[group, row : row + 2, :] = values[pl.ds(channel * 2, 2), :]
        for k in range(3):
            row = AT_NORMALS + 4 * k + c
            out[group, row : row + 1, :] = normals[pl.ds(k * 32 + channel, 1), :]
        row = AT_COEFFS + c
        out[group, row : row + 1, :16] = by_channel[pl.ds(channel, 1), :]


def coefficient(expanded, lag, z):
    block, local = divmod(z, 4)
    k = (lag - 1) * 4 + local
    return jnp.broadcast_to(expanded[block, :, k : k + 1], (16, 128))


def expand_coeffs(chunks, expanded, table, scale, root):
    for block in range(8):
        for c in range(4):
            row = AT_COEFFS + c
            expanded[block, 4 * c : 4 * c + 4, :] = jnp.broadcast_to(
                chunks[block, row : row + 1, :], (4, 128)
            )
    for z in range(32):
        lags = [coefficient(expanded, lag, z) for lag in range(1, 5)]
        for lag in range(4):
            table[z, lag] = lags[lag]
        scale[z] = 1.0 - ((lags[0] + lags[1]) + (lags[2] + lags[3]))
        root[z] = jnp.sqrt(scale[z])


def recurrence(source, factor, emit, order):
    history = []
    for t in order:
        total = source(t)
        for lag in range(len(history), 0, -1):
            before, value = history[lag - 1]
            total = total + factor(lag, t, before) * value
        history = [(t, total)] + history[:3]
        emit(t, total)


COEFF_SCRATCH = [
    pltpu.VMEM((8, 16, 128), jnp.float32),
    pltpu.VMEM((32, 4, 16, 128), jnp.float32),
    pltpu.VMEM((32, 16, 128), jnp.float32),
    pltpu.VMEM((32, 16, 128), jnp.float32),
]


def depth_rows(chunks, z):
    return chunks[z // 4, (z % 4) * 16 : (z % 4) * 16 + 16, :]


def smooth_kernel(chunks, smoothed, even, odd, expanded, table, scale, root, first, rows):
    expand_coeffs(chunks, expanded, table, scale, root)

    def keep_first(z, value):
        first[z] = scale[z] * value

    def keep_rows(z, value):
        rows[z * 16 : z * 16 + 16, :] = value

    recurrence(
        lambda z: root[z] * depth_rows(chunks, z),
        lambda lag, z, before: table[z, lag - 1],
        keep_first,
        range(32),
    )
    recurrence(
        lambda z: first[z],
        lambda lag, z, before: table[z, lag - 1],
        keep_rows,
        range(31, -1, -1),
    )
    parity = lax.axis_index("inline") % 2
    for y in range(4):
        for c in range(4):
            smoothed[y, c] = rows[pl.ds(c * 4 + y, 32, stride=16), :]
    for y in range(2):
        even[y] = smoothed[2 - 2 * parity + y]
        odd[y] = smoothed[2 * parity + y]


def tap(table, a, b, h, w):
    row = ((a * 5 + h) * 5 + w) * 4 + b
    return jnp.broadcast_to(table[row : row + 1, :], (8, 128))


def conv_rows(read, rows_in, start, table, adjoint, write):
    lane = lane_index((8, 128))

    def moved(value, shift):
        if shift == 0:
            return value
        inside = lane >= -shift if shift < 0 else lane < 128 - shift
        return jnp.where(inside, pltpu.roll(value, -shift % 128, 1), 0.0)

    def some_depths(k, carry):
        depths = pl.ds(pl.multiple_of(k * 8, 8), 8)
        total = [[start(y, o, depths) for o in range(4)] for y in range(4)]
        for i in range(4):
            lines = {row: read(row, i, depths) for row in rows_in}
            for w in range(5):
                if adjoint:
                    taps = [[tap(table, i, o, h, w) for h in range(5)] for o in range(4)]
                else:
                    taps = [[tap(table, o, i, h, w) for h in range(5)] for o in range(4)]
                for row in rows_in:
                    line = moved(lines[row], 2 - w if adjoint else w - 2)
                    for y in range(4):
                        h = y - row + 2 if adjoint else row - y + 2
                        if 0 <= h < 5:
                            for o in range(4):
                                total[y][o] = total[y][o] + taps[o][h] * line
        for y in range(4):
            for o in range(4):
                write(y, o, depths, total[y][o])
        return carry

    lax.fori_loop(0, 4, some_depths, 0)


OWN = (0, 1, 2, 3)
HALO = (-2, -1, 4, 5)


def halo_reader(even, odd):
    parity = lax.axis_index("inline") % 2

    def read(row, c, depths):
        y = row + 2 if row < 0 else row - 4
        through_even, through_odd = even[y, c, depths, :], odd[y, c, depths, :]
        below = parity == 1 if row < 0 else parity == 0
        return jnp.where(below, through_even, through_odd)

    return read


def split(value):
    high = value.astype(jnp.bfloat16)
    return high, (value - high.astype(jnp.float32)).astype(jnp.bfloat16)


def point_fields(chunks, constant, weight, oweight):
    row = lax.broadcasted_iota(jnp.int32, (16, 256), 0)
    orow = lax.broadcasted_iota(jnp.int32, (16, 128), 0)
    column = lax.broadcasted_iota(jnp.int32, (128, 384), 0)
    for block in range(8):

        def line(k, block=block):
            return chunks[block, k : k + 1, :]

        def double(k, line=line):
            return jnp.concatenate([line(k), line(k + 1)], axis=1)

        flat = double(AT_MISC).astype(jnp.int32)
        oflat = line(AT_MISC + 2).astype(jnp.int32)
        w, ow = double(AT_MISC + 3), line(AT_MISC + 5)
        cell, ocell = flat >> 7, oflat >> 7
        at_cross = jnp.concatenate([flat & 127, oflat & 127], axis=1)
        columns = (column == at_cross).astype(jnp.float32).astype(jnp.bfloat16)
        here, ohere = row == cell, orow == ocell
        below, beside = orow == ocell + 1, orow == ocell + 4
        main, along = [], []
        for c in range(4):
            value = w * double(AT_VALUES + 2 * c)
            n0, n1, n2 = (ow * line(AT_NORMALS + 4 * k + c) for k in range(3))
            placed = (
                jnp.where(below, n0, 0.0)
                + jnp.where(beside, n1, 0.0)
                - jnp.where(ohere, n0 + n1 + n2, 0.0)
            )
            main.append(jnp.concatenate([jnp.where(here, value, 0.0), placed], axis=1))
            along.append(
                jnp.concatenate([jnp.zeros((16, 256), jnp.float32), jnp.where(ohere, n2, 0.0)], axis=1)
            )
        both = [
            jnp.concatenate([jnp.where(here, w, 0.0), jnp.zeros((16, 128), jnp.float32)], axis=1),
            jnp.concatenate([jnp.zeros((16, 256), jnp.float32), jnp.where(ohere, ow, 0.0)], axis=1),
        ]
        high, low = split(jnp.concatenate(main + both + along, axis=0))
        sums = lax.dot_general(
            jnp.concatenate([high, low], axis=0),
            columns,
            (((1,), (1,)), ((), ())),
            preferred_element_type=jnp.float32,
        )
        sums = sums[:160] + sums[160:]
        moved = pltpu.roll(sums[96:160], 1, 1)
        z = 4 * block
        for y in range(4):
            for c in range(4):
                k = 16 * c + 4 * y
                constant[y, c, z : z + 4, :] = sums[k : k + 4] + moved[k : k + 4]
            weight[y, z : z + 4, :] = sums[64 + 4 * y : 68 + 4 * y]
            oweight[y, z : z + 4, :] = sums[80 + 4 * y : 84 + 4 * y]


def own_kernel(chunks, smoothed, kernels, partial, constant, weight, oweight, table):
    group = lax.axis_index("depth")
    picked = jnp.where(lane_index((400, 8)) == group, kernels[...], 0.0)
    table[...] = jnp.broadcast_to(jnp.sum(picked, axis=1, keepdims=True), (400, 128))
    point_fields(chunks, constant, weight, oweight)

    def write(y, o, depths, value):
        partial[y, o, depths, :] = value

    conv_rows(
        lambda row, c, depths: smoothed[row, c, depths, :],
        OWN,
        lambda y, o, depths: jnp.zeros((8, 128), jnp.float32),
        table,
        False,
        write,
    )


def forcing_kernel(
    partial, even_in, odd_in, table, constant, weight, oweight, potential, forcing, even, odd
):
    def write(y, o, depths, value):
        potential[y, o, depths, :] = value

    conv_rows(
        halo_reader(even_in, odd_in),
        HALO,
        lambda y, o, depths: partial[y, o, depths, :],
        table,
        False,
        write,
    )

    def one_channel(c, carry):
        lines = [potential[y, c] for y in range(4)]
        sums = [weight[y] * lines[y] - constant[y, c] for y in range(4)]
        for y in range(4):
            share = oweight[y]
            deeper = share * (pltpu.roll(lines[y], 31, 0) - lines[y])
            across = share * (pltpu.roll(lines[y], 127, 1) - lines[y])
            sums[y] = sums[y] - deeper + pltpu.roll(deeper, 1, 0)
            sums[y] = sums[y] - across + pltpu.roll(across, 1, 1)
            if y < 3:
                beside = share * (lines[y + 1] - lines[y])
                sums[y] = sums[y] - beside
                sums[y + 1] = sums[y + 1] + beside
        for y in range(4):
            forcing[y, c] = sums[y]
        return carry

    lax.fori_loop(0, 4, one_channel, 0)
    parity = lax.axis_index("inline") % 2
    for y in range(2):
        even[y] = forcing[2 - 2 * parity + y]
        odd[y] = forcing[2 * parity + y]


def spread_kernel(forcing, table, partial):
    def write(y, o, depths, value):
        partial[y, o, depths, :] = value

    conv_rows(
        lambda row, c, depths: forcing[row, c, depths, :],
        OWN,
        lambda y, o, depths: jnp.zeros((8, 128), jnp.float32),
        table,
        True,
        write,
    )


def gradient_kernel(
    chunks, partial, even_in, odd_in, taps, potential, out, expanded, table, scale, root, first, rows
):
    expand_coeffs(chunks, expanded, table, scale, root)
    for y in range(4):
        for c in range(4):
            rows[pl.ds((c * 4 + y) * 32, 32), :] = potential[y, c]
    for z in range(32):
        out[z // 4, (z % 4) * 16 : (z % 4) * 16 + 16, :] = rows[pl.ds(z, 16, stride=32), :]

    def write(y, o, depths, value):
        rows[pl.ds(pl.multiple_of((o * 4 + y) * 32 + depths.start, 8), 8), :] = value

    conv_rows(
        halo_reader(even_in, odd_in),
        HALO,
        lambda y, o, depths: partial[y, o, depths, :],
        taps,
        True,
        write,
    )

    def keep_first(z, value):
        first[z] = scale[z] * value

    def keep_out(z, value):
        row = 64 + (z % 4) * 16
        out[z // 4, row : row + 16, :] = depth_rows(chunks, z) + root[z] * value

    recurrence(
        lambda z: rows[pl.ds(z, 16, stride=32), :],
        lambda lag, z, before: table[before, lag - 1],
        keep_first,
        range(32),
    )
    recurrence(
        lambda z: first[z],
        lambda lag, z, before: table[before, lag - 1],
        keep_out,
        range(31, -1, -1),
    )


def unpack_kernel(order, chunks, potential, gradient):
    for slot in range(32):
        group, c = divmod(slot, 4)
        channel = order[slot]
        for out, base in ((potential, 0), (gradient, 64)):
            pieces = [
                chunks[group, base + z * 16 + c * 4 : base + z * 16 + c * 4 + 4, :] for z in range(4)
            ]
            out[channel] = jnp.concatenate(pieces, axis=0)


def swapped(even, odd):
    count = lax.axis_size("inline")

    def pairs(first):
        below = [(i, i + 1) for i in range(first, count - 1, 2)]
        return below + [(j, i) for i, j in below]

    return lax.ppermute(even, "inline", pairs(0)), lax.ppermute(odd, "inline", pairs(1))


def by_group(
    control,
    filter_coeffs,
    conv_kernels,
    channel_order,
    point_cells,
    point_values,
    point_weights,
    orient_cells,
    orient_normals,
    orient_weights,
):
    params = pltpu.CompilerParams(vmem_limit_bytes=48 << 20)
    in_smem = pl.BlockSpec(memory_space=pltpu.SMEM)

    def call(kernel, outs, operands, scratch=(), first=None):
        specs = in_vmem(len(operands))
        if first is not None:
            specs[0] = first
        return pl.pallas_call(
            kernel,
            out_shape=outs,
            in_specs=specs,
            out_specs=jax.tree.map(lambda _: pl.BlockSpec(memory_space=pltpu.VMEM), outs),
            scratch_shapes=list(scratch),
            compiler_params=params,
        )(*operands)

    chunks = call(
        pack_kernel,
        f32(8, CHUNK, 128),
        (
            channel_order,
            control.reshape(32, 16, 128),
            jnp.transpose(filter_coeffs, (0, 2, 1)).reshape(16, 32),
            point_values.reshape(64, 128),
            orient_normals.reshape(96, 128),
            point_cells,
            point_weights,
            orient_cells,
            orient_weights,
        ),
        (pltpu.VMEM((128, 16), jnp.float32),),
        in_smem,
    )
    chunks = lax.all_to_all(chunks, "depth", 0, 0)
    field, edge, plane = f32(4, 4, 32, 128), f32(2, 4, 32, 128), f32(4, 32, 128)
    rows = pltpu.VMEM((512, 128), jnp.float32)
    first = pltpu.VMEM((32, 16, 128), jnp.float32)
    smoothed, even, odd = call(
        smooth_kernel, (field, edge, edge), (chunks,), COEFF_SCRATCH + [first, rows]
    )
    even, odd = swapped(even, odd)
    kernels = jnp.transpose(conv_kernels, (1, 3, 4, 2, 0)).reshape(400, 8)
    partial, constant, weight, oweight, taps = call(
        own_kernel, (field, field, plane, plane, f32(400, 128)), (chunks, smoothed, kernels)
    )
    potential, forcing, even, odd = call(
        forcing_kernel,
        (field, field, edge, edge),
        (partial, even, odd, taps, constant, weight, oweight),
    )
    even, odd = swapped(even, odd)
    partial = call(spread_kernel, field, (forcing, taps))
    results = call(
        gradient_kernel,
        f32(8, 128, 128),
        (chunks, partial, even, odd, taps, potential),
        COEFF_SCRATCH + [first, rows],
    )
    results = lax.all_to_all(results, "depth", 0, 0)
    block = f32(32, 16, 128)
    potential, gradient = call(
        unpack_kernel, (block, block), (channel_order, results), (), in_smem
    )
    return potential.reshape(control.shape), gradient.reshape(control.shape)


def solution(mesh):
    placed = (
        P(None, "depth", "inline", None),
        P(None, None, "depth"),
        P(),
        P(),
        P(None, "depth", "inline", None),
        P(None, "depth", "inline", None),
        P("depth", "inline", None),
        P(None, "depth", "inline", None),
        P(None, None, "depth", "inline", None),
        P("depth", "inline", None),
    )

    def body(control, filter_coeffs, conv_kernels, *rest):
        groups, block = conv_kernels.shape, control.shape
        fits = groups[:3] == (mesh.shape["depth"], 4, 4) and groups[0] == 8
        if fits and block == (32, 4, 4, 128):
            return by_group(control, filter_coeffs, conv_kernels, *rest)
        return shards(control, filter_coeffs, conv_kernels, *rest)

    return jax.shard_map(
        body,
        mesh=mesh,
        in_specs=placed,
        out_specs=(P(None, "depth", "inline", None), P(None, "depth", "inline", None)),
        check_vma=False,
    )
```

```python
import jax
import jax.numpy as jnp
from jax import lax
from jax.experimental import pallas as pl
from jax.experimental.pallas import tpu as pltpu
from jax.sharding import PartitionSpec as P

HIGHEST = lax.Precision.HIGHEST


def entering(value, axis, join, neutral, backward):
    count, mine = (lax.axis_size(axis), lax.axis_index(axis))
    pieces = jax.tree.map(lambda part: lax.all_gather(part, axis), value)
    if backward:
        pieces = jax.tree.map(lambda part: part[::-1], pieces)
        mine = count - 1 - mine
    so_far = jax.tree.map(
        lambda part, zero: jnp.full_like(part, 0) + jnp.asarray(zero, part.dtype), value, neutral
    )

    def hop(position, so_far):
        longer = join(so_far, jax.tree.map(lambda part: part[position], pieces))
        return jax.tree.map(lambda new, old: jnp.where(position < mine, new, old), longer, so_far)

    return lax.fori_loop(0, count - 1, hop, so_far)


def extended_2(cells, sides, width):
    for axis, dim in sides:
        count = lax.axis_size(axis)
        ends = count - 1
        head = lax.slice_in_dim(cells, 0, width, axis=dim)
        tail = lax.slice_in_dim(cells, cells.shape[dim] - width, cells.shape[dim], axis=dim)
        cells = jnp.concatenate(
            [
                lax.ppermute(tail, axis, [(i, (i + 1) % count) for i in range(ends)]),
                cells,
                lax.ppermute(head, axis, [((i + 1) % count, i) for i in range(ends)]),
            ],
            axis=dim,
        )
    return cells


def mixing(kernels, channel_order):
    groups = kernels.shape[0]
    group_size = kernels.shape[1]
    channels = groups * group_size
    slots = jnp.arange(channels, dtype=jnp.int32)
    chooser = (channel_order[:, None] == slots[None, :]).astype(jnp.float32)
    in_group = (
        slots[:, None] // group_size == jnp.arange(groups, dtype=jnp.int32)[None, :]
    ).astype(jnp.float32)
    in_place = (
        slots[:, None] % group_size == jnp.arange(group_size, dtype=jnp.int32)[None, :]
    ).astype(jnp.float32)
    block_mix = jnp.einsum(
        "sg,sa,tg,tb,gabhw->sthw",
        in_group,
        in_place,
        in_group,
        in_place,
        kernels,
        precision=HIGHEST,
    )
    return jnp.einsum("sc,td,sthw->cdhw", chooser, chooser, block_mix, precision=HIGHEST)


def padded_conv(padded, weights):
    return lax.conv_general_dilated(
        padded,
        weights,
        (1, 1),
        ((0, 0), (2, 2)),
        dimension_numbers=("CNHW", "OIHW", "CNHW"),
        precision=HIGHEST,
    )


def compose(earlier, later):
    first_map, first_shift = earlier
    second_map, second_shift = later
    joined_map = jnp.einsum("cnij,cnjk->cnik", second_map, first_map, precision=HIGHEST)
    joined_shift = (
        jnp.einsum("cnij,cnjk->cnik", second_map, first_shift, precision=HIGHEST) + second_shift
    )
    return (joined_map, joined_shift)


def build_tiles(coeffs, by_column, block_len):
    lead = coeffs.shape[1:3]
    lag_steps = jnp.arange(1, 5, dtype=jnp.int32)[:, None, None]
    if by_column:
        row_ids = jnp.arange(block_len + 4, dtype=jnp.int32)[None, :, None]
        col_ids = jnp.arange(block_len, dtype=jnp.int32)[None, None, :]
        picker = (row_ids == col_ids + lag_steps).astype(jnp.float32)
        extended = jnp.einsum("lcnk,lzk->cnzk", coeffs, picker, precision=HIGHEST)
        lower_tile = extended[:, :, :block_len, :]
        exit_map = extended[:, :, block_len:, :]
        entry_base = (
            jnp.arange(block_len, dtype=jnp.int32)[:, None]
            == jnp.arange(4, dtype=jnp.int32)[None, :]
        ).astype(jnp.float32)
        entry_map = jnp.broadcast_to(entry_base, lead + (block_len, 4))
    else:
        row_ids = jnp.arange(block_len, dtype=jnp.int32)[None, :, None]
        col_ids = jnp.arange(block_len + 4, dtype=jnp.int32)[None, None, :]
        picker = (col_ids == row_ids - lag_steps + 4).astype(jnp.float32)
        extended = jnp.einsum("lcnz,lzk->cnzk", coeffs, picker, precision=HIGHEST)
        lower_tile = extended[:, :, :, 4:]
        entry_map = extended[:, :, :, :4]
        exit_base = (
            jnp.arange(block_len, dtype=jnp.int32)[None, :]
            == jnp.arange(4, dtype=jnp.int32)[:, None] + block_len - 4
        ).astype(jnp.float32)
        exit_map = jnp.broadcast_to(exit_base, lead + (4, block_len))
    return (lower_tile, entry_map, exit_map)


def sweep_blocks(field, coeffs, by_column, upward, prefix):
    if upward:
        field = field[:, ::-1, ::-1]
        coeffs = coeffs[:, :, ::-1, ::-1]
    block_len = coeffs.shape[3]
    lower_tile, entry_map, exit_map = build_tiles(coeffs, by_column, block_len)
    identity_tile = jnp.eye(block_len, dtype=jnp.float32)
    inverse = identity_tile + lower_tile
    power = lower_tile
    power = jnp.einsum("cnij,cnjk->cnik", power, power, precision=HIGHEST)
    inverse = inverse + jnp.einsum("cnij,cnjk->cnik", inverse, power, precision=HIGHEST)
    reach_map = jnp.einsum("cnzk,cnkj->cnzj", inverse, entry_map, precision=HIGHEST)
    carry_map = jnp.einsum("cniz,cnzj->cnij", exit_map, reach_map, precision=HIGHEST)
    local_part = jnp.einsum("cnzk,cnkm->cnzm", inverse, field, precision=HIGHEST)
    carry_out = jnp.einsum("cniz,cnzm->cnim", exit_map, local_part, precision=HIGHEST)
    incoming = prefix((carry_map, carry_out), upward)
    result = local_part + jnp.einsum("cnzj,cnjm->cnzm", reach_map, incoming, precision=HIGHEST)
    if upward:
        result = result[:, ::-1, ::-1]
    return result


def shards(
    control,
    filter_coeffs,
    conv_kernels,
    channel_order,
    point_cells,
    point_values,
    point_weights,
    orient_cells,
    orient_normals,
    orient_weights,
):
    channels, block_len, inline_rows, cross_cols = control.shape
    plane_cells = inline_rows * cross_cols
    source = control.reshape(channels, block_len, plane_cells)
    coeffs = filter_coeffs[:, :, None, :]

    def to_blocks(field):
        return field[:, None]

    def from_blocks(field):
        return field[:, 0]

    def scaled(field, factor):
        return factor[..., None] * field

    def prefix(maps, upward):
        start = (
            jnp.broadcast_to(jnp.eye(4, dtype=jnp.float32), maps[0].shape),
            jnp.zeros_like(maps[1]),
        )
        return entering(maps, "depth", compose, start, upward)[1]

    scaling = 1.0 - jnp.sum(coeffs, axis=0)
    root_scale = jnp.sqrt(scaling)
    filtered = sweep_blocks(scaled(to_blocks(source), root_scale), coeffs, False, False, prefix)
    smoothed = sweep_blocks(scaled(filtered, scaling), coeffs, False, True, prefix)
    smoothed_field = from_blocks(smoothed).reshape(control.shape)
    weights = mixing(conv_kernels, channel_order)
    smoothed_padded = extended_2(smoothed_field, (("inline", 2),), 2)
    potential = padded_conv(smoothed_padded, weights)
    flat_field = potential.reshape(channels, -1)
    depth_base = lax.axis_index("depth") * block_len
    inline_base = lax.axis_index("inline") * inline_rows
    cells = point_cells.reshape(3, -1)
    flat_index = (
        (cells[0] - depth_base) * inline_rows + cells[1] - inline_base
    ) * cross_cols + cells[2]
    misfit = (
        flat_field[:, flat_index] - point_values.reshape(channels, -1)
    ) * point_weights.reshape(-1)[None, :]
    ocells = orient_cells.reshape(3, -1)
    base_cell = (
        (ocells[0] - depth_base) * inline_rows + ocells[1] - inline_base
    ) * cross_cols + ocells[2]
    normals = orient_normals.reshape(3, channels, -1)
    oweight = orient_weights.reshape(-1)[None, :]
    update_values = [misfit]
    update_cells = [flat_index]
    for component, stride in enumerate((plane_cells, cross_cols, 1)):
        mismatch = flat_field[:, base_cell + stride] - flat_field[:, base_cell] - normals[component]
        weighted = mismatch * oweight
        update_values.append(weighted)
        update_cells.append(base_cell + stride)
        update_values.append(-weighted)
        update_cells.append(base_cell)
    all_values = jnp.concatenate(update_values, axis=1)
    all_cells = jnp.concatenate(update_cells, axis=0)
    adjoint_weights = jnp.transpose(weights, (1, 0, 2, 3))[:, :, ::-1, ::-1]
    forcing = jnp.zeros_like(flat_field).at[:, all_cells].add(all_values)
    forcing_padded = extended_2(forcing.reshape(control.shape), (("inline", 2),), 2)
    spread = padded_conv(forcing_padded, adjoint_weights).reshape(channels, block_len, plane_cells)
    adjoint_back = scaled(sweep_blocks(to_blocks(spread), coeffs, True, False, prefix), scaling)
    adjoint_fore = scaled(sweep_blocks(adjoint_back, coeffs, True, True, prefix), root_scale)
    gradient = control + from_blocks(adjoint_fore).reshape(control.shape)
    return (potential, gradient)


CHUNK = 96
AT_VALUES, AT_NORMALS, AT_COEFFS, AT_MISC = 64, 72, 84, 88


def f32(*shape):
    return jax.ShapeDtypeStruct(shape, jnp.float32)


def lane_index(shape):
    return lax.broadcasted_iota(jnp.int32, shape, len(shape) - 1)


def pack_kernel(*refs):
    sources, out, by_channel, arrived, held = refs[:9], refs[9], refs[10], refs[11], refs[12:]
    copies = [
        pltpu.make_async_copy(source, target, arrived.at[k])
        for k, (source, target) in enumerate(zip(sources, held))
    ]
    for copy in copies:
        copy.start()
    order, coeffs, values, normals, cells, weights, ocells, oweights, control = held

    def flat_cell(ref):
        z, y, x = (ref[k, 0] for k in range(3))
        return (((y & 3) * 4 + (z & 3)) * 128 + x).astype(jnp.float32)

    for copy in copies[:-1]:
        copy.wait()
    flat, oflat = flat_cell(cells), flat_cell(ocells)
    weight = weights[0]
    misc = jnp.concatenate(
        [flat[:, :128], flat[:, 128:], oflat, weight[:, :128], weight[:, 128:], oweights[0]]
        + [jnp.zeros((2, 128), jnp.float32)],
        axis=0,
    )
    by_channel[...] = jnp.transpose(
        jnp.concatenate([coeffs[...], jnp.zeros((16, 96), jnp.float32)], axis=1)
    )
    for group in range(8):
        out[group, AT_MISC:CHUNK, :] = misc
    for slot in range(32):
        group, c = divmod(slot, 4)
        channel = order[slot]
        row = AT_VALUES + 2 * c
        out[group, row : row + 2, :] = values[pl.ds(channel * 2, 2), :]
        for k in range(3):
            row = AT_NORMALS + 4 * k + c
            out[group, row : row + 1, :] = normals[pl.ds(k * 32 + channel, 1), :]
        row = AT_COEFFS + c
        out[group, row : row + 1, :16] = by_channel[pl.ds(channel, 1), :]
    copies[-1].wait()
    for slot in range(32):
        group, c = divmod(slot, 4)
        plane = control[order[slot]]
        for z in range(4):
            row = z * 16 + c * 4
            out[group, row : row + 4, :] = plane[z * 4 : z * 4 + 4]


def coefficient(expanded, lag, z):
    block, local = divmod(z, 4)
    k = (lag - 1) * 4 + local
    return jnp.broadcast_to(expanded[block, :, k : k + 1], (16, 128))


def expand_coeffs(chunks, expanded, table, scale, root):
    for block in range(8):
        for c in range(4):
            row = AT_COEFFS + c
            expanded[block, 4 * c : 4 * c + 4, :] = jnp.broadcast_to(
                chunks[block, row : row + 1, :], (4, 128)
            )
    for z in range(32):
        lags = [coefficient(expanded, lag, z) for lag in range(1, 5)]
        for lag in range(4):
            table[z, lag] = lags[lag]
        scale[z] = 1.0 - ((lags[0] + lags[1]) + (lags[2] + lags[3]))
        root[z] = jnp.sqrt(scale[z])


def recurrence(source, factor, emit, order):
    history = []
    for t in order:
        total = source(t)
        for lag in range(len(history), 0, -1):
            before, value = history[lag - 1]
            total = total + factor(lag, t, before) * value
        history = [(t, total)] + history[:3]
        emit(t, total)


def depth_rows(chunks, z):
    return chunks[z // 4, (z % 4) * 16 : (z % 4) * 16 + 16, :]


def smooth_kernel(chunks, smoothed, even, odd, table, scale, root, expanded, first, rows):
    expand_coeffs(chunks, expanded, table, scale, root)

    def keep_first(z, value):
        first[z] = scale[z] * value

    def keep_rows(z, value):
        rows[z * 16 : z * 16 + 16, :] = value

    recurrence(
        lambda z: root[z] * depth_rows(chunks, z),
        lambda lag, z, before: table[z, lag - 1],
        keep_first,
        range(32),
    )
    recurrence(
        lambda z: first[z],
        lambda lag, z, before: table[z, lag - 1],
        keep_rows,
        range(31, -1, -1),
    )
    parity = lax.axis_index("inline") % 2
    for y in range(4):
        for c in range(4):
            smoothed[y, c] = rows[pl.ds(c * 4 + y, 32, stride=16), :]
    for y in range(2):
        even[y] = smoothed[2 - 2 * parity + y]
        odd[y] = smoothed[2 * parity + y]


def tap(table, a, b, h, w):
    row = ((a * 5 + h) * 5 + w) * 4 + b
    return jnp.broadcast_to(table[row : row + 1, :], (8, 128))


def conv_rows(read, rows_in, start, table, adjoint, write):
    lane = lane_index((8, 128))

    def moved(value, shift):
        if shift == 0:
            return value
        inside = lane >= -shift if shift < 0 else lane < 128 - shift
        return jnp.where(inside, pltpu.roll(value, -shift % 128, 1), 0.0)

    def some_depths(k, carry):
        depths = pl.ds(pl.multiple_of(k * 8, 8), 8)
        total = [[start(y, o, depths) for o in range(4)] for y in range(4)]
        for i in range(4):
            lines = {row: read(row, i, depths) for row in rows_in}
            for w in range(5):
                if adjoint:
                    taps = [[tap(table, i, o, h, w) for h in range(5)] for o in range(4)]
                else:
                    taps = [[tap(table, o, i, h, w) for h in range(5)] for o in range(4)]
                for row in rows_in:
                    line = moved(lines[row], 2 - w if adjoint else w - 2)
                    for y in range(4):
                        h = y - row + 2 if adjoint else row - y + 2
                        if 0 <= h < 5:
                            for o in range(4):
                                total[y][o] = total[y][o] + taps[o][h] * line
        for y in range(4):
            for o in range(4):
                write(y, o, depths, total[y][o])
        return carry

    lax.fori_loop(0, 4, some_depths, 0)


OWN = (0, 1, 2, 3)
HALO = (-2, -1, 4, 5)


def halo_reader(even, odd):
    parity = lax.axis_index("inline") % 2

    def read(row, c, depths):
        y = row + 2 if row < 0 else row - 4
        through_even, through_odd = even[y, c, depths, :], odd[y, c, depths, :]
        below = parity == 1 if row < 0 else parity == 0
        return jnp.where(below, through_even, through_odd)

    return read


def split(value):
    high = value.astype(jnp.bfloat16)
    return high, (value - high.astype(jnp.float32)).astype(jnp.bfloat16)


def point_fields(chunks, constant, weight, oweight):
    row = lax.broadcasted_iota(jnp.int32, (16, 256), 0)
    orow = lax.broadcasted_iota(jnp.int32, (16, 128), 0)
    column = lax.broadcasted_iota(jnp.int32, (128, 384), 0)
    for block in range(8):

        def line(k, block=block):
            return chunks[block, k : k + 1, :]

        def double(k, line=line):
            return jnp.concatenate([line(k), line(k + 1)], axis=1)

        flat = double(AT_MISC).astype(jnp.int32)
        oflat = line(AT_MISC + 2).astype(jnp.int32)
        w, ow = double(AT_MISC + 3), line(AT_MISC + 5)
        cell, ocell = flat >> 7, oflat >> 7
        at_cross = jnp.concatenate([flat & 127, oflat & 127], axis=1)
        columns = (column == at_cross).astype(jnp.float32).astype(jnp.bfloat16)
        here, ohere = row == cell, orow == ocell
        below, beside = orow == ocell + 1, orow == ocell + 4
        main, along = [], []
        for c in range(4):
            value = w * double(AT_VALUES + 2 * c)
            n0, n1, n2 = (ow * line(AT_NORMALS + 4 * k + c) for k in range(3))
            placed = (
                jnp.where(below, n0, 0.0)
                + jnp.where(beside, n1, 0.0)
                - jnp.where(ohere, n0 + n1 + n2, 0.0)
            )
            main.append(jnp.concatenate([jnp.where(here, value, 0.0), placed], axis=1))
            along.append(
                jnp.concatenate([jnp.zeros((16, 256), jnp.float32), jnp.where(ohere, n2, 0.0)], axis=1)
            )
        both = [
            jnp.concatenate([jnp.where(here, w, 0.0), jnp.zeros((16, 128), jnp.float32)], axis=1),
            jnp.concatenate([jnp.zeros((16, 256), jnp.float32), jnp.where(ohere, ow, 0.0)], axis=1),
        ]
        high, low = split(jnp.concatenate(main + both + along, axis=0))
        sums = lax.dot_general(
            jnp.concatenate([high, low], axis=0),
            columns,
            (((1,), (1,)), ((), ())),
            preferred_element_type=jnp.float32,
        )
        sums = sums[:160] + sums[160:]
        moved = pltpu.roll(sums[96:160], 1, 1)
        z = 4 * block
        for y in range(4):
            for c in range(4):
                k = 16 * c + 4 * y
                constant[y, c, z : z + 4, :] = sums[k : k + 4] + moved[k : k + 4]
            weight[y, z : z + 4, :] = sums[64 + 4 * y : 68 + 4 * y]
            oweight[y, z : z + 4, :] = sums[80 + 4 * y : 84 + 4 * y]


def own_kernel(chunks, smoothed, kernels, partial, constant, weight, oweight, table):
    group = lax.axis_index("depth")
    picked = jnp.where(lane_index((400, 8)) == group, kernels[...], 0.0)
    table[...] = jnp.broadcast_to(jnp.sum(picked, axis=1, keepdims=True), (400, 128))
    point_fields(chunks, constant, weight, oweight)

    def write(y, o, depths, value):
        partial[y, o, depths, :] = value

    conv_rows(
        lambda row, c, depths: smoothed[row, c, depths, :],
        OWN,
        lambda y, o, depths: jnp.zeros((8, 128), jnp.float32),
        table,
        False,
        write,
    )


def forcing_kernel(
    partial, even_in, odd_in, table, constant, weight, oweight, potential, forcing, even, odd
):
    def write(y, o, depths, value):
        potential[y, o, depths, :] = value

    conv_rows(
        halo_reader(even_in, odd_in),
        HALO,
        lambda y, o, depths: partial[y, o, depths, :],
        table,
        False,
        write,
    )

    def one_channel(c, carry):
        lines = [potential[y, c] for y in range(4)]
        sums = [weight[y] * lines[y] - constant[y, c] for y in range(4)]
        for y in range(4):
            share = oweight[y]
            deeper = share * (pltpu.roll(lines[y], 31, 0) - lines[y])
            across = share * (pltpu.roll(lines[y], 127, 1) - lines[y])
            sums[y] = sums[y] - deeper + pltpu.roll(deeper, 1, 0)
            sums[y] = sums[y] - across + pltpu.roll(across, 1, 1)
            if y < 3:
                beside = share * (lines[y + 1] - lines[y])
                sums[y] = sums[y] - beside
                sums[y + 1] = sums[y + 1] + beside
        for y in range(4):
            forcing[y, c] = sums[y]
        return carry

    lax.fori_loop(0, 4, one_channel, 0)
    parity = lax.axis_index("inline") % 2
    for y in range(2):
        even[y] = forcing[2 - 2 * parity + y]
        odd[y] = forcing[2 * parity + y]


def spread_kernel(forcing, table, potential, partial, out, rows):
    def write(y, o, depths, value):
        partial[y, o, depths, :] = value

    conv_rows(
        lambda row, c, depths: forcing[row, c, depths, :],
        OWN,
        lambda y, o, depths: jnp.zeros((8, 128), jnp.float32),
        table,
        True,
        write,
    )
    for y in range(4):
        for c in range(4):
            rows[pl.ds((c * 4 + y) * 32, 32), :] = potential[y, c]
    for z in range(32):
        out[z // 4, (z % 4) * 16 : (z % 4) * 16 + 16, :] = rows[pl.ds(z, 16, stride=32), :]


def gradient_kernel(
    results, chunks, partial, even_in, odd_in, taps, table, scale, root, out, first, rows
):
    def write(y, o, depths, value):
        rows[pl.ds(pl.multiple_of((o * 4 + y) * 32 + depths.start, 8), 8), :] = value

    conv_rows(
        halo_reader(even_in, odd_in),
        HALO,
        lambda y, o, depths: partial[y, o, depths, :],
        taps,
        True,
        write,
    )

    def keep_first(z, value):
        first[z] = scale[z] * value

    def keep_out(z, value):
        row = 64 + (z % 4) * 16
        out[z // 4, row : row + 16, :] = depth_rows(chunks, z) + root[z] * value

    recurrence(
        lambda z: rows[pl.ds(z, 16, stride=32), :],
        lambda lag, z, before: table[before, lag - 1],
        keep_first,
        range(32),
    )
    recurrence(
        lambda z: first[z],
        lambda lag, z, before: table[before, lag - 1],
        keep_out,
        range(31, -1, -1),
    )


def unpack_kernel(order, chunks, potential, gradient, planes, sent):
    for half, out in enumerate((potential, gradient)):
        for slot in range(32):
            group, c = divmod(slot, 4)
            rows = [64 * half + z * 16 + c * 4 for z in range(4)]
            pieces = [chunks[group, row : row + 4, :] for row in rows]
            planes[half, slot] = jnp.concatenate(pieces, axis=0)
            pltpu.make_async_copy(planes.at[half, slot], out.at[order[slot]], sent.at[half]).start()
    for half, out in enumerate((potential, gradient)):
        pltpu.make_async_copy(planes.at[half], out, sent.at[half]).wait()


def swapped(even, odd):
    count = lax.axis_size("inline")

    def pairs(first):
        below = [(i, i + 1) for i in range(first, count - 1, 2)]
        return below + [(j, i) for i, j in below]

    return lax.ppermute(even, "inline", pairs(0)), lax.ppermute(odd, "inline", pairs(1))


def by_group(
    control,
    filter_coeffs,
    conv_kernels,
    channel_order,
    point_cells,
    point_values,
    point_weights,
    orient_cells,
    orient_normals,
    orient_weights,
):
    params = pltpu.CompilerParams(vmem_limit_bytes=48 << 20)
    in_vmem, in_smem, in_hbm = (
        pl.BlockSpec(memory_space=space) for space in (pltpu.VMEM, pltpu.SMEM, pltpu.HBM)
    )

    def call(kernel, outs, operands, scratch=(), ins=None, to=in_vmem, aliases=None):
        return pl.pallas_call(
            kernel,
            out_shape=outs,
            in_specs=ins or [in_vmem] * len(operands),
            out_specs=jax.tree.map(lambda _: to, outs),
            scratch_shapes=list(scratch),
            input_output_aliases=aliases or {},
            compiler_params=params,
        )(*operands)

    sources = (
        channel_order,
        jnp.transpose(filter_coeffs, (0, 2, 1)).reshape(16, 32),
        point_values.reshape(64, 128),
        orient_normals.reshape(96, 128),
        point_cells,
        point_weights,
        orient_cells,
        orient_weights,
        control.reshape(32, 16, 128),
    )
    sources = tuple(pltpu.with_memory_space_constraint(x, pltpu.HBM) for x in sources)
    held = [pltpu.VMEM(source.shape, source.dtype) for source in sources]
    held[0] = pltpu.SMEM((32,), jnp.int32)
    chunks = call(
        pack_kernel,
        f32(8, CHUNK, 128),
        sources,
        [pltpu.VMEM((128, 16), jnp.float32), pltpu.SemaphoreType.DMA((9,))] + held,
        [in_hbm] * 9,
    )
    chunks = lax.all_to_all(chunks, "depth", 0, 0)
    field, edge, plane = f32(4, 4, 32, 128), f32(2, 4, 32, 128), f32(4, 32, 128)
    by_depth = f32(32, 16, 128)
    rows = pltpu.VMEM((512, 128), jnp.float32)
    first = pltpu.VMEM((32, 16, 128), jnp.float32)
    smoothed, even, odd, table, scale, root = call(
        smooth_kernel,
        (field, edge, edge, f32(32, 4, 16, 128), by_depth, by_depth),
        (chunks,),
        [pltpu.VMEM((8, 16, 128), jnp.float32), first, rows],
    )
    even, odd = swapped(even, odd)
    kernels = jnp.transpose(conv_kernels, (1, 3, 4, 2, 0)).reshape(400, 8)
    partial, constant, weight, oweight, taps = call(
        own_kernel, (field, field, plane, plane, f32(400, 128)), (chunks, smoothed, kernels)
    )
    potential, forcing, even, odd = call(
        forcing_kernel,
        (field, field, edge, edge),
        (partial, even, odd, taps, constant, weight, oweight),
    )
    even, odd = swapped(even, odd)
    partial, results = call(
        spread_kernel, (field, f32(8, 128, 128)), (forcing, taps, potential), [rows]
    )
    results = call(
        gradient_kernel,
        f32(8, 128, 128),
        (results, chunks, partial, even, odd, taps, table, scale, root),
        [first, rows],
        aliases={0: 0},
    )
    results = lax.all_to_all(results, "depth", 0, 0)
    potential, gradient = call(
        unpack_kernel,
        (by_depth, by_depth),
        (channel_order, results),
        [pltpu.VMEM((2, 32, 16, 128), jnp.float32), pltpu.SemaphoreType.DMA((2,))],
        [in_smem, in_vmem],
        in_hbm,
    )
    return potential.reshape(control.shape), gradient.reshape(control.shape)


def solution(mesh):
    placed = (
        P(None, "depth", "inline", None),
        P(None, None, "depth"),
        P(),
        P(),
        P(None, "depth", "inline", None),
        P(None, "depth", "inline", None),
        P("depth", "inline", None),
        P(None, "depth", "inline", None),
        P(None, None, "depth", "inline", None),
        P("depth", "inline", None),
    )

    def body(control, filter_coeffs, conv_kernels, *rest):
        groups, block = conv_kernels.shape, control.shape
        fits = groups[:3] == (mesh.shape["depth"], 4, 4) and groups[0] == 8
        if fits and block == (32, 4, 4, 128):
            return by_group(control, filter_coeffs, conv_kernels, *rest)
        return shards(control, filter_coeffs, conv_kernels, *rest)

    return jax.shard_map(
        body,
        mesh=mesh,
        in_specs=placed,
        out_specs=(P(None, "depth", "inline", None), P(None, "depth", "inline", None)),
        check_vma=False,
    )
```

```python
import jax
import jax.numpy as jnp
from jax import lax
from jax.experimental import pallas as pl
from jax.experimental.pallas import tpu as pltpu
from jax.sharding import PartitionSpec as P

HIGHEST = lax.Precision.HIGHEST


def entering(value, axis, join, neutral, backward):
    count, mine = (lax.axis_size(axis), lax.axis_index(axis))
    pieces = jax.tree.map(lambda part: lax.all_gather(part, axis), value)
    if backward:
        pieces = jax.tree.map(lambda part: part[::-1], pieces)
        mine = count - 1 - mine
    so_far = jax.tree.map(
        lambda part, zero: jnp.full_like(part, 0) + jnp.asarray(zero, part.dtype), value, neutral
    )

    def hop(position, so_far):
        longer = join(so_far, jax.tree.map(lambda part: part[position], pieces))
        return jax.tree.map(lambda new, old: jnp.where(position < mine, new, old), longer, so_far)

    return lax.fori_loop(0, count - 1, hop, so_far)


def extended_2(cells, sides, width):
    for axis, dim in sides:
        count = lax.axis_size(axis)
        ends = count - 1
        head = lax.slice_in_dim(cells, 0, width, axis=dim)
        tail = lax.slice_in_dim(cells, cells.shape[dim] - width, cells.shape[dim], axis=dim)
        cells = jnp.concatenate(
            [
                lax.ppermute(tail, axis, [(i, (i + 1) % count) for i in range(ends)]),
                cells,
                lax.ppermute(head, axis, [((i + 1) % count, i) for i in range(ends)]),
            ],
            axis=dim,
        )
    return cells


def mixing(kernels, channel_order):
    groups = kernels.shape[0]
    group_size = kernels.shape[1]
    channels = groups * group_size
    slots = jnp.arange(channels, dtype=jnp.int32)
    chooser = (channel_order[:, None] == slots[None, :]).astype(jnp.float32)
    in_group = (
        slots[:, None] // group_size == jnp.arange(groups, dtype=jnp.int32)[None, :]
    ).astype(jnp.float32)
    in_place = (
        slots[:, None] % group_size == jnp.arange(group_size, dtype=jnp.int32)[None, :]
    ).astype(jnp.float32)
    block_mix = jnp.einsum(
        "sg,sa,tg,tb,gabhw->sthw",
        in_group,
        in_place,
        in_group,
        in_place,
        kernels,
        precision=HIGHEST,
    )
    return jnp.einsum("sc,td,sthw->cdhw", chooser, chooser, block_mix, precision=HIGHEST)


def padded_conv(padded, weights):
    return lax.conv_general_dilated(
        padded,
        weights,
        (1, 1),
        ((0, 0), (2, 2)),
        dimension_numbers=("CNHW", "OIHW", "CNHW"),
        precision=HIGHEST,
    )


def compose(earlier, later):
    first_map, first_shift = earlier
    second_map, second_shift = later
    joined_map = jnp.einsum("cnij,cnjk->cnik", second_map, first_map, precision=HIGHEST)
    joined_shift = (
        jnp.einsum("cnij,cnjk->cnik", second_map, first_shift, precision=HIGHEST) + second_shift
    )
    return (joined_map, joined_shift)


def build_tiles(coeffs, by_column, block_len):
    lead = coeffs.shape[1:3]
    lag_steps = jnp.arange(1, 5, dtype=jnp.int32)[:, None, None]
    if by_column:
        row_ids = jnp.arange(block_len + 4, dtype=jnp.int32)[None, :, None]
        col_ids = jnp.arange(block_len, dtype=jnp.int32)[None, None, :]
        picker = (row_ids == col_ids + lag_steps).astype(jnp.float32)
        extended = jnp.einsum("lcnk,lzk->cnzk", coeffs, picker, precision=HIGHEST)
        lower_tile = extended[:, :, :block_len, :]
        exit_map = extended[:, :, block_len:, :]
        entry_base = (
            jnp.arange(block_len, dtype=jnp.int32)[:, None]
            == jnp.arange(4, dtype=jnp.int32)[None, :]
        ).astype(jnp.float32)
        entry_map = jnp.broadcast_to(entry_base, lead + (block_len, 4))
    else:
        row_ids = jnp.arange(block_len, dtype=jnp.int32)[None, :, None]
        col_ids = jnp.arange(block_len + 4, dtype=jnp.int32)[None, None, :]
        picker = (col_ids == row_ids - lag_steps + 4).astype(jnp.float32)
        extended = jnp.einsum("lcnz,lzk->cnzk", coeffs, picker, precision=HIGHEST)
        lower_tile = extended[:, :, :, 4:]
        entry_map = extended[:, :, :, :4]
        exit_base = (
            jnp.arange(block_len, dtype=jnp.int32)[None, :]
            == jnp.arange(4, dtype=jnp.int32)[:, None] + block_len - 4
        ).astype(jnp.float32)
        exit_map = jnp.broadcast_to(exit_base, lead + (4, block_len))
    return (lower_tile, entry_map, exit_map)


def sweep_blocks(field, coeffs, by_column, upward, prefix):
    if upward:
        field = field[:, ::-1, ::-1]
        coeffs = coeffs[:, :, ::-1, ::-1]
    block_len = coeffs.shape[3]
    lower_tile, entry_map, exit_map = build_tiles(coeffs, by_column, block_len)
    identity_tile = jnp.eye(block_len, dtype=jnp.float32)
    inverse = identity_tile + lower_tile
    power = lower_tile
    power = jnp.einsum("cnij,cnjk->cnik", power, power, precision=HIGHEST)
    inverse = inverse + jnp.einsum("cnij,cnjk->cnik", inverse, power, precision=HIGHEST)
    reach_map = jnp.einsum("cnzk,cnkj->cnzj", inverse, entry_map, precision=HIGHEST)
    carry_map = jnp.einsum("cniz,cnzj->cnij", exit_map, reach_map, precision=HIGHEST)
    local_part = jnp.einsum("cnzk,cnkm->cnzm", inverse, field, precision=HIGHEST)
    carry_out = jnp.einsum("cniz,cnzm->cnim", exit_map, local_part, precision=HIGHEST)
    incoming = prefix((carry_map, carry_out), upward)
    result = local_part + jnp.einsum("cnzj,cnjm->cnzm", reach_map, incoming, precision=HIGHEST)
    if upward:
        result = result[:, ::-1, ::-1]
    return result


def shards(
    control,
    filter_coeffs,
    conv_kernels,
    channel_order,
    point_cells,
    point_values,
    point_weights,
    orient_cells,
    orient_normals,
    orient_weights,
):
    channels, block_len, inline_rows, cross_cols = control.shape
    plane_cells = inline_rows * cross_cols
    source = control.reshape(channels, block_len, plane_cells)
    coeffs = filter_coeffs[:, :, None, :]

    def to_blocks(field):
        return field[:, None]

    def from_blocks(field):
        return field[:, 0]

    def scaled(field, factor):
        return factor[..., None] * field

    def prefix(maps, upward):
        start = (
            jnp.broadcast_to(jnp.eye(4, dtype=jnp.float32), maps[0].shape),
            jnp.zeros_like(maps[1]),
        )
        return entering(maps, "depth", compose, start, upward)[1]

    scaling = 1.0 - jnp.sum(coeffs, axis=0)
    root_scale = jnp.sqrt(scaling)
    filtered = sweep_blocks(scaled(to_blocks(source), root_scale), coeffs, False, False, prefix)
    smoothed = sweep_blocks(scaled(filtered, scaling), coeffs, False, True, prefix)
    smoothed_field = from_blocks(smoothed).reshape(control.shape)
    weights = mixing(conv_kernels, channel_order)
    smoothed_padded = extended_2(smoothed_field, (("inline", 2),), 2)
    potential = padded_conv(smoothed_padded, weights)
    flat_field = potential.reshape(channels, -1)
    depth_base = lax.axis_index("depth") * block_len
    inline_base = lax.axis_index("inline") * inline_rows
    cells = point_cells.reshape(3, -1)
    flat_index = (
        (cells[0] - depth_base) * inline_rows + cells[1] - inline_base
    ) * cross_cols + cells[2]
    misfit = (
        flat_field[:, flat_index] - point_values.reshape(channels, -1)
    ) * point_weights.reshape(-1)[None, :]
    ocells = orient_cells.reshape(3, -1)
    base_cell = (
        (ocells[0] - depth_base) * inline_rows + ocells[1] - inline_base
    ) * cross_cols + ocells[2]
    normals = orient_normals.reshape(3, channels, -1)
    oweight = orient_weights.reshape(-1)[None, :]
    update_values = [misfit]
    update_cells = [flat_index]
    for component, stride in enumerate((plane_cells, cross_cols, 1)):
        mismatch = flat_field[:, base_cell + stride] - flat_field[:, base_cell] - normals[component]
        weighted = mismatch * oweight
        update_values.append(weighted)
        update_cells.append(base_cell + stride)
        update_values.append(-weighted)
        update_cells.append(base_cell)
    all_values = jnp.concatenate(update_values, axis=1)
    all_cells = jnp.concatenate(update_cells, axis=0)
    adjoint_weights = jnp.transpose(weights, (1, 0, 2, 3))[:, :, ::-1, ::-1]
    forcing = jnp.zeros_like(flat_field).at[:, all_cells].add(all_values)
    forcing_padded = extended_2(forcing.reshape(control.shape), (("inline", 2),), 2)
    spread = padded_conv(forcing_padded, adjoint_weights).reshape(channels, block_len, plane_cells)
    adjoint_back = scaled(sweep_blocks(to_blocks(spread), coeffs, True, False, prefix), scaling)
    adjoint_fore = scaled(sweep_blocks(adjoint_back, coeffs, True, True, prefix), root_scale)
    gradient = control + from_blocks(adjoint_fore).reshape(control.shape)
    return (potential, gradient)


CHUNK = 96
AT_VALUES, AT_NORMALS, AT_COEFFS, AT_MISC = 64, 72, 84, 88


def f32(*shape):
    return jax.ShapeDtypeStruct(shape, jnp.float32)


def lane_index(shape):
    return lax.broadcasted_iota(jnp.int32, shape, len(shape) - 1)


def pack_kernel(*refs):
    sources, out, by_channel, arrived, held = refs[:9], refs[9], refs[10], refs[11], refs[12:]
    copies = [
        pltpu.make_async_copy(source, target, arrived.at[k])
        for k, (source, target) in enumerate(zip(sources, held))
    ]
    for copy in copies:
        copy.start()
    order, coeffs, values, normals, cells, weights, ocells, oweights, control = held

    def flat_cell(ref):
        z, y, x = (ref[k, 0] for k in range(3))
        return (((y & 3) * 4 + (z & 3)) * 128 + x).astype(jnp.float32)

    for copy in copies[:-1]:
        copy.wait()
    flat, oflat = flat_cell(cells), flat_cell(ocells)
    weight = weights[0]
    misc = jnp.concatenate(
        [flat[:, :128], flat[:, 128:], oflat, weight[:, :128], weight[:, 128:], oweights[0]]
        + [jnp.zeros((2, 128), jnp.float32)],
        axis=0,
    )
    by_channel[...] = jnp.transpose(
        jnp.concatenate([coeffs[...], jnp.zeros((16, 96), jnp.float32)], axis=1)
    )
    for group in range(8):
        out[group, AT_MISC:CHUNK, :] = misc
    for slot in range(32):
        group, c = divmod(slot, 4)
        channel = order[slot]
        row = AT_VALUES + 2 * c
        out[group, row : row + 2, :] = values[pl.ds(channel * 2, 2), :]
        for k in range(3):
            row = AT_NORMALS + 4 * k + c
            out[group, row : row + 1, :] = normals[pl.ds(k * 32 + channel, 1), :]
        row = AT_COEFFS + c
        out[group, row : row + 1, :16] = by_channel[pl.ds(channel, 1), :]
    copies[-1].wait()
    for slot in range(32):
        group, c = divmod(slot, 4)
        plane = control[order[slot]]
        for z in range(4):
            row = z * 16 + c * 4
            out[group, row : row + 4, :] = plane[z * 4 : z * 4 + 4]


def coefficient(expanded, lag, z):
    block, local = divmod(z, 4)
    k = (lag - 1) * 4 + local
    return jnp.broadcast_to(expanded[block, :, k : k + 1], (16, 128))


def expand_coeffs(chunks, expanded, table, scale, root):
    for block in range(8):
        for c in range(4):
            row = AT_COEFFS + c
            expanded[block, 4 * c : 4 * c + 4, :] = jnp.broadcast_to(
                chunks[block, row : row + 1, :], (4, 128)
            )
    for z in range(32):
        lags = [coefficient(expanded, lag, z) for lag in range(1, 5)]
        for lag in range(4):
            table[z, lag] = lags[lag]
        scale[z] = 1.0 - ((lags[0] + lags[1]) + (lags[2] + lags[3]))
        root[z] = jnp.sqrt(scale[z])


def recurrence(source, factor, emit, order):
    history = []
    for t in order:
        total = source(t)
        for lag in range(len(history), 0, -1):
            before, value = history[lag - 1]
            total = total + factor(lag, t, before) * value
        history = [(t, total)] + history[:3]
        emit(t, total)


def depth_rows(chunks, z):
    return chunks[z // 4, (z % 4) * 16 : (z % 4) * 16 + 16, :]


def smooth_kernel(chunks, smoothed, even, odd, table, scale, root, expanded, first, rows):
    expand_coeffs(chunks, expanded, table, scale, root)

    def keep_first(z, value):
        first[z] = scale[z] * value

    def keep_rows(z, value):
        rows[z * 16 : z * 16 + 16, :] = value

    recurrence(
        lambda z: root[z] * depth_rows(chunks, z),
        lambda lag, z, before: table[z, lag - 1],
        keep_first,
        range(32),
    )
    recurrence(
        lambda z: first[z],
        lambda lag, z, before: table[z, lag - 1],
        keep_rows,
        range(31, -1, -1),
    )
    parity = lax.axis_index("inline") % 2
    for y in range(4):
        for c in range(4):
            smoothed[y, c] = rows[pl.ds(c * 4 + y, 32, stride=16), :]
    for y in range(2):
        even[y] = smoothed[2 - 2 * parity + y]
        odd[y] = smoothed[2 * parity + y]


def tap(table, a, b, h, w):
    row = ((a * 5 + h) * 5 + w) * 4 + b
    return jnp.broadcast_to(table[row : row + 1, :], (8, 128))


def conv_rows(read, rows_in, start, table, adjoint, write):
    lane = lane_index((8, 128))

    def moved(value, shift):
        if shift == 0:
            return value
        inside = lane >= -shift if shift < 0 else lane < 128 - shift
        return jnp.where(inside, pltpu.roll(value, -shift % 128, 1), 0.0)

    def some_depths(k, carry):
        depths = pl.ds(pl.multiple_of(k * 8, 8), 8)
        total = [[start(y, o, depths) for o in range(4)] for y in range(4)]
        for i in range(4):
            lines = {row: read(row, i, depths) for row in rows_in}
            for w in range(5):
                if adjoint:
                    taps = [[tap(table, i, o, h, w) for h in range(5)] for o in range(4)]
                else:
                    taps = [[tap(table, o, i, h, w) for h in range(5)] for o in range(4)]
                for row in rows_in:
                    line = moved(lines[row], 2 - w if adjoint else w - 2)
                    for y in range(4):
                        h = y - row + 2 if adjoint else row - y + 2
                        if 0 <= h < 5:
                            for o in range(4):
                                total[y][o] = total[y][o] + taps[o][h] * line
        for y in range(4):
            for o in range(4):
                write(y, o, depths, total[y][o])
        return carry

    lax.fori_loop(0, 4, some_depths, 0)


OWN = (0, 1, 2, 3)
HALO = (-2, -1, 4, 5)


def halo_reader(even, odd):
    slab, last = lax.axis_index("inline"), lax.axis_size("inline") - 1
    parity = slab % 2

    def read(row, c, depths):
        y = row + 2 if row < 0 else row - 4
        through_even, through_odd = even[y, c, depths, :], odd[y, c, depths, :]
        below = parity == 1 if row < 0 else parity == 0
        outside = slab == 0 if row < 0 else slab == last
        return jnp.where(outside, 0.0, jnp.where(below, through_even, through_odd))

    return read


def split(value):
    high = value.astype(jnp.bfloat16)
    return high, (value - high.astype(jnp.float32)).astype(jnp.bfloat16)


def point_fields(chunks, constant, weight, oweight):
    row = lax.broadcasted_iota(jnp.int32, (16, 256), 0)
    orow = lax.broadcasted_iota(jnp.int32, (16, 128), 0)
    column = lax.broadcasted_iota(jnp.int32, (128, 384), 0)
    for block in range(8):

        def line(k, block=block):
            return chunks[block, k : k + 1, :]

        def double(k, line=line):
            return jnp.concatenate([line(k), line(k + 1)], axis=1)

        flat = double(AT_MISC).astype(jnp.int32)
        oflat = line(AT_MISC + 2).astype(jnp.int32)
        w, ow = double(AT_MISC + 3), line(AT_MISC + 5)
        cell, ocell = flat >> 7, oflat >> 7
        at_cross = jnp.concatenate([flat & 127, oflat & 127], axis=1)
        columns = (column == at_cross).astype(jnp.float32).astype(jnp.bfloat16)
        here, ohere = row == cell, orow == ocell
        below, beside = orow == ocell + 1, orow == ocell + 4
        main, along = [], []
        for c in range(4):
            value = w * double(AT_VALUES + 2 * c)
            n0, n1, n2 = (ow * line(AT_NORMALS + 4 * k + c) for k in range(3))
            placed = (
                jnp.where(below, n0, 0.0)
                + jnp.where(beside, n1, 0.0)
                - jnp.where(ohere, n0 + n1 + n2, 0.0)
            )
            main.append(jnp.concatenate([jnp.where(here, value, 0.0), placed], axis=1))
            along.append(
                jnp.concatenate([jnp.zeros((16, 256), jnp.float32), jnp.where(ohere, n2, 0.0)], axis=1)
            )
        both = [
            jnp.concatenate([jnp.where(here, w, 0.0), jnp.zeros((16, 128), jnp.float32)], axis=1),
            jnp.concatenate([jnp.zeros((16, 256), jnp.float32), jnp.where(ohere, ow, 0.0)], axis=1),
        ]
        high, low = split(jnp.concatenate(main + both + along, axis=0))
        sums = lax.dot_general(
            jnp.concatenate([high, low], axis=0),
            columns,
            (((1,), (1,)), ((), ())),
            preferred_element_type=jnp.float32,
        )
        sums = sums[:160] + sums[160:]
        moved = pltpu.roll(sums[96:160], 1, 1)
        z = 4 * block
        for y in range(4):
            for c in range(4):
                k = 16 * c + 4 * y
                constant[y, c, z : z + 4, :] = sums[k : k + 4] + moved[k : k + 4]
            weight[y, z : z + 4, :] = sums[64 + 4 * y : 68 + 4 * y]
            oweight[y, z : z + 4, :] = sums[80 + 4 * y : 84 + 4 * y]


def own_kernel(chunks, smoothed, kernels, partial, constant, weight, oweight, table):
    group = lax.axis_index("depth")
    picked = jnp.where(lane_index((400, 8)) == group, kernels[...], 0.0)
    table[...] = jnp.broadcast_to(jnp.sum(picked, axis=1, keepdims=True), (400, 128))
    point_fields(chunks, constant, weight, oweight)

    def write(y, o, depths, value):
        partial[y, o, depths, :] = value

    conv_rows(
        lambda row, c, depths: smoothed[row, c, depths, :],
        OWN,
        lambda y, o, depths: jnp.zeros((8, 128), jnp.float32),
        table,
        False,
        write,
    )


def forcing_kernel(
    partial, even_in, odd_in, table, constant, weight, oweight, potential, forcing, even, odd
):
    def write(y, o, depths, value):
        potential[y, o, depths, :] = value

    conv_rows(
        halo_reader(even_in, odd_in),
        HALO,
        lambda y, o, depths: partial[y, o, depths, :],
        table,
        False,
        write,
    )

    def one_channel(c, carry):
        lines = [potential[y, c] for y in range(4)]
        sums = [weight[y] * lines[y] - constant[y, c] for y in range(4)]
        for y in range(4):
            share = oweight[y]
            deeper = share * (pltpu.roll(lines[y], 31, 0) - lines[y])
            across = share * (pltpu.roll(lines[y], 127, 1) - lines[y])
            sums[y] = sums[y] - deeper + pltpu.roll(deeper, 1, 0)
            sums[y] = sums[y] - across + pltpu.roll(across, 1, 1)
            if y < 3:
                beside = share * (lines[y + 1] - lines[y])
                sums[y] = sums[y] - beside
                sums[y + 1] = sums[y + 1] + beside
        for y in range(4):
            forcing[y, c] = sums[y]
        return carry

    lax.fori_loop(0, 4, one_channel, 0)
    parity = lax.axis_index("inline") % 2
    for y in range(2):
        even[y] = forcing[2 - 2 * parity + y]
        odd[y] = forcing[2 * parity + y]


def spread_kernel(forcing, table, potential, partial, out, rows):
    def write(y, o, depths, value):
        partial[y, o, depths, :] = value

    conv_rows(
        lambda row, c, depths: forcing[row, c, depths, :],
        OWN,
        lambda y, o, depths: jnp.zeros((8, 128), jnp.float32),
        table,
        True,
        write,
    )
    for y in range(4):
        for c in range(4):
            rows[pl.ds((c * 4 + y) * 32, 32), :] = potential[y, c]
    for z in range(32):
        out[z // 4, (z % 4) * 16 : (z % 4) * 16 + 16, :] = rows[pl.ds(z, 16, stride=32), :]


def gradient_kernel(
    results, chunks, partial, even_in, odd_in, taps, table, scale, root, out, first, rows
):
    def write(y, o, depths, value):
        rows[pl.ds(pl.multiple_of((o * 4 + y) * 32 + depths.start, 8), 8), :] = value

    conv_rows(
        halo_reader(even_in, odd_in),
        HALO,
        lambda y, o, depths: partial[y, o, depths, :],
        taps,
        True,
        write,
    )

    def keep_first(z, value):
        first[z] = scale[z] * value

    def keep_out(z, value):
        row = 64 + (z % 4) * 16
        out[z // 4, row : row + 16, :] = depth_rows(chunks, z) + root[z] * value

    recurrence(
        lambda z: rows[pl.ds(z, 16, stride=32), :],
        lambda lag, z, before: table[before, lag - 1],
        keep_first,
        range(32),
    )
    recurrence(
        lambda z: first[z],
        lambda lag, z, before: table[before, lag - 1],
        keep_out,
        range(31, -1, -1),
    )


def unpack_kernel(order, chunks, potential, gradient, planes, sent):
    for half, out in enumerate((potential, gradient)):
        for slot in range(32):
            group, c = divmod(slot, 4)
            rows = [64 * half + z * 16 + c * 4 for z in range(4)]
            pieces = [chunks[group, row : row + 4, :] for row in rows]
            planes[half, slot] = jnp.concatenate(pieces, axis=0)
            pltpu.make_async_copy(planes.at[half, slot], out.at[order[slot]], sent.at[half]).start()
    for half, out in enumerate((potential, gradient)):
        pltpu.make_async_copy(planes.at[half], out, sent.at[half]).wait()


def swapped(even, odd):
    depths, slabs = lax.axis_size("depth"), lax.axis_size("inline")

    def swap(value, first):
        pairs = []
        for d in range(depths):
            for i in range(slabs):
                other = i + 1 if (i - first) % 2 == 0 else i - 1
                to = (d, other) if 0 <= other < slabs else (d ^ 1, i)
                pairs.append((d * slabs + i, to[0] * slabs + to[1]))
        return lax.ppermute(value, ("depth", "inline"), pairs)

    return swap(even, 0), swap(odd, 1)


def by_group(
    control,
    filter_coeffs,
    conv_kernels,
    channel_order,
    point_cells,
    point_values,
    point_weights,
    orient_cells,
    orient_normals,
    orient_weights,
):
    params = pltpu.CompilerParams(vmem_limit_bytes=48 << 20)
    in_vmem, in_smem, in_hbm = (
        pl.BlockSpec(memory_space=space) for space in (pltpu.VMEM, pltpu.SMEM, pltpu.HBM)
    )

    def call(kernel, outs, operands, scratch=(), ins=None, to=in_vmem, aliases=None):
        return pl.pallas_call(
            kernel,
            out_shape=outs,
            in_specs=ins or [in_vmem] * len(operands),
            out_specs=jax.tree.map(lambda _: to, outs),
            scratch_shapes=list(scratch),
            input_output_aliases=aliases or {},
            compiler_params=params,
        )(*operands)

    sources = (
        channel_order,
        jnp.transpose(filter_coeffs, (0, 2, 1)).reshape(16, 32),
        point_values.reshape(64, 128),
        orient_normals.reshape(96, 128),
        point_cells,
        point_weights,
        orient_cells,
        orient_weights,
        control.reshape(32, 16, 128),
    )
    sources = tuple(pltpu.with_memory_space_constraint(x, pltpu.HBM) for x in sources)
    held = [pltpu.VMEM(source.shape, source.dtype) for source in sources]
    held[0] = pltpu.SMEM((32,), jnp.int32)
    chunks = call(
        pack_kernel,
        f32(8, CHUNK, 128),
        sources,
        [pltpu.VMEM((128, 16), jnp.float32), pltpu.SemaphoreType.DMA((9,))] + held,
        [in_hbm] * 9,
    )
    chunks = lax.all_to_all(chunks, "depth", 0, 0)
    field, edge, plane = f32(4, 4, 32, 128), f32(2, 4, 32, 128), f32(4, 32, 128)
    by_depth = f32(32, 16, 128)
    rows = pltpu.VMEM((512, 128), jnp.float32)
    first = pltpu.VMEM((32, 16, 128), jnp.float32)
    smoothed, even, odd, table, scale, root = call(
        smooth_kernel,
        (field, edge, edge, f32(32, 4, 16, 128), by_depth, by_depth),
        (chunks,),
        [pltpu.VMEM((8, 16, 128), jnp.float32), first, rows],
    )
    even, odd = swapped(even, odd)
    kernels = jnp.transpose(conv_kernels, (1, 3, 4, 2, 0)).reshape(400, 8)
    partial, constant, weight, oweight, taps = call(
        own_kernel, (field, field, plane, plane, f32(400, 128)), (chunks, smoothed, kernels)
    )
    potential, forcing, even, odd = call(
        forcing_kernel,
        (field, field, edge, edge),
        (partial, even, odd, taps, constant, weight, oweight),
    )
    even, odd = swapped(even, odd)
    partial, results = call(
        spread_kernel, (field, f32(8, 128, 128)), (forcing, taps, potential), [rows]
    )
    results = call(
        gradient_kernel,
        f32(8, 128, 128),
        (results, chunks, partial, even, odd, taps, table, scale, root),
        [first, rows],
        aliases={0: 0},
    )
    results = lax.all_to_all(results, "depth", 0, 0)
    potential, gradient = call(
        unpack_kernel,
        (by_depth, by_depth),
        (channel_order, results),
        [pltpu.VMEM((2, 32, 16, 128), jnp.float32), pltpu.SemaphoreType.DMA((2,))],
        [in_smem, in_vmem],
        in_hbm,
    )
    return potential.reshape(control.shape), gradient.reshape(control.shape)


def solution(mesh):
    placed = (
        P(None, "depth", "inline", None),
        P(None, None, "depth"),
        P(),
        P(),
        P(None, "depth", "inline", None),
        P(None, "depth", "inline", None),
        P("depth", "inline", None),
        P(None, "depth", "inline", None),
        P(None, None, "depth", "inline", None),
        P("depth", "inline", None),
    )

    def body(control, filter_coeffs, conv_kernels, *rest):
        groups, block = conv_kernels.shape, control.shape
        fits = groups[:3] == (mesh.shape["depth"], 4, 4) and groups[0] == 8
        if fits and block == (32, 4, 4, 128):
            return by_group(control, filter_coeffs, conv_kernels, *rest)
        return shards(control, filter_coeffs, conv_kernels, *rest)

    return jax.shard_map(
        body,
        mesh=mesh,
        in_specs=placed,
        out_specs=(P(None, "depth", "inline", None), P(None, "depth", "inline", None)),
        check_vma=False,
    )
```

```python
import functools

import jax
import jax.numpy as jnp
from jax import lax
from jax.experimental import pallas as pl
from jax.experimental.pallas import tpu as pltpu
from jax.sharding import PartitionSpec as P

HIGHEST = lax.Precision.HIGHEST


def entering(value, axis, join, neutral, backward):
    count, mine = (lax.axis_size(axis), lax.axis_index(axis))
    pieces = jax.tree.map(lambda part: lax.all_gather(part, axis), value)
    if backward:
        pieces = jax.tree.map(lambda part: part[::-1], pieces)
        mine = count - 1 - mine
    so_far = jax.tree.map(
        lambda part, zero: jnp.full_like(part, 0) + jnp.asarray(zero, part.dtype), value, neutral
    )

    def hop(position, so_far):
        longer = join(so_far, jax.tree.map(lambda part: part[position], pieces))
        return jax.tree.map(lambda new, old: jnp.where(position < mine, new, old), longer, so_far)

    return lax.fori_loop(0, count - 1, hop, so_far)


def extended_2(cells, sides, width):
    for axis, dim in sides:
        count = lax.axis_size(axis)
        ends = count - 1
        head = lax.slice_in_dim(cells, 0, width, axis=dim)
        tail = lax.slice_in_dim(cells, cells.shape[dim] - width, cells.shape[dim], axis=dim)
        cells = jnp.concatenate(
            [
                lax.ppermute(tail, axis, [(i, (i + 1) % count) for i in range(ends)]),
                cells,
                lax.ppermute(head, axis, [((i + 1) % count, i) for i in range(ends)]),
            ],
            axis=dim,
        )
    return cells


def mixing(kernels, channel_order):
    groups = kernels.shape[0]
    group_size = kernels.shape[1]
    channels = groups * group_size
    slots = jnp.arange(channels, dtype=jnp.int32)
    chooser = (channel_order[:, None] == slots[None, :]).astype(jnp.float32)
    in_group = (
        slots[:, None] // group_size == jnp.arange(groups, dtype=jnp.int32)[None, :]
    ).astype(jnp.float32)
    in_place = (
        slots[:, None] % group_size == jnp.arange(group_size, dtype=jnp.int32)[None, :]
    ).astype(jnp.float32)
    block_mix = jnp.einsum(
        "sg,sa,tg,tb,gabhw->sthw",
        in_group,
        in_place,
        in_group,
        in_place,
        kernels,
        precision=HIGHEST,
    )
    return jnp.einsum("sc,td,sthw->cdhw", chooser, chooser, block_mix, precision=HIGHEST)


def padded_conv(padded, weights):
    return lax.conv_general_dilated(
        padded,
        weights,
        (1, 1),
        ((0, 0), (2, 2)),
        dimension_numbers=("CNHW", "OIHW", "CNHW"),
        precision=HIGHEST,
    )


def compose(earlier, later):
    first_map, first_shift = earlier
    second_map, second_shift = later
    joined_map = jnp.einsum("cnij,cnjk->cnik", second_map, first_map, precision=HIGHEST)
    joined_shift = (
        jnp.einsum("cnij,cnjk->cnik", second_map, first_shift, precision=HIGHEST) + second_shift
    )
    return (joined_map, joined_shift)


def build_tiles(coeffs, by_column, block_len):
    lead = coeffs.shape[1:3]
    lag_steps = jnp.arange(1, 5, dtype=jnp.int32)[:, None, None]
    if by_column:
        row_ids = jnp.arange(block_len + 4, dtype=jnp.int32)[None, :, None]
        col_ids = jnp.arange(block_len, dtype=jnp.int32)[None, None, :]
        picker = (row_ids == col_ids + lag_steps).astype(jnp.float32)
        extended = jnp.einsum("lcnk,lzk->cnzk", coeffs, picker, precision=HIGHEST)
        lower_tile = extended[:, :, :block_len, :]
        exit_map = extended[:, :, block_len:, :]
        entry_base = (
            jnp.arange(block_len, dtype=jnp.int32)[:, None]
            == jnp.arange(4, dtype=jnp.int32)[None, :]
        ).astype(jnp.float32)
        entry_map = jnp.broadcast_to(entry_base, lead + (block_len, 4))
    else:
        row_ids = jnp.arange(block_len, dtype=jnp.int32)[None, :, None]
        col_ids = jnp.arange(block_len + 4, dtype=jnp.int32)[None, None, :]
        picker = (col_ids == row_ids - lag_steps + 4).astype(jnp.float32)
        extended = jnp.einsum("lcnz,lzk->cnzk", coeffs, picker, precision=HIGHEST)
        lower_tile = extended[:, :, :, 4:]
        entry_map = extended[:, :, :, :4]
        exit_base = (
            jnp.arange(block_len, dtype=jnp.int32)[None, :]
            == jnp.arange(4, dtype=jnp.int32)[:, None] + block_len - 4
        ).astype(jnp.float32)
        exit_map = jnp.broadcast_to(exit_base, lead + (4, block_len))
    return (lower_tile, entry_map, exit_map)


def sweep_blocks(field, coeffs, by_column, upward, prefix):
    if upward:
        field = field[:, ::-1, ::-1]
        coeffs = coeffs[:, :, ::-1, ::-1]
    block_len = coeffs.shape[3]
    lower_tile, entry_map, exit_map = build_tiles(coeffs, by_column, block_len)
    identity_tile = jnp.eye(block_len, dtype=jnp.float32)
    inverse = identity_tile + lower_tile
    power = lower_tile
    power = jnp.einsum("cnij,cnjk->cnik", power, power, precision=HIGHEST)
    inverse = inverse + jnp.einsum("cnij,cnjk->cnik", inverse, power, precision=HIGHEST)
    reach_map = jnp.einsum("cnzk,cnkj->cnzj", inverse, entry_map, precision=HIGHEST)
    carry_map = jnp.einsum("cniz,cnzj->cnij", exit_map, reach_map, precision=HIGHEST)
    local_part = jnp.einsum("cnzk,cnkm->cnzm", inverse, field, precision=HIGHEST)
    carry_out = jnp.einsum("cniz,cnzm->cnim", exit_map, local_part, precision=HIGHEST)
    incoming = prefix((carry_map, carry_out), upward)
    result = local_part + jnp.einsum("cnzj,cnjm->cnzm", reach_map, incoming, precision=HIGHEST)
    if upward:
        result = result[:, ::-1, ::-1]
    return result


def shards(
    control,
    filter_coeffs,
    conv_kernels,
    channel_order,
    point_cells,
    point_values,
    point_weights,
    orient_cells,
    orient_normals,
    orient_weights,
):
    channels, block_len, inline_rows, cross_cols = control.shape
    plane_cells = inline_rows * cross_cols
    source = control.reshape(channels, block_len, plane_cells)
    coeffs = filter_coeffs[:, :, None, :]

    def to_blocks(field):
        return field[:, None]

    def from_blocks(field):
        return field[:, 0]

    def scaled(field, factor):
        return factor[..., None] * field

    def prefix(maps, upward):
        start = (
            jnp.broadcast_to(jnp.eye(4, dtype=jnp.float32), maps[0].shape),
            jnp.zeros_like(maps[1]),
        )
        return entering(maps, "depth", compose, start, upward)[1]

    scaling = 1.0 - jnp.sum(coeffs, axis=0)
    root_scale = jnp.sqrt(scaling)
    filtered = sweep_blocks(scaled(to_blocks(source), root_scale), coeffs, False, False, prefix)
    smoothed = sweep_blocks(scaled(filtered, scaling), coeffs, False, True, prefix)
    smoothed_field = from_blocks(smoothed).reshape(control.shape)
    weights = mixing(conv_kernels, channel_order)
    smoothed_padded = extended_2(smoothed_field, (("inline", 2),), 2)
    potential = padded_conv(smoothed_padded, weights)
    flat_field = potential.reshape(channels, -1)
    depth_base = lax.axis_index("depth") * block_len
    inline_base = lax.axis_index("inline") * inline_rows
    cells = point_cells.reshape(3, -1)
    flat_index = (
        (cells[0] - depth_base) * inline_rows + cells[1] - inline_base
    ) * cross_cols + cells[2]
    misfit = (
        flat_field[:, flat_index] - point_values.reshape(channels, -1)
    ) * point_weights.reshape(-1)[None, :]
    ocells = orient_cells.reshape(3, -1)
    base_cell = (
        (ocells[0] - depth_base) * inline_rows + ocells[1] - inline_base
    ) * cross_cols + ocells[2]
    normals = orient_normals.reshape(3, channels, -1)
    oweight = orient_weights.reshape(-1)[None, :]
    update_values = [misfit]
    update_cells = [flat_index]
    for component, stride in enumerate((plane_cells, cross_cols, 1)):
        mismatch = flat_field[:, base_cell + stride] - flat_field[:, base_cell] - normals[component]
        weighted = mismatch * oweight
        update_values.append(weighted)
        update_cells.append(base_cell + stride)
        update_values.append(-weighted)
        update_cells.append(base_cell)
    all_values = jnp.concatenate(update_values, axis=1)
    all_cells = jnp.concatenate(update_cells, axis=0)
    adjoint_weights = jnp.transpose(weights, (1, 0, 2, 3))[:, :, ::-1, ::-1]
    forcing = jnp.zeros_like(flat_field).at[:, all_cells].add(all_values)
    forcing_padded = extended_2(forcing.reshape(control.shape), (("inline", 2),), 2)
    spread = padded_conv(forcing_padded, adjoint_weights).reshape(channels, block_len, plane_cells)
    adjoint_back = scaled(sweep_blocks(to_blocks(spread), coeffs, True, False, prefix), scaling)
    adjoint_fore = scaled(sweep_blocks(adjoint_back, coeffs, True, True, prefix), root_scale)
    gradient = control + from_blocks(adjoint_fore).reshape(control.shape)
    return (potential, gradient)


CHUNK = 96
AT_VALUES, AT_NORMALS, AT_COEFFS, AT_MISC = 64, 72, 84, 88


def f32(*shape):
    return jax.ShapeDtypeStruct(shape, jnp.float32)


def lane_index(shape):
    return lax.broadcasted_iota(jnp.int32, shape, len(shape) - 1)


def pack_kernel(*refs):
    sources, give, keep, by_channel = refs[:9], refs[9], refs[10:14], refs[14]
    arrived, held = refs[15], refs[16:]
    copies = [
        pltpu.make_async_copy(source, target, arrived.at[k])
        for k, (source, target) in enumerate(zip(sources, held))
    ]
    for copy in copies:
        copy.start()
    order, coeffs, values, normals, cells, weights, ocells, oweights, control = held

    def flat_cell(ref):
        z, y, x = (ref[k, 0] for k in range(3))
        return (((y & 3) * 4 + (z & 3)) * 128 + x).astype(jnp.float32)

    for copy in copies[:-1]:
        copy.wait()
    flat, oflat = flat_cell(cells), flat_cell(ocells)
    weight = weights[0]
    misc = jnp.concatenate(
        [flat[:, :128], flat[:, 128:], oflat, weight[:, :128], weight[:, 128:], oweights[0]]
        + [jnp.zeros((2, 128), jnp.float32)],
        axis=0,
    )
    by_channel[...] = jnp.transpose(
        jnp.concatenate([coeffs[...], jnp.zeros((16, 96), jnp.float32)], axis=1)
    )
    me = lax.axis_index("depth")
    places = []
    for place in range(8):
        target = give.at[place // 2] if place % 2 else keep[place // 2].at[0]
        places.append((target, [order[(me ^ place) * 4 + c] for c in range(4)]))
    for target, channels in places:
        target[AT_MISC:CHUNK, :] = misc
        for c, channel in enumerate(channels):
            row = AT_VALUES + 2 * c
            target[row : row + 2, :] = values[pl.ds(channel * 2, 2), :]
            for k in range(3):
                row = AT_NORMALS + 4 * k + c
                target[row : row + 1, :] = normals[pl.ds(k * 32 + channel, 1), :]
            row = AT_COEFFS + c
            target[row : row + 1, :16] = by_channel[pl.ds(channel, 1), :]
    copies[-1].wait()
    for target, channels in places:
        for c, channel in enumerate(channels):
            plane = control[channel]
            for z in range(4):
                row = z * 16 + c * 4
                target[row : row + 4, :] = plane[z * 4 : z * 4 + 4]


def join_kernel(got, *refs):
    keep, joined = refs[:4], refs[4:]
    for k in range(4):
        joined[k][0] = keep[k][0]
        joined[k][1] = got[k]


def coefficient(expanded, lag, z):
    block, local = divmod(z, 4)
    k = (lag - 1) * 4 + local
    return jnp.broadcast_to(expanded[block, :, k : k + 1], (16, 128))


def expand_coeffs(chunks, expanded, table, scale, root):
    for block in range(8):
        for c in range(4):
            row = AT_COEFFS + c
            expanded[block, 4 * c : 4 * c + 4, :] = jnp.broadcast_to(
                chunks[block, row : row + 1, :], (4, 128)
            )
    for z in range(32):
        lags = [coefficient(expanded, lag, z) for lag in range(1, 5)]
        for lag in range(4):
            table[z, lag] = lags[lag]
        scale[z] = 1.0 - ((lags[0] + lags[1]) + (lags[2] + lags[3]))
        root[z] = jnp.sqrt(scale[z])


def recurrence(source, factor, emit, order):
    history = []
    for t in order:
        total = source(t)
        for lag in range(len(history), 0, -1):
            before, value = history[lag - 1]
            total = total + factor(lag, t, before) * value
        history = [(t, total)] + history[:3]
        emit(t, total)


def depth_rows(chunks, z):
    return chunks[z // 4, (z % 4) * 16 : (z % 4) * 16 + 16, :]


def smooth_kernel(*refs):
    parts, refs = refs[:4], refs[4:]
    chunks, smoothed, even, odd, table, scale, root, expanded, first, rows = refs
    me = lax.axis_index("depth")
    for k in range(4):
        for half in range(2):
            chunks[me ^ (2 * k + half)] = parts[k][half]
    expand_coeffs(chunks, expanded, table, scale, root)

    def keep_first(z, value):
        first[z] = scale[z] * value

    def keep_rows(z, value):
        rows[z * 16 : z * 16 + 16, :] = value

    recurrence(
        lambda z: root[z] * depth_rows(chunks, z),
        lambda lag, z, before: table[z, lag - 1],
        keep_first,
        range(32),
    )
    recurrence(
        lambda z: first[z],
        lambda lag, z, before: table[z, lag - 1],
        keep_rows,
        range(31, -1, -1),
    )
    parity = lax.axis_index("inline") % 2
    for y in range(4):
        for c in range(4):
            smoothed[y, c] = rows[pl.ds(c * 4 + y, 32, stride=16), :]
    for y in range(2):
        even[y] = smoothed[2 - 2 * parity + y]
        odd[y] = smoothed[2 * parity + y]


def tap(table, a, b, h, w):
    row = ((a * 5 + h) * 5 + w) * 4 + b
    return jnp.broadcast_to(table[row : row + 1, :], (8, 128))


def conv_rows(read, rows_in, start, table, adjoint, write):
    lane = lane_index((8, 128))

    def moved(value, shift):
        if shift == 0:
            return value
        inside = lane >= -shift if shift < 0 else lane < 128 - shift
        return jnp.where(inside, pltpu.roll(value, -shift % 128, 1), 0.0)

    def some_depths(k, carry):
        depths = pl.ds(pl.multiple_of(k * 8, 8), 8)
        total = [[start(y, o, depths) for o in range(4)] for y in range(4)]
        for i in range(4):
            lines = {row: read(row, i, depths) for row in rows_in}
            for w in range(5):
                if adjoint:
                    taps = [[tap(table, i, o, h, w) for h in range(5)] for o in range(4)]
                else:
                    taps = [[tap(table, o, i, h, w) for h in range(5)] for o in range(4)]
                for row in rows_in:
                    line = moved(lines[row], 2 - w if adjoint else w - 2)
                    for y in range(4):
                        h = y - row + 2 if adjoint else row - y + 2
                        if 0 <= h < 5:
                            for o in range(4):
                                total[y][o] = total[y][o] + taps[o][h] * line
        for y in range(4):
            for o in range(4):
                write(y, o, depths, total[y][o])
        return carry

    lax.fori_loop(0, 4, some_depths, 0)


OWN = (0, 1, 2, 3)
HALO = (-2, -1, 4, 5)


def halo_reader(even, odd):
    slab, last = lax.axis_index("inline"), lax.axis_size("inline") - 1
    parity = slab % 2

    def read(row, c, depths):
        y = row + 2 if row < 0 else row - 4
        through_even, through_odd = even[y, c, depths, :], odd[y, c, depths, :]
        below = parity == 1 if row < 0 else parity == 0
        outside = slab == 0 if row < 0 else slab == last
        return jnp.where(outside, 0.0, jnp.where(below, through_even, through_odd))

    return read


def split(value):
    high = value.astype(jnp.bfloat16)
    return high, (value - high.astype(jnp.float32)).astype(jnp.bfloat16)


def point_fields(chunks, constant, weight, oweight):
    row = lax.broadcasted_iota(jnp.int32, (16, 256), 0)
    orow = lax.broadcasted_iota(jnp.int32, (16, 128), 0)
    column = lax.broadcasted_iota(jnp.int32, (128, 384), 0)
    for block in range(8):

        def line(k, block=block):
            return chunks[block, k : k + 1, :]

        def double(k, line=line):
            return jnp.concatenate([line(k), line(k + 1)], axis=1)

        flat = double(AT_MISC).astype(jnp.int32)
        oflat = line(AT_MISC + 2).astype(jnp.int32)
        w, ow = double(AT_MISC + 3), line(AT_MISC + 5)
        cell, ocell = flat >> 7, oflat >> 7
        at_cross = jnp.concatenate([flat & 127, oflat & 127], axis=1)
        columns = (column == at_cross).astype(jnp.float32).astype(jnp.bfloat16)
        here, ohere = row == cell, orow == ocell
        below, beside = orow == ocell + 1, orow == ocell + 4
        main, along = [], []
        for c in range(4):
            value = w * double(AT_VALUES + 2 * c)
            n0, n1, n2 = (ow * line(AT_NORMALS + 4 * k + c) for k in range(3))
            placed = (
                jnp.where(below, n0, 0.0)
                + jnp.where(beside, n1, 0.0)
                - jnp.where(ohere, n0 + n1 + n2, 0.0)
            )
            main.append(jnp.concatenate([jnp.where(here, value, 0.0), placed], axis=1))
            along.append(
                jnp.concatenate([jnp.zeros((16, 256), jnp.float32), jnp.where(ohere, n2, 0.0)], axis=1)
            )
        both = [
            jnp.concatenate([jnp.where(here, w, 0.0), jnp.zeros((16, 128), jnp.float32)], axis=1),
            jnp.concatenate([jnp.zeros((16, 256), jnp.float32), jnp.where(ohere, ow, 0.0)], axis=1),
        ]
        high, low = split(jnp.concatenate(main + both + along, axis=0))
        sums = lax.dot_general(
            jnp.concatenate([high, low], axis=0),
            columns,
            (((1,), (1,)), ((), ())),
            preferred_element_type=jnp.float32,
        )
        sums = sums[:160] + sums[160:]
        moved = pltpu.roll(sums[96:160], 1, 1)
        z = 4 * block
        for y in range(4):
            for c in range(4):
                k = 16 * c + 4 * y
                constant[y, c, z : z + 4, :] = sums[k : k + 4] + moved[k : k + 4]
            weight[y, z : z + 4, :] = sums[64 + 4 * y : 68 + 4 * y]
            oweight[y, z : z + 4, :] = sums[80 + 4 * y : 84 + 4 * y]


def own_kernel(chunks, smoothed, kernels, partial, constant, weight, oweight, table):
    group = lax.axis_index("depth")
    picked = jnp.where(lane_index((400, 8)) == group, kernels[...], 0.0)
    table[...] = jnp.broadcast_to(jnp.sum(picked, axis=1, keepdims=True), (400, 128))
    point_fields(chunks, constant, weight, oweight)

    def write(y, o, depths, value):
        partial[y, o, depths, :] = value

    conv_rows(
        lambda row, c, depths: smoothed[row, c, depths, :],
        OWN,
        lambda y, o, depths: jnp.zeros((8, 128), jnp.float32),
        table,
        False,
        write,
    )


def forcing_kernel(
    partial, even_in, odd_in, table, constant, weight, oweight, potential, forcing, even, odd
):
    def write(y, o, depths, value):
        potential[y, o, depths, :] = value

    conv_rows(
        halo_reader(even_in, odd_in),
        HALO,
        lambda y, o, depths: partial[y, o, depths, :],
        table,
        False,
        write,
    )

    def one_channel(c, carry):
        lines = [potential[y, c] for y in range(4)]
        sums = [weight[y] * lines[y] - constant[y, c] for y in range(4)]
        for y in range(4):
            share = oweight[y]
            deeper = share * (pltpu.roll(lines[y], 31, 0) - lines[y])
            across = share * (pltpu.roll(lines[y], 127, 1) - lines[y])
            sums[y] = sums[y] - deeper + pltpu.roll(deeper, 1, 0)
            sums[y] = sums[y] - across + pltpu.roll(across, 1, 1)
            if y < 3:
                beside = share * (lines[y + 1] - lines[y])
                sums[y] = sums[y] - beside
                sums[y + 1] = sums[y + 1] + beside
        for y in range(4):
            forcing[y, c] = sums[y]
        return carry

    lax.fori_loop(0, 4, one_channel, 0)
    parity = lax.axis_index("inline") % 2
    for y in range(2):
        even[y] = forcing[2 - 2 * parity + y]
        odd[y] = forcing[2 * parity + y]


def spread_kernel(forcing, table, potential, partial, out, rows):
    def write(y, o, depths, value):
        partial[y, o, depths, :] = value

    conv_rows(
        lambda row, c, depths: forcing[row, c, depths, :],
        OWN,
        lambda y, o, depths: jnp.zeros((8, 128), jnp.float32),
        table,
        True,
        write,
    )
    for y in range(4):
        for c in range(4):
            rows[pl.ds((c * 4 + y) * 32, 32), :] = potential[y, c]
    for z in range(32):
        out[z // 4, (z % 4) * 16 : (z % 4) * 16 + 16, :] = rows[pl.ds(z, 16, stride=32), :]


def gradient_kernel(*refs):
    chunks, partial, even_in, odd_in, taps, table, scale, root, potential = refs[:9]
    give, keep, (first, rows, out) = refs[9], refs[10:14], refs[14:]
    me = lax.axis_index("depth")
    targets = [
        give.at[place // 2] if place % 2 else keep[place // 2].at[0] for place in range(8)
    ]
    for place, target in enumerate(targets):
        target[:64, :] = potential[me ^ place]

    def write(y, o, depths, value):
        rows[pl.ds(pl.multiple_of((o * 4 + y) * 32 + depths.start, 8), 8), :] = value

    conv_rows(
        halo_reader(even_in, odd_in),
        HALO,
        lambda y, o, depths: partial[y, o, depths, :],
        taps,
        True,
        write,
    )

    def keep_first(z, value):
        first[z] = scale[z] * value

    def keep_out(z, value):
        row = (z % 4) * 16
        out[z // 4, row : row + 16, :] = depth_rows(chunks, z) + root[z] * value

    recurrence(
        lambda z: rows[pl.ds(z, 16, stride=32), :],
        lambda lag, z, before: table[before, lag - 1],
        keep_first,
        range(32),
    )
    recurrence(
        lambda z: first[z],
        lambda lag, z, before: table[before, lag - 1],
        keep_out,
        range(31, -1, -1),
    )
    for place, target in enumerate(targets):
        target[64:, :] = out[me ^ place]


def unpack_kernel(first, count, order, *refs):
    parts, (potential, gradient, planes, sent) = refs[:count], refs[-4:]
    me = lax.axis_index("depth")
    for half, out in enumerate((potential, gradient)):
        slot = 0
        for k in range(count):
            for source in range(2):
                group = me ^ (2 * (first + k) + source)
                for c in range(4):
                    rows = [64 * half + z * 16 + c * 4 for z in range(4)]
                    pieces = [parts[k][source, row : row + 4, :] for row in rows]
                    planes[half, slot] = jnp.concatenate(pieces, axis=0)
                    channel = order[group * 4 + c]
                    pltpu.make_async_copy(
                        planes.at[half, slot], out.at[channel], sent.at[half]
                    ).start()
                    slot += 1
    for half, out in enumerate((potential, gradient)):
        pltpu.make_async_copy(planes.at[half], out.at[: 8 * count], sent.at[half]).wait()


def swapped(even, odd):
    depths, slabs = lax.axis_size("depth"), lax.axis_size("inline")

    def swap(value, first):
        pairs = []
        for d in range(depths):
            for i in range(slabs):
                other = i + 1 if (i - first) % 2 == 0 else i - 1
                to = (d, other) if 0 <= other < slabs else (d ^ 1, i)
                pairs.append((d * slabs + i, to[0] * slabs + to[1]))
        return lax.ppermute(value, ("depth", "inline"), pairs)

    return swap(even, 0), swap(odd, 1)


def by_group(
    control,
    filter_coeffs,
    conv_kernels,
    channel_order,
    point_cells,
    point_values,
    point_weights,
    orient_cells,
    orient_normals,
    orient_weights,
):
    params = pltpu.CompilerParams(vmem_limit_bytes=48 << 20)
    in_vmem, in_smem, in_hbm = (
        pl.BlockSpec(memory_space=space) for space in (pltpu.VMEM, pltpu.SMEM, pltpu.HBM)
    )

    def call(kernel, outs, operands, scratch=(), ins=None, to=in_vmem, aliases=None):
        return pl.pallas_call(
            kernel,
            out_shape=outs,
            in_specs=ins or [in_vmem] * len(operands),
            out_specs=jax.tree.map(lambda _: to, outs),
            scratch_shapes=list(scratch),
            input_output_aliases=aliases or {},
            compiler_params=params,
        )(*operands)

    sources = (
        channel_order,
        jnp.transpose(filter_coeffs, (0, 2, 1)).reshape(16, 32),
        point_values.reshape(64, 128),
        orient_normals.reshape(96, 128),
        point_cells,
        point_weights,
        orient_cells,
        orient_weights,
        control.reshape(32, 16, 128),
    )
    sources = tuple(pltpu.with_memory_space_constraint(x, pltpu.HBM) for x in sources)
    held = [pltpu.VMEM(source.shape, source.dtype) for source in sources]
    held[0] = pltpu.SMEM((32,), jnp.int32)

    def exchange(rows, give, *keep):
        def swap(value, flip):
            return lax.ppermute(value, "depth", [(i, i ^ flip) for i in range(8)])

        both = f32(2, rows, 128)
        joined = call(join_kernel, (both,) * 4, (swap(give, 1), *keep))
        return [joined[0]] + [swap(joined[k], 2 * k) for k in range(1, 4)]

    def staged(rows):
        return (f32(4, rows, 128),) + (f32(2, rows, 128),) * 4

    packed = call(
        pack_kernel,
        staged(CHUNK),
        sources,
        [pltpu.VMEM((128, 16), jnp.float32), pltpu.SemaphoreType.DMA((9,))] + held,
        [in_hbm] * 9,
    )
    parts = exchange(CHUNK, *packed)
    field, edge, plane = f32(4, 4, 32, 128), f32(2, 4, 32, 128), f32(4, 32, 128)
    by_depth = f32(32, 16, 128)
    rows = pltpu.VMEM((512, 128), jnp.float32)
    first = pltpu.VMEM((32, 16, 128), jnp.float32)
    chunks, smoothed, even, odd, table, scale, root = call(
        smooth_kernel,
        (f32(8, CHUNK, 128), field, edge, edge, f32(32, 4, 16, 128), by_depth, by_depth),
        parts,
        [pltpu.VMEM((8, 16, 128), jnp.float32), first, rows],
    )
    even, odd = swapped(even, odd)
    kernels = jnp.transpose(conv_kernels, (1, 3, 4, 2, 0)).reshape(400, 8)
    partial, constant, weight, oweight, taps = call(
        own_kernel, (field, field, plane, plane, f32(400, 128)), (chunks, smoothed, kernels)
    )
    potential, forcing, even, odd = call(
        forcing_kernel,
        (field, field, edge, edge),
        (partial, even, odd, taps, constant, weight, oweight),
    )
    even, odd = swapped(even, odd)
    partial, potential = call(
        spread_kernel, (field, f32(8, 64, 128)), (forcing, taps, potential), [rows]
    )
    results = call(
        gradient_kernel,
        staged(128),
        (chunks, partial, even, odd, taps, table, scale, root, potential),
        [first, rows, pltpu.VMEM((8, 64, 128), jnp.float32)],
    )
    parts = exchange(128, *results)
    outs = ()
    for k, count in ((0, 1), (1, 1), (2, 2)):
        outs = call(
            functools.partial(unpack_kernel, k, count),
            (by_depth, by_depth),
            (channel_order, *parts[k : k + count], *outs),
            [pltpu.VMEM((2, 8 * count, 16, 128), jnp.float32), pltpu.SemaphoreType.DMA((2,))],
            [in_smem] + [in_vmem] * count + [in_hbm] * len(outs),
            in_hbm,
            {count + 1: 0, count + 2: 1} if outs else None,
        )
    potential, gradient = outs
    return potential.reshape(control.shape), gradient.reshape(control.shape)


def solution(mesh):
    placed = (
        P(None, "depth", "inline", None),
        P(None, None, "depth"),
        P(),
        P(),
        P(None, "depth", "inline", None),
        P(None, "depth", "inline", None),
        P("depth", "inline", None),
        P(None, "depth", "inline", None),
        P(None, None, "depth", "inline", None),
        P("depth", "inline", None),
    )

    def body(control, filter_coeffs, conv_kernels, *rest):
        groups, block = conv_kernels.shape, control.shape
        fits = groups[:3] == (mesh.shape["depth"], 4, 4) and groups[0] == 8
        if fits and block == (32, 4, 4, 128):
            return by_group(control, filter_coeffs, conv_kernels, *rest)
        return shards(control, filter_coeffs, conv_kernels, *rest)

    return jax.shard_map(
        body,
        mesh=mesh,
        in_specs=placed,
        out_specs=(P(None, "depth", "inline", None), P(None, "depth", "inline", None)),
        check_vma=False,
    )
```

```python
import functools

import jax
import jax.numpy as jnp
from jax import lax
from jax.experimental import pallas as pl
from jax.experimental.pallas import tpu as pltpu
from jax.sharding import PartitionSpec as P

HIGHEST = lax.Precision.HIGHEST


def entering(value, axis, join, neutral, backward):
    count, mine = (lax.axis_size(axis), lax.axis_index(axis))
    pieces = jax.tree.map(lambda part: lax.all_gather(part, axis), value)
    if backward:
        pieces = jax.tree.map(lambda part: part[::-1], pieces)
        mine = count - 1 - mine
    so_far = jax.tree.map(
        lambda part, zero: jnp.full_like(part, 0) + jnp.asarray(zero, part.dtype), value, neutral
    )

    def hop(position, so_far):
        longer = join(so_far, jax.tree.map(lambda part: part[position], pieces))
        return jax.tree.map(lambda new, old: jnp.where(position < mine, new, old), longer, so_far)

    return lax.fori_loop(0, count - 1, hop, so_far)


def extended_2(cells, sides, width):
    for axis, dim in sides:
        count = lax.axis_size(axis)
        ends = count - 1
        head = lax.slice_in_dim(cells, 0, width, axis=dim)
        tail = lax.slice_in_dim(cells, cells.shape[dim] - width, cells.shape[dim], axis=dim)
        cells = jnp.concatenate(
            [
                lax.ppermute(tail, axis, [(i, (i + 1) % count) for i in range(ends)]),
                cells,
                lax.ppermute(head, axis, [((i + 1) % count, i) for i in range(ends)]),
            ],
            axis=dim,
        )
    return cells


def mixing(kernels, channel_order):
    groups = kernels.shape[0]
    group_size = kernels.shape[1]
    channels = groups * group_size
    slots = jnp.arange(channels, dtype=jnp.int32)
    chooser = (channel_order[:, None] == slots[None, :]).astype(jnp.float32)
    in_group = (
        slots[:, None] // group_size == jnp.arange(groups, dtype=jnp.int32)[None, :]
    ).astype(jnp.float32)
    in_place = (
        slots[:, None] % group_size == jnp.arange(group_size, dtype=jnp.int32)[None, :]
    ).astype(jnp.float32)
    block_mix = jnp.einsum(
        "sg,sa,tg,tb,gabhw->sthw",
        in_group,
        in_place,
        in_group,
        in_place,
        kernels,
        precision=HIGHEST,
    )
    return jnp.einsum("sc,td,sthw->cdhw", chooser, chooser, block_mix, precision=HIGHEST)


def padded_conv(padded, weights):
    return lax.conv_general_dilated(
        padded,
        weights,
        (1, 1),
        ((0, 0), (2, 2)),
        dimension_numbers=("CNHW", "OIHW", "CNHW"),
        precision=HIGHEST,
    )


def compose(earlier, later):
    first_map, first_shift = earlier
    second_map, second_shift = later
    joined_map = jnp.einsum("cnij,cnjk->cnik", second_map, first_map, precision=HIGHEST)
    joined_shift = (
        jnp.einsum("cnij,cnjk->cnik", second_map, first_shift, precision=HIGHEST) + second_shift
    )
    return (joined_map, joined_shift)


def build_tiles(coeffs, by_column, block_len):
    lead = coeffs.shape[1:3]
    lag_steps = jnp.arange(1, 5, dtype=jnp.int32)[:, None, None]
    if by_column:
        row_ids = jnp.arange(block_len + 4, dtype=jnp.int32)[None, :, None]
        col_ids = jnp.arange(block_len, dtype=jnp.int32)[None, None, :]
        picker = (row_ids == col_ids + lag_steps).astype(jnp.float32)
        extended = jnp.einsum("lcnk,lzk->cnzk", coeffs, picker, precision=HIGHEST)
        lower_tile = extended[:, :, :block_len, :]
        exit_map = extended[:, :, block_len:, :]
        entry_base = (
            jnp.arange(block_len, dtype=jnp.int32)[:, None]
            == jnp.arange(4, dtype=jnp.int32)[None, :]
        ).astype(jnp.float32)
        entry_map = jnp.broadcast_to(entry_base, lead + (block_len, 4))
    else:
        row_ids = jnp.arange(block_len, dtype=jnp.int32)[None, :, None]
        col_ids = jnp.arange(block_len + 4, dtype=jnp.int32)[None, None, :]
        picker = (col_ids == row_ids - lag_steps + 4).astype(jnp.float32)
        extended = jnp.einsum("lcnz,lzk->cnzk", coeffs, picker, precision=HIGHEST)
        lower_tile = extended[:, :, :, 4:]
        entry_map = extended[:, :, :, :4]
        exit_base = (
            jnp.arange(block_len, dtype=jnp.int32)[None, :]
            == jnp.arange(4, dtype=jnp.int32)[:, None] + block_len - 4
        ).astype(jnp.float32)
        exit_map = jnp.broadcast_to(exit_base, lead + (4, block_len))
    return (lower_tile, entry_map, exit_map)


def sweep_blocks(field, coeffs, by_column, upward, prefix):
    if upward:
        field = field[:, ::-1, ::-1]
        coeffs = coeffs[:, :, ::-1, ::-1]
    block_len = coeffs.shape[3]
    lower_tile, entry_map, exit_map = build_tiles(coeffs, by_column, block_len)
    identity_tile = jnp.eye(block_len, dtype=jnp.float32)
    inverse = identity_tile + lower_tile
    power = lower_tile
    power = jnp.einsum("cnij,cnjk->cnik", power, power, precision=HIGHEST)
    inverse = inverse + jnp.einsum("cnij,cnjk->cnik", inverse, power, precision=HIGHEST)
    reach_map = jnp.einsum("cnzk,cnkj->cnzj", inverse, entry_map, precision=HIGHEST)
    carry_map = jnp.einsum("cniz,cnzj->cnij", exit_map, reach_map, precision=HIGHEST)
    local_part = jnp.einsum("cnzk,cnkm->cnzm", inverse, field, precision=HIGHEST)
    carry_out = jnp.einsum("cniz,cnzm->cnim", exit_map, local_part, precision=HIGHEST)
    incoming = prefix((carry_map, carry_out), upward)
    result = local_part + jnp.einsum("cnzj,cnjm->cnzm", reach_map, incoming, precision=HIGHEST)
    if upward:
        result = result[:, ::-1, ::-1]
    return result


def shards(
    control,
    filter_coeffs,
    conv_kernels,
    channel_order,
    point_cells,
    point_values,
    point_weights,
    orient_cells,
    orient_normals,
    orient_weights,
):
    channels, block_len, inline_rows, cross_cols = control.shape
    plane_cells = inline_rows * cross_cols
    source = control.reshape(channels, block_len, plane_cells)
    coeffs = filter_coeffs[:, :, None, :]

    def to_blocks(field):
        return field[:, None]

    def from_blocks(field):
        return field[:, 0]

    def scaled(field, factor):
        return factor[..., None] * field

    def prefix(maps, upward):
        start = (
            jnp.broadcast_to(jnp.eye(4, dtype=jnp.float32), maps[0].shape),
            jnp.zeros_like(maps[1]),
        )
        return entering(maps, "depth", compose, start, upward)[1]

    scaling = 1.0 - jnp.sum(coeffs, axis=0)
    root_scale = jnp.sqrt(scaling)
    filtered = sweep_blocks(scaled(to_blocks(source), root_scale), coeffs, False, False, prefix)
    smoothed = sweep_blocks(scaled(filtered, scaling), coeffs, False, True, prefix)
    smoothed_field = from_blocks(smoothed).reshape(control.shape)
    weights = mixing(conv_kernels, channel_order)
    smoothed_padded = extended_2(smoothed_field, (("inline", 2),), 2)
    potential = padded_conv(smoothed_padded, weights)
    flat_field = potential.reshape(channels, -1)
    depth_base = lax.axis_index("depth") * block_len
    inline_base = lax.axis_index("inline") * inline_rows
    cells = point_cells.reshape(3, -1)
    flat_index = (
        (cells[0] - depth_base) * inline_rows + cells[1] - inline_base
    ) * cross_cols + cells[2]
    misfit = (
        flat_field[:, flat_index] - point_values.reshape(channels, -1)
    ) * point_weights.reshape(-1)[None, :]
    ocells = orient_cells.reshape(3, -1)
    base_cell = (
        (ocells[0] - depth_base) * inline_rows + ocells[1] - inline_base
    ) * cross_cols + ocells[2]
    normals = orient_normals.reshape(3, channels, -1)
    oweight = orient_weights.reshape(-1)[None, :]
    update_values = [misfit]
    update_cells = [flat_index]
    for component, stride in enumerate((plane_cells, cross_cols, 1)):
        mismatch = flat_field[:, base_cell + stride] - flat_field[:, base_cell] - normals[component]
        weighted = mismatch * oweight
        update_values.append(weighted)
        update_cells.append(base_cell + stride)
        update_values.append(-weighted)
        update_cells.append(base_cell)
    all_values = jnp.concatenate(update_values, axis=1)
    all_cells = jnp.concatenate(update_cells, axis=0)
    adjoint_weights = jnp.transpose(weights, (1, 0, 2, 3))[:, :, ::-1, ::-1]
    forcing = jnp.zeros_like(flat_field).at[:, all_cells].add(all_values)
    forcing_padded = extended_2(forcing.reshape(control.shape), (("inline", 2),), 2)
    spread = padded_conv(forcing_padded, adjoint_weights).reshape(channels, block_len, plane_cells)
    adjoint_back = scaled(sweep_blocks(to_blocks(spread), coeffs, True, False, prefix), scaling)
    adjoint_fore = scaled(sweep_blocks(adjoint_back, coeffs, True, True, prefix), root_scale)
    gradient = control + from_blocks(adjoint_fore).reshape(control.shape)
    return (potential, gradient)


CHUNK = 96
AT_VALUES, AT_NORMALS, AT_COEFFS, AT_MISC = 64, 72, 84, 88


def f32(*shape):
    return jax.ShapeDtypeStruct(shape, jnp.float32)


def lane_index(shape):
    return lax.broadcasted_iota(jnp.int32, shape, len(shape) - 1)


def pack_kernel(*refs):
    sources, give, keep, by_channel = refs[:9], refs[9], refs[10:14], refs[14]
    arrived, held = refs[15], refs[16:]
    copies = [
        pltpu.make_async_copy(source, target, arrived.at[k])
        for k, (source, target) in enumerate(zip(sources, held))
    ]
    for copy in copies:
        copy.start()
    order, coeffs, values, normals, cells, weights, ocells, oweights, control = held

    def flat_cell(ref):
        z, y, x = (ref[k, 0] for k in range(3))
        return (((y & 3) * 4 + (z & 3)) * 128 + x).astype(jnp.float32)

    for copy in copies[:-1]:
        copy.wait()
    flat, oflat = flat_cell(cells), flat_cell(ocells)
    weight = weights[0]
    misc = jnp.concatenate(
        [flat[:, :128], flat[:, 128:], oflat, weight[:, :128], weight[:, 128:], oweights[0]]
        + [jnp.zeros((2, 128), jnp.float32)],
        axis=0,
    )
    by_channel[...] = jnp.transpose(
        jnp.concatenate([coeffs[...], jnp.zeros((16, 96), jnp.float32)], axis=1)
    )
    me = lax.axis_index("depth")
    places = []
    for place in range(8):
        target = give.at[place // 2] if place % 2 else keep[place // 2].at[0]
        places.append((target, [order[(me ^ place) * 4 + c] for c in range(4)]))
    for target, channels in places:
        target[AT_MISC:CHUNK, :] = misc
        for c, channel in enumerate(channels):
            row = AT_VALUES + 2 * c
            target[row : row + 2, :] = values[pl.ds(channel * 2, 2), :]
            for k in range(3):
                row = AT_NORMALS + 4 * k + c
                target[row : row + 1, :] = normals[pl.ds(k * 32 + channel, 1), :]
            row = AT_COEFFS + c
            target[row : row + 1, :16] = by_channel[pl.ds(channel, 1), :]
    copies[-1].wait()
    for target, channels in places:
        for c, channel in enumerate(channels):
            plane = control[channel]
            for z in range(4):
                row = z * 16 + c * 4
                target[row : row + 4, :] = plane[z * 4 : z * 4 + 4]


def join_kernel(got, *refs):
    keep, joined = refs[:4], refs[4:]
    for k in range(4):
        joined[k][0] = keep[k][0]
        joined[k][1] = got[k]


def coefficient(expanded, lag, z):
    block, local = divmod(z, 4)
    k = (lag - 1) * 4 + local
    return jnp.broadcast_to(expanded[block, :, k : k + 1], (16, 128))


def repeat_coeffs(chunks, expanded):
    for block in range(8):
        for c in range(4):
            row = AT_COEFFS + c
            expanded[block, 4 * c : 4 * c + 4, :] = jnp.broadcast_to(
                chunks[block, row : row + 1, :], (4, 128)
            )


def recurrence(source, factor, emit, order):
    history = []
    for t in order:
        total = source(t)
        for lag in range(len(history), 0, -1):
            before, value = history[lag - 1]
            total = total + factor(lag, t, before) * value
        history = [(t, total)] + history[:3]
        emit(t, total)


def depth_rows(chunks, z):
    return chunks[z // 4, (z % 4) * 16 : (z % 4) * 16 + 16, :]


def smooth_kernel(*refs):
    parts, refs = refs[:4], refs[4:]
    chunks, smoothed, even, odd, table, scale, root, expanded, first, rows = refs
    me = lax.axis_index("depth")
    for k in range(4):
        for half in range(2):
            chunks[me ^ (2 * k + half)] = parts[k][half]
    repeat_coeffs(chunks, expanded)
    lags = {}

    def start(z):
        lags.clear()
        lags.update({lag: coefficient(expanded, lag, z) for lag in range(1, 5)})
        for lag in range(1, 5):
            table[z, lag - 1] = lags[lag]
        lags[0] = 1.0 - ((lags[1] + lags[2]) + (lags[3] + lags[4]))
        scale[z] = lags[0]
        lags[-1] = jnp.sqrt(lags[0])
        root[z] = lags[-1]
        return lags[-1] * depth_rows(chunks, z)

    def keep_first(z, value):
        first[z] = lags[0] * value

    def keep_rows(z, value):
        rows[z * 16 : z * 16 + 16, :] = value

    recurrence(start, lambda lag, z, before: lags[lag], keep_first, range(32))
    recurrence(
        lambda z: first[z],
        lambda lag, z, before: table[z, lag - 1],
        keep_rows,
        range(31, -1, -1),
    )
    parity = lax.axis_index("inline") % 2
    for y in range(4):
        for c in range(4):
            smoothed[y, c] = rows[pl.ds(c * 4 + y, 32, stride=16), :]
    for y in range(2):
        even[y] = smoothed[2 - 2 * parity + y]
        odd[y] = smoothed[2 * parity + y]


def tap(table, a, b, h, w):
    row = ((a * 5 + h) * 5 + w) * 4 + b
    return jnp.broadcast_to(table[row : row + 1, :], (8, 128))


def conv_rows(read, rows_in, start, table, adjoint, write):
    lane = lane_index((8, 128))

    def moved(value, shift):
        if shift == 0:
            return value
        inside = lane >= -shift if shift < 0 else lane < 128 - shift
        return jnp.where(inside, pltpu.roll(value, -shift % 128, 1), 0.0)

    def some_depths(k, carry):
        depths = pl.ds(pl.multiple_of(k * 8, 8), 8)
        total = [[start(y, o, depths) for o in range(4)] for y in range(4)]
        for i in range(4):
            lines = {row: read(row, i, depths) for row in rows_in}
            for w in range(5):
                if adjoint:
                    taps = [[tap(table, i, o, h, w) for h in range(5)] for o in range(4)]
                else:
                    taps = [[tap(table, o, i, h, w) for h in range(5)] for o in range(4)]
                for row in rows_in:
                    line = moved(lines[row], 2 - w if adjoint else w - 2)
                    for y in range(4):
                        h = y - row + 2 if adjoint else row - y + 2
                        if 0 <= h < 5:
                            for o in range(4):
                                total[y][o] = total[y][o] + taps[o][h] * line
        for y in range(4):
            for o in range(4):
                write(y, o, depths, total[y][o])
        return carry

    lax.fori_loop(0, 4, some_depths, 0)


OWN = (0, 1, 2, 3)
HALO = (-2, -1, 4, 5)


def halo_reader(even, odd):
    slab, last = lax.axis_index("inline"), lax.axis_size("inline") - 1
    parity = slab % 2

    def read(row, c, depths):
        y = row + 2 if row < 0 else row - 4
        through_even, through_odd = even[y, c, depths, :], odd[y, c, depths, :]
        below = parity == 1 if row < 0 else parity == 0
        outside = slab == 0 if row < 0 else slab == last
        return jnp.where(outside, 0.0, jnp.where(below, through_even, through_odd))

    return read


def split(value):
    high = value.astype(jnp.bfloat16)
    return high, (value - high.astype(jnp.float32)).astype(jnp.bfloat16)


def point_fields(chunks, constant, weight, oweight):
    row = lax.broadcasted_iota(jnp.int32, (16, 256), 0)
    orow = lax.broadcasted_iota(jnp.int32, (16, 128), 0)
    column = lax.broadcasted_iota(jnp.int32, (128, 384), 0)
    for block in range(8):

        def line(k, block=block):
            return chunks[block, k : k + 1, :]

        def double(k, line=line):
            return jnp.concatenate([line(k), line(k + 1)], axis=1)

        flat = double(AT_MISC).astype(jnp.int32)
        oflat = line(AT_MISC + 2).astype(jnp.int32)
        w, ow = double(AT_MISC + 3), line(AT_MISC + 5)
        cell, ocell = flat >> 7, oflat >> 7
        at_cross = jnp.concatenate([flat & 127, oflat & 127], axis=1)
        columns = (column == at_cross).astype(jnp.float32).astype(jnp.bfloat16)
        here, ohere = row == cell, orow == ocell
        below, beside = orow == ocell + 1, orow == ocell + 4
        main, along = [], []
        for c in range(4):
            value = w * double(AT_VALUES + 2 * c)
            n0, n1, n2 = (ow * line(AT_NORMALS + 4 * k + c) for k in range(3))
            placed = (
                jnp.where(below, n0, 0.0)
                + jnp.where(beside, n1, 0.0)
                - jnp.where(ohere, n0 + n1 + n2, 0.0)
            )
            main.append(jnp.concatenate([jnp.where(here, value, 0.0), placed], axis=1))
            along.append(
                jnp.concatenate([jnp.zeros((16, 256), jnp.float32), jnp.where(ohere, n2, 0.0)], axis=1)
            )
        both = [
            jnp.concatenate([jnp.where(here, w, 0.0), jnp.zeros((16, 128), jnp.float32)], axis=1),
            jnp.concatenate([jnp.zeros((16, 256), jnp.float32), jnp.where(ohere, ow, 0.0)], axis=1),
        ]
        high, low = split(jnp.concatenate(main + both + along, axis=0))
        sums = lax.dot_general(
            jnp.concatenate([high, low], axis=0),
            columns,
            (((1,), (1,)), ((), ())),
            preferred_element_type=jnp.float32,
        )
        sums = sums[:160] + sums[160:]
        moved = pltpu.roll(sums[96:160], 1, 1)
        z = 4 * block
        for y in range(4):
            for c in range(4):
                k = 16 * c + 4 * y
                constant[y, c, z : z + 4, :] = sums[k : k + 4] + moved[k : k + 4]
            weight[y, z : z + 4, :] = sums[64 + 4 * y : 68 + 4 * y]
            oweight[y, z : z + 4, :] = sums[80 + 4 * y : 84 + 4 * y]


def own_kernel(chunks, smoothed, kernels, partial, constant, weight, oweight, table):
    group = lax.axis_index("depth")
    picked = jnp.where(lane_index((400, 8)) == group, kernels[...], 0.0)
    table[...] = jnp.broadcast_to(jnp.sum(picked, axis=1, keepdims=True), (400, 128))
    point_fields(chunks, constant, weight, oweight)

    def write(y, o, depths, value):
        partial[y, o, depths, :] = value

    conv_rows(
        lambda row, c, depths: smoothed[row, c, depths, :],
        OWN,
        lambda y, o, depths: jnp.zeros((8, 128), jnp.float32),
        table,
        False,
        write,
    )


def forcing_kernel(
    partial, even_in, odd_in, table, constant, weight, oweight, potential, forcing, even, odd
):
    def write(y, o, depths, value):
        potential[y, o, depths, :] = value

    conv_rows(
        halo_reader(even_in, odd_in),
        HALO,
        lambda y, o, depths: partial[y, o, depths, :],
        table,
        False,
        write,
    )

    parity = lax.axis_index("inline") % 2

    def some_depths(k, carry):
        depths = pl.ds(pl.multiple_of(k * 8, 8), 8)
        shares = [oweight[y, depths, :] for y in range(4)]
        weights = [weight[y, depths, :] for y in range(4)]
        for c in range(4):
            lines = [potential[y, c, depths, :] for y in range(4)]
            sums = [weights[y] * lines[y] - constant[y, c, depths, :] for y in range(4)]
            for y in range(4):
                deeper = shares[y] * (pltpu.roll(lines[y], 7, 0) - lines[y])
                across = shares[y] * (pltpu.roll(lines[y], 127, 1) - lines[y])
                sums[y] = sums[y] - deeper + pltpu.roll(deeper, 1, 0)
                sums[y] = sums[y] - across + pltpu.roll(across, 1, 1)
                if y < 3:
                    beside = shares[y] * (lines[y + 1] - lines[y])
                    sums[y] = sums[y] - beside
                    sums[y + 1] = sums[y + 1] + beside
            for y in range(4):
                forcing[y, c, depths, :] = sums[y]
            for y in range(2):
                even[y, c, depths, :] = jnp.where(parity == 0, sums[2 + y], sums[y])
                odd[y, c, depths, :] = jnp.where(parity == 0, sums[y], sums[2 + y])
        return carry

    lax.fori_loop(0, 4, some_depths, 0)


def spread_kernel(forcing, table, potential, partial, out, rows):
    def write(y, o, depths, value):
        partial[y, o, depths, :] = value

    conv_rows(
        lambda row, c, depths: forcing[row, c, depths, :],
        OWN,
        lambda y, o, depths: jnp.zeros((8, 128), jnp.float32),
        table,
        True,
        write,
    )
    for y in range(4):
        for c in range(4):
            rows[pl.ds((c * 4 + y) * 32, 32), :] = potential[y, c]
    for z in range(32):
        out[z // 4, (z % 4) * 16 : (z % 4) * 16 + 16, :] = rows[pl.ds(z, 16, stride=32), :]


def gradient_kernel(*refs):
    chunks, partial, even_in, odd_in, taps, table, scale, root, potential = refs[:9]
    give, keep, (first, rows, out) = refs[9], refs[10:14], refs[14:]
    me = lax.axis_index("depth")
    targets = [
        give.at[place // 2] if place % 2 else keep[place // 2].at[0] for place in range(8)
    ]
    for place, target in enumerate(targets):
        target[:64, :] = potential[me ^ place]

    def write(y, o, depths, value):
        rows[pl.ds(pl.multiple_of((o * 4 + y) * 32 + depths.start, 8), 8), :] = value

    conv_rows(
        halo_reader(even_in, odd_in),
        HALO,
        lambda y, o, depths: partial[y, o, depths, :],
        taps,
        True,
        write,
    )

    def keep_first(z, value):
        first[z] = scale[z] * value

    def keep_out(z, value):
        row = (z % 4) * 16
        out[z // 4, row : row + 16, :] = depth_rows(chunks, z) + root[z] * value

    recurrence(
        lambda z: rows[pl.ds(z, 16, stride=32), :],
        lambda lag, z, before: table[before, lag - 1],
        keep_first,
        range(32),
    )
    recurrence(
        lambda z: first[z],
        lambda lag, z, before: table[before, lag - 1],
        keep_out,
        range(31, -1, -1),
    )
    for place, target in enumerate(targets):
        target[64:, :] = out[me ^ place]


def unpack_kernel(first, count, order_in, *refs):
    parts, (potential, gradient, planes, order, sent) = refs[:count], refs[-5:]
    numbers = pltpu.make_async_copy(order_in, order, sent.at[2])
    numbers.start()
    for half in range(2):
        for slot in range(8 * count):
            k, source, c = slot // 8, slot // 4 % 2, slot % 4
            rows = [64 * half + z * 16 + c * 4 for z in range(4)]
            pieces = [parts[k][source, row : row + 4, :] for row in rows]
            planes[half, slot] = jnp.concatenate(pieces, axis=0)
    numbers.wait()
    me = lax.axis_index("depth")
    for slot in range(8 * count):
        channel = order[(me ^ (2 * first + slot // 4)) * 4 + slot % 4]
        for half, out in enumerate((potential, gradient)):
            pltpu.make_async_copy(planes.at[half, slot], out.at[channel], sent.at[half]).start()
    for half, out in enumerate((potential, gradient)):
        pltpu.make_async_copy(planes.at[half], out.at[: 8 * count], sent.at[half]).wait()


def swapped(even, odd):
    depths, slabs = lax.axis_size("depth"), lax.axis_size("inline")

    def swap(value, first):
        pairs = []
        for d in range(depths):
            for i in range(slabs):
                other = i + 1 if (i - first) % 2 == 0 else i - 1
                to = (d, other) if 0 <= other < slabs else (d ^ 1, i)
                pairs.append((d * slabs + i, to[0] * slabs + to[1]))
        return lax.ppermute(value, ("depth", "inline"), pairs)

    return swap(even, 0), swap(odd, 1)


def by_group(
    control,
    filter_coeffs,
    conv_kernels,
    channel_order,
    point_cells,
    point_values,
    point_weights,
    orient_cells,
    orient_normals,
    orient_weights,
):
    params = pltpu.CompilerParams(vmem_limit_bytes=48 << 20)
    in_vmem, in_hbm = (pl.BlockSpec(memory_space=space) for space in (pltpu.VMEM, pltpu.HBM))

    def call(kernel, outs, operands, scratch=(), ins=None, to=in_vmem, aliases=None):
        return pl.pallas_call(
            kernel,
            out_shape=outs,
            in_specs=ins or [in_vmem] * len(operands),
            out_specs=jax.tree.map(lambda _: to, outs),
            scratch_shapes=list(scratch),
            input_output_aliases=aliases or {},
            compiler_params=params,
        )(*operands)

    sources = (
        channel_order,
        jnp.transpose(filter_coeffs, (0, 2, 1)).reshape(16, 32),
        point_values.reshape(64, 128),
        orient_normals.reshape(96, 128),
        point_cells,
        point_weights,
        orient_cells,
        orient_weights,
        control.reshape(32, 16, 128),
    )
    sources = tuple(pltpu.with_memory_space_constraint(x, pltpu.HBM) for x in sources)
    held = [pltpu.VMEM(source.shape, source.dtype) for source in sources]
    held[0] = pltpu.SMEM((32,), jnp.int32)

    def exchange(rows, give, *keep):
        def swap(value, flip):
            return lax.ppermute(value, "depth", [(i, i ^ flip) for i in range(8)])

        both = f32(2, rows, 128)
        joined = call(join_kernel, (both,) * 4, (swap(give, 1), *keep))
        return [joined[0]] + [swap(joined[k], 2 * k) for k in range(1, 4)]

    def staged(rows):
        return (f32(4, rows, 128),) + (f32(2, rows, 128),) * 4

    packed = call(
        pack_kernel,
        staged(CHUNK),
        sources,
        [pltpu.VMEM((128, 16), jnp.float32), pltpu.SemaphoreType.DMA((9,))] + held,
        [in_hbm] * 9,
    )
    parts = exchange(CHUNK, *packed)
    field, edge, plane = f32(4, 4, 32, 128), f32(2, 4, 32, 128), f32(4, 32, 128)
    by_depth = f32(32, 16, 128)
    rows = pltpu.VMEM((512, 128), jnp.float32)
    first = pltpu.VMEM((32, 16, 128), jnp.float32)
    chunks, smoothed, even, odd, table, scale, root = call(
        smooth_kernel,
        (f32(8, CHUNK, 128), field, edge, edge, f32(32, 4, 16, 128), by_depth, by_depth),
        parts,
        [pltpu.VMEM((8, 16, 128), jnp.float32), first, rows],
    )
    even, odd = swapped(even, odd)
    kernels = jnp.transpose(conv_kernels, (1, 3, 4, 2, 0)).reshape(400, 8)
    partial, constant, weight, oweight, taps = call(
        own_kernel, (field, field, plane, plane, f32(400, 128)), (chunks, smoothed, kernels)
    )
    potential, forcing, even, odd = call(
        forcing_kernel,
        (field, field, edge, edge),
        (partial, even, odd, taps, constant, weight, oweight),
    )
    even, odd = swapped(even, odd)
    partial, potential = call(
        spread_kernel, (field, f32(8, 64, 128)), (forcing, taps, potential), [rows]
    )
    results = call(
        gradient_kernel,
        staged(128),
        (chunks, partial, even, odd, taps, table, scale, root, potential),
        [first, rows, pltpu.VMEM((8, 64, 128), jnp.float32)],
    )
    parts = exchange(128, *results)
    outs = ()
    for k, count in ((0, 1), (1, 1), (2, 2)):
        outs = call(
            functools.partial(unpack_kernel, k, count),
            (by_depth, by_depth),
            (channel_order, *parts[k : k + count], *outs),
            [
                pltpu.VMEM((2, 8 * count, 16, 128), jnp.float32),
                pltpu.SMEM((32,), jnp.int32),
                pltpu.SemaphoreType.DMA((3,)),
            ],
            [in_vmem] * (count + 1) + [in_hbm] * len(outs),
            in_hbm,
            {count + 1: 0, count + 2: 1} if outs else None,
        )
    potential, gradient = outs
    return potential.reshape(control.shape), gradient.reshape(control.shape)


def solution(mesh):
    placed = (
        P(None, "depth", "inline", None),
        P(None, None, "depth"),
        P(),
        P(),
        P(None, "depth", "inline", None),
        P(None, "depth", "inline", None),
        P("depth", "inline", None),
        P(None, "depth", "inline", None),
        P(None, None, "depth", "inline", None),
        P("depth", "inline", None),
    )

    def body(control, filter_coeffs, conv_kernels, *rest):
        groups, block = conv_kernels.shape, control.shape
        fits = groups[:3] == (mesh.shape["depth"], 4, 4) and groups[0] == 8
        if fits and block == (32, 4, 4, 128):
            return by_group(control, filter_coeffs, conv_kernels, *rest)
        return shards(control, filter_coeffs, conv_kernels, *rest)

    return jax.shard_map(
        body,
        mesh=mesh,
        in_specs=placed,
        out_specs=(P(None, "depth", "inline", None), P(None, "depth", "inline", None)),
        check_vma=False,
    )
```

```python
import functools

import jax
import jax.numpy as jnp
from jax import lax
from jax.experimental import pallas as pl
from jax.experimental.pallas import tpu as pltpu
from jax.sharding import PartitionSpec as P

HIGHEST = lax.Precision.HIGHEST


def entering(value, axis, join, neutral, backward):
    count, mine = (lax.axis_size(axis), lax.axis_index(axis))
    pieces = jax.tree.map(lambda part: lax.all_gather(part, axis), value)
    if backward:
        pieces = jax.tree.map(lambda part: part[::-1], pieces)
        mine = count - 1 - mine
    so_far = jax.tree.map(
        lambda part, zero: jnp.full_like(part, 0) + jnp.asarray(zero, part.dtype), value, neutral
    )

    def hop(position, so_far):
        longer = join(so_far, jax.tree.map(lambda part: part[position], pieces))
        return jax.tree.map(lambda new, old: jnp.where(position < mine, new, old), longer, so_far)

    return lax.fori_loop(0, count - 1, hop, so_far)


def extended_2(cells, sides, width):
    for axis, dim in sides:
        count = lax.axis_size(axis)
        ends = count - 1
        head = lax.slice_in_dim(cells, 0, width, axis=dim)
        tail = lax.slice_in_dim(cells, cells.shape[dim] - width, cells.shape[dim], axis=dim)
        cells = jnp.concatenate(
            [
                lax.ppermute(tail, axis, [(i, (i + 1) % count) for i in range(ends)]),
                cells,
                lax.ppermute(head, axis, [((i + 1) % count, i) for i in range(ends)]),
            ],
            axis=dim,
        )
    return cells


def mixing(kernels, channel_order):
    groups = kernels.shape[0]
    group_size = kernels.shape[1]
    channels = groups * group_size
    slots = jnp.arange(channels, dtype=jnp.int32)
    chooser = (channel_order[:, None] == slots[None, :]).astype(jnp.float32)
    in_group = (
        slots[:, None] // group_size == jnp.arange(groups, dtype=jnp.int32)[None, :]
    ).astype(jnp.float32)
    in_place = (
        slots[:, None] % group_size == jnp.arange(group_size, dtype=jnp.int32)[None, :]
    ).astype(jnp.float32)
    block_mix = jnp.einsum(
        "sg,sa,tg,tb,gabhw->sthw",
        in_group,
        in_place,
        in_group,
        in_place,
        kernels,
        precision=HIGHEST,
    )
    return jnp.einsum("sc,td,sthw->cdhw", chooser, chooser, block_mix, precision=HIGHEST)


def padded_conv(padded, weights):
    return lax.conv_general_dilated(
        padded,
        weights,
        (1, 1),
        ((0, 0), (2, 2)),
        dimension_numbers=("CNHW", "OIHW", "CNHW"),
        precision=HIGHEST,
    )


def compose(earlier, later):
    first_map, first_shift = earlier
    second_map, second_shift = later
    joined_map = jnp.einsum("cnij,cnjk->cnik", second_map, first_map, precision=HIGHEST)
    joined_shift = (
        jnp.einsum("cnij,cnjk->cnik", second_map, first_shift, precision=HIGHEST) + second_shift
    )
    return (joined_map, joined_shift)


def build_tiles(coeffs, by_column, block_len):
    lead = coeffs.shape[1:3]
    lag_steps = jnp.arange(1, 5, dtype=jnp.int32)[:, None, None]
    if by_column:
        row_ids = jnp.arange(block_len + 4, dtype=jnp.int32)[None, :, None]
        col_ids = jnp.arange(block_len, dtype=jnp.int32)[None, None, :]
        picker = (row_ids == col_ids + lag_steps).astype(jnp.float32)
        extended = jnp.einsum("lcnk,lzk->cnzk", coeffs, picker, precision=HIGHEST)
        lower_tile = extended[:, :, :block_len, :]
        exit_map = extended[:, :, block_len:, :]
        entry_base = (
            jnp.arange(block_len, dtype=jnp.int32)[:, None]
            == jnp.arange(4, dtype=jnp.int32)[None, :]
        ).astype(jnp.float32)
        entry_map = jnp.broadcast_to(entry_base, lead + (block_len, 4))
    else:
        row_ids = jnp.arange(block_len, dtype=jnp.int32)[None, :, None]
        col_ids = jnp.arange(block_len + 4, dtype=jnp.int32)[None, None, :]
        picker = (col_ids == row_ids - lag_steps + 4).astype(jnp.float32)
        extended = jnp.einsum("lcnz,lzk->cnzk", coeffs, picker, precision=HIGHEST)
        lower_tile = extended[:, :, :, 4:]
        entry_map = extended[:, :, :, :4]
        exit_base = (
            jnp.arange(block_len, dtype=jnp.int32)[None, :]
            == jnp.arange(4, dtype=jnp.int32)[:, None] + block_len - 4
        ).astype(jnp.float32)
        exit_map = jnp.broadcast_to(exit_base, lead + (4, block_len))
    return (lower_tile, entry_map, exit_map)


def sweep_blocks(field, coeffs, by_column, upward, prefix):
    if upward:
        field = field[:, ::-1, ::-1]
        coeffs = coeffs[:, :, ::-1, ::-1]
    block_len = coeffs.shape[3]
    lower_tile, entry_map, exit_map = build_tiles(coeffs, by_column, block_len)
    identity_tile = jnp.eye(block_len, dtype=jnp.float32)
    inverse = identity_tile + lower_tile
    power = lower_tile
    power = jnp.einsum("cnij,cnjk->cnik", power, power, precision=HIGHEST)
    inverse = inverse + jnp.einsum("cnij,cnjk->cnik", inverse, power, precision=HIGHEST)
    reach_map = jnp.einsum("cnzk,cnkj->cnzj", inverse, entry_map, precision=HIGHEST)
    carry_map = jnp.einsum("cniz,cnzj->cnij", exit_map, reach_map, precision=HIGHEST)
    local_part = jnp.einsum("cnzk,cnkm->cnzm", inverse, field, precision=HIGHEST)
    carry_out = jnp.einsum("cniz,cnzm->cnim", exit_map, local_part, precision=HIGHEST)
    incoming = prefix((carry_map, carry_out), upward)
    result = local_part + jnp.einsum("cnzj,cnjm->cnzm", reach_map, incoming, precision=HIGHEST)
    if upward:
        result = result[:, ::-1, ::-1]
    return result


def shards(
    control,
    filter_coeffs,
    conv_kernels,
    channel_order,
    point_cells,
    point_values,
    point_weights,
    orient_cells,
    orient_normals,
    orient_weights,
):
    channels, block_len, inline_rows, cross_cols = control.shape
    plane_cells = inline_rows * cross_cols
    source = control.reshape(channels, block_len, plane_cells)
    coeffs = filter_coeffs[:, :, None, :]

    def to_blocks(field):
        return field[:, None]

    def from_blocks(field):
        return field[:, 0]

    def scaled(field, factor):
        return factor[..., None] * field

    def prefix(maps, upward):
        start = (
            jnp.broadcast_to(jnp.eye(4, dtype=jnp.float32), maps[0].shape),
            jnp.zeros_like(maps[1]),
        )
        return entering(maps, "depth", compose, start, upward)[1]

    scaling = 1.0 - jnp.sum(coeffs, axis=0)
    root_scale = jnp.sqrt(scaling)
    filtered = sweep_blocks(scaled(to_blocks(source), root_scale), coeffs, False, False, prefix)
    smoothed = sweep_blocks(scaled(filtered, scaling), coeffs, False, True, prefix)
    smoothed_field = from_blocks(smoothed).reshape(control.shape)
    weights = mixing(conv_kernels, channel_order)
    smoothed_padded = extended_2(smoothed_field, (("inline", 2),), 2)
    potential = padded_conv(smoothed_padded, weights)
    flat_field = potential.reshape(channels, -1)
    depth_base = lax.axis_index("depth") * block_len
    inline_base = lax.axis_index("inline") * inline_rows
    cells = point_cells.reshape(3, -1)
    flat_index = (
        (cells[0] - depth_base) * inline_rows + cells[1] - inline_base
    ) * cross_cols + cells[2]
    misfit = (
        flat_field[:, flat_index] - point_values.reshape(channels, -1)
    ) * point_weights.reshape(-1)[None, :]
    ocells = orient_cells.reshape(3, -1)
    base_cell = (
        (ocells[0] - depth_base) * inline_rows + ocells[1] - inline_base
    ) * cross_cols + ocells[2]
    normals = orient_normals.reshape(3, channels, -1)
    oweight = orient_weights.reshape(-1)[None, :]
    update_values = [misfit]
    update_cells = [flat_index]
    for component, stride in enumerate((plane_cells, cross_cols, 1)):
        mismatch = flat_field[:, base_cell + stride] - flat_field[:, base_cell] - normals[component]
        weighted = mismatch * oweight
        update_values.append(weighted)
        update_cells.append(base_cell + stride)
        update_values.append(-weighted)
        update_cells.append(base_cell)
    all_values = jnp.concatenate(update_values, axis=1)
    all_cells = jnp.concatenate(update_cells, axis=0)
    adjoint_weights = jnp.transpose(weights, (1, 0, 2, 3))[:, :, ::-1, ::-1]
    forcing = jnp.zeros_like(flat_field).at[:, all_cells].add(all_values)
    forcing_padded = extended_2(forcing.reshape(control.shape), (("inline", 2),), 2)
    spread = padded_conv(forcing_padded, adjoint_weights).reshape(channels, block_len, plane_cells)
    adjoint_back = scaled(sweep_blocks(to_blocks(spread), coeffs, True, False, prefix), scaling)
    adjoint_fore = scaled(sweep_blocks(adjoint_back, coeffs, True, True, prefix), root_scale)
    gradient = control + from_blocks(adjoint_fore).reshape(control.shape)
    return (potential, gradient)


CHUNK = 96
CHIPS = (0, 3, 1, 2)
AT_VALUES, AT_NORMALS, AT_COEFFS, AT_MISC = 64, 72, 84, 88


def f32(*shape):
    return jax.ShapeDtypeStruct(shape, jnp.float32)


def lane_index(shape):
    return lax.broadcasted_iota(jnp.int32, shape, len(shape) - 1)


def pack_kernel(*refs):
    sources, give, keep, by_channel = refs[:9], refs[9], refs[10:14], refs[14]
    arrived, held = refs[15], refs[16:]
    copies = [
        pltpu.make_async_copy(source, target, arrived.at[k])
        for k, (source, target) in enumerate(zip(sources, held))
    ]
    for copy in copies:
        copy.start()
    order, coeffs, values, normals, cells, weights, ocells, oweights, control = held

    def flat_cell(ref):
        z, y, x = (ref[k, 0] for k in range(3))
        return (((y & 3) * 4 + (z & 3)) * 128 + x).astype(jnp.float32)

    for copy in copies[:-1]:
        copy.wait()
    flat, oflat = flat_cell(cells), flat_cell(ocells)
    weight = weights[0]
    misc = jnp.concatenate(
        [flat[:, :128], flat[:, 128:], oflat, weight[:, :128], weight[:, 128:], oweights[0]]
        + [jnp.zeros((2, 128), jnp.float32)],
        axis=0,
    )
    by_channel[...] = jnp.transpose(
        jnp.concatenate([coeffs[...], jnp.zeros((16, 96), jnp.float32)], axis=1)
    )
    me = lax.axis_index("depth")
    places = []
    for place in range(8):
        target = give.at[place // 2] if place % 2 else keep[place // 2].at[0]
        places.append((target, [order[(me ^ place) * 4 + c] for c in range(4)]))
    for target, channels in places:
        target[AT_MISC:CHUNK, :] = misc
        for c, channel in enumerate(channels):
            row = AT_VALUES + 2 * c
            target[row : row + 2, :] = values[pl.ds(channel * 2, 2), :]
            for k in range(3):
                row = AT_NORMALS + 4 * k + c
                target[row : row + 1, :] = normals[pl.ds(k * 32 + channel, 1), :]
            row = AT_COEFFS + c
            target[row : row + 1, :16] = by_channel[pl.ds(channel, 1), :]
    copies[-1].wait()
    for target, channels in places:
        for c, channel in enumerate(channels):
            plane = control[channel]
            for z in range(4):
                row = z * 16 + c * 4
                target[row : row + 4, :] = plane[z * 4 : z * 4 + 4]


def join_kernel(got, *refs):
    keep, joined = refs[:4], refs[4:]
    for k in range(4):
        joined[k][0] = keep[k][0]
        joined[k][1] = got[k]


def coefficient(expanded, lag, z):
    block, local = divmod(z, 4)
    k = (lag - 1) * 4 + local
    return jnp.broadcast_to(expanded[block, :, k : k + 1], (16, 128))


def repeat_coeffs(chunks, expanded):
    for block in range(8):
        for c in range(4):
            row = AT_COEFFS + c
            expanded[block, 4 * c : 4 * c + 4, :] = jnp.broadcast_to(
                chunks[block, row : row + 1, :], (4, 128)
            )


def recurrence(source, factor, emit, order):
    history = []
    for t in order:
        total = source(t)
        for lag in range(len(history), 0, -1):
            before, value = history[lag - 1]
            total = total + factor(lag, t, before) * value
        history = [(t, total)] + history[:3]
        emit(t, total)


def depth_rows(chunks, z):
    return chunks[z // 4, (z % 4) * 16 : (z % 4) * 16 + 16, :]


def smooth_kernel(*refs):
    parts, refs = refs[:4], refs[4:]
    chunks, smoothed, even, odd, table, scale, root, expanded, first, rows = refs
    me = lax.axis_index("depth")
    for k, part in zip(CHIPS, parts):
        for half in range(2):
            chunks[me ^ (2 * k + half)] = part[half]
    repeat_coeffs(chunks, expanded)
    lags = {}

    def start(z):
        lags.clear()
        lags.update({lag: coefficient(expanded, lag, z) for lag in range(1, 5)})
        for lag in range(1, 5):
            table[z, lag - 1] = lags[lag]
        lags[0] = 1.0 - ((lags[1] + lags[2]) + (lags[3] + lags[4]))
        scale[z] = lags[0]
        lags[-1] = jnp.sqrt(lags[0])
        root[z] = lags[-1]
        return lags[-1] * depth_rows(chunks, z)

    def keep_first(z, value):
        first[z] = lags[0] * value

    def keep_rows(z, value):
        rows[z * 16 : z * 16 + 16, :] = value

    recurrence(start, lambda lag, z, before: lags[lag], keep_first, range(32))
    recurrence(
        lambda z: first[z],
        lambda lag, z, before: table[z, lag - 1],
        keep_rows,
        range(31, -1, -1),
    )
    parity = lax.axis_index("inline") % 2
    for y in range(4):
        for c in range(4):
            smoothed[y, c] = rows[pl.ds(c * 4 + y, 32, stride=16), :]
    for y in range(2):
        even[y] = smoothed[2 - 2 * parity + y]
        odd[y] = smoothed[2 * parity + y]


def tap(table, a, b, h, w):
    row = ((a * 5 + h) * 5 + w) * 4 + b
    return jnp.broadcast_to(table[row : row + 1, :], (8, 128))


def conv_rows(read, rows_in, start, table, adjoint, write):
    lane = lane_index((8, 128))

    def moved(value, shift):
        if shift == 0:
            return value
        inside = lane >= -shift if shift < 0 else lane < 128 - shift
        return jnp.where(inside, pltpu.roll(value, -shift % 128, 1), 0.0)

    def some_depths(k, carry):
        pieces = [pl.ds(pl.multiple_of(k * 16 + 8 * n, 8), 8) for n in range(2)]
        total = [[[start(y, o, at) for at in pieces] for o in range(4)] for y in range(4)]
        for i in range(4):
            lines = {row: [read(row, i, at) for at in pieces] for row in rows_in}
            for w in range(5):
                shift = 2 - w if adjoint else w - 2
                shifted_lines = {
                    row: [moved(value, shift) for value in lines[row]] for row in rows_in
                }
                for h in range(5):
                    rows = [y - h + 2 if adjoint else y + h - 2 for y in range(4)]
                    for o in range(4):
                        weight = tap(table, i, o, h, w) if adjoint else tap(table, o, i, h, w)
                        for y, row in enumerate(rows):
                            if row in rows_in:
                                for n in range(2):
                                    line = shifted_lines[row][n]
                                    total[y][o][n] = total[y][o][n] + weight * line
        for y in range(4):
            for o in range(4):
                for n in range(2):
                    write(y, o, pieces[n], total[y][o][n])
        return carry

    lax.fori_loop(0, 2, some_depths, 0)


OWN = (0, 1, 2, 3)
HALO = (-2, -1, 4, 5)


def halo_reader(even, odd):
    slab, last = lax.axis_index("inline"), lax.axis_size("inline") - 1
    parity = slab % 2

    def read(row, c, depths):
        y = row + 2 if row < 0 else row - 4
        through_even, through_odd = even[y, c, depths, :], odd[y, c, depths, :]
        below = parity == 1 if row < 0 else parity == 0
        outside = slab == 0 if row < 0 else slab == last
        return jnp.where(outside, 0.0, jnp.where(below, through_even, through_odd))

    return read


def split(value):
    high = value.astype(jnp.bfloat16)
    return high, (value - high.astype(jnp.float32)).astype(jnp.bfloat16)


def point_fields(chunks, constant, weight, oweight):
    row = lax.broadcasted_iota(jnp.int32, (16, 256), 0)
    orow = lax.broadcasted_iota(jnp.int32, (16, 128), 0)
    column = lax.broadcasted_iota(jnp.int32, (128, 384), 0)
    for block in range(8):

        def line(k, block=block):
            return chunks[block, k : k + 1, :]

        def double(k, line=line):
            return jnp.concatenate([line(k), line(k + 1)], axis=1)

        flat = double(AT_MISC).astype(jnp.int32)
        oflat = line(AT_MISC + 2).astype(jnp.int32)
        w, ow = double(AT_MISC + 3), line(AT_MISC + 5)
        cell, ocell = flat >> 7, oflat >> 7
        at_cross = jnp.concatenate([flat & 127, oflat & 127], axis=1)
        columns = (column == at_cross).astype(jnp.float32).astype(jnp.bfloat16)
        here, ohere = row == cell, orow == ocell
        below, beside = orow == ocell + 1, orow == ocell + 4
        main, along = [], []
        for c in range(4):
            value = w * double(AT_VALUES + 2 * c)
            n0, n1, n2 = (ow * line(AT_NORMALS + 4 * k + c) for k in range(3))
            placed = (
                jnp.where(below, n0, 0.0)
                + jnp.where(beside, n1, 0.0)
                - jnp.where(ohere, n0 + n1 + n2, 0.0)
            )
            main.append(jnp.concatenate([jnp.where(here, value, 0.0), placed], axis=1))
            along.append(
                jnp.concatenate([jnp.zeros((16, 256), jnp.float32), jnp.where(ohere, n2, 0.0)], axis=1)
            )
        both = [
            jnp.concatenate([jnp.where(here, w, 0.0), jnp.zeros((16, 128), jnp.float32)], axis=1),
            jnp.concatenate([jnp.zeros((16, 256), jnp.float32), jnp.where(ohere, ow, 0.0)], axis=1),
        ]
        high, low = split(jnp.concatenate(main + both + along, axis=0))
        sums = lax.dot_general(
            jnp.concatenate([high, low], axis=0),
            columns,
            (((1,), (1,)), ((), ())),
            preferred_element_type=jnp.float32,
        )
        sums = sums[:160] + sums[160:]
        moved = pltpu.roll(sums[96:160], 1, 1)
        z = 4 * block
        for y in range(4):
            for c in range(4):
                k = 16 * c + 4 * y
                constant[y, c, z : z + 4, :] = sums[k : k + 4] + moved[k : k + 4]
            weight[y, z : z + 4, :] = sums[64 + 4 * y : 68 + 4 * y]
            oweight[y, z : z + 4, :] = sums[80 + 4 * y : 84 + 4 * y]


def own_kernel(chunks, smoothed, kernels, partial, constant, weight, oweight, table):
    group = lax.axis_index("depth")
    picked = jnp.where(lane_index((400, 8)) == group, kernels[...], 0.0)
    table[...] = jnp.broadcast_to(jnp.sum(picked, axis=1, keepdims=True), (400, 128))
    point_fields(chunks, constant, weight, oweight)

    def write(y, o, depths, value):
        partial[y, o, depths, :] = value

    conv_rows(
        lambda row, c, depths: smoothed[row, c, depths, :],
        OWN,
        lambda y, o, depths: jnp.zeros((8, 128), jnp.float32),
        table,
        False,
        write,
    )


def forcing_kernel(
    partial, even_in, odd_in, table, constant, weight, oweight, potential, forcing, even, odd
):
    def write(y, o, depths, value):
        potential[y, o, depths, :] = value

    conv_rows(
        halo_reader(even_in, odd_in),
        HALO,
        lambda y, o, depths: partial[y, o, depths, :],
        table,
        False,
        write,
    )

    parity = lax.axis_index("inline") % 2

    def some_depths(k, carry):
        depths = pl.ds(pl.multiple_of(k * 8, 8), 8)
        shares = [oweight[y, depths, :] for y in range(4)]
        weights = [weight[y, depths, :] for y in range(4)]
        for c in range(4):
            lines = [potential[y, c, depths, :] for y in range(4)]
            sums = [weights[y] * lines[y] - constant[y, c, depths, :] for y in range(4)]
            for y in range(4):
                deeper = shares[y] * (pltpu.roll(lines[y], 7, 0) - lines[y])
                across = shares[y] * (pltpu.roll(lines[y], 127, 1) - lines[y])
                sums[y] = sums[y] - deeper + pltpu.roll(deeper, 1, 0)
                sums[y] = sums[y] - across + pltpu.roll(across, 1, 1)
                if y < 3:
                    beside = shares[y] * (lines[y + 1] - lines[y])
                    sums[y] = sums[y] - beside
                    sums[y + 1] = sums[y + 1] + beside
            for y in range(4):
                forcing[y, c, depths, :] = sums[y]
            for y in range(2):
                even[y, c, depths, :] = jnp.where(parity == 0, sums[2 + y], sums[y])
                odd[y, c, depths, :] = jnp.where(parity == 0, sums[y], sums[2 + y])
        return carry

    lax.fori_loop(0, 4, some_depths, 0)


def spread_kernel(forcing, table, potential, partial, out, rows):
    def write(y, o, depths, value):
        partial[y, o, depths, :] = value

    conv_rows(
        lambda row, c, depths: forcing[row, c, depths, :],
        OWN,
        lambda y, o, depths: jnp.zeros((8, 128), jnp.float32),
        table,
        True,
        write,
    )
    for y in range(4):
        for c in range(4):
            rows[pl.ds((c * 4 + y) * 32, 32), :] = potential[y, c]
    for z in range(32):
        out[z // 4, (z % 4) * 16 : (z % 4) * 16 + 16, :] = rows[pl.ds(z, 16, stride=32), :]


def gradient_kernel(*refs):
    chunks, partial, even_in, odd_in, taps, table, scale, root, potential = refs[:9]
    give, keep, (first, rows, out) = refs[9], refs[10:14], refs[14:]
    me = lax.axis_index("depth")
    targets = [
        give.at[place // 2] if place % 2 else keep[place // 2].at[0] for place in range(8)
    ]
    for place, target in enumerate(targets):
        target[:64, :] = potential[me ^ place]

    def write(y, o, depths, value):
        rows[pl.ds(pl.multiple_of((o * 4 + y) * 32 + depths.start, 8), 8), :] = value

    conv_rows(
        halo_reader(even_in, odd_in),
        HALO,
        lambda y, o, depths: partial[y, o, depths, :],
        taps,
        True,
        write,
    )

    def keep_first(z, value):
        first[z] = scale[z] * value

    def keep_out(z, value):
        row = (z % 4) * 16
        out[z // 4, row : row + 16, :] = depth_rows(chunks, z) + root[z] * value

    recurrence(
        lambda z: rows[pl.ds(z, 16, stride=32), :],
        lambda lag, z, before: table[before, lag - 1],
        keep_first,
        range(32),
    )
    recurrence(
        lambda z: first[z],
        lambda lag, z, before: table[before, lag - 1],
        keep_out,
        range(31, -1, -1),
    )
    for place, target in enumerate(targets):
        target[64:, :] = out[me ^ place]


def unpack_kernel(chips, order_in, *refs):
    count = len(chips)
    parts, (potential, gradient, planes, order, sent) = refs[:count], refs[-5:]
    numbers = pltpu.make_async_copy(order_in, order, sent.at[2])
    numbers.start()
    for half in range(2):
        for slot in range(8 * count):
            k, source, c = slot // 8, slot // 4 % 2, slot % 4
            rows = [64 * half + z * 16 + c * 4 for z in range(4)]
            pieces = [parts[k][source, row : row + 4, :] for row in rows]
            planes[half, slot] = jnp.concatenate(pieces, axis=0)
    numbers.wait()
    me = lax.axis_index("depth")
    for slot in range(8 * count):
        place = 2 * chips[slot // 8] + slot // 4 % 2
        channel = order[(me ^ place) * 4 + slot % 4]
        for half, out in enumerate((potential, gradient)):
            pltpu.make_async_copy(planes.at[half, slot], out.at[channel], sent.at[half]).start()
    for half, out in enumerate((potential, gradient)):
        pltpu.make_async_copy(planes.at[half], out.at[: 8 * count], sent.at[half]).wait()


def swapped(even, odd):
    depths, slabs = lax.axis_size("depth"), lax.axis_size("inline")

    def swap(value, first):
        pairs = []
        for d in range(depths):
            for i in range(slabs):
                other = i + 1 if (i - first) % 2 == 0 else i - 1
                to = (d, other) if 0 <= other < slabs else (d ^ 1, i)
                pairs.append((d * slabs + i, to[0] * slabs + to[1]))
        return lax.ppermute(value, ("depth", "inline"), pairs)

    return swap(even, 0), swap(odd, 1)


def by_group(
    control,
    filter_coeffs,
    conv_kernels,
    channel_order,
    point_cells,
    point_values,
    point_weights,
    orient_cells,
    orient_normals,
    orient_weights,
):
    params = pltpu.CompilerParams(vmem_limit_bytes=48 << 20)
    in_vmem, in_hbm = (pl.BlockSpec(memory_space=space) for space in (pltpu.VMEM, pltpu.HBM))

    def call(kernel, outs, operands, scratch=(), ins=None, to=in_vmem, aliases=None):
        return pl.pallas_call(
            kernel,
            out_shape=outs,
            in_specs=ins or [in_vmem] * len(operands),
            out_specs=jax.tree.map(lambda _: to, outs),
            scratch_shapes=list(scratch),
            input_output_aliases=aliases or {},
            compiler_params=params,
        )(*operands)

    sources = (
        channel_order,
        jnp.transpose(filter_coeffs, (0, 2, 1)).reshape(16, 32),
        point_values.reshape(64, 128),
        orient_normals.reshape(96, 128),
        point_cells,
        point_weights,
        orient_cells,
        orient_weights,
        control.reshape(32, 16, 128),
    )
    sources = tuple(pltpu.with_memory_space_constraint(x, pltpu.HBM) for x in sources)
    held = [pltpu.VMEM(source.shape, source.dtype) for source in sources]
    held[0] = pltpu.SMEM((32,), jnp.int32)

    def exchange(rows, give, *keep):
        def swap(value, flip):
            return lax.ppermute(value, "depth", [(i, i ^ flip) for i in range(8)])

        both = f32(2, rows, 128)
        joined = call(join_kernel, (both,) * 4, (swap(give, 1), *keep))
        return [joined[k] if k == 0 else swap(joined[k], 2 * k) for k in CHIPS]

    def staged(rows):
        return (f32(4, rows, 128),) + (f32(2, rows, 128),) * 4

    packed = call(
        pack_kernel,
        staged(CHUNK),
        sources,
        [pltpu.VMEM((128, 16), jnp.float32), pltpu.SemaphoreType.DMA((9,))] + held,
        [in_hbm] * 9,
    )
    parts = exchange(CHUNK, *packed)
    field, edge, plane = f32(4, 4, 32, 128), f32(2, 4, 32, 128), f32(4, 32, 128)
    by_depth = f32(32, 16, 128)
    rows = pltpu.VMEM((512, 128), jnp.float32)
    first = pltpu.VMEM((32, 16, 128), jnp.float32)
    chunks, smoothed, even, odd, table, scale, root = call(
        smooth_kernel,
        (f32(8, CHUNK, 128), field, edge, edge, f32(32, 4, 16, 128), by_depth, by_depth),
        parts,
        [pltpu.VMEM((8, 16, 128), jnp.float32), first, rows],
    )
    even, odd = swapped(even, odd)
    kernels = jnp.transpose(conv_kernels, (1, 3, 4, 2, 0)).reshape(400, 8)
    partial, constant, weight, oweight, taps = call(
        own_kernel, (field, field, plane, plane, f32(400, 128)), (chunks, smoothed, kernels)
    )
    potential, forcing, even, odd = call(
        forcing_kernel,
        (field, field, edge, edge),
        (partial, even, odd, taps, constant, weight, oweight),
    )
    even, odd = swapped(even, odd)
    partial, potential = call(
        spread_kernel, (field, f32(8, 64, 128)), (forcing, taps, potential), [rows]
    )
    results = call(
        gradient_kernel,
        staged(128),
        (chunks, partial, even, odd, taps, table, scale, root, potential),
        [first, rows, pltpu.VMEM((8, 64, 128), jnp.float32)],
    )
    parts = exchange(128, *results)
    outs = ()
    for some in (slice(0, 1), slice(1, 2), slice(2, 4)):
        count = len(CHIPS[some])
        outs = call(
            functools.partial(unpack_kernel, CHIPS[some]),
            (by_depth, by_depth),
            (channel_order, *parts[some], *outs),
            [
                pltpu.VMEM((2, 8 * count, 16, 128), jnp.float32),
                pltpu.SMEM((32,), jnp.int32),
                pltpu.SemaphoreType.DMA((3,)),
            ],
            [in_vmem] * (count + 1) + [in_hbm] * len(outs),
            in_hbm,
            {count + 1: 0, count + 2: 1} if outs else None,
        )
    potential, gradient = outs
    return potential.reshape(control.shape), gradient.reshape(control.shape)


def solution(mesh):
    placed = (
        P(None, "depth", "inline", None),
        P(None, None, "depth"),
        P(),
        P(),
        P(None, "depth", "inline", None),
        P(None, "depth", "inline", None),
        P("depth", "inline", None),
        P(None, "depth", "inline", None),
        P(None, None, "depth", "inline", None),
        P("depth", "inline", None),
    )

    def body(control, filter_coeffs, conv_kernels, *rest):
        groups, block = conv_kernels.shape, control.shape
        fits = groups[:3] == (mesh.shape["depth"], 4, 4) and groups[0] == 8
        if fits and block == (32, 4, 4, 128):
            return by_group(control, filter_coeffs, conv_kernels, *rest)
        return shards(control, filter_coeffs, conv_kernels, *rest)

    return jax.shard_map(
        body,
        mesh=mesh,
        in_specs=placed,
        out_specs=(P(None, "depth", "inline", None), P(None, "depth", "inline", None)),
        check_vma=False,
    )
```

```python
import functools

import jax
import jax.numpy as jnp
from jax import lax
from jax.experimental import pallas as pl
from jax.experimental.pallas import tpu as pltpu
from jax.sharding import PartitionSpec as P

HIGHEST = lax.Precision.HIGHEST


def entering(value, axis, join, neutral, backward):
    count, mine = (lax.axis_size(axis), lax.axis_index(axis))
    pieces = jax.tree.map(lambda part: lax.all_gather(part, axis), value)
    if backward:
        pieces = jax.tree.map(lambda part: part[::-1], pieces)
        mine = count - 1 - mine
    so_far = jax.tree.map(
        lambda part, zero: jnp.full_like(part, 0) + jnp.asarray(zero, part.dtype), value, neutral
    )

    def hop(position, so_far):
        longer = join(so_far, jax.tree.map(lambda part: part[position], pieces))
        return jax.tree.map(lambda new, old: jnp.where(position < mine, new, old), longer, so_far)

    return lax.fori_loop(0, count - 1, hop, so_far)


def extended_2(cells, sides, width):
    for axis, dim in sides:
        count = lax.axis_size(axis)
        ends = count - 1
        head = lax.slice_in_dim(cells, 0, width, axis=dim)
        tail = lax.slice_in_dim(cells, cells.shape[dim] - width, cells.shape[dim], axis=dim)
        cells = jnp.concatenate(
            [
                lax.ppermute(tail, axis, [(i, (i + 1) % count) for i in range(ends)]),
                cells,
                lax.ppermute(head, axis, [((i + 1) % count, i) for i in range(ends)]),
            ],
            axis=dim,
        )
    return cells


def mixing(kernels, channel_order):
    groups = kernels.shape[0]
    group_size = kernels.shape[1]
    channels = groups * group_size
    slots = jnp.arange(channels, dtype=jnp.int32)
    chooser = (channel_order[:, None] == slots[None, :]).astype(jnp.float32)
    in_group = (
        slots[:, None] // group_size == jnp.arange(groups, dtype=jnp.int32)[None, :]
    ).astype(jnp.float32)
    in_place = (
        slots[:, None] % group_size == jnp.arange(group_size, dtype=jnp.int32)[None, :]
    ).astype(jnp.float32)
    block_mix = jnp.einsum(
        "sg,sa,tg,tb,gabhw->sthw",
        in_group,
        in_place,
        in_group,
        in_place,
        kernels,
        precision=HIGHEST,
    )
    return jnp.einsum("sc,td,sthw->cdhw", chooser, chooser, block_mix, precision=HIGHEST)


def padded_conv(padded, weights):
    return lax.conv_general_dilated(
        padded,
        weights,
        (1, 1),
        ((0, 0), (2, 2)),
        dimension_numbers=("CNHW", "OIHW", "CNHW"),
        precision=HIGHEST,
    )


def compose(earlier, later):
    first_map, first_shift = earlier
    second_map, second_shift = later
    joined_map = jnp.einsum("cnij,cnjk->cnik", second_map, first_map, precision=HIGHEST)
    joined_shift = (
        jnp.einsum("cnij,cnjk->cnik", second_map, first_shift, precision=HIGHEST) + second_shift
    )
    return (joined_map, joined_shift)


def build_tiles(coeffs, by_column, block_len):
    lead = coeffs.shape[1:3]
    lag_steps = jnp.arange(1, 5, dtype=jnp.int32)[:, None, None]
    if by_column:
        row_ids = jnp.arange(block_len + 4, dtype=jnp.int32)[None, :, None]
        col_ids = jnp.arange(block_len, dtype=jnp.int32)[None, None, :]
        picker = (row_ids == col_ids + lag_steps).astype(jnp.float32)
        extended = jnp.einsum("lcnk,lzk->cnzk", coeffs, picker, precision=HIGHEST)
        lower_tile = extended[:, :, :block_len, :]
        exit_map = extended[:, :, block_len:, :]
        entry_base = (
            jnp.arange(block_len, dtype=jnp.int32)[:, None]
            == jnp.arange(4, dtype=jnp.int32)[None, :]
        ).astype(jnp.float32)
        entry_map = jnp.broadcast_to(entry_base, lead + (block_len, 4))
    else:
        row_ids = jnp.arange(block_len, dtype=jnp.int32)[None, :, None]
        col_ids = jnp.arange(block_len + 4, dtype=jnp.int32)[None, None, :]
        picker = (col_ids == row_ids - lag_steps + 4).astype(jnp.float32)
        extended = jnp.einsum("lcnz,lzk->cnzk", coeffs, picker, precision=HIGHEST)
        lower_tile = extended[:, :, :, 4:]
        entry_map = extended[:, :, :, :4]
        exit_base = (
            jnp.arange(block_len, dtype=jnp.int32)[None, :]
            == jnp.arange(4, dtype=jnp.int32)[:, None] + block_len - 4
        ).astype(jnp.float32)
        exit_map = jnp.broadcast_to(exit_base, lead + (4, block_len))
    return (lower_tile, entry_map, exit_map)


def sweep_blocks(field, coeffs, by_column, upward, prefix):
    if upward:
        field = field[:, ::-1, ::-1]
        coeffs = coeffs[:, :, ::-1, ::-1]
    block_len = coeffs.shape[3]
    lower_tile, entry_map, exit_map = build_tiles(coeffs, by_column, block_len)
    identity_tile = jnp.eye(block_len, dtype=jnp.float32)
    inverse = identity_tile + lower_tile
    power = lower_tile
    power = jnp.einsum("cnij,cnjk->cnik", power, power, precision=HIGHEST)
    inverse = inverse + jnp.einsum("cnij,cnjk->cnik", inverse, power, precision=HIGHEST)
    reach_map = jnp.einsum("cnzk,cnkj->cnzj", inverse, entry_map, precision=HIGHEST)
    carry_map = jnp.einsum("cniz,cnzj->cnij", exit_map, reach_map, precision=HIGHEST)
    local_part = jnp.einsum("cnzk,cnkm->cnzm", inverse, field, precision=HIGHEST)
    carry_out = jnp.einsum("cniz,cnzm->cnim", exit_map, local_part, precision=HIGHEST)
    incoming = prefix((carry_map, carry_out), upward)
    result = local_part + jnp.einsum("cnzj,cnjm->cnzm", reach_map, incoming, precision=HIGHEST)
    if upward:
        result = result[:, ::-1, ::-1]
    return result


def shards(
    control,
    filter_coeffs,
    conv_kernels,
    channel_order,
    point_cells,
    point_values,
    point_weights,
    orient_cells,
    orient_normals,
    orient_weights,
):
    channels, block_len, inline_rows, cross_cols = control.shape
    plane_cells = inline_rows * cross_cols
    source = control.reshape(channels, block_len, plane_cells)
    coeffs = filter_coeffs[:, :, None, :]

    def to_blocks(field):
        return field[:, None]

    def from_blocks(field):
        return field[:, 0]

    def scaled(field, factor):
        return factor[..., None] * field

    def prefix(maps, upward):
        start = (
            jnp.broadcast_to(jnp.eye(4, dtype=jnp.float32), maps[0].shape),
            jnp.zeros_like(maps[1]),
        )
        return entering(maps, "depth", compose, start, upward)[1]

    scaling = 1.0 - jnp.sum(coeffs, axis=0)
    root_scale = jnp.sqrt(scaling)
    filtered = sweep_blocks(scaled(to_blocks(source), root_scale), coeffs, False, False, prefix)
    smoothed = sweep_blocks(scaled(filtered, scaling), coeffs, False, True, prefix)
    smoothed_field = from_blocks(smoothed).reshape(control.shape)
    weights = mixing(conv_kernels, channel_order)
    smoothed_padded = extended_2(smoothed_field, (("inline", 2),), 2)
    potential = padded_conv(smoothed_padded, weights)
    flat_field = potential.reshape(channels, -1)
    depth_base = lax.axis_index("depth") * block_len
    inline_base = lax.axis_index("inline") * inline_rows
    cells = point_cells.reshape(3, -1)
    flat_index = (
        (cells[0] - depth_base) * inline_rows + cells[1] - inline_base
    ) * cross_cols + cells[2]
    misfit = (
        flat_field[:, flat_index] - point_values.reshape(channels, -1)
    ) * point_weights.reshape(-1)[None, :]
    ocells = orient_cells.reshape(3, -1)
    base_cell = (
        (ocells[0] - depth_base) * inline_rows + ocells[1] - inline_base
    ) * cross_cols + ocells[2]
    normals = orient_normals.reshape(3, channels, -1)
    oweight = orient_weights.reshape(-1)[None, :]
    update_values = [misfit]
    update_cells = [flat_index]
    for component, stride in enumerate((plane_cells, cross_cols, 1)):
        mismatch = flat_field[:, base_cell + stride] - flat_field[:, base_cell] - normals[component]
        weighted = mismatch * oweight
        update_values.append(weighted)
        update_cells.append(base_cell + stride)
        update_values.append(-weighted)
        update_cells.append(base_cell)
    all_values = jnp.concatenate(update_values, axis=1)
    all_cells = jnp.concatenate(update_cells, axis=0)
    adjoint_weights = jnp.transpose(weights, (1, 0, 2, 3))[:, :, ::-1, ::-1]
    forcing = jnp.zeros_like(flat_field).at[:, all_cells].add(all_values)
    forcing_padded = extended_2(forcing.reshape(control.shape), (("inline", 2),), 2)
    spread = padded_conv(forcing_padded, adjoint_weights).reshape(channels, block_len, plane_cells)
    adjoint_back = scaled(sweep_blocks(to_blocks(spread), coeffs, True, False, prefix), scaling)
    adjoint_fore = scaled(sweep_blocks(adjoint_back, coeffs, True, True, prefix), root_scale)
    gradient = control + from_blocks(adjoint_fore).reshape(control.shape)
    return (potential, gradient)


CHUNK = 96
CHIPS = (0, 3, 2, 1)
AT_VALUES, AT_NORMALS, AT_COEFFS, AT_MISC = 64, 72, 84, 88


def f32(*shape):
    return jax.ShapeDtypeStruct(shape, jnp.float32)


def lane_index(shape):
    return lax.broadcasted_iota(jnp.int32, shape, len(shape) - 1)


def place_points(target, channels, values, normals, misc, by_channel):
    target[AT_MISC:CHUNK, :] = misc
    for c, channel in enumerate(channels):
        row = AT_VALUES + 2 * c
        target[row : row + 2, :] = values[pl.ds(channel * 2, 2), :]
        for k in range(3):
            row = AT_NORMALS + 4 * k + c
            target[row : row + 1, :] = normals[pl.ds(k * 32 + channel, 1), :]
        row = AT_COEFFS + c
        target[row : row + 1, :] = by_channel[pl.ds(channel, 1), :]


def place_control(target, channels, control):
    for c, channel in enumerate(channels):
        plane = control[channel]
        for z in range(4):
            row = z * 16 + c * 4
            target[row : row + 4, :] = plane[z * 4 : z * 4 + 4]


def pack_kernel(*refs):
    sources, give, misc, by_channel, number = refs[:9], refs[9], refs[10], refs[11], refs[12]
    control, values, normals, order, coeffs, cells, weights, ocells, oweights, arrived = refs[13:]
    held = (order, number, coeffs, cells, weights, ocells, oweights, values, normals, control)
    copies = [
        pltpu.make_async_copy(source, target, arrived.at[k])
        for k, (source, target) in enumerate(zip(sources[:1] + sources, held))
    ]
    for copy in copies:
        copy.start()

    def flat_cell(ref):
        z, y, x = (ref[k, 0] for k in range(3))
        return (((y & 3) * 4 + (z & 3)) * 128 + x).astype(jnp.float32)

    for copy in copies[:-1]:
        copy.wait()
    flat, oflat = flat_cell(cells), flat_cell(ocells)
    weight = weights[0]
    misc[...] = jnp.concatenate(
        [flat[:, :128], flat[:, 128:], oflat, weight[:, :128], weight[:, 128:], oweights[0]]
        + [jnp.zeros((2, 128), jnp.float32)],
        axis=0,
    )
    by_channel[:, :16] = jnp.transpose(
        jnp.concatenate([coeffs[...], jnp.zeros((16, 96), jnp.float32)], axis=1)
    )
    by_channel[:, 16:] = jnp.zeros((128, 112), jnp.float32)
    me = lax.axis_index("depth")
    places = [
        (give.at[k], [order[(me ^ (2 * k + 1)) * 4 + c] for c in range(4)]) for k in range(4)
    ]
    for target, channels in places:
        place_points(target, channels, values, normals, misc[...], by_channel)
    copies[-1].wait()
    for target, channels in places:
        place_control(target, channels, control)


def keep_kernel(misc, by_channel, number, control, values, normals, *refs):
    keep, order, arrived = refs[:4], refs[4], refs[5]
    numbers = pltpu.make_async_copy(number, order, arrived)
    numbers.start()
    numbers.wait()
    me = lax.axis_index("depth")
    for k in range(4):
        channels = [order[(me ^ (2 * k)) * 4 + c] for c in range(4)]
        place_points(keep[k], channels, values, normals, misc[...], by_channel)
        place_control(keep[k], channels, control)


def join_kernel(got, *refs):
    keep, joined = refs[:4], refs[4:]
    for k in range(4):
        joined[k][0] = keep[k][...]
        joined[k][1] = got[k]


def coefficient(expanded, lag, z):
    block, local = divmod(z, 4)
    k = (lag - 1) * 4 + local
    return jnp.broadcast_to(expanded[block, :, k : k + 1], (16, 128))


def repeat_coeffs(chunks, expanded):
    for block in range(8):
        for c in range(4):
            row = AT_COEFFS + c
            expanded[block, 4 * c : 4 * c + 4, :] = jnp.broadcast_to(
                chunks[block, row : row + 1, :], (4, 128)
            )


def recurrence(source, factor, emit, order):
    history = []
    for t in order:
        total = source(t)
        for lag in range(len(history), 0, -1):
            before, value = history[lag - 1]
            total = total + factor(lag, t, before) * value
        history = [(t, total)] + history[:3]
        emit(t, total)


def depth_rows(chunks, z):
    return chunks[z // 4, (z % 4) * 16 : (z % 4) * 16 + 16, :]


def smooth_kernel(*refs):
    parts, refs = refs[:4], refs[4:]
    chunks, smoothed, even, odd, table, scale, root, expanded, first, rows = refs
    me = lax.axis_index("depth")
    for k, part in zip(CHIPS, parts):
        for half in range(2):
            chunks[me ^ (2 * k + half)] = part[half]
    repeat_coeffs(chunks, expanded)
    lags = {}

    def start(z):
        lags.clear()
        lags.update({lag: coefficient(expanded, lag, z) for lag in range(1, 5)})
        for lag in range(1, 5):
            table[z, lag - 1] = lags[lag]
        lags[0] = 1.0 - ((lags[1] + lags[2]) + (lags[3] + lags[4]))
        scale[z] = lags[0]
        lags[-1] = jnp.sqrt(lags[0])
        root[z] = lags[-1]
        return lags[-1] * depth_rows(chunks, z)

    def keep_first(z, value):
        first[z] = lags[0] * value

    def keep_rows(z, value):
        rows[z * 16 : z * 16 + 16, :] = value

    recurrence(start, lambda lag, z, before: lags[lag], keep_first, range(32))
    recurrence(
        lambda z: first[z],
        lambda lag, z, before: table[z, lag - 1],
        keep_rows,
        range(31, -1, -1),
    )
    parity = lax.axis_index("inline") % 2
    for y in range(4):
        for c in range(4):
            smoothed[y, c] = rows[pl.ds(c * 4 + y, 32, stride=16), :]
    for y in range(2):
        even[y] = smoothed[2 - 2 * parity + y]
        odd[y] = smoothed[2 * parity + y]


def tap(table, a, b, h, w):
    row = ((a * 5 + h) * 5 + w) * 4 + b
    return jnp.broadcast_to(table[row : row + 1, :], (8, 128))


def conv_rows(read, rows_in, start, table, adjoint, write):
    lane = lane_index((8, 128))

    def moved(value, shift):
        if shift == 0:
            return value
        inside = lane >= -shift if shift < 0 else lane < 128 - shift
        return jnp.where(inside, pltpu.roll(value, -shift % 128, 1), 0.0)

    def some_depths(k, carry):
        pieces = [pl.ds(pl.multiple_of(k * 16 + 8 * n, 8), 8) for n in range(2)]
        total = [[[start(y, o, at) for at in pieces] for o in range(4)] for y in range(4)]
        for i in range(4):
            lines = {row: [read(row, i, at) for at in pieces] for row in rows_in}
            for w in range(5):
                shift = 2 - w if adjoint else w - 2
                shifted_lines = {
                    row: [moved(value, shift) for value in lines[row]] for row in rows_in
                }
                for h in range(5):
                    rows = [y - h + 2 if adjoint else y + h - 2 for y in range(4)]
                    for o in range(4):
                        weight = tap(table, i, o, h, w) if adjoint else tap(table, o, i, h, w)
                        for y, row in enumerate(rows):
                            if row in rows_in:
                                for n in range(2):
                                    line = shifted_lines[row][n]
                                    total[y][o][n] = total[y][o][n] + weight * line
        for y in range(4):
            for o in range(4):
                for n in range(2):
                    write(y, o, pieces[n], total[y][o][n])
        return carry

    lax.fori_loop(0, 2, some_depths, 0)


OWN = (0, 1, 2, 3)
HALO = (-2, -1, 4, 5)


def halo_reader(even, odd):
    slab, last = lax.axis_index("inline"), lax.axis_size("inline") - 1
    parity = slab % 2

    def read(row, c, depths):
        y = row + 2 if row < 0 else row - 4
        through_even, through_odd = even[y, c, depths, :], odd[y, c, depths, :]
        below = parity == 1 if row < 0 else parity == 0
        outside = slab == 0 if row < 0 else slab == last
        return jnp.where(outside, 0.0, jnp.where(below, through_even, through_odd))

    return read


def split(value):
    high = value.astype(jnp.bfloat16)
    return high, (value - high.astype(jnp.float32)).astype(jnp.bfloat16)


def point_fields(chunks, constant, weight, oweight):
    row = lax.broadcasted_iota(jnp.int32, (16, 256), 0)
    orow = lax.broadcasted_iota(jnp.int32, (16, 128), 0)
    column = lax.broadcasted_iota(jnp.int32, (128, 384), 0)
    for block in range(8):

        def line(k, block=block):
            return chunks[block, k : k + 1, :]

        def double(k, line=line):
            return jnp.concatenate([line(k), line(k + 1)], axis=1)

        flat = double(AT_MISC).astype(jnp.int32)
        oflat = line(AT_MISC + 2).astype(jnp.int32)
        w, ow = double(AT_MISC + 3), line(AT_MISC + 5)
        cell, ocell = flat >> 7, oflat >> 7
        at_cross = jnp.concatenate([flat & 127, oflat & 127], axis=1)
        columns = (column == at_cross).astype(jnp.float32).astype(jnp.bfloat16)
        here, ohere = row == cell, orow == ocell
        below, beside = orow == ocell + 1, orow == ocell + 4
        main, along = [], []
        for c in range(4):
            value = w * double(AT_VALUES + 2 * c)
            n0, n1, n2 = (ow * line(AT_NORMALS + 4 * k + c) for k in range(3))
            placed = (
                jnp.where(below, n0, 0.0)
                + jnp.where(beside, n1, 0.0)
                - jnp.where(ohere, n0 + n1 + n2, 0.0)
            )
            main.append(jnp.concatenate([jnp.where(here, value, 0.0), placed], axis=1))
            along.append(
                jnp.concatenate([jnp.zeros((16, 256), jnp.float32), jnp.where(ohere, n2, 0.0)], axis=1)
            )
        both = [
            jnp.concatenate([jnp.where(here, w, 0.0), jnp.zeros((16, 128), jnp.float32)], axis=1),
            jnp.concatenate([jnp.zeros((16, 256), jnp.float32), jnp.where(ohere, ow, 0.0)], axis=1),
        ]
        high, low = split(jnp.concatenate(main + both + along, axis=0))
        sums = lax.dot_general(
            jnp.concatenate([high, low], axis=0),
            columns,
            (((1,), (1,)), ((), ())),
            preferred_element_type=jnp.float32,
        )
        sums = sums[:160] + sums[160:]
        moved = pltpu.roll(sums[96:160], 1, 1)
        z = 4 * block
        for y in range(4):
            for c in range(4):
                k = 16 * c + 4 * y
                constant[y, c, z : z + 4, :] = sums[k : k + 4] + moved[k : k + 4]
            weight[y, z : z + 4, :] = sums[64 + 4 * y : 68 + 4 * y]
            oweight[y, z : z + 4, :] = sums[80 + 4 * y : 84 + 4 * y]


def own_kernel(chunks, smoothed, kernels, partial, constant, weight, oweight, table):
    group = lax.axis_index("depth")
    picked = jnp.where(lane_index((400, 8)) == group, kernels[...], 0.0)
    table[...] = jnp.broadcast_to(jnp.sum(picked, axis=1, keepdims=True), (400, 128))
    point_fields(chunks, constant, weight, oweight)

    def write(y, o, depths, value):
        partial[y, o, depths, :] = value

    conv_rows(
        lambda row, c, depths: smoothed[row, c, depths, :],
        OWN,
        lambda y, o, depths: jnp.zeros((8, 128), jnp.float32),
        table,
        False,
        write,
    )


def forcing_kernel(
    partial, even_in, odd_in, table, constant, weight, oweight, potential, forcing, even, odd
):
    def write(y, o, depths, value):
        potential[y, o, depths, :] = value

    conv_rows(
        halo_reader(even_in, odd_in),
        HALO,
        lambda y, o, depths: partial[y, o, depths, :],
        table,
        False,
        write,
    )

    parity = lax.axis_index("inline") % 2

    def some_depths(k, carry):
        depths = pl.ds(pl.multiple_of(k * 8, 8), 8)
        shares = [oweight[y, depths, :] for y in range(4)]
        weights = [weight[y, depths, :] for y in range(4)]
        for c in range(4):
            lines = [potential[y, c, depths, :] for y in range(4)]
            sums = [weights[y] * lines[y] - constant[y, c, depths, :] for y in range(4)]
            for y in range(4):
                deeper = shares[y] * (pltpu.roll(lines[y], 7, 0) - lines[y])
                across = shares[y] * (pltpu.roll(lines[y], 127, 1) - lines[y])
                sums[y] = sums[y] - deeper + pltpu.roll(deeper, 1, 0)
                sums[y] = sums[y] - across + pltpu.roll(across, 1, 1)
                if y < 3:
                    beside = shares[y] * (lines[y + 1] - lines[y])
                    sums[y] = sums[y] - beside
                    sums[y + 1] = sums[y + 1] + beside
            for y in range(4):
                forcing[y, c, depths, :] = sums[y]
            for y in range(2):
                even[y, c, depths, :] = jnp.where(parity == 0, sums[2 + y], sums[y])
                odd[y, c, depths, :] = jnp.where(parity == 0, sums[y], sums[2 + y])
        return carry

    lax.fori_loop(0, 4, some_depths, 0)


def spread_kernel(forcing, table, potential, partial, out, rows):
    def write(y, o, depths, value):
        partial[y, o, depths, :] = value

    conv_rows(
        lambda row, c, depths: forcing[row, c, depths, :],
        OWN,
        lambda y, o, depths: jnp.zeros((8, 128), jnp.float32),
        table,
        True,
        write,
    )
    for y in range(4):
        for c in range(4):
            rows[pl.ds((c * 4 + y) * 32, 32), :] = potential[y, c]
    for z in range(32):
        out[z // 4, (z % 4) * 16 : (z % 4) * 16 + 16, :] = rows[pl.ds(z, 16, stride=32), :]


def gradient_kernel(*refs):
    chunks, partial, even_in, odd_in, taps, table, scale, root, potential = refs[:9]
    give, keep, (first, rows, out) = refs[9], refs[10:14], refs[14:]
    me = lax.axis_index("depth")
    targets = [
        give.at[place // 2] if place % 2 else keep[place // 2] for place in range(8)
    ]
    for place, target in enumerate(targets):
        target[:64, :] = potential[me ^ place]

    def write(y, o, depths, value):
        rows[pl.ds(pl.multiple_of((o * 4 + y) * 32 + depths.start, 8), 8), :] = value

    conv_rows(
        halo_reader(even_in, odd_in),
        HALO,
        lambda y, o, depths: partial[y, o, depths, :],
        taps,
        True,
        write,
    )

    def keep_first(z, value):
        first[z] = scale[z] * value

    def keep_out(z, value):
        row = (z % 4) * 16
        out[z // 4, row : row + 16, :] = depth_rows(chunks, z) + root[z] * value

    recurrence(
        lambda z: rows[pl.ds(z, 16, stride=32), :],
        lambda lag, z, before: table[before, lag - 1],
        keep_first,
        range(32),
    )
    recurrence(
        lambda z: first[z],
        lambda lag, z, before: table[before, lag - 1],
        keep_out,
        range(31, -1, -1),
    )
    for place, target in enumerate(targets):
        target[64:, :] = out[me ^ place]


def unpack_kernel(chips, number, *refs):
    count = len(chips)
    parts, (potential, gradient, planes, sent) = refs[:count], refs[-4:]
    me = lax.axis_index("depth")
    order = number[...].reshape(1, 32)
    lane = lane_index((1, 32))
    channels = []
    for slot in range(8 * count):
        place = 2 * chips[slot // 8] + slot // 4 % 2
        here = lane == (me ^ place) * 4 + slot % 4
        channels.append(jnp.sum(jnp.where(here, order, 0)))
    for half in range(2):
        for slot in range(8 * count):
            k, source, c = slot // 8, slot // 4 % 2, slot % 4
            rows = [64 * half + z * 16 + c * 4 for z in range(4)]
            pieces = [parts[k][source, row : row + 4, :] for row in rows]
            planes[half, slot] = jnp.concatenate(pieces, axis=0)
    for slot in range(8 * count):
        for half, out in enumerate((potential, gradient)):
            pltpu.make_async_copy(
                planes.at[half, slot], out.at[channels[slot]], sent.at[half]
            ).start()
    for half, out in enumerate((potential, gradient)):
        pltpu.make_async_copy(planes.at[half], out.at[: 8 * count], sent.at[half]).wait()


def swapped(even, odd):
    depths, slabs = lax.axis_size("depth"), lax.axis_size("inline")

    def swap(value, first):
        pairs = []
        for d in range(depths):
            for i in range(slabs):
                other = i + 1 if (i - first) % 2 == 0 else i - 1
                to = (d, other) if 0 <= other < slabs else (d ^ 1, i)
                pairs.append((d * slabs + i, to[0] * slabs + to[1]))
        return lax.ppermute(value, ("depth", "inline"), pairs)

    return swap(even, 0), swap(odd, 1)


def by_group(
    control,
    filter_coeffs,
    conv_kernels,
    channel_order,
    point_cells,
    point_values,
    point_weights,
    orient_cells,
    orient_normals,
    orient_weights,
):
    params = pltpu.CompilerParams(vmem_limit_bytes=48 << 20)
    in_vmem, in_hbm = (pl.BlockSpec(memory_space=space) for space in (pltpu.VMEM, pltpu.HBM))

    def call(kernel, outs, operands, scratch=(), ins=None, to=in_vmem, aliases=None):
        return pl.pallas_call(
            kernel,
            out_shape=outs,
            in_specs=ins or [in_vmem] * len(operands),
            out_specs=jax.tree.map(lambda _: to, outs),
            scratch_shapes=list(scratch),
            input_output_aliases=aliases or {},
            compiler_params=params,
        )(*operands)

    sources = (
        channel_order,
        jnp.transpose(filter_coeffs, (0, 2, 1)).reshape(16, 32),
        point_cells,
        point_weights,
        orient_cells,
        orient_weights,
        point_values.reshape(64, 128),
        orient_normals.reshape(96, 128),
        control.reshape(32, 16, 128),
    )
    sources = tuple(pltpu.with_memory_space_constraint(x, pltpu.HBM) for x in sources)
    held = [pltpu.VMEM(source.shape, source.dtype) for source in sources[1:6]]

    def exchange(rows, give, keep, chips):
        def swap(value, flip):
            return lax.ppermute(value, "depth", [(i, i ^ flip) for i in range(8)])

        both = f32(2, rows, 128)
        joined = call(join_kernel, (both,) * 4, (swap(give, 1), *keep))
        return [joined[k] if k == 0 else swap(joined[k], 2 * k) for k in chips]

    give, *held = call(
        pack_kernel,
        (
            f32(4, CHUNK, 128),
            f32(8, 128),
            f32(128, 128),
            jax.ShapeDtypeStruct((32,), jnp.int32),
            f32(32, 16, 128),
            f32(64, 128),
            f32(96, 128),
        ),
        sources,
        [pltpu.SMEM((32,), jnp.int32), *held, pltpu.SemaphoreType.DMA((10,))],
        [in_hbm] * 9,
    )
    keep = call(
        keep_kernel,
        (f32(CHUNK, 128),) * 4,
        held,
        [pltpu.SMEM((32,), jnp.int32), pltpu.SemaphoreType.DMA],
    )
    number = held[2]
    parts = exchange(CHUNK, give, keep, CHIPS)
    field, edge, plane = f32(4, 4, 32, 128), f32(2, 4, 32, 128), f32(4, 32, 128)
    by_depth = f32(32, 16, 128)
    rows = pltpu.VMEM((512, 128), jnp.float32)
    first = pltpu.VMEM((32, 16, 128), jnp.float32)
    chunks, smoothed, even, odd, table, scale, root = call(
        smooth_kernel,
        (f32(8, CHUNK, 128), field, edge, edge, f32(32, 4, 16, 128), by_depth, by_depth),
        parts,
        [pltpu.VMEM((8, 16, 128), jnp.float32), first, rows],
    )
    even, odd = swapped(even, odd)
    kernels = jnp.transpose(conv_kernels, (1, 3, 4, 2, 0)).reshape(400, 8)
    partial, constant, weight, oweight, taps = call(
        own_kernel, (field, field, plane, plane, f32(400, 128)), (chunks, smoothed, kernels)
    )
    potential, forcing, even, odd = call(
        forcing_kernel,
        (field, field, edge, edge),
        (partial, even, odd, taps, constant, weight, oweight),
    )
    even, odd = swapped(even, odd)
    partial, potential = call(
        spread_kernel, (field, f32(8, 64, 128)), (forcing, taps, potential), [rows]
    )
    give, *keep = call(
        gradient_kernel,
        (f32(4, 128, 128),) + (f32(128, 128),) * 4,
        (chunks, partial, even, odd, taps, table, scale, root, potential),
        [first, rows, pltpu.VMEM((8, 64, 128), jnp.float32)],
    )
    parts = exchange(128, give, keep, range(4))
    outs = ()
    for some in (range(1), range(1, 2), range(2, 4)):
        count = len(some)
        outs = call(
            functools.partial(unpack_kernel, some),
            (by_depth, by_depth),
            (number, *parts[some.start : some.stop], *outs),
            [
                pltpu.VMEM((2, 8 * count, 16, 128), jnp.float32),
                pltpu.SemaphoreType.DMA((2,)),
            ],
            [in_vmem] * (count + 1) + [in_hbm] * len(outs),
            in_hbm,
            {count + 1: 0, count + 2: 1} if outs else None,
        )
    potential, gradient = outs
    return potential.reshape(control.shape), gradient.reshape(control.shape)


def solution(mesh):
    placed = (
        P(None, "depth", "inline", None),
        P(None, None, "depth"),
        P(),
        P(),
        P(None, "depth", "inline", None),
        P(None, "depth", "inline", None),
        P("depth", "inline", None),
        P(None, "depth", "inline", None),
        P(None, None, "depth", "inline", None),
        P("depth", "inline", None),
    )

    def body(control, filter_coeffs, conv_kernels, *rest):
        groups, block = conv_kernels.shape, control.shape
        fits = groups[:3] == (mesh.shape["depth"], 4, 4) and groups[0] == 8
        if fits and block == (32, 4, 4, 128):
            return by_group(control, filter_coeffs, conv_kernels, *rest)
        return shards(control, filter_coeffs, conv_kernels, *rest)

    return jax.shard_map(
        body,
        mesh=mesh,
        in_specs=placed,
        out_specs=(P(None, "depth", "inline", None), P(None, "depth", "inline", None)),
        check_vma=False,
    )
```

```python
import functools

import jax
import jax.numpy as jnp
from jax import lax
from jax.experimental import pallas as pl
from jax.experimental.pallas import tpu as pltpu
from jax.sharding import PartitionSpec as P

HIGHEST = lax.Precision.HIGHEST


def entering(value, axis, join, neutral, backward):
    count, mine = (lax.axis_size(axis), lax.axis_index(axis))
    pieces = jax.tree.map(lambda part: lax.all_gather(part, axis), value)
    if backward:
        pieces = jax.tree.map(lambda part: part[::-1], pieces)
        mine = count - 1 - mine
    so_far = jax.tree.map(
        lambda part, zero: jnp.full_like(part, 0) + jnp.asarray(zero, part.dtype), value, neutral
    )

    def hop(position, so_far):
        longer = join(so_far, jax.tree.map(lambda part: part[position], pieces))
        return jax.tree.map(lambda new, old: jnp.where(position < mine, new, old), longer, so_far)

    return lax.fori_loop(0, count - 1, hop, so_far)


def extended_2(cells, sides, width):
    for axis, dim in sides:
        count = lax.axis_size(axis)
        ends = count - 1
        head = lax.slice_in_dim(cells, 0, width, axis=dim)
        tail = lax.slice_in_dim(cells, cells.shape[dim] - width, cells.shape[dim], axis=dim)
        cells = jnp.concatenate(
            [
                lax.ppermute(tail, axis, [(i, (i + 1) % count) for i in range(ends)]),
                cells,
                lax.ppermute(head, axis, [((i + 1) % count, i) for i in range(ends)]),
            ],
            axis=dim,
        )
    return cells


def mixing(kernels, channel_order):
    groups = kernels.shape[0]
    group_size = kernels.shape[1]
    channels = groups * group_size
    slots = jnp.arange(channels, dtype=jnp.int32)
    chooser = (channel_order[:, None] == slots[None, :]).astype(jnp.float32)
    in_group = (
        slots[:, None] // group_size == jnp.arange(groups, dtype=jnp.int32)[None, :]
    ).astype(jnp.float32)
    in_place = (
        slots[:, None] % group_size == jnp.arange(group_size, dtype=jnp.int32)[None, :]
    ).astype(jnp.float32)
    block_mix = jnp.einsum(
        "sg,sa,tg,tb,gabhw->sthw",
        in_group,
        in_place,
        in_group,
        in_place,
        kernels,
        precision=HIGHEST,
    )
    return jnp.einsum("sc,td,sthw->cdhw", chooser, chooser, block_mix, precision=HIGHEST)


def padded_conv(padded, weights):
    return lax.conv_general_dilated(
        padded,
        weights,
        (1, 1),
        ((0, 0), (2, 2)),
        dimension_numbers=("CNHW", "OIHW", "CNHW"),
        precision=HIGHEST,
    )


def compose(earlier, later):
    first_map, first_shift = earlier
    second_map, second_shift = later
    joined_map = jnp.einsum("cnij,cnjk->cnik", second_map, first_map, precision=HIGHEST)
    joined_shift = (
        jnp.einsum("cnij,cnjk->cnik", second_map, first_shift, precision=HIGHEST) + second_shift
    )
    return (joined_map, joined_shift)


def build_tiles(coeffs, by_column, block_len):
    lead = coeffs.shape[1:3]
    lag_steps = jnp.arange(1, 5, dtype=jnp.int32)[:, None, None]
    if by_column:
        row_ids = jnp.arange(block_len + 4, dtype=jnp.int32)[None, :, None]
        col_ids = jnp.arange(block_len, dtype=jnp.int32)[None, None, :]
        picker = (row_ids == col_ids + lag_steps).astype(jnp.float32)
        extended = jnp.einsum("lcnk,lzk->cnzk", coeffs, picker, precision=HIGHEST)
        lower_tile = extended[:, :, :block_len, :]
        exit_map = extended[:, :, block_len:, :]
        entry_base = (
            jnp.arange(block_len, dtype=jnp.int32)[:, None]
            == jnp.arange(4, dtype=jnp.int32)[None, :]
        ).astype(jnp.float32)
        entry_map = jnp.broadcast_to(entry_base, lead + (block_len, 4))
    else:
        row_ids = jnp.arange(block_len, dtype=jnp.int32)[None, :, None]
        col_ids = jnp.arange(block_len + 4, dtype=jnp.int32)[None, None, :]
        picker = (col_ids == row_ids - lag_steps + 4).astype(jnp.float32)
        extended = jnp.einsum("lcnz,lzk->cnzk", coeffs, picker, precision=HIGHEST)
        lower_tile = extended[:, :, :, 4:]
        entry_map = extended[:, :, :, :4]
        exit_base = (
            jnp.arange(block_len, dtype=jnp.int32)[None, :]
            == jnp.arange(4, dtype=jnp.int32)[:, None] + block_len - 4
        ).astype(jnp.float32)
        exit_map = jnp.broadcast_to(exit_base, lead + (4, block_len))
    return (lower_tile, entry_map, exit_map)


def sweep_blocks(field, coeffs, by_column, upward, prefix):
    if upward:
        field = field[:, ::-1, ::-1]
        coeffs = coeffs[:, :, ::-1, ::-1]
    block_len = coeffs.shape[3]
    lower_tile, entry_map, exit_map = build_tiles(coeffs, by_column, block_len)
    identity_tile = jnp.eye(block_len, dtype=jnp.float32)
    inverse = identity_tile + lower_tile
    power = lower_tile
    power = jnp.einsum("cnij,cnjk->cnik", power, power, precision=HIGHEST)
    inverse = inverse + jnp.einsum("cnij,cnjk->cnik", inverse, power, precision=HIGHEST)
    reach_map = jnp.einsum("cnzk,cnkj->cnzj", inverse, entry_map, precision=HIGHEST)
    carry_map = jnp.einsum("cniz,cnzj->cnij", exit_map, reach_map, precision=HIGHEST)
    local_part = jnp.einsum("cnzk,cnkm->cnzm", inverse, field, precision=HIGHEST)
    carry_out = jnp.einsum("cniz,cnzm->cnim", exit_map, local_part, precision=HIGHEST)
    incoming = prefix((carry_map, carry_out), upward)
    result = local_part + jnp.einsum("cnzj,cnjm->cnzm", reach_map, incoming, precision=HIGHEST)
    if upward:
        result = result[:, ::-1, ::-1]
    return result


def shards(
    control,
    filter_coeffs,
    conv_kernels,
    channel_order,
    point_cells,
    point_values,
    point_weights,
    orient_cells,
    orient_normals,
    orient_weights,
):
    channels, block_len, inline_rows, cross_cols = control.shape
    plane_cells = inline_rows * cross_cols
    source = control.reshape(channels, block_len, plane_cells)
    coeffs = filter_coeffs[:, :, None, :]

    def to_blocks(field):
        return field[:, None]

    def from_blocks(field):
        return field[:, 0]

    def scaled(field, factor):
        return factor[..., None] * field

    def prefix(maps, upward):
        start = (
            jnp.broadcast_to(jnp.eye(4, dtype=jnp.float32), maps[0].shape),
            jnp.zeros_like(maps[1]),
        )
        return entering(maps, "depth", compose, start, upward)[1]

    scaling = 1.0 - jnp.sum(coeffs, axis=0)
    root_scale = jnp.sqrt(scaling)
    filtered = sweep_blocks(scaled(to_blocks(source), root_scale), coeffs, False, False, prefix)
    smoothed = sweep_blocks(scaled(filtered, scaling), coeffs, False, True, prefix)
    smoothed_field = from_blocks(smoothed).reshape(control.shape)
    weights = mixing(conv_kernels, channel_order)
    smoothed_padded = extended_2(smoothed_field, (("inline", 2),), 2)
    potential = padded_conv(smoothed_padded, weights)
    flat_field = potential.reshape(channels, -1)
    depth_base = lax.axis_index("depth") * block_len
    inline_base = lax.axis_index("inline") * inline_rows
    cells = point_cells.reshape(3, -1)
    flat_index = (
        (cells[0] - depth_base) * inline_rows + cells[1] - inline_base
    ) * cross_cols + cells[2]
    misfit = (
        flat_field[:, flat_index] - point_values.reshape(channels, -1)
    ) * point_weights.reshape(-1)[None, :]
    ocells = orient_cells.reshape(3, -1)
    base_cell = (
        (ocells[0] - depth_base) * inline_rows + ocells[1] - inline_base
    ) * cross_cols + ocells[2]
    normals = orient_normals.reshape(3, channels, -1)
    oweight = orient_weights.reshape(-1)[None, :]
    update_values = [misfit]
    update_cells = [flat_index]
    for component, stride in enumerate((plane_cells, cross_cols, 1)):
        mismatch = flat_field[:, base_cell + stride] - flat_field[:, base_cell] - normals[component]
        weighted = mismatch * oweight
        update_values.append(weighted)
        update_cells.append(base_cell + stride)
        update_values.append(-weighted)
        update_cells.append(base_cell)
    all_values = jnp.concatenate(update_values, axis=1)
    all_cells = jnp.concatenate(update_cells, axis=0)
    adjoint_weights = jnp.transpose(weights, (1, 0, 2, 3))[:, :, ::-1, ::-1]
    forcing = jnp.zeros_like(flat_field).at[:, all_cells].add(all_values)
    forcing_padded = extended_2(forcing.reshape(control.shape), (("inline", 2),), 2)
    spread = padded_conv(forcing_padded, adjoint_weights).reshape(channels, block_len, plane_cells)
    adjoint_back = scaled(sweep_blocks(to_blocks(spread), coeffs, True, False, prefix), scaling)
    adjoint_fore = scaled(sweep_blocks(adjoint_back, coeffs, True, True, prefix), root_scale)
    gradient = control + from_blocks(adjoint_fore).reshape(control.shape)
    return (potential, gradient)


CHUNK = 96
CHIPS = (0, 3, 2, 1)
AT_VALUES, AT_NORMALS, AT_COEFFS, AT_MISC = 64, 72, 84, 88


def f32(*shape):
    return jax.ShapeDtypeStruct(shape, jnp.float32)


def lane_index(shape):
    return lax.broadcasted_iota(jnp.int32, shape, len(shape) - 1)


def place_points(target, channels, values, normals, misc, by_channel):
    target[AT_MISC:CHUNK, :] = misc
    for c, channel in enumerate(channels):
        row = AT_VALUES + 2 * c
        target[row : row + 2, :] = values[pl.ds(channel * 2, 2), :]
        for k in range(3):
            row = AT_NORMALS + 4 * k + c
            target[row : row + 1, :] = normals[pl.ds(k * 32 + channel, 1), :]
        row = AT_COEFFS + c
        target[row : row + 1, :] = by_channel[pl.ds(channel, 1), :]


def place_control(target, channels, control):
    for c, channel in enumerate(channels):
        plane = control[channel]
        for z in range(4):
            row = z * 16 + c * 4
            target[row : row + 4, :] = plane[z * 4 : z * 4 + 4]


def pack_kernel(*refs):
    sources, give, misc, by_channel, number = refs[:9], refs[9], refs[10], refs[11], refs[12]
    control, values, normals, order, coeffs, cells, weights, ocells, oweights, arrived = refs[13:]
    held = (order, number, coeffs, cells, weights, ocells, oweights, values, normals)
    pairs = [(sources[8].at[8 * k : 8 * k + 8], control.at[8 * k : 8 * k + 8]) for k in range(4)]
    pairs += zip(sources[:1] + sources[:8], held)
    copies = [
        pltpu.make_async_copy(source, target, arrived.at[k])
        for k, (source, target) in enumerate(pairs)
    ]
    for copy in copies:
        copy.start()

    def flat_cell(ref):
        z, y, x = (ref[k, 0] for k in range(3))
        return (((y & 3) * 4 + (z & 3)) * 128 + x).astype(jnp.float32)

    for copy in copies[4:]:
        copy.wait()
    flat, oflat = flat_cell(cells), flat_cell(ocells)
    weight = weights[0]
    misc[...] = jnp.concatenate(
        [flat[:, :128], flat[:, 128:], oflat, weight[:, :128], weight[:, 128:], oweights[0]]
        + [jnp.zeros((2, 128), jnp.float32)],
        axis=0,
    )
    by_channel[:, :16] = jnp.transpose(
        jnp.concatenate([coeffs[...], jnp.zeros((16, 96), jnp.float32)], axis=1)
    )
    by_channel[:, 16:] = jnp.zeros((128, 112), jnp.float32)
    me = lax.axis_index("depth")
    places = [
        (give.at[k], [order[(me ^ (2 * k + 1)) * 4 + c] for c in range(4)]) for k in range(4)
    ]
    for target, channels in places:
        place_points(target, channels, values, normals, misc[...], by_channel)
    for copy in copies[:4]:
        copy.wait()
    for target, channels in places:
        place_control(target, channels, control)


def keep_kernel(misc, by_channel, number, control, values, normals, *refs):
    keep, order, arrived = refs[:4], refs[4], refs[5]
    numbers = pltpu.make_async_copy(number, order, arrived)
    numbers.start()
    numbers.wait()
    me = lax.axis_index("depth")
    for k in range(4):
        channels = [order[(me ^ (2 * k)) * 4 + c] for c in range(4)]
        place_points(keep[k], channels, values, normals, misc[...], by_channel)
        place_control(keep[k], channels, control)


def join_kernel(got, *refs):
    keep, joined = refs[:4], refs[4:]
    for k in range(4):
        joined[k][0] = keep[k][...]
        joined[k][1] = got[k]


def coefficient(expanded, lag, z):
    block, local = divmod(z, 4)
    k = (lag - 1) * 4 + local
    return jnp.broadcast_to(expanded[block, :, k : k + 1], (16, 128))


def repeat_coeffs(chunks, expanded):
    for block in range(8):
        for c in range(4):
            row = AT_COEFFS + c
            expanded[block, 4 * c : 4 * c + 4, :] = jnp.broadcast_to(
                chunks[block, row : row + 1, :], (4, 128)
            )


def recurrence(source, factor, emit, order):
    history = []
    for t in order:
        total = source(t)
        for lag in range(len(history), 0, -1):
            before, value = history[lag - 1]
            total = total + factor(lag, t, before) * value
        history = [(t, total)] + history[:3]
        emit(t, total)


def depth_rows(chunks, z):
    return chunks[z // 4, (z % 4) * 16 : (z % 4) * 16 + 16, :]


def smooth_kernel(*refs):
    parts, refs = refs[:4], refs[4:]
    chunks, smoothed, even, odd, table, scale, root, expanded, first, rows = refs
    me = lax.axis_index("depth")
    for k, part in zip(CHIPS, parts):
        for half in range(2):
            chunks[me ^ (2 * k + half)] = part[half]
    repeat_coeffs(chunks, expanded)
    lags = {}

    def start(z):
        lags.clear()
        lags.update({lag: coefficient(expanded, lag, z) for lag in range(1, 5)})
        for lag in range(1, 5):
            table[z, lag - 1] = lags[lag]
        lags[0] = 1.0 - ((lags[1] + lags[2]) + (lags[3] + lags[4]))
        scale[z] = lags[0]
        lags[-1] = jnp.sqrt(lags[0])
        root[z] = lags[-1]
        return lags[-1] * depth_rows(chunks, z)

    def keep_first(z, value):
        first[z] = lags[0] * value

    def keep_rows(z, value):
        rows[z * 16 : z * 16 + 16, :] = value

    recurrence(start, lambda lag, z, before: lags[lag], keep_first, range(32))
    recurrence(
        lambda z: first[z],
        lambda lag, z, before: table[z, lag - 1],
        keep_rows,
        range(31, -1, -1),
    )
    parity = lax.axis_index("inline") % 2
    for y in range(4):
        for c in range(4):
            smoothed[y, c] = rows[pl.ds(c * 4 + y, 32, stride=16), :]
    for y in range(2):
        even[y] = smoothed[2 - 2 * parity + y]
        odd[y] = smoothed[2 * parity + y]


def tap(table, a, b, h, w):
    row = ((a * 5 + h) * 5 + w) * 4 + b
    return jnp.broadcast_to(table[row : row + 1, :], (8, 128))


def conv_rows(read, rows_in, start, table, adjoint, write):
    lane = lane_index((8, 128))

    def moved(value, shift):
        if shift == 0:
            return value
        inside = lane >= -shift if shift < 0 else lane < 128 - shift
        return jnp.where(inside, pltpu.roll(value, -shift % 128, 1), 0.0)

    def some_depths(k, carry):
        pieces = [pl.ds(pl.multiple_of(k * 16 + 8 * n, 8), 8) for n in range(2)]
        total = [[[start(y, o, at) for at in pieces] for o in range(4)] for y in range(4)]
        for i in range(4):
            lines = {row: [read(row, i, at) for at in pieces] for row in rows_in}
            for w in range(5):
                shift = 2 - w if adjoint else w - 2
                shifted_lines = {
                    row: [moved(value, shift) for value in lines[row]] for row in rows_in
                }
                for h in range(5):
                    rows = [y - h + 2 if adjoint else y + h - 2 for y in range(4)]
                    for o in range(4):
                        weight = tap(table, i, o, h, w) if adjoint else tap(table, o, i, h, w)
                        for y, row in enumerate(rows):
                            if row in rows_in:
                                for n in range(2):
                                    line = shifted_lines[row][n]
                                    total[y][o][n] = total[y][o][n] + weight * line
        for y in range(4):
            for o in range(4):
                for n in range(2):
                    write(y, o, pieces[n], total[y][o][n])
        return carry

    lax.fori_loop(0, 2, some_depths, 0)


OWN = (0, 1, 2, 3)
HALO = (-2, -1, 4, 5)


def halo_reader(even, odd):
    slab, last = lax.axis_index("inline"), lax.axis_size("inline") - 1
    parity = slab % 2

    def read(row, c, depths):
        y = row + 2 if row < 0 else row - 4
        through_even, through_odd = even[y, c, depths, :], odd[y, c, depths, :]
        below = parity == 1 if row < 0 else parity == 0
        outside = slab == 0 if row < 0 else slab == last
        return jnp.where(outside, 0.0, jnp.where(below, through_even, through_odd))

    return read


def split(value):
    high = value.astype(jnp.bfloat16)
    return high, (value - high.astype(jnp.float32)).astype(jnp.bfloat16)


def point_fields(chunks, constant, weight, oweight):
    row = lax.broadcasted_iota(jnp.int32, (16, 256), 0)
    orow = lax.broadcasted_iota(jnp.int32, (16, 128), 0)
    column = lax.broadcasted_iota(jnp.int32, (128, 384), 0)
    for block in range(8):

        def line(k, block=block):
            return chunks[block, k : k + 1, :]

        def double(k, line=line):
            return jnp.concatenate([line(k), line(k + 1)], axis=1)

        flat = double(AT_MISC).astype(jnp.int32)
        oflat = line(AT_MISC + 2).astype(jnp.int32)
        w, ow = double(AT_MISC + 3), line(AT_MISC + 5)
        cell, ocell = flat >> 7, oflat >> 7
        at_cross = jnp.concatenate([flat & 127, oflat & 127], axis=1)
        columns = (column == at_cross).astype(jnp.float32).astype(jnp.bfloat16)
        here, ohere = row == cell, orow == ocell
        below, beside = orow == ocell + 1, orow == ocell + 4
        main, along = [], []
        for c in range(4):
            value = w * double(AT_VALUES + 2 * c)
            n0, n1, n2 = (ow * line(AT_NORMALS + 4 * k + c) for k in range(3))
            placed = (
                jnp.where(below, n0, 0.0)
                + jnp.where(beside, n1, 0.0)
                - jnp.where(ohere, n0 + n1 + n2, 0.0)
            )
            main.append(jnp.concatenate([jnp.where(here, value, 0.0), placed], axis=1))
            along.append(
                jnp.concatenate([jnp.zeros((16, 256), jnp.float32), jnp.where(ohere, n2, 0.0)], axis=1)
            )
        both = [
            jnp.concatenate([jnp.where(here, w, 0.0), jnp.zeros((16, 128), jnp.float32)], axis=1),
            jnp.concatenate([jnp.zeros((16, 256), jnp.float32), jnp.where(ohere, ow, 0.0)], axis=1),
        ]
        high, low = split(jnp.concatenate(main + both + along, axis=0))
        sums = lax.dot_general(
            jnp.concatenate([high, low], axis=0),
            columns,
            (((1,), (1,)), ((), ())),
            preferred_element_type=jnp.float32,
        )
        sums = sums[:160] + sums[160:]
        moved = pltpu.roll(sums[96:160], 1, 1)
        z = 4 * block
        for y in range(4):
            for c in range(4):
                k = 16 * c + 4 * y
                constant[y, c, z : z + 4, :] = sums[k : k + 4] + moved[k : k + 4]
            weight[y, z : z + 4, :] = sums[64 + 4 * y : 68 + 4 * y]
            oweight[y, z : z + 4, :] = sums[80 + 4 * y : 84 + 4 * y]


def own_kernel(chunks, smoothed, kernels, partial, constant, weight, oweight, table):
    group = lax.axis_index("depth")
    picked = jnp.where(lane_index((400, 8)) == group, kernels[...], 0.0)
    table[...] = jnp.broadcast_to(jnp.sum(picked, axis=1, keepdims=True), (400, 128))
    point_fields(chunks, constant, weight, oweight)

    def write(y, o, depths, value):
        partial[y, o, depths, :] = value

    conv_rows(
        lambda row, c, depths: smoothed[row, c, depths, :],
        OWN,
        lambda y, o, depths: jnp.zeros((8, 128), jnp.float32),
        table,
        False,
        write,
    )


def forcing_kernel(
    partial, even_in, odd_in, table, constant, weight, oweight, potential, forcing, even, odd
):
    def write(y, o, depths, value):
        potential[y, o, depths, :] = value

    conv_rows(
        halo_reader(even_in, odd_in),
        HALO,
        lambda y, o, depths: partial[y, o, depths, :],
        table,
        False,
        write,
    )

    parity = lax.axis_index("inline") % 2

    def some_depths(k, carry):
        depths = pl.ds(pl.multiple_of(k * 8, 8), 8)
        shares = [oweight[y, depths, :] for y in range(4)]
        weights = [weight[y, depths, :] for y in range(4)]
        for c in range(4):
            lines = [potential[y, c, depths, :] for y in range(4)]
            sums = [weights[y] * lines[y] - constant[y, c, depths, :] for y in range(4)]
            for y in range(4):
                deeper = shares[y] * (pltpu.roll(lines[y], 7, 0) - lines[y])
                across = shares[y] * (pltpu.roll(lines[y], 127, 1) - lines[y])
                sums[y] = sums[y] - deeper + pltpu.roll(deeper, 1, 0)
                sums[y] = sums[y] - across + pltpu.roll(across, 1, 1)
                if y < 3:
                    beside = shares[y] * (lines[y + 1] - lines[y])
                    sums[y] = sums[y] - beside
                    sums[y + 1] = sums[y + 1] + beside
            for y in range(4):
                forcing[y, c, depths, :] = sums[y]
            for y in range(2):
                even[y, c, depths, :] = jnp.where(parity == 0, sums[2 + y], sums[y])
                odd[y, c, depths, :] = jnp.where(parity == 0, sums[y], sums[2 + y])
        return carry

    lax.fori_loop(0, 4, some_depths, 0)


def spread_kernel(forcing, table, potential, partial, out, rows):
    def write(y, o, depths, value):
        partial[y, o, depths, :] = value

    conv_rows(
        lambda row, c, depths: forcing[row, c, depths, :],
        OWN,
        lambda y, o, depths: jnp.zeros((8, 128), jnp.float32),
        table,
        True,
        write,
    )
    for y in range(4):
        for c in range(4):
            rows[pl.ds((c * 4 + y) * 32, 32), :] = potential[y, c]
    for z in range(32):
        out[z // 4, (z % 4) * 16 : (z % 4) * 16 + 16, :] = rows[pl.ds(z, 16, stride=32), :]


def gradient_kernel(*refs):
    chunks, partial, even_in, odd_in, taps, table, scale, root, potential = refs[:9]
    give, keep, (first, rows, out) = refs[9], refs[10:14], refs[14:]
    me = lax.axis_index("depth")
    targets = [
        give.at[place // 2] if place % 2 else keep[place // 2] for place in range(8)
    ]
    for place, target in enumerate(targets):
        target[:64, :] = potential[me ^ place]

    def write(y, o, depths, value):
        rows[pl.ds(pl.multiple_of((o * 4 + y) * 32 + depths.start, 8), 8), :] = value

    conv_rows(
        halo_reader(even_in, odd_in),
        HALO,
        lambda y, o, depths: partial[y, o, depths, :],
        taps,
        True,
        write,
    )

    def keep_first(z, value):
        first[z] = scale[z] * value

    def keep_out(z, value):
        row = (z % 4) * 16
        out[z // 4, row : row + 16, :] = depth_rows(chunks, z) + root[z] * value

    recurrence(
        lambda z: rows[pl.ds(z, 16, stride=32), :],
        lambda lag, z, before: table[before, lag - 1],
        keep_first,
        range(32),
    )
    recurrence(
        lambda z: first[z],
        lambda lag, z, before: table[before, lag - 1],
        keep_out,
        range(31, -1, -1),
    )
    for place, target in enumerate(targets):
        target[64:, :] = out[me ^ place]


def unpack_kernel(chips, number, *refs):
    count = len(chips)
    parts, (potential, gradient, planes, sent) = refs[:count], refs[-4:]
    me = lax.axis_index("depth")
    order = number[...].reshape(1, 32)
    lane = lane_index((1, 32))
    channels = []
    for slot in range(8 * count):
        place = 2 * chips[slot // 8] + slot // 4 % 2
        here = lane == (me ^ place) * 4 + slot % 4
        channels.append(jnp.sum(jnp.where(here, order, 0)))
    for half in range(2):
        for slot in range(8 * count):
            k, source, c = slot // 8, slot // 4 % 2, slot % 4
            rows = [64 * half + z * 16 + c * 4 for z in range(4)]
            pieces = [parts[k][source, row : row + 4, :] for row in rows]
            planes[half, slot] = jnp.concatenate(pieces, axis=0)
    for slot in range(8 * count):
        for half, out in enumerate((potential, gradient)):
            pltpu.make_async_copy(
                planes.at[half, slot], out.at[channels[slot]], sent.at[half]
            ).start()
    for half, out in enumerate((potential, gradient)):
        pltpu.make_async_copy(planes.at[half], out.at[: 8 * count], sent.at[half]).wait()


def swapped(even, odd):
    depths, slabs = lax.axis_size("depth"), lax.axis_size("inline")

    def swap(value, first):
        pairs = []
        for d in range(depths):
            for i in range(slabs):
                other = i + 1 if (i - first) % 2 == 0 else i - 1
                to = (d, other) if 0 <= other < slabs else (d ^ 1, i)
                pairs.append((d * slabs + i, to[0] * slabs + to[1]))
        return lax.ppermute(value, ("depth", "inline"), pairs)

    return swap(even, 0), swap(odd, 1)


def by_group(
    control,
    filter_coeffs,
    conv_kernels,
    channel_order,
    point_cells,
    point_values,
    point_weights,
    orient_cells,
    orient_normals,
    orient_weights,
):
    params = pltpu.CompilerParams(vmem_limit_bytes=48 << 20)
    in_vmem, in_hbm = (pl.BlockSpec(memory_space=space) for space in (pltpu.VMEM, pltpu.HBM))

    def call(kernel, outs, operands, scratch=(), ins=None, to=in_vmem, aliases=None):
        return pl.pallas_call(
            kernel,
            out_shape=outs,
            in_specs=ins or [in_vmem] * len(operands),
            out_specs=jax.tree.map(lambda _: to, outs),
            scratch_shapes=list(scratch),
            input_output_aliases=aliases or {},
            compiler_params=params,
        )(*operands)

    sources = (
        channel_order,
        jnp.transpose(filter_coeffs, (0, 2, 1)).reshape(16, 32),
        point_cells,
        point_weights,
        orient_cells,
        orient_weights,
        point_values.reshape(64, 128),
        orient_normals.reshape(96, 128),
        control.reshape(32, 16, 128),
    )
    sources = tuple(pltpu.with_memory_space_constraint(x, pltpu.HBM) for x in sources)
    held = [pltpu.VMEM(source.shape, source.dtype) for source in sources[1:6]]

    def exchange(rows, give, keep, chips):
        def swap(value, flip):
            return lax.ppermute(value, "depth", [(i, i ^ flip) for i in range(8)])

        both = f32(2, rows, 128)
        joined = call(join_kernel, (both,) * 4, (swap(give, 1), *keep))
        return [joined[k] if k == 0 else swap(joined[k], 2 * k) for k in chips]

    give, *held = call(
        pack_kernel,
        (
            f32(4, CHUNK, 128),
            f32(8, 128),
            f32(128, 128),
            jax.ShapeDtypeStruct((32,), jnp.int32),
            f32(32, 16, 128),
            f32(64, 128),
            f32(96, 128),
        ),
        sources,
        [pltpu.SMEM((32,), jnp.int32), *held, pltpu.SemaphoreType.DMA((13,))],
        [in_hbm] * 9,
    )
    keep = call(
        keep_kernel,
        (f32(CHUNK, 128),) * 4,
        held,
        [pltpu.SMEM((32,), jnp.int32), pltpu.SemaphoreType.DMA],
    )
    number = held[2]
    parts = exchange(CHUNK, give, keep, CHIPS)
    field, edge, plane = f32(4, 4, 32, 128), f32(2, 4, 32, 128), f32(4, 32, 128)
    by_depth = f32(32, 16, 128)
    rows = pltpu.VMEM((512, 128), jnp.float32)
    first = pltpu.VMEM((32, 16, 128), jnp.float32)
    chunks, smoothed, even, odd, table, scale, root = call(
        smooth_kernel,
        (f32(8, CHUNK, 128), field, edge, edge, f32(32, 4, 16, 128), by_depth, by_depth),
        parts,
        [pltpu.VMEM((8, 16, 128), jnp.float32), first, rows],
    )
    even, odd = swapped(even, odd)
    kernels = jnp.transpose(conv_kernels, (1, 3, 4, 2, 0)).reshape(400, 8)
    partial, constant, weight, oweight, taps = call(
        own_kernel, (field, field, plane, plane, f32(400, 128)), (chunks, smoothed, kernels)
    )
    potential, forcing, even, odd = call(
        forcing_kernel,
        (field, field, edge, edge),
        (partial, even, odd, taps, constant, weight, oweight),
    )
    even, odd = swapped(even, odd)
    partial, potential = call(
        spread_kernel, (field, f32(8, 64, 128)), (forcing, taps, potential), [rows]
    )
    give, *keep = call(
        gradient_kernel,
        (f32(4, 128, 128),) + (f32(128, 128),) * 4,
        (chunks, partial, even, odd, taps, table, scale, root, potential),
        [first, rows, pltpu.VMEM((8, 64, 128), jnp.float32)],
    )
    parts = exchange(128, give, keep, CHIPS)
    outs = ()
    for some in (slice(0, 1), slice(1, 2), slice(2, 4)):
        count = len(CHIPS[some])
        outs = call(
            functools.partial(unpack_kernel, CHIPS[some]),
            (by_depth, by_depth),
            (number, *parts[some], *outs),
            [
                pltpu.VMEM((2, 8 * count, 16, 128), jnp.float32),
                pltpu.SemaphoreType.DMA((2,)),
            ],
            [in_vmem] * (count + 1) + [in_hbm] * len(outs),
            in_hbm,
            {count + 1: 0, count + 2: 1} if outs else None,
        )
    potential, gradient = outs
    return potential.reshape(control.shape), gradient.reshape(control.shape)


def solution(mesh):
    placed = (
        P(None, "depth", "inline", None),
        P(None, None, "depth"),
        P(),
        P(),
        P(None, "depth", "inline", None),
        P(None, "depth", "inline", None),
        P("depth", "inline", None),
        P(None, "depth", "inline", None),
        P(None, None, "depth", "inline", None),
        P("depth", "inline", None),
    )

    def body(control, filter_coeffs, conv_kernels, *rest):
        groups, block = conv_kernels.shape, control.shape
        fits = groups[:3] == (mesh.shape["depth"], 4, 4) and groups[0] == 8
        if fits and block == (32, 4, 4, 128):
            return by_group(control, filter_coeffs, conv_kernels, *rest)
        return shards(control, filter_coeffs, conv_kernels, *rest)

    return jax.shard_map(
        body,
        mesh=mesh,
        in_specs=placed,
        out_specs=(P(None, "depth", "inline", None), P(None, "depth", "inline", None)),
        check_vma=False,
    )
```

```python
import functools

import jax
import jax.numpy as jnp
from jax import lax
from jax.experimental import pallas as pl
from jax.experimental.pallas import tpu as pltpu
from jax.sharding import PartitionSpec as P

HIGHEST = lax.Precision.HIGHEST


def entering(value, axis, join, neutral, backward):
    count, mine = (lax.axis_size(axis), lax.axis_index(axis))
    pieces = jax.tree.map(lambda part: lax.all_gather(part, axis), value)
    if backward:
        pieces = jax.tree.map(lambda part: part[::-1], pieces)
        mine = count - 1 - mine
    so_far = jax.tree.map(
        lambda part, zero: jnp.full_like(part, 0) + jnp.asarray(zero, part.dtype), value, neutral
    )

    def hop(position, so_far):
        longer = join(so_far, jax.tree.map(lambda part: part[position], pieces))
        return jax.tree.map(lambda new, old: jnp.where(position < mine, new, old), longer, so_far)

    return lax.fori_loop(0, count - 1, hop, so_far)


def extended_2(cells, sides, width):
    for axis, dim in sides:
        count = lax.axis_size(axis)
        ends = count - 1
        head = lax.slice_in_dim(cells, 0, width, axis=dim)
        tail = lax.slice_in_dim(cells, cells.shape[dim] - width, cells.shape[dim], axis=dim)
        cells = jnp.concatenate(
            [
                lax.ppermute(tail, axis, [(i, (i + 1) % count) for i in range(ends)]),
                cells,
                lax.ppermute(head, axis, [((i + 1) % count, i) for i in range(ends)]),
            ],
            axis=dim,
        )
    return cells


def mixing(kernels, channel_order):
    groups = kernels.shape[0]
    group_size = kernels.shape[1]
    channels = groups * group_size
    slots = jnp.arange(channels, dtype=jnp.int32)
    chooser = (channel_order[:, None] == slots[None, :]).astype(jnp.float32)
    in_group = (
        slots[:, None] // group_size == jnp.arange(groups, dtype=jnp.int32)[None, :]
    ).astype(jnp.float32)
    in_place = (
        slots[:, None] % group_size == jnp.arange(group_size, dtype=jnp.int32)[None, :]
    ).astype(jnp.float32)
    block_mix = jnp.einsum(
        "sg,sa,tg,tb,gabhw->sthw",
        in_group,
        in_place,
        in_group,
        in_place,
        kernels,
        precision=HIGHEST,
    )
    return jnp.einsum("sc,td,sthw->cdhw", chooser, chooser, block_mix, precision=HIGHEST)


def padded_conv(padded, weights):
    return lax.conv_general_dilated(
        padded,
        weights,
        (1, 1),
        ((0, 0), (2, 2)),
        dimension_numbers=("CNHW", "OIHW", "CNHW"),
        precision=HIGHEST,
    )


def compose(earlier, later):
    first_map, first_shift = earlier
    second_map, second_shift = later
    joined_map = jnp.einsum("cnij,cnjk->cnik", second_map, first_map, precision=HIGHEST)
    joined_shift = (
        jnp.einsum("cnij,cnjk->cnik", second_map, first_shift, precision=HIGHEST) + second_shift
    )
    return (joined_map, joined_shift)


def build_tiles(coeffs, by_column, block_len):
    lead = coeffs.shape[1:3]
    lag_steps = jnp.arange(1, 5, dtype=jnp.int32)[:, None, None]
    if by_column:
        row_ids = jnp.arange(block_len + 4, dtype=jnp.int32)[None, :, None]
        col_ids = jnp.arange(block_len, dtype=jnp.int32)[None, None, :]
        picker = (row_ids == col_ids + lag_steps).astype(jnp.float32)
        extended = jnp.einsum("lcnk,lzk->cnzk", coeffs, picker, precision=HIGHEST)
        lower_tile = extended[:, :, :block_len, :]
        exit_map = extended[:, :, block_len:, :]
        entry_base = (
            jnp.arange(block_len, dtype=jnp.int32)[:, None]
            == jnp.arange(4, dtype=jnp.int32)[None, :]
        ).astype(jnp.float32)
        entry_map = jnp.broadcast_to(entry_base, lead + (block_len, 4))
    else:
        row_ids = jnp.arange(block_len, dtype=jnp.int32)[None, :, None]
        col_ids = jnp.arange(block_len + 4, dtype=jnp.int32)[None, None, :]
        picker = (col_ids == row_ids - lag_steps + 4).astype(jnp.float32)
        extended = jnp.einsum("lcnz,lzk->cnzk", coeffs, picker, precision=HIGHEST)
        lower_tile = extended[:, :, :, 4:]
        entry_map = extended[:, :, :, :4]
        exit_base = (
            jnp.arange(block_len, dtype=jnp.int32)[None, :]
            == jnp.arange(4, dtype=jnp.int32)[:, None] + block_len - 4
        ).astype(jnp.float32)
        exit_map = jnp.broadcast_to(exit_base, lead + (4, block_len))
    return (lower_tile, entry_map, exit_map)


def sweep_blocks(field, coeffs, by_column, upward, prefix):
    if upward:
        field = field[:, ::-1, ::-1]
        coeffs = coeffs[:, :, ::-1, ::-1]
    block_len = coeffs.shape[3]
    lower_tile, entry_map, exit_map = build_tiles(coeffs, by_column, block_len)
    identity_tile = jnp.eye(block_len, dtype=jnp.float32)
    inverse = identity_tile + lower_tile
    power = lower_tile
    power = jnp.einsum("cnij,cnjk->cnik", power, power, precision=HIGHEST)
    inverse = inverse + jnp.einsum("cnij,cnjk->cnik", inverse, power, precision=HIGHEST)
    reach_map = jnp.einsum("cnzk,cnkj->cnzj", inverse, entry_map, precision=HIGHEST)
    carry_map = jnp.einsum("cniz,cnzj->cnij", exit_map, reach_map, precision=HIGHEST)
    local_part = jnp.einsum("cnzk,cnkm->cnzm", inverse, field, precision=HIGHEST)
    carry_out = jnp.einsum("cniz,cnzm->cnim", exit_map, local_part, precision=HIGHEST)
    incoming = prefix((carry_map, carry_out), upward)
    result = local_part + jnp.einsum("cnzj,cnjm->cnzm", reach_map, incoming, precision=HIGHEST)
    if upward:
        result = result[:, ::-1, ::-1]
    return result


def shards(
    control,
    filter_coeffs,
    conv_kernels,
    channel_order,
    point_cells,
    point_values,
    point_weights,
    orient_cells,
    orient_normals,
    orient_weights,
):
    channels, block_len, inline_rows, cross_cols = control.shape
    plane_cells = inline_rows * cross_cols
    source = control.reshape(channels, block_len, plane_cells)
    coeffs = filter_coeffs[:, :, None, :]

    def to_blocks(field):
        return field[:, None]

    def from_blocks(field):
        return field[:, 0]

    def scaled(field, factor):
        return factor[..., None] * field

    def prefix(maps, upward):
        start = (
            jnp.broadcast_to(jnp.eye(4, dtype=jnp.float32), maps[0].shape),
            jnp.zeros_like(maps[1]),
        )
        return entering(maps, "depth", compose, start, upward)[1]

    scaling = 1.0 - jnp.sum(coeffs, axis=0)
    root_scale = jnp.sqrt(scaling)
    filtered = sweep_blocks(scaled(to_blocks(source), root_scale), coeffs, False, False, prefix)
    smoothed = sweep_blocks(scaled(filtered, scaling), coeffs, False, True, prefix)
    smoothed_field = from_blocks(smoothed).reshape(control.shape)
    weights = mixing(conv_kernels, channel_order)
    smoothed_padded = extended_2(smoothed_field, (("inline", 2),), 2)
    potential = padded_conv(smoothed_padded, weights)
    flat_field = potential.reshape(channels, -1)
    depth_base = lax.axis_index("depth") * block_len
    inline_base = lax.axis_index("inline") * inline_rows
    cells = point_cells.reshape(3, -1)
    flat_index = (
        (cells[0] - depth_base) * inline_rows + cells[1] - inline_base
    ) * cross_cols + cells[2]
    misfit = (
        flat_field[:, flat_index] - point_values.reshape(channels, -1)
    ) * point_weights.reshape(-1)[None, :]
    ocells = orient_cells.reshape(3, -1)
    base_cell = (
        (ocells[0] - depth_base) * inline_rows + ocells[1] - inline_base
    ) * cross_cols + ocells[2]
    normals = orient_normals.reshape(3, channels, -1)
    oweight = orient_weights.reshape(-1)[None, :]
    update_values = [misfit]
    update_cells = [flat_index]
    for component, stride in enumerate((plane_cells, cross_cols, 1)):
        mismatch = flat_field[:, base_cell + stride] - flat_field[:, base_cell] - normals[component]
        weighted = mismatch * oweight
        update_values.append(weighted)
        update_cells.append(base_cell + stride)
        update_values.append(-weighted)
        update_cells.append(base_cell)
    all_values = jnp.concatenate(update_values, axis=1)
    all_cells = jnp.concatenate(update_cells, axis=0)
    adjoint_weights = jnp.transpose(weights, (1, 0, 2, 3))[:, :, ::-1, ::-1]
    forcing = jnp.zeros_like(flat_field).at[:, all_cells].add(all_values)
    forcing_padded = extended_2(forcing.reshape(control.shape), (("inline", 2),), 2)
    spread = padded_conv(forcing_padded, adjoint_weights).reshape(channels, block_len, plane_cells)
    adjoint_back = scaled(sweep_blocks(to_blocks(spread), coeffs, True, False, prefix), scaling)
    adjoint_fore = scaled(sweep_blocks(adjoint_back, coeffs, True, True, prefix), root_scale)
    gradient = control + from_blocks(adjoint_fore).reshape(control.shape)
    return (potential, gradient)


CHUNK = 96
CHIPS = (0, 3, 2, 1)
AT_VALUES, AT_NORMALS, AT_COEFFS, AT_MISC = 64, 72, 84, 88


def f32(*shape):
    return jax.ShapeDtypeStruct(shape, jnp.float32)


def lane_index(shape):
    return lax.broadcasted_iota(jnp.int32, shape, len(shape) - 1)


def place_points(target, channels, values, normals, misc, by_channel):
    target[AT_MISC:CHUNK, :] = misc
    for c, channel in enumerate(channels):
        row = AT_VALUES + 2 * c
        target[row : row + 2, :] = values[pl.ds(channel * 2, 2), :]
        for k in range(3):
            row = AT_NORMALS + 4 * k + c
            target[row : row + 1, :] = normals[pl.ds(k * 32 + channel, 1), :]
        row = AT_COEFFS + c
        target[row : row + 1, :] = by_channel[pl.ds(channel, 1), :]


def place_control(target, channels, control):
    for c, channel in enumerate(channels):
        plane = control[channel]
        for z in range(4):
            row = z * 16 + c * 4
            target[row : row + 4, :] = plane[z * 4 : z * 4 + 4]


def pack_kernel(*refs):
    sources, chips, number, by_channel, control = refs[:9], refs[9:13], refs[13], refs[14], refs[15]
    order, coeffs, cells, weights, ocells, oweights, values, normals, arrived = refs[16:]
    held = (order, number, coeffs, cells, weights, ocells, oweights, values, normals)
    pairs = [(sources[8].at[8 * k : 8 * k + 8], control.at[8 * k : 8 * k + 8]) for k in range(4)]
    pairs += zip(sources[:1] + sources[:8], held)
    copies = [
        pltpu.make_async_copy(source, target, arrived.at[k])
        for k, (source, target) in enumerate(pairs)
    ]
    for copy in copies:
        copy.start()

    def flat_cell(ref):
        z, y, x = (ref[k, 0] for k in range(3))
        return (((y & 3) * 4 + (z & 3)) * 128 + x).astype(jnp.float32)

    for copy in copies[4:]:
        copy.wait()
    flat, oflat = flat_cell(cells), flat_cell(ocells)
    weight = weights[0]
    misc = jnp.concatenate(
        [flat[:, :128], flat[:, 128:], oflat, weight[:, :128], weight[:, 128:], oweights[0]]
        + [jnp.zeros((2, 128), jnp.float32)],
        axis=0,
    )
    by_channel[:, :16] = jnp.transpose(
        jnp.concatenate([coeffs[...], jnp.zeros((16, 96), jnp.float32)], axis=1)
    )
    by_channel[:, 16:] = jnp.zeros((128, 112), jnp.float32)
    me = lax.axis_index("depth")
    places = [
        (chips[place // 2].at[place % 2], [order[(me ^ place) * 4 + c] for c in range(4)])
        for place in range(8)
    ]
    for target, channels in places:
        place_points(target, channels, values, normals, misc, by_channel)
    for copy in copies[:4]:
        copy.wait()
    for target, channels in places:
        place_control(target, channels, control)


def coefficient(expanded, lag, z):
    block, local = divmod(z, 4)
    k = (lag - 1) * 4 + local
    return jnp.broadcast_to(expanded[block, :, k : k + 1], (16, 128))


def repeat_coeffs(chunks, expanded):
    for block in range(8):
        for c in range(4):
            row = AT_COEFFS + c
            expanded[block, 4 * c : 4 * c + 4, :] = jnp.broadcast_to(
                chunks[block, row : row + 1, :], (4, 128)
            )


def recurrence(source, factor, emit, order):
    history = []
    for t in order:
        total = source(t)
        for lag in range(len(history), 0, -1):
            before, value = history[lag - 1]
            total = total + factor(lag, t, before) * value
        history = [(t, total)] + history[:3]
        emit(t, total)


def depth_rows(chunks, z):
    return chunks[z // 4, (z % 4) * 16 : (z % 4) * 16 + 16, :]


def smooth_kernel(*refs):
    direct, passed, refs = refs[:4], refs[4:8], refs[8:]
    chunks, smoothed, even, odd, table, scale, root, expanded, first, rows = refs
    me = lax.axis_index("depth")
    for n, k in enumerate(CHIPS):
        chunks[me ^ (2 * k)] = direct[n][0]
        chunks[me ^ (2 * k + 1)] = passed[n][...]
    repeat_coeffs(chunks, expanded)
    lags = {}

    def start(z):
        lags.clear()
        lags.update({lag: coefficient(expanded, lag, z) for lag in range(1, 5)})
        for lag in range(1, 5):
            table[z, lag - 1] = lags[lag]
        lags[0] = 1.0 - ((lags[1] + lags[2]) + (lags[3] + lags[4]))
        scale[z] = lags[0]
        lags[-1] = jnp.sqrt(lags[0])
        root[z] = lags[-1]
        return lags[-1] * depth_rows(chunks, z)

    def keep_first(z, value):
        first[z] = lags[0] * value

    def keep_rows(z, value):
        rows[z * 16 : z * 16 + 16, :] = value

    recurrence(start, lambda lag, z, before: lags[lag], keep_first, range(32))
    recurrence(
        lambda z: first[z],
        lambda lag, z, before: table[z, lag - 1],
        keep_rows,
        range(31, -1, -1),
    )
    parity = lax.axis_index("inline") % 2
    for y in range(4):
        for c in range(4):
            smoothed[y, c] = rows[pl.ds(c * 4 + y, 32, stride=16), :]
    for y in range(2):
        even[y] = smoothed[2 - 2 * parity + y]
        odd[y] = smoothed[2 * parity + y]


def tap(table, a, b, h, w):
    row = ((a * 5 + h) * 5 + w) * 4 + b
    return jnp.broadcast_to(table[row : row + 1, :], (8, 128))


def conv_rows(read, rows_in, start, table, adjoint, write):
    lane = lane_index((8, 128))

    def moved(value, shift):
        if shift == 0:
            return value
        inside = lane >= -shift if shift < 0 else lane < 128 - shift
        return jnp.where(inside, pltpu.roll(value, -shift % 128, 1), 0.0)

    def some_depths(k, carry):
        pieces = [pl.ds(pl.multiple_of(k * 16 + 8 * n, 8), 8) for n in range(2)]
        total = [[[start(y, o, at) for at in pieces] for o in range(4)] for y in range(4)]
        for i in range(4):
            lines = {row: [read(row, i, at) for at in pieces] for row in rows_in}
            for w in range(5):
                shift = 2 - w if adjoint else w - 2
                shifted_lines = {
                    row: [moved(value, shift) for value in lines[row]] for row in rows_in
                }
                for h in range(5):
                    rows = [y - h + 2 if adjoint else y + h - 2 for y in range(4)]
                    for o in range(4):
                        weight = tap(table, i, o, h, w) if adjoint else tap(table, o, i, h, w)
                        for y, row in enumerate(rows):
                            if row in rows_in:
                                for n in range(2):
                                    line = shifted_lines[row][n]
                                    total[y][o][n] = total[y][o][n] + weight * line
        for y in range(4):
            for o in range(4):
                for n in range(2):
                    write(y, o, pieces[n], total[y][o][n])
        return carry

    lax.fori_loop(0, 2, some_depths, 0)


OWN = (0, 1, 2, 3)
HALO = (-2, -1, 4, 5)


def halo_reader(even, odd):
    slab, last = lax.axis_index("inline"), lax.axis_size("inline") - 1
    parity = slab % 2

    def read(row, c, depths):
        y = row + 2 if row < 0 else row - 4
        through_even, through_odd = even[y, c, depths, :], odd[y, c, depths, :]
        below = parity == 1 if row < 0 else parity == 0
        outside = slab == 0 if row < 0 else slab == last
        return jnp.where(outside, 0.0, jnp.where(below, through_even, through_odd))

    return read


def split(value):
    high = value.astype(jnp.bfloat16)
    return high, (value - high.astype(jnp.float32)).astype(jnp.bfloat16)


def point_fields(chunks, constant, weight, oweight):
    row = lax.broadcasted_iota(jnp.int32, (16, 256), 0)
    orow = lax.broadcasted_iota(jnp.int32, (16, 128), 0)
    column = lax.broadcasted_iota(jnp.int32, (128, 384), 0)
    for block in range(8):

        def line(k, block=block):
            return chunks[block, k : k + 1, :]

        def double(k, line=line):
            return jnp.concatenate([line(k), line(k + 1)], axis=1)

        flat = double(AT_MISC).astype(jnp.int32)
        oflat = line(AT_MISC + 2).astype(jnp.int32)
        w, ow = double(AT_MISC + 3), line(AT_MISC + 5)
        cell, ocell = flat >> 7, oflat >> 7
        at_cross = jnp.concatenate([flat & 127, oflat & 127], axis=1)
        columns = (column == at_cross).astype(jnp.float32).astype(jnp.bfloat16)
        here, ohere = row == cell, orow == ocell
        below, beside = orow == ocell + 1, orow == ocell + 4
        main, along = [], []
        for c in range(4):
            value = w * double(AT_VALUES + 2 * c)
            n0, n1, n2 = (ow * line(AT_NORMALS + 4 * k + c) for k in range(3))
            placed = (
                jnp.where(below, n0, 0.0)
                + jnp.where(beside, n1, 0.0)
                - jnp.where(ohere, n0 + n1 + n2, 0.0)
            )
            main.append(jnp.concatenate([jnp.where(here, value, 0.0), placed], axis=1))
            along.append(
                jnp.concatenate([jnp.zeros((16, 256), jnp.float32), jnp.where(ohere, n2, 0.0)], axis=1)
            )
        both = [
            jnp.concatenate([jnp.where(here, w, 0.0), jnp.zeros((16, 128), jnp.float32)], axis=1),
            jnp.concatenate([jnp.zeros((16, 256), jnp.float32), jnp.where(ohere, ow, 0.0)], axis=1),
        ]
        high, low = split(jnp.concatenate(main + both + along, axis=0))
        sums = lax.dot_general(
            jnp.concatenate([high, low], axis=0),
            columns,
            (((1,), (1,)), ((), ())),
            preferred_element_type=jnp.float32,
        )
        sums = sums[:160] + sums[160:]
        moved = pltpu.roll(sums[96:160], 1, 1)
        z = 4 * block
        for y in range(4):
            for c in range(4):
                k = 16 * c + 4 * y
                constant[y, c, z : z + 4, :] = sums[k : k + 4] + moved[k : k + 4]
            weight[y, z : z + 4, :] = sums[64 + 4 * y : 68 + 4 * y]
            oweight[y, z : z + 4, :] = sums[80 + 4 * y : 84 + 4 * y]


def own_kernel(chunks, smoothed, kernels, partial, constant, weight, oweight, table):
    group = lax.axis_index("depth")
    picked = jnp.where(lane_index((400, 8)) == group, kernels[...], 0.0)
    table[...] = jnp.broadcast_to(jnp.sum(picked, axis=1, keepdims=True), (400, 128))
    point_fields(chunks, constant, weight, oweight)

    def write(y, o, depths, value):
        partial[y, o, depths, :] = value

    conv_rows(
        lambda row, c, depths: smoothed[row, c, depths, :],
        OWN,
        lambda y, o, depths: jnp.zeros((8, 128), jnp.float32),
        table,
        False,
        write,
    )


def forcing_kernel(
    partial, even_in, odd_in, table, constant, weight, oweight, potential, forcing, even, odd
):
    def write(y, o, depths, value):
        potential[y, o, depths, :] = value

    conv_rows(
        halo_reader(even_in, odd_in),
        HALO,
        lambda y, o, depths: partial[y, o, depths, :],
        table,
        False,
        write,
    )

    parity = lax.axis_index("inline") % 2

    def some_depths(k, carry):
        depths = pl.ds(pl.multiple_of(k * 8, 8), 8)
        shares = [oweight[y, depths, :] for y in range(4)]
        weights = [weight[y, depths, :] for y in range(4)]
        for c in range(4):
            lines = [potential[y, c, depths, :] for y in range(4)]
            sums = [weights[y] * lines[y] - constant[y, c, depths, :] for y in range(4)]
            for y in range(4):
                deeper = shares[y] * (pltpu.roll(lines[y], 7, 0) - lines[y])
                across = shares[y] * (pltpu.roll(lines[y], 127, 1) - lines[y])
                sums[y] = sums[y] - deeper + pltpu.roll(deeper, 1, 0)
                sums[y] = sums[y] - across + pltpu.roll(across, 1, 1)
                if y < 3:
                    beside = shares[y] * (lines[y + 1] - lines[y])
                    sums[y] = sums[y] - beside
                    sums[y + 1] = sums[y + 1] + beside
            for y in range(4):
                forcing[y, c, depths, :] = sums[y]
            for y in range(2):
                even[y, c, depths, :] = jnp.where(parity == 0, sums[2 + y], sums[y])
                odd[y, c, depths, :] = jnp.where(parity == 0, sums[y], sums[2 + y])
        return carry

    lax.fori_loop(0, 4, some_depths, 0)


def spread_kernel(forcing, table, potential, partial, out, rows):
    def write(y, o, depths, value):
        partial[y, o, depths, :] = value

    conv_rows(
        lambda row, c, depths: forcing[row, c, depths, :],
        OWN,
        lambda y, o, depths: jnp.zeros((8, 128), jnp.float32),
        table,
        True,
        write,
    )
    for y in range(4):
        for c in range(4):
            rows[pl.ds((c * 4 + y) * 32, 32), :] = potential[y, c]
    for z in range(32):
        out[z // 4, (z % 4) * 16 : (z % 4) * 16 + 16, :] = rows[pl.ds(z, 16, stride=32), :]


def gradient_kernel(*refs):
    chunks, partial, even_in, odd_in, taps, table, scale, root, potential = refs[:9]
    chips, (first, rows, out) = refs[9:13], refs[13:]
    me = lax.axis_index("depth")
    targets = [chips[place // 2].at[place % 2] for place in range(8)]
    for place, target in enumerate(targets):
        target[:64, :] = potential[me ^ place]

    def write(y, o, depths, value):
        rows[pl.ds(pl.multiple_of((o * 4 + y) * 32 + depths.start, 8), 8), :] = value

    conv_rows(
        halo_reader(even_in, odd_in),
        HALO,
        lambda y, o, depths: partial[y, o, depths, :],
        taps,
        True,
        write,
    )

    def keep_first(z, value):
        first[z] = scale[z] * value

    def keep_out(z, value):
        row = (z % 4) * 16
        out[z // 4, row : row + 16, :] = depth_rows(chunks, z) + root[z] * value

    recurrence(
        lambda z: rows[pl.ds(z, 16, stride=32), :],
        lambda lag, z, before: table[before, lag - 1],
        keep_first,
        range(32),
    )
    recurrence(
        lambda z: first[z],
        lambda lag, z, before: table[before, lag - 1],
        keep_out,
        range(31, -1, -1),
    )
    for place, target in enumerate(targets):
        target[64:, :] = out[me ^ place]


def unpack_kernel(places, number, *refs):
    count = len(places)
    parts, (potential, gradient, planes, sent) = refs[:count], refs[-4:]
    me = lax.axis_index("depth")
    order = number[...].reshape(1, 32)
    lane = lane_index((1, 32))
    channels = []
    for slot in range(4 * count):
        here = lane == (me ^ places[slot // 4]) * 4 + slot % 4
        channels.append(jnp.sum(jnp.where(here, order, 0)))
    for half in range(2):
        for slot in range(4 * count):
            place, part = places[slot // 4], parts[slot // 4]
            part = part if place % 2 else part.at[0]
            rows = [64 * half + z * 16 + slot % 4 * 4 for z in range(4)]
            planes[half, slot] = jnp.concatenate([part[row : row + 4, :] for row in rows], axis=0)
    for slot in range(4 * count):
        for half, out in enumerate((potential, gradient)):
            pltpu.make_async_copy(
                planes.at[half, slot], out.at[channels[slot]], sent.at[half]
            ).start()
    for half, out in enumerate((potential, gradient)):
        pltpu.make_async_copy(planes.at[half], out.at[: 4 * count], sent.at[half]).wait()


def swapped(even, odd):
    depths, slabs = lax.axis_size("depth"), lax.axis_size("inline")

    def swap(value, first):
        pairs = []
        for d in range(depths):
            for i in range(slabs):
                other = i + 1 if (i - first) % 2 == 0 else i - 1
                to = (d, other) if 0 <= other < slabs else (d ^ 1, i)
                pairs.append((d * slabs + i, to[0] * slabs + to[1]))
        return lax.ppermute(value, ("depth", "inline"), pairs)

    return swap(even, 0), swap(odd, 1)


def by_group(
    control,
    filter_coeffs,
    conv_kernels,
    channel_order,
    point_cells,
    point_values,
    point_weights,
    orient_cells,
    orient_normals,
    orient_weights,
):
    params = pltpu.CompilerParams(vmem_limit_bytes=48 << 20)
    in_vmem, in_hbm = (pl.BlockSpec(memory_space=space) for space in (pltpu.VMEM, pltpu.HBM))

    def call(kernel, outs, operands, scratch=(), ins=None, to=in_vmem, aliases=None):
        return pl.pallas_call(
            kernel,
            out_shape=outs,
            in_specs=ins or [in_vmem] * len(operands),
            out_specs=jax.tree.map(lambda _: to, outs),
            scratch_shapes=list(scratch),
            input_output_aliases=aliases or {},
            compiler_params=params,
        )(*operands)

    sources = (
        channel_order,
        jnp.transpose(filter_coeffs, (0, 2, 1)).reshape(16, 32),
        point_cells,
        point_weights,
        orient_cells,
        orient_weights,
        point_values.reshape(64, 128),
        orient_normals.reshape(96, 128),
        control.reshape(32, 16, 128),
    )
    sources = tuple(pltpu.with_memory_space_constraint(x, pltpu.HBM) for x in sources)
    held = [pltpu.VMEM(source.shape, source.dtype) for source in sources[1:8]]

    def exchange(*chips):
        def swap(value, flip):
            return lax.ppermute(value, "depth", [(i, i ^ flip) for i in range(8)])

        direct = [chips[k] if k == 0 else swap(chips[k], 2 * k) for k in CHIPS]
        return direct, [swap(part[1], 1) for part in direct]

    *chips, number = call(
        pack_kernel,
        (f32(2, CHUNK, 128),) * 4 + (jax.ShapeDtypeStruct((32,), jnp.int32),),
        sources,
        [
            pltpu.VMEM((128, 128), jnp.float32),
            pltpu.VMEM((32, 16, 128), jnp.float32),
            pltpu.SMEM((32,), jnp.int32),
            *held,
            pltpu.SemaphoreType.DMA((13,)),
        ],
        [in_hbm] * 9,
    )
    direct, passed = exchange(*chips)
    field, edge, plane = f32(4, 4, 32, 128), f32(2, 4, 32, 128), f32(4, 32, 128)
    by_depth = f32(32, 16, 128)
    rows = pltpu.VMEM((512, 128), jnp.float32)
    first = pltpu.VMEM((32, 16, 128), jnp.float32)
    chunks, smoothed, even, odd, table, scale, root = call(
        smooth_kernel,
        (f32(8, CHUNK, 128), field, edge, edge, f32(32, 4, 16, 128), by_depth, by_depth),
        (*direct, *passed),
        [pltpu.VMEM((8, 16, 128), jnp.float32), first, rows],
    )
    even, odd = swapped(even, odd)
    kernels = jnp.transpose(conv_kernels, (1, 3, 4, 2, 0)).reshape(400, 8)
    partial, constant, weight, oweight, taps = call(
        own_kernel, (field, field, plane, plane, f32(400, 128)), (chunks, smoothed, kernels)
    )
    potential, forcing, even, odd = call(
        forcing_kernel,
        (field, field, edge, edge),
        (partial, even, odd, taps, constant, weight, oweight),
    )
    even, odd = swapped(even, odd)
    partial, potential = call(
        spread_kernel, (field, f32(8, 64, 128)), (forcing, taps, potential), [rows]
    )
    chips = call(
        gradient_kernel,
        (f32(2, 128, 128),) * 4,
        (chunks, partial, even, odd, taps, table, scale, root, potential),
        [first, rows, pltpu.VMEM((8, 64, 128), jnp.float32)],
    )
    direct, passed = exchange(*chips)
    came = {2 * k: part for k, part in zip(CHIPS, direct)}
    came |= {2 * k + 1: part for k, part in zip(CHIPS, passed)}
    outs = ()
    for places in ((0, 1), (2 * CHIPS[1], 2 * CHIPS[2]), (2 * CHIPS[3], 7, 5, 3)):
        count = len(places)
        outs = call(
            functools.partial(unpack_kernel, places),
            (by_depth, by_depth),
            (number, *(came[place] for place in places), *outs),
            [
                pltpu.VMEM((2, 4 * count, 16, 128), jnp.float32),
                pltpu.SemaphoreType.DMA((2,)),
            ],
            [in_vmem] * (count + 1) + [in_hbm] * len(outs),
            in_hbm,
            {count + 1: 0, count + 2: 1} if outs else None,
        )
    potential, gradient = outs
    return potential.reshape(control.shape), gradient.reshape(control.shape)


def solution(mesh):
    placed = (
        P(None, "depth", "inline", None),
        P(None, None, "depth"),
        P(),
        P(),
        P(None, "depth", "inline", None),
        P(None, "depth", "inline", None),
        P("depth", "inline", None),
        P(None, "depth", "inline", None),
        P(None, None, "depth", "inline", None),
        P("depth", "inline", None),
    )

    def body(control, filter_coeffs, conv_kernels, *rest):
        groups, block = conv_kernels.shape, control.shape
        fits = groups[:3] == (mesh.shape["depth"], 4, 4) and groups[0] == 8
        if fits and block == (32, 4, 4, 128):
            return by_group(control, filter_coeffs, conv_kernels, *rest)
        return shards(control, filter_coeffs, conv_kernels, *rest)

    return jax.shard_map(
        body,
        mesh=mesh,
        in_specs=placed,
        out_specs=(P(None, "depth", "inline", None), P(None, "depth", "inline", None)),
        check_vma=False,
    )
```

```python
import functools

import jax
import jax.numpy as jnp
from jax import lax
from jax.experimental import pallas as pl
from jax.experimental.pallas import tpu as pltpu
from jax.sharding import PartitionSpec as P

HIGHEST = lax.Precision.HIGHEST


def entering(value, axis, join, neutral, backward):
    count, mine = (lax.axis_size(axis), lax.axis_index(axis))
    pieces = jax.tree.map(lambda part: lax.all_gather(part, axis), value)
    if backward:
        pieces = jax.tree.map(lambda part: part[::-1], pieces)
        mine = count - 1 - mine
    so_far = jax.tree.map(
        lambda part, zero: jnp.full_like(part, 0) + jnp.asarray(zero, part.dtype), value, neutral
    )

    def hop(position, so_far):
        longer = join(so_far, jax.tree.map(lambda part: part[position], pieces))
        return jax.tree.map(lambda new, old: jnp.where(position < mine, new, old), longer, so_far)

    return lax.fori_loop(0, count - 1, hop, so_far)


def extended_2(cells, sides, width):
    for axis, dim in sides:
        count = lax.axis_size(axis)
        ends = count - 1
        head = lax.slice_in_dim(cells, 0, width, axis=dim)
        tail = lax.slice_in_dim(cells, cells.shape[dim] - width, cells.shape[dim], axis=dim)
        cells = jnp.concatenate(
            [
                lax.ppermute(tail, axis, [(i, (i + 1) % count) for i in range(ends)]),
                cells,
                lax.ppermute(head, axis, [((i + 1) % count, i) for i in range(ends)]),
            ],
            axis=dim,
        )
    return cells


def mixing(kernels, channel_order):
    groups = kernels.shape[0]
    group_size = kernels.shape[1]
    channels = groups * group_size
    slots = jnp.arange(channels, dtype=jnp.int32)
    chooser = (channel_order[:, None] == slots[None, :]).astype(jnp.float32)
    in_group = (
        slots[:, None] // group_size == jnp.arange(groups, dtype=jnp.int32)[None, :]
    ).astype(jnp.float32)
    in_place = (
        slots[:, None] % group_size == jnp.arange(group_size, dtype=jnp.int32)[None, :]
    ).astype(jnp.float32)
    block_mix = jnp.einsum(
        "sg,sa,tg,tb,gabhw->sthw",
        in_group,
        in_place,
        in_group,
        in_place,
        kernels,
        precision=HIGHEST,
    )
    return jnp.einsum("sc,td,sthw->cdhw", chooser, chooser, block_mix, precision=HIGHEST)


def padded_conv(padded, weights):
    return lax.conv_general_dilated(
        padded,
        weights,
        (1, 1),
        ((0, 0), (2, 2)),
        dimension_numbers=("CNHW", "OIHW", "CNHW"),
        precision=HIGHEST,
    )


def compose(earlier, later):
    first_map, first_shift = earlier
    second_map, second_shift = later
    joined_map = jnp.einsum("cnij,cnjk->cnik", second_map, first_map, precision=HIGHEST)
    joined_shift = (
        jnp.einsum("cnij,cnjk->cnik", second_map, first_shift, precision=HIGHEST) + second_shift
    )
    return (joined_map, joined_shift)


def build_tiles(coeffs, by_column, block_len):
    lead = coeffs.shape[1:3]
    lag_steps = jnp.arange(1, 5, dtype=jnp.int32)[:, None, None]
    if by_column:
        row_ids = jnp.arange(block_len + 4, dtype=jnp.int32)[None, :, None]
        col_ids = jnp.arange(block_len, dtype=jnp.int32)[None, None, :]
        picker = (row_ids == col_ids + lag_steps).astype(jnp.float32)
        extended = jnp.einsum("lcnk,lzk->cnzk", coeffs, picker, precision=HIGHEST)
        lower_tile = extended[:, :, :block_len, :]
        exit_map = extended[:, :, block_len:, :]
        entry_base = (
            jnp.arange(block_len, dtype=jnp.int32)[:, None]
            == jnp.arange(4, dtype=jnp.int32)[None, :]
        ).astype(jnp.float32)
        entry_map = jnp.broadcast_to(entry_base, lead + (block_len, 4))
    else:
        row_ids = jnp.arange(block_len, dtype=jnp.int32)[None, :, None]
        col_ids = jnp.arange(block_len + 4, dtype=jnp.int32)[None, None, :]
        picker = (col_ids == row_ids - lag_steps + 4).astype(jnp.float32)
        extended = jnp.einsum("lcnz,lzk->cnzk", coeffs, picker, precision=HIGHEST)
        lower_tile = extended[:, :, :, 4:]
        entry_map = extended[:, :, :, :4]
        exit_base = (
            jnp.arange(block_len, dtype=jnp.int32)[None, :]
            == jnp.arange(4, dtype=jnp.int32)[:, None] + block_len - 4
        ).astype(jnp.float32)
        exit_map = jnp.broadcast_to(exit_base, lead + (4, block_len))
    return (lower_tile, entry_map, exit_map)


def sweep_blocks(field, coeffs, by_column, upward, prefix):
    if upward:
        field = field[:, ::-1, ::-1]
        coeffs = coeffs[:, :, ::-1, ::-1]
    block_len = coeffs.shape[3]
    lower_tile, entry_map, exit_map = build_tiles(coeffs, by_column, block_len)
    identity_tile = jnp.eye(block_len, dtype=jnp.float32)
    inverse = identity_tile + lower_tile
    power = lower_tile
    power = jnp.einsum("cnij,cnjk->cnik", power, power, precision=HIGHEST)
    inverse = inverse + jnp.einsum("cnij,cnjk->cnik", inverse, power, precision=HIGHEST)
    reach_map = jnp.einsum("cnzk,cnkj->cnzj", inverse, entry_map, precision=HIGHEST)
    carry_map = jnp.einsum("cniz,cnzj->cnij", exit_map, reach_map, precision=HIGHEST)
    local_part = jnp.einsum("cnzk,cnkm->cnzm", inverse, field, precision=HIGHEST)
    carry_out = jnp.einsum("cniz,cnzm->cnim", exit_map, local_part, precision=HIGHEST)
    incoming = prefix((carry_map, carry_out), upward)
    result = local_part + jnp.einsum("cnzj,cnjm->cnzm", reach_map, incoming, precision=HIGHEST)
    if upward:
        result = result[:, ::-1, ::-1]
    return result


def shards(
    control,
    filter_coeffs,
    conv_kernels,
    channel_order,
    point_cells,
    point_values,
    point_weights,
    orient_cells,
    orient_normals,
    orient_weights,
):
    channels, block_len, inline_rows, cross_cols = control.shape
    plane_cells = inline_rows * cross_cols
    source = control.reshape(channels, block_len, plane_cells)
    coeffs = filter_coeffs[:, :, None, :]

    def to_blocks(field):
        return field[:, None]

    def from_blocks(field):
        return field[:, 0]

    def scaled(field, factor):
        return factor[..., None] * field

    def prefix(maps, upward):
        start = (
            jnp.broadcast_to(jnp.eye(4, dtype=jnp.float32), maps[0].shape),
            jnp.zeros_like(maps[1]),
        )
        return entering(maps, "depth", compose, start, upward)[1]

    scaling = 1.0 - jnp.sum(coeffs, axis=0)
    root_scale = jnp.sqrt(scaling)
    filtered = sweep_blocks(scaled(to_blocks(source), root_scale), coeffs, False, False, prefix)
    smoothed = sweep_blocks(scaled(filtered, scaling), coeffs, False, True, prefix)
    smoothed_field = from_blocks(smoothed).reshape(control.shape)
    weights = mixing(conv_kernels, channel_order)
    smoothed_padded = extended_2(smoothed_field, (("inline", 2),), 2)
    potential = padded_conv(smoothed_padded, weights)
    flat_field = potential.reshape(channels, -1)
    depth_base = lax.axis_index("depth") * block_len
    inline_base = lax.axis_index("inline") * inline_rows
    cells = point_cells.reshape(3, -1)
    flat_index = (
        (cells[0] - depth_base) * inline_rows + cells[1] - inline_base
    ) * cross_cols + cells[2]
    misfit = (
        flat_field[:, flat_index] - point_values.reshape(channels, -1)
    ) * point_weights.reshape(-1)[None, :]
    ocells = orient_cells.reshape(3, -1)
    base_cell = (
        (ocells[0] - depth_base) * inline_rows + ocells[1] - inline_base
    ) * cross_cols + ocells[2]
    normals = orient_normals.reshape(3, channels, -1)
    oweight = orient_weights.reshape(-1)[None, :]
    update_values = [misfit]
    update_cells = [flat_index]
    for component, stride in enumerate((plane_cells, cross_cols, 1)):
        mismatch = flat_field[:, base_cell + stride] - flat_field[:, base_cell] - normals[component]
        weighted = mismatch * oweight
        update_values.append(weighted)
        update_cells.append(base_cell + stride)
        update_values.append(-weighted)
        update_cells.append(base_cell)
    all_values = jnp.concatenate(update_values, axis=1)
    all_cells = jnp.concatenate(update_cells, axis=0)
    adjoint_weights = jnp.transpose(weights, (1, 0, 2, 3))[:, :, ::-1, ::-1]
    forcing = jnp.zeros_like(flat_field).at[:, all_cells].add(all_values)
    forcing_padded = extended_2(forcing.reshape(control.shape), (("inline", 2),), 2)
    spread = padded_conv(forcing_padded, adjoint_weights).reshape(channels, block_len, plane_cells)
    adjoint_back = scaled(sweep_blocks(to_blocks(spread), coeffs, True, False, prefix), scaling)
    adjoint_fore = scaled(sweep_blocks(adjoint_back, coeffs, True, True, prefix), root_scale)
    gradient = control + from_blocks(adjoint_fore).reshape(control.shape)
    return (potential, gradient)


CHUNK = 96
CHIPS = (0, 3, 2, 1)
AT_VALUES, AT_NORMALS, AT_COEFFS, AT_MISC = 64, 72, 84, 88


def f32(*shape):
    return jax.ShapeDtypeStruct(shape, jnp.float32)


def lane_index(shape):
    return lax.broadcasted_iota(jnp.int32, shape, len(shape) - 1)


def place_points(target, channels, values, normals, misc, by_channel):
    target[AT_MISC:CHUNK, :] = misc
    for c, channel in enumerate(channels):
        row = AT_VALUES + 2 * c
        target[row : row + 2, :] = values[pl.ds(channel * 2, 2), :]
        for k in range(3):
            row = AT_NORMALS + 4 * k + c
            target[row : row + 1, :] = normals[pl.ds(k * 32 + channel, 1), :]
        row = AT_COEFFS + c
        target[row : row + 1, :] = by_channel[pl.ds(channel, 1), :]


def place_control(target, channels, control):
    for c, channel in enumerate(channels):
        plane = control[channel]
        for z in range(4):
            row = z * 16 + c * 4
            target[row : row + 4, :] = plane[z * 4 : z * 4 + 4]


def pack_kernel(*refs):
    sources, chips, number, by_channel, control = refs[:9], refs[9:13], refs[13], refs[14], refs[15]
    order, coeffs, cells, weights, ocells, oweights, values, normals, arrived = refs[16:]
    held = (order, number, coeffs, cells, weights, ocells, oweights, values, normals)
    pairs = [(sources[8].at[8 * k : 8 * k + 8], control.at[8 * k : 8 * k + 8]) for k in range(4)]
    pairs += zip(sources[:1] + sources[:8], held)
    copies = [
        pltpu.make_async_copy(source, target, arrived.at[k])
        for k, (source, target) in enumerate(pairs)
    ]
    for copy in copies:
        copy.start()

    def flat_cell(ref):
        z, y, x = (ref[k, 0] for k in range(3))
        return (((y & 3) * 4 + (z & 3)) * 128 + x).astype(jnp.float32)

    for copy in copies[4:]:
        copy.wait()
    flat, oflat = flat_cell(cells), flat_cell(ocells)
    weight = weights[0]
    misc = jnp.concatenate(
        [flat[:, :128], flat[:, 128:], oflat, weight[:, :128], weight[:, 128:], oweights[0]]
        + [jnp.zeros((2, 128), jnp.float32)],
        axis=0,
    )
    by_channel[:, :16] = jnp.transpose(
        jnp.concatenate([coeffs[...], jnp.zeros((16, 96), jnp.float32)], axis=1)
    )
    by_channel[:, 16:] = jnp.zeros((128, 112), jnp.float32)
    me = lax.axis_index("depth")
    places = [
        (chips[place // 2].at[place % 2], [order[(me ^ place) * 4 + c] for c in range(4)])
        for place in range(8)
    ]
    for target, channels in places:
        place_points(target, channels, values, normals, misc, by_channel)
    for copy in copies[:4]:
        copy.wait()
    for target, channels in places:
        place_control(target, channels, control)


def join_kernel(got, *refs):
    keep, joined = refs[:4], refs[4:]
    for k in range(4):
        joined[k][0] = keep[k][...]
        joined[k][1] = got[k]


def second_kernel(both, out):
    out[...] = both[1]


def coefficient(expanded, lag, z):
    block, local = divmod(z, 4)
    k = (lag - 1) * 4 + local
    return jnp.broadcast_to(expanded[block, :, k : k + 1], (16, 128))


def repeat_coeffs(chunks, expanded):
    for block in range(8):
        for c in range(4):
            row = AT_COEFFS + c
            expanded[block, 4 * c : 4 * c + 4, :] = jnp.broadcast_to(
                chunks[block, row : row + 1, :], (4, 128)
            )


def recurrence(source, factor, emit, order):
    history = []
    for t in order:
        total = source(t)
        for lag in range(len(history), 0, -1):
            before, value = history[lag - 1]
            total = total + factor(lag, t, before) * value
        history = [(t, total)] + history[:3]
        emit(t, total)


def depth_rows(chunks, z):
    return chunks[z // 4, (z % 4) * 16 : (z % 4) * 16 + 16, :]


def smooth_kernel(*refs):
    direct, passed, refs = refs[:4], refs[4:8], refs[8:]
    chunks, smoothed, even, odd, table, scale, root, expanded, first, rows = refs
    me = lax.axis_index("depth")
    for n, k in enumerate(CHIPS):
        chunks[me ^ (2 * k)] = direct[n][0]
        chunks[me ^ (2 * k + 1)] = passed[n][...]
    repeat_coeffs(chunks, expanded)
    lags = {}

    def start(z):
        lags.clear()
        lags.update({lag: coefficient(expanded, lag, z) for lag in range(1, 5)})
        for lag in range(1, 5):
            table[z, lag - 1] = lags[lag]
        lags[0] = 1.0 - ((lags[1] + lags[2]) + (lags[3] + lags[4]))
        scale[z] = lags[0]
        lags[-1] = jnp.sqrt(lags[0])
        root[z] = lags[-1]
        return lags[-1] * depth_rows(chunks, z)

    def keep_first(z, value):
        first[z] = lags[0] * value

    def keep_rows(z, value):
        rows[z * 16 : z * 16 + 16, :] = value

    recurrence(start, lambda lag, z, before: lags[lag], keep_first, range(32))
    recurrence(
        lambda z: first[z],
        lambda lag, z, before: table[z, lag - 1],
        keep_rows,
        range(31, -1, -1),
    )
    parity = lax.axis_index("inline") % 2
    for y in range(4):
        for c in range(4):
            smoothed[y, c] = rows[pl.ds(c * 4 + y, 32, stride=16), :]
    for y in range(2):
        even[y] = smoothed[2 - 2 * parity + y]
        odd[y] = smoothed[2 * parity + y]


def tap(table, a, b, h, w):
    row = ((a * 5 + h) * 5 + w) * 4 + b
    return jnp.broadcast_to(table[row : row + 1, :], (8, 128))


def conv_rows(read, rows_in, start, table, adjoint, write):
    lane = lane_index((8, 128))

    def moved(value, shift):
        if shift == 0:
            return value
        inside = lane >= -shift if shift < 0 else lane < 128 - shift
        return jnp.where(inside, pltpu.roll(value, -shift % 128, 1), 0.0)

    def some_depths(k, carry):
        pieces = [pl.ds(pl.multiple_of(k * 16 + 8 * n, 8), 8) for n in range(2)]
        total = [[[start(y, o, at) for at in pieces] for o in range(4)] for y in range(4)]
        for i in range(4):
            lines = {row: [read(row, i, at) for at in pieces] for row in rows_in}
            for w in range(5):
                shift = 2 - w if adjoint else w - 2
                shifted_lines = {
                    row: [moved(value, shift) for value in lines[row]] for row in rows_in
                }
                for h in range(5):
                    rows = [y - h + 2 if adjoint else y + h - 2 for y in range(4)]
                    for o in range(4):
                        weight = tap(table, i, o, h, w) if adjoint else tap(table, o, i, h, w)
                        for y, row in enumerate(rows):
                            if row in rows_in:
                                for n in range(2):
                                    line = shifted_lines[row][n]
                                    total[y][o][n] = total[y][o][n] + weight * line
        for y in range(4):
            for o in range(4):
                for n in range(2):
                    write(y, o, pieces[n], total[y][o][n])
        return carry

    lax.fori_loop(0, 2, some_depths, 0)


OWN = (0, 1, 2, 3)
HALO = (-2, -1, 4, 5)


def halo_reader(even, odd):
    slab, last = lax.axis_index("inline"), lax.axis_size("inline") - 1
    parity = slab % 2

    def read(row, c, depths):
        y = row + 2 if row < 0 else row - 4
        through_even, through_odd = even[y, c, depths, :], odd[y, c, depths, :]
        below = parity == 1 if row < 0 else parity == 0
        outside = slab == 0 if row < 0 else slab == last
        return jnp.where(outside, 0.0, jnp.where(below, through_even, through_odd))

    return read


def split(value):
    high = value.astype(jnp.bfloat16)
    return high, (value - high.astype(jnp.float32)).astype(jnp.bfloat16)


def point_fields(chunks, constant, weight, oweight):
    row = lax.broadcasted_iota(jnp.int32, (16, 256), 0)
    orow = lax.broadcasted_iota(jnp.int32, (16, 128), 0)
    column = lax.broadcasted_iota(jnp.int32, (128, 384), 0)
    for block in range(8):

        def line(k, block=block):
            return chunks[block, k : k + 1, :]

        def double(k, line=line):
            return jnp.concatenate([line(k), line(k + 1)], axis=1)

        flat = double(AT_MISC).astype(jnp.int32)
        oflat = line(AT_MISC + 2).astype(jnp.int32)
        w, ow = double(AT_MISC + 3), line(AT_MISC + 5)
        cell, ocell = flat >> 7, oflat >> 7
        at_cross = jnp.concatenate([flat & 127, oflat & 127], axis=1)
        columns = (column == at_cross).astype(jnp.float32).astype(jnp.bfloat16)
        here, ohere = row == cell, orow == ocell
        below, beside = orow == ocell + 1, orow == ocell + 4
        main, along = [], []
        for c in range(4):
            value = w * double(AT_VALUES + 2 * c)
            n0, n1, n2 = (ow * line(AT_NORMALS + 4 * k + c) for k in range(3))
            placed = (
                jnp.where(below, n0, 0.0)
                + jnp.where(beside, n1, 0.0)
                - jnp.where(ohere, n0 + n1 + n2, 0.0)
            )
            main.append(jnp.concatenate([jnp.where(here, value, 0.0), placed], axis=1))
            along.append(
                jnp.concatenate([jnp.zeros((16, 256), jnp.float32), jnp.where(ohere, n2, 0.0)], axis=1)
            )
        both = [
            jnp.concatenate([jnp.where(here, w, 0.0), jnp.zeros((16, 128), jnp.float32)], axis=1),
            jnp.concatenate([jnp.zeros((16, 256), jnp.float32), jnp.where(ohere, ow, 0.0)], axis=1),
        ]
        high, low = split(jnp.concatenate(main + both + along, axis=0))
        sums = lax.dot_general(
            jnp.concatenate([high, low], axis=0),
            columns,
            (((1,), (1,)), ((), ())),
            preferred_element_type=jnp.float32,
        )
        sums = sums[:160] + sums[160:]
        moved = pltpu.roll(sums[96:160], 1, 1)
        z = 4 * block
        for y in range(4):
            for c in range(4):
                k = 16 * c + 4 * y
                constant[y, c, z : z + 4, :] = sums[k : k + 4] + moved[k : k + 4]
            weight[y, z : z + 4, :] = sums[64 + 4 * y : 68 + 4 * y]
            oweight[y, z : z + 4, :] = sums[80 + 4 * y : 84 + 4 * y]


def own_kernel(chunks, smoothed, kernels, partial, constant, weight, oweight, table):
    group = lax.axis_index("depth")
    picked = jnp.where(lane_index((400, 8)) == group, kernels[...], 0.0)
    table[...] = jnp.broadcast_to(jnp.sum(picked, axis=1, keepdims=True), (400, 128))
    point_fields(chunks, constant, weight, oweight)

    def write(y, o, depths, value):
        partial[y, o, depths, :] = value

    conv_rows(
        lambda row, c, depths: smoothed[row, c, depths, :],
        OWN,
        lambda y, o, depths: jnp.zeros((8, 128), jnp.float32),
        table,
        False,
        write,
    )


def forcing_kernel(
    partial, even_in, odd_in, table, constant, weight, oweight, potential, forcing, even, odd
):
    def write(y, o, depths, value):
        potential[y, o, depths, :] = value

    conv_rows(
        halo_reader(even_in, odd_in),
        HALO,
        lambda y, o, depths: partial[y, o, depths, :],
        table,
        False,
        write,
    )

    parity = lax.axis_index("inline") % 2

    def some_depths(k, carry):
        depths = pl.ds(pl.multiple_of(k * 8, 8), 8)
        shares = [oweight[y, depths, :] for y in range(4)]
        weights = [weight[y, depths, :] for y in range(4)]
        for c in range(4):
            lines = [potential[y, c, depths, :] for y in range(4)]
            sums = [weights[y] * lines[y] - constant[y, c, depths, :] for y in range(4)]
            for y in range(4):
                deeper = shares[y] * (pltpu.roll(lines[y], 7, 0) - lines[y])
                across = shares[y] * (pltpu.roll(lines[y], 127, 1) - lines[y])
                sums[y] = sums[y] - deeper + pltpu.roll(deeper, 1, 0)
                sums[y] = sums[y] - across + pltpu.roll(across, 1, 1)
                if y < 3:
                    beside = shares[y] * (lines[y + 1] - lines[y])
                    sums[y] = sums[y] - beside
                    sums[y + 1] = sums[y + 1] + beside
            for y in range(4):
                forcing[y, c, depths, :] = sums[y]
            for y in range(2):
                even[y, c, depths, :] = jnp.where(parity == 0, sums[2 + y], sums[y])
                odd[y, c, depths, :] = jnp.where(parity == 0, sums[y], sums[2 + y])
        return carry

    lax.fori_loop(0, 4, some_depths, 0)


def spread_kernel(forcing, table, potential, partial, out, rows):
    def write(y, o, depths, value):
        partial[y, o, depths, :] = value

    conv_rows(
        lambda row, c, depths: forcing[row, c, depths, :],
        OWN,
        lambda y, o, depths: jnp.zeros((8, 128), jnp.float32),
        table,
        True,
        write,
    )
    for y in range(4):
        for c in range(4):
            rows[pl.ds((c * 4 + y) * 32, 32), :] = potential[y, c]
    for z in range(32):
        out[z // 4, (z % 4) * 16 : (z % 4) * 16 + 16, :] = rows[pl.ds(z, 16, stride=32), :]


def gradient_kernel(*refs):
    chunks, partial, even_in, odd_in, taps, table, scale, root, potential = refs[:9]
    give, keep, (first, rows, out) = refs[9], refs[10:14], refs[14:]
    me = lax.axis_index("depth")
    targets = [
        give.at[place // 2] if place % 2 else keep[place // 2] for place in range(8)
    ]
    for place, target in enumerate(targets):
        target[:64, :] = potential[me ^ place]

    def write(y, o, depths, value):
        rows[pl.ds(pl.multiple_of((o * 4 + y) * 32 + depths.start, 8), 8), :] = value

    conv_rows(
        halo_reader(even_in, odd_in),
        HALO,
        lambda y, o, depths: partial[y, o, depths, :],
        taps,
        True,
        write,
    )

    def keep_first(z, value):
        first[z] = scale[z] * value

    def keep_out(z, value):
        row = (z % 4) * 16
        out[z // 4, row : row + 16, :] = depth_rows(chunks, z) + root[z] * value

    recurrence(
        lambda z: rows[pl.ds(z, 16, stride=32), :],
        lambda lag, z, before: table[before, lag - 1],
        keep_first,
        range(32),
    )
    recurrence(
        lambda z: first[z],
        lambda lag, z, before: table[before, lag - 1],
        keep_out,
        range(31, -1, -1),
    )
    for place, target in enumerate(targets):
        target[64:, :] = out[me ^ place]


def unpack_kernel(chips, number, *refs):
    count = len(chips)
    parts, (potential, gradient, planes, sent) = refs[:count], refs[-4:]
    me = lax.axis_index("depth")
    order = number[...].reshape(1, 32)
    lane = lane_index((1, 32))
    channels = []
    for slot in range(8 * count):
        place = 2 * chips[slot // 8] + slot // 4 % 2
        here = lane == (me ^ place) * 4 + slot % 4
        channels.append(jnp.sum(jnp.where(here, order, 0)))
    for half in range(2):
        for slot in range(8 * count):
            k, source, c = slot // 8, slot // 4 % 2, slot % 4
            rows = [64 * half + z * 16 + c * 4 for z in range(4)]
            pieces = [parts[k][source, row : row + 4, :] for row in rows]
            planes[half, slot] = jnp.concatenate(pieces, axis=0)
    for slot in range(8 * count):
        for half, out in enumerate((potential, gradient)):
            pltpu.make_async_copy(
                planes.at[half, slot], out.at[channels[slot]], sent.at[half]
            ).start()
    for half, out in enumerate((potential, gradient)):
        pltpu.make_async_copy(planes.at[half], out.at[: 8 * count], sent.at[half]).wait()


def swapped(even, odd):
    depths, slabs = lax.axis_size("depth"), lax.axis_size("inline")

    def swap(value, first):
        pairs = []
        for d in range(depths):
            for i in range(slabs):
                other = i + 1 if (i - first) % 2 == 0 else i - 1
                to = (d, other) if 0 <= other < slabs else (d ^ 1, i)
                pairs.append((d * slabs + i, to[0] * slabs + to[1]))
        return lax.ppermute(value, ("depth", "inline"), pairs)

    return swap(even, 0), swap(odd, 1)


def by_group(
    control,
    filter_coeffs,
    conv_kernels,
    channel_order,
    point_cells,
    point_values,
    point_weights,
    orient_cells,
    orient_normals,
    orient_weights,
):
    params = pltpu.CompilerParams(vmem_limit_bytes=48 << 20)
    in_vmem, in_hbm = (pl.BlockSpec(memory_space=space) for space in (pltpu.VMEM, pltpu.HBM))

    def call(kernel, outs, operands, scratch=(), ins=None, to=in_vmem, aliases=None):
        return pl.pallas_call(
            kernel,
            out_shape=outs,
            in_specs=ins or [in_vmem] * len(operands),
            out_specs=jax.tree.map(lambda _: to, outs),
            scratch_shapes=list(scratch),
            input_output_aliases=aliases or {},
            compiler_params=params,
        )(*operands)

    sources = (
        channel_order,
        jnp.transpose(filter_coeffs, (0, 2, 1)).reshape(16, 32),
        point_cells,
        point_weights,
        orient_cells,
        orient_weights,
        point_values.reshape(64, 128),
        orient_normals.reshape(96, 128),
        control.reshape(32, 16, 128),
    )
    sources = tuple(pltpu.with_memory_space_constraint(x, pltpu.HBM) for x in sources)
    held = [pltpu.VMEM(source.shape, source.dtype) for source in sources[1:8]]

    def swap(value, flip):
        return lax.ppermute(value, "depth", [(i, i ^ flip) for i in range(8)])

    def exchange(*chips):
        direct = [chips[k] if k == 0 else swap(chips[k], 2 * k) for k in CHIPS]
        passed = [call(second_kernel, f32(*part.shape[1:]), (part,)) for part in direct]
        return direct, [swap(part, 1) for part in passed]

    def exchange_home(give, *keep):
        joined = call(join_kernel, (f32(2, 128, 128),) * 4, (swap(give, 1), *keep))
        return [joined[k] if k == 0 else swap(joined[k], 2 * k) for k in CHIPS]

    *chips, number = call(
        pack_kernel,
        (f32(2, CHUNK, 128),) * 4 + (jax.ShapeDtypeStruct((32,), jnp.int32),),
        sources,
        [
            pltpu.VMEM((128, 128), jnp.float32),
            pltpu.VMEM((32, 16, 128), jnp.float32),
            pltpu.SMEM((32,), jnp.int32),
            *held,
            pltpu.SemaphoreType.DMA((13,)),
        ],
        [in_hbm] * 9,
    )
    direct, passed = exchange(*chips)
    field, edge, plane = f32(4, 4, 32, 128), f32(2, 4, 32, 128), f32(4, 32, 128)
    by_depth = f32(32, 16, 128)
    rows = pltpu.VMEM((512, 128), jnp.float32)
    first = pltpu.VMEM((32, 16, 128), jnp.float32)
    chunks, smoothed, even, odd, table, scale, root = call(
        smooth_kernel,
        (f32(8, CHUNK, 128), field, edge, edge, f32(32, 4, 16, 128), by_depth, by_depth),
        (*direct, *passed),
        [pltpu.VMEM((8, 16, 128), jnp.float32), first, rows],
    )
    even, odd = swapped(even, odd)
    kernels = jnp.transpose(conv_kernels, (1, 3, 4, 2, 0)).reshape(400, 8)
    partial, constant, weight, oweight, taps = call(
        own_kernel, (field, field, plane, plane, f32(400, 128)), (chunks, smoothed, kernels)
    )
    potential, forcing, even, odd = call(
        forcing_kernel,
        (field, field, edge, edge),
        (partial, even, odd, taps, constant, weight, oweight),
    )
    even, odd = swapped(even, odd)
    partial, potential = call(
        spread_kernel, (field, f32(8, 64, 128)), (forcing, taps, potential), [rows]
    )
    give, *keep = call(
        gradient_kernel,
        (f32(4, 128, 128),) + (f32(128, 128),) * 4,
        (chunks, partial, even, odd, taps, table, scale, root, potential),
        [first, rows, pltpu.VMEM((8, 64, 128), jnp.float32)],
    )
    parts = exchange_home(give, *keep)
    outs = ()
    for some in (slice(0, 1), slice(1, 2), slice(2, 4)):
        count = len(CHIPS[some])
        outs = call(
            functools.partial(unpack_kernel, CHIPS[some]),
            (by_depth, by_depth),
            (number, *parts[some], *outs),
            [
                pltpu.VMEM((2, 8 * count, 16, 128), jnp.float32),
                pltpu.SemaphoreType.DMA((2,)),
            ],
            [in_vmem] * (count + 1) + [in_hbm] * len(outs),
            in_hbm,
            {count + 1: 0, count + 2: 1} if outs else None,
        )
    potential, gradient = outs
    return potential.reshape(control.shape), gradient.reshape(control.shape)


def solution(mesh):
    placed = (
        P(None, "depth", "inline", None),
        P(None, None, "depth"),
        P(),
        P(),
        P(None, "depth", "inline", None),
        P(None, "depth", "inline", None),
        P("depth", "inline", None),
        P(None, "depth", "inline", None),
        P(None, None, "depth", "inline", None),
        P("depth", "inline", None),
    )

    def body(control, filter_coeffs, conv_kernels, *rest):
        groups, block = conv_kernels.shape, control.shape
        fits = groups[:3] == (mesh.shape["depth"], 4, 4) and groups[0] == 8
        if fits and block == (32, 4, 4, 128):
            return by_group(control, filter_coeffs, conv_kernels, *rest)
        return shards(control, filter_coeffs, conv_kernels, *rest)

    return jax.shard_map(
        body,
        mesh=mesh,
        in_specs=placed,
        out_specs=(P(None, "depth", "inline", None), P(None, "depth", "inline", None)),
        check_vma=False,
    )
```

```python
import functools

import jax
import jax.numpy as jnp
from jax import lax
from jax.experimental import pallas as pl
from jax.experimental.pallas import tpu as pltpu
from jax.sharding import PartitionSpec as P

HIGHEST = lax.Precision.HIGHEST


def entering(value, axis, join, neutral, backward):
    count, mine = (lax.axis_size(axis), lax.axis_index(axis))
    pieces = jax.tree.map(lambda part: lax.all_gather(part, axis), value)
    if backward:
        pieces = jax.tree.map(lambda part: part[::-1], pieces)
        mine = count - 1 - mine
    so_far = jax.tree.map(
        lambda part, zero: jnp.full_like(part, 0) + jnp.asarray(zero, part.dtype), value, neutral
    )

    def hop(position, so_far):
        longer = join(so_far, jax.tree.map(lambda part: part[position], pieces))
        return jax.tree.map(lambda new, old: jnp.where(position < mine, new, old), longer, so_far)

    return lax.fori_loop(0, count - 1, hop, so_far)


def extended_2(cells, sides, width):
    for axis, dim in sides:
        count = lax.axis_size(axis)
        ends = count - 1
        head = lax.slice_in_dim(cells, 0, width, axis=dim)
        tail = lax.slice_in_dim(cells, cells.shape[dim] - width, cells.shape[dim], axis=dim)
        cells = jnp.concatenate(
            [
                lax.ppermute(tail, axis, [(i, (i + 1) % count) for i in range(ends)]),
                cells,
                lax.ppermute(head, axis, [((i + 1) % count, i) for i in range(ends)]),
            ],
            axis=dim,
        )
    return cells


def mixing(kernels, channel_order):
    groups = kernels.shape[0]
    group_size = kernels.shape[1]
    channels = groups * group_size
    slots = jnp.arange(channels, dtype=jnp.int32)
    chooser = (channel_order[:, None] == slots[None, :]).astype(jnp.float32)
    in_group = (
        slots[:, None] // group_size == jnp.arange(groups, dtype=jnp.int32)[None, :]
    ).astype(jnp.float32)
    in_place = (
        slots[:, None] % group_size == jnp.arange(group_size, dtype=jnp.int32)[None, :]
    ).astype(jnp.float32)
    block_mix = jnp.einsum(
        "sg,sa,tg,tb,gabhw->sthw",
        in_group,
        in_place,
        in_group,
        in_place,
        kernels,
        precision=HIGHEST,
    )
    return jnp.einsum("sc,td,sthw->cdhw", chooser, chooser, block_mix, precision=HIGHEST)


def padded_conv(padded, weights):
    return lax.conv_general_dilated(
        padded,
        weights,
        (1, 1),
        ((0, 0), (2, 2)),
        dimension_numbers=("CNHW", "OIHW", "CNHW"),
        precision=HIGHEST,
    )


def compose(earlier, later):
    first_map, first_shift = earlier
    second_map, second_shift = later
    joined_map = jnp.einsum("cnij,cnjk->cnik", second_map, first_map, precision=HIGHEST)
    joined_shift = (
        jnp.einsum("cnij,cnjk->cnik", second_map, first_shift, precision=HIGHEST) + second_shift
    )
    return (joined_map, joined_shift)


def build_tiles(coeffs, by_column, block_len):
    lead = coeffs.shape[1:3]
    lag_steps = jnp.arange(1, 5, dtype=jnp.int32)[:, None, None]
    if by_column:
        row_ids = jnp.arange(block_len + 4, dtype=jnp.int32)[None, :, None]
        col_ids = jnp.arange(block_len, dtype=jnp.int32)[None, None, :]
        picker = (row_ids == col_ids + lag_steps).astype(jnp.float32)
        extended = jnp.einsum("lcnk,lzk->cnzk", coeffs, picker, precision=HIGHEST)
        lower_tile = extended[:, :, :block_len, :]
        exit_map = extended[:, :, block_len:, :]
        entry_base = (
            jnp.arange(block_len, dtype=jnp.int32)[:, None]
            == jnp.arange(4, dtype=jnp.int32)[None, :]
        ).astype(jnp.float32)
        entry_map = jnp.broadcast_to(entry_base, lead + (block_len, 4))
    else:
        row_ids = jnp.arange(block_len, dtype=jnp.int32)[None, :, None]
        col_ids = jnp.arange(block_len + 4, dtype=jnp.int32)[None, None, :]
        picker = (col_ids == row_ids - lag_steps + 4).astype(jnp.float32)
        extended = jnp.einsum("lcnz,lzk->cnzk", coeffs, picker, precision=HIGHEST)
        lower_tile = extended[:, :, :, 4:]
        entry_map = extended[:, :, :, :4]
        exit_base = (
            jnp.arange(block_len, dtype=jnp.int32)[None, :]
            == jnp.arange(4, dtype=jnp.int32)[:, None] + block_len - 4
        ).astype(jnp.float32)
        exit_map = jnp.broadcast_to(exit_base, lead + (4, block_len))
    return (lower_tile, entry_map, exit_map)


def sweep_blocks(field, coeffs, by_column, upward, prefix):
    if upward:
        field = field[:, ::-1, ::-1]
        coeffs = coeffs[:, :, ::-1, ::-1]
    block_len = coeffs.shape[3]
    lower_tile, entry_map, exit_map = build_tiles(coeffs, by_column, block_len)
    identity_tile = jnp.eye(block_len, dtype=jnp.float32)
    inverse = identity_tile + lower_tile
    power = lower_tile
    power = jnp.einsum("cnij,cnjk->cnik", power, power, precision=HIGHEST)
    inverse = inverse + jnp.einsum("cnij,cnjk->cnik", inverse, power, precision=HIGHEST)
    reach_map = jnp.einsum("cnzk,cnkj->cnzj", inverse, entry_map, precision=HIGHEST)
    carry_map = jnp.einsum("cniz,cnzj->cnij", exit_map, reach_map, precision=HIGHEST)
    local_part = jnp.einsum("cnzk,cnkm->cnzm", inverse, field, precision=HIGHEST)
    carry_out = jnp.einsum("cniz,cnzm->cnim", exit_map, local_part, precision=HIGHEST)
    incoming = prefix((carry_map, carry_out), upward)
    result = local_part + jnp.einsum("cnzj,cnjm->cnzm", reach_map, incoming, precision=HIGHEST)
    if upward:
        result = result[:, ::-1, ::-1]
    return result


def shards(
    control,
    filter_coeffs,
    conv_kernels,
    channel_order,
    point_cells,
    point_values,
    point_weights,
    orient_cells,
    orient_normals,
    orient_weights,
):
    channels, block_len, inline_rows, cross_cols = control.shape
    plane_cells = inline_rows * cross_cols
    source = control.reshape(channels, block_len, plane_cells)
    coeffs = filter_coeffs[:, :, None, :]

    def to_blocks(field):
        return field[:, None]

    def from_blocks(field):
        return field[:, 0]

    def scaled(field, factor):
        return factor[..., None] * field

    def prefix(maps, upward):
        start = (
            jnp.broadcast_to(jnp.eye(4, dtype=jnp.float32), maps[0].shape),
            jnp.zeros_like(maps[1]),
        )
        return entering(maps, "depth", compose, start, upward)[1]

    scaling = 1.0 - jnp.sum(coeffs, axis=0)
    root_scale = jnp.sqrt(scaling)
    filtered = sweep_blocks(scaled(to_blocks(source), root_scale), coeffs, False, False, prefix)
    smoothed = sweep_blocks(scaled(filtered, scaling), coeffs, False, True, prefix)
    smoothed_field = from_blocks(smoothed).reshape(control.shape)
    weights = mixing(conv_kernels, channel_order)
    smoothed_padded = extended_2(smoothed_field, (("inline", 2),), 2)
    potential = padded_conv(smoothed_padded, weights)
    flat_field = potential.reshape(channels, -1)
    depth_base = lax.axis_index("depth") * block_len
    inline_base = lax.axis_index("inline") * inline_rows
    cells = point_cells.reshape(3, -1)
    flat_index = (
        (cells[0] - depth_base) * inline_rows + cells[1] - inline_base
    ) * cross_cols + cells[2]
    misfit = (
        flat_field[:, flat_index] - point_values.reshape(channels, -1)
    ) * point_weights.reshape(-1)[None, :]
    ocells = orient_cells.reshape(3, -1)
    base_cell = (
        (ocells[0] - depth_base) * inline_rows + ocells[1] - inline_base
    ) * cross_cols + ocells[2]
    normals = orient_normals.reshape(3, channels, -1)
    oweight = orient_weights.reshape(-1)[None, :]
    update_values = [misfit]
    update_cells = [flat_index]
    for component, stride in enumerate((plane_cells, cross_cols, 1)):
        mismatch = flat_field[:, base_cell + stride] - flat_field[:, base_cell] - normals[component]
        weighted = mismatch * oweight
        update_values.append(weighted)
        update_cells.append(base_cell + stride)
        update_values.append(-weighted)
        update_cells.append(base_cell)
    all_values = jnp.concatenate(update_values, axis=1)
    all_cells = jnp.concatenate(update_cells, axis=0)
    adjoint_weights = jnp.transpose(weights, (1, 0, 2, 3))[:, :, ::-1, ::-1]
    forcing = jnp.zeros_like(flat_field).at[:, all_cells].add(all_values)
    forcing_padded = extended_2(forcing.reshape(control.shape), (("inline", 2),), 2)
    spread = padded_conv(forcing_padded, adjoint_weights).reshape(channels, block_len, plane_cells)
    adjoint_back = scaled(sweep_blocks(to_blocks(spread), coeffs, True, False, prefix), scaling)
    adjoint_fore = scaled(sweep_blocks(adjoint_back, coeffs, True, True, prefix), root_scale)
    gradient = control + from_blocks(adjoint_fore).reshape(control.shape)
    return (potential, gradient)


CHUNK = 96
CHIPS = (0, 3, 2, 1)
AT_VALUES, AT_NORMALS, AT_COEFFS, AT_MISC = 64, 72, 84, 88


def f32(*shape):
    return jax.ShapeDtypeStruct(shape, jnp.float32)


def lane_index(shape):
    return lax.broadcasted_iota(jnp.int32, shape, len(shape) - 1)


def place_points(target, channels, values, normals, misc, by_channel):
    target[AT_MISC:CHUNK, :] = misc
    for c, channel in enumerate(channels):
        row = AT_VALUES + 2 * c
        target[row : row + 2, :] = values[pl.ds(channel * 2, 2), :]
        for k in range(3):
            row = AT_NORMALS + 4 * k + c
            target[row : row + 1, :] = normals[pl.ds(k * 32 + channel, 1), :]
        row = AT_COEFFS + c
        target[row : row + 1, :] = by_channel[pl.ds(channel, 1), :]


def place_control(target, channels, control):
    for c, channel in enumerate(channels):
        plane = control[channel]
        for z in range(4):
            row = z * 16 + c * 4
            target[row : row + 4, :] = plane[z * 4 : z * 4 + 4]


def pack_kernel(*refs):
    sources, give, misc, by_channel, number = refs[:9], refs[9], refs[10], refs[11], refs[12]
    control, values, normals, order, coeffs, cells, weights, ocells, oweights, arrived = refs[13:]
    held = (order, number, coeffs, cells, weights, ocells, oweights, values, normals)
    copies = [
        pltpu.make_async_copy(source, target, arrived.at[k])
        for k, (source, target) in enumerate(zip(sources[:1] + sources, held + (control,)))
    ]
    for copy in copies:
        copy.start()

    def flat_cell(ref):
        z, y, x = (ref[k, 0] for k in range(3))
        return (((y & 3) * 4 + (z & 3)) * 128 + x).astype(jnp.float32)

    for copy in copies[:-1]:
        copy.wait()
    flat, oflat = flat_cell(cells), flat_cell(ocells)
    weight = weights[0]
    misc[...] = jnp.concatenate(
        [flat[:, :128], flat[:, 128:], oflat, weight[:, :128], weight[:, 128:], oweights[0]]
        + [jnp.zeros((2, 128), jnp.float32)],
        axis=0,
    )
    by_channel[:, :16] = jnp.transpose(
        jnp.concatenate([coeffs[...], jnp.zeros((16, 96), jnp.float32)], axis=1)
    )
    by_channel[:, 16:] = jnp.zeros((128, 112), jnp.float32)
    me = lax.axis_index("depth")
    places = [
        (give.at[k], [order[(me ^ (2 * k + 1)) * 4 + c] for c in range(4)]) for k in range(4)
    ]
    for target, channels in places:
        place_points(target, channels, values, normals, misc[...], by_channel)
    copies[-1].wait()
    for target, channels in places:
        place_control(target, channels, control)


def keep_kernel(misc, by_channel, number, control, values, normals, *refs):
    keep, order, arrived = refs[:4], refs[4], refs[5]
    numbers = pltpu.make_async_copy(number, order, arrived)
    numbers.start()
    numbers.wait()
    me = lax.axis_index("depth")
    for k in range(4):
        channels = [order[(me ^ (2 * k)) * 4 + c] for c in range(4)]
        place_points(keep[k], channels, values, normals, misc[...], by_channel)
        place_control(keep[k], channels, control)


def join_kernel(got, *refs):
    keep, joined = refs[:4], refs[4:]
    for k in range(4):
        joined[k][0] = keep[k][...]
        joined[k][1] = got[k]


def coefficient(expanded, lag, z):
    block, local = divmod(z, 4)
    k = (lag - 1) * 4 + local
    return jnp.broadcast_to(expanded[block, :, k : k + 1], (16, 128))


def repeat_coeffs(chunks, expanded):
    for block in range(8):
        for c in range(4):
            row = AT_COEFFS + c
            expanded[block, 4 * c : 4 * c + 4, :] = jnp.broadcast_to(
                chunks[block, row : row + 1, :], (4, 128)
            )


def recurrence(source, factor, emit, order):
    history = []
    for t in order:
        total = source(t)
        for lag in range(len(history), 0, -1):
            before, value = history[lag - 1]
            total = total + factor(lag, t, before) * value
        history = [(t, total)] + history[:3]
        emit(t, total)


def depth_rows(chunks, z):
    return chunks[z // 4, (z % 4) * 16 : (z % 4) * 16 + 16, :]


def smooth_kernel(*refs):
    parts, refs = refs[:4], refs[4:]
    chunks, smoothed, even, odd, table, scale, root, expanded, first, rows = refs
    me = lax.axis_index("depth")
    for k, part in zip(CHIPS, parts):
        for half in range(2):
            chunks[me ^ (2 * k + half)] = part[half]
    repeat_coeffs(chunks, expanded)
    lags = {}

    def start(z):
        lags.clear()
        lags.update({lag: coefficient(expanded, lag, z) for lag in range(1, 5)})
        for lag in range(1, 5):
            table[z, lag - 1] = lags[lag]
        lags[0] = 1.0 - ((lags[1] + lags[2]) + (lags[3] + lags[4]))
        scale[z] = lags[0]
        lags[-1] = jnp.sqrt(lags[0])
        root[z] = lags[-1]
        return lags[-1] * depth_rows(chunks, z)

    def keep_first(z, value):
        first[z] = lags[0] * value

    def keep_rows(z, value):
        rows[z * 16 : z * 16 + 16, :] = value

    recurrence(start, lambda lag, z, before: lags[lag], keep_first, range(32))
    recurrence(
        lambda z: first[z],
        lambda lag, z, before: table[z, lag - 1],
        keep_rows,
        range(31, -1, -1),
    )
    parity = lax.axis_index("inline") % 2
    for y in range(4):
        for c in range(4):
            smoothed[y, c] = rows[pl.ds(c * 4 + y, 32, stride=16), :]
    for y in range(2):
        even[y] = smoothed[2 - 2 * parity + y]
        odd[y] = smoothed[2 * parity + y]


def tap(table, a, b, h, w):
    row = ((a * 5 + h) * 5 + w) * 4 + b
    return jnp.broadcast_to(table[row : row + 1, :], (8, 128))


def conv_rows(read, rows_in, start, table, adjoint, write):
    lane = lane_index((8, 128))

    def moved(value, shift):
        if shift == 0:
            return value
        inside = lane >= -shift if shift < 0 else lane < 128 - shift
        return jnp.where(inside, pltpu.roll(value, -shift % 128, 1), 0.0)

    def some_depths(k, carry):
        pieces = [pl.ds(pl.multiple_of(k * 16 + 8 * n, 8), 8) for n in range(2)]
        total = [[[start(y, o, at) for at in pieces] for o in range(4)] for y in range(4)]
        for i in range(4):
            lines = {row: [read(row, i, at) for at in pieces] for row in rows_in}
            for w in range(5):
                shift = 2 - w if adjoint else w - 2
                shifted_lines = {
                    row: [moved(value, shift) for value in lines[row]] for row in rows_in
                }
                for h in range(5):
                    rows = [y - h + 2 if adjoint else y + h - 2 for y in range(4)]
                    for o in range(4):
                        weight = tap(table, i, o, h, w) if adjoint else tap(table, o, i, h, w)
                        for y, row in enumerate(rows):
                            if row in rows_in:
                                for n in range(2):
                                    line = shifted_lines[row][n]
                                    total[y][o][n] = total[y][o][n] + weight * line
        for y in range(4):
            for o in range(4):
                for n in range(2):
                    write(y, o, pieces[n], total[y][o][n])
        return carry

    lax.fori_loop(0, 2, some_depths, 0)


OWN = (0, 1, 2, 3)
HALO = (-2, -1, 4, 5)


def halo_reader(even, odd):
    slab, last = lax.axis_index("inline"), lax.axis_size("inline") - 1
    parity = slab % 2

    def read(row, c, depths):
        y = row + 2 if row < 0 else row - 4
        through_even, through_odd = even[y, c, depths, :], odd[y, c, depths, :]
        below = parity == 1 if row < 0 else parity == 0
        outside = slab == 0 if row < 0 else slab == last
        return jnp.where(outside, 0.0, jnp.where(below, through_even, through_odd))

    return read


def split(value):
    high = value.astype(jnp.bfloat16)
    return high, (value - high.astype(jnp.float32)).astype(jnp.bfloat16)


def point_fields(chunks, constant, weight, oweight):
    row = lax.broadcasted_iota(jnp.int32, (16, 256), 0)
    orow = lax.broadcasted_iota(jnp.int32, (16, 128), 0)
    column = lax.broadcasted_iota(jnp.int32, (128, 384), 0)
    for block in range(8):

        def line(k, block=block):
            return chunks[block, k : k + 1, :]

        def double(k, line=line):
            return jnp.concatenate([line(k), line(k + 1)], axis=1)

        flat = double(AT_MISC).astype(jnp.int32)
        oflat = line(AT_MISC + 2).astype(jnp.int32)
        w, ow = double(AT_MISC + 3), line(AT_MISC + 5)
        cell, ocell = flat >> 7, oflat >> 7
        at_cross = jnp.concatenate([flat & 127, oflat & 127], axis=1)
        columns = (column == at_cross).astype(jnp.float32).astype(jnp.bfloat16)
        here, ohere = row == cell, orow == ocell
        below, beside = orow == ocell + 1, orow == ocell + 4
        main, along = [], []
        for c in range(4):
            value = w * double(AT_VALUES + 2 * c)
            n0, n1, n2 = (ow * line(AT_NORMALS + 4 * k + c) for k in range(3))
            placed = (
                jnp.where(below, n0, 0.0)
                + jnp.where(beside, n1, 0.0)
                - jnp.where(ohere, n0 + n1 + n2, 0.0)
            )
            main.append(jnp.concatenate([jnp.where(here, value, 0.0), placed], axis=1))
            along.append(
                jnp.concatenate([jnp.zeros((16, 256), jnp.float32), jnp.where(ohere, n2, 0.0)], axis=1)
            )
        both = [
            jnp.concatenate([jnp.where(here, w, 0.0), jnp.zeros((16, 128), jnp.float32)], axis=1),
            jnp.concatenate([jnp.zeros((16, 256), jnp.float32), jnp.where(ohere, ow, 0.0)], axis=1),
        ]
        high, low = split(jnp.concatenate(main + both + along, axis=0))
        sums = lax.dot_general(
            jnp.concatenate([high, low], axis=0),
            columns,
            (((1,), (1,)), ((), ())),
            preferred_element_type=jnp.float32,
        )
        sums = sums[:160] + sums[160:]
        moved = pltpu.roll(sums[96:160], 1, 1)
        z = 4 * block
        for y in range(4):
            for c in range(4):
                k = 16 * c + 4 * y
                constant[y, c, z : z + 4, :] = sums[k : k + 4] + moved[k : k + 4]
            weight[y, z : z + 4, :] = sums[64 + 4 * y : 68 + 4 * y]
            oweight[y, z : z + 4, :] = sums[80 + 4 * y : 84 + 4 * y]


def own_kernel(chunks, smoothed, kernels, partial, constant, weight, oweight, table):
    group = lax.axis_index("depth")
    picked = jnp.where(lane_index((400, 8)) == group, kernels[...], 0.0)
    table[...] = jnp.broadcast_to(jnp.sum(picked, axis=1, keepdims=True), (400, 128))
    point_fields(chunks, constant, weight, oweight)

    def write(y, o, depths, value):
        partial[y, o, depths, :] = value

    conv_rows(
        lambda row, c, depths: smoothed[row, c, depths, :],
        OWN,
        lambda y, o, depths: jnp.zeros((8, 128), jnp.float32),
        table,
        False,
        write,
    )


def fold_rows(came, through, partial, table, out):
    slab, last = lax.axis_index("inline"), lax.axis_size("inline") - 1

    def fold(rows, outside):
        def read(row, c, depths):
            line = came[row + 2 if row < 0 else row - 4, c, depths, :]
            return jnp.where(outside, 0.0, line)

        def write(y, o, depths, value):
            out[y, o, depths, :] = value

        conv_rows(
            read, rows, lambda y, o, depths: partial[y, o, depths, :], table, False, write
        )

    @pl.when(slab % 2 == through)
    def _():
        fold(HALO[2:], slab == last)

    @pl.when(slab % 2 != through)
    def _():
        fold(HALO[:2], slab == 0)


def even_kernel(partial, even_in, table, out):
    fold_rows(even_in, 0, partial, table, out)


def forcing_kernel(
    partial, odd_in, table, constant, weight, oweight, potential, forcing, even, odd
):
    fold_rows(odd_in, 1, partial, table, potential)
    parity = lax.axis_index("inline") % 2

    def some_depths(k, carry):
        depths = pl.ds(pl.multiple_of(k * 8, 8), 8)
        shares = [oweight[y, depths, :] for y in range(4)]
        weights = [weight[y, depths, :] for y in range(4)]
        for c in range(4):
            lines = [potential[y, c, depths, :] for y in range(4)]
            sums = [weights[y] * lines[y] - constant[y, c, depths, :] for y in range(4)]
            for y in range(4):
                deeper = shares[y] * (pltpu.roll(lines[y], 7, 0) - lines[y])
                across = shares[y] * (pltpu.roll(lines[y], 127, 1) - lines[y])
                sums[y] = sums[y] - deeper + pltpu.roll(deeper, 1, 0)
                sums[y] = sums[y] - across + pltpu.roll(across, 1, 1)
                if y < 3:
                    beside = shares[y] * (lines[y + 1] - lines[y])
                    sums[y] = sums[y] - beside
                    sums[y + 1] = sums[y + 1] + beside
            for y in range(4):
                forcing[y, c, depths, :] = sums[y]
            for y in range(2):
                even[y, c, depths, :] = jnp.where(parity == 0, sums[2 + y], sums[y])
                odd[y, c, depths, :] = jnp.where(parity == 0, sums[y], sums[2 + y])
        return carry

    lax.fori_loop(0, 4, some_depths, 0)


def spread_kernel(forcing, table, potential, partial, out, rows):
    def write(y, o, depths, value):
        partial[y, o, depths, :] = value

    conv_rows(
        lambda row, c, depths: forcing[row, c, depths, :],
        OWN,
        lambda y, o, depths: jnp.zeros((8, 128), jnp.float32),
        table,
        True,
        write,
    )
    for y in range(4):
        for c in range(4):
            rows[pl.ds((c * 4 + y) * 32, 32), :] = potential[y, c]
    for z in range(32):
        out[z // 4, (z % 4) * 16 : (z % 4) * 16 + 16, :] = rows[pl.ds(z, 16, stride=32), :]


def gradient_kernel(*refs):
    chunks, partial, even_in, odd_in, taps, table, scale, root, potential = refs[:9]
    give, keep, (first, rows, out) = refs[9], refs[10:14], refs[14:]
    me = lax.axis_index("depth")
    targets = [
        give.at[place // 2] if place % 2 else keep[place // 2] for place in range(8)
    ]
    for place, target in enumerate(targets):
        target[:64, :] = potential[me ^ place]

    def write(y, o, depths, value):
        rows[pl.ds(pl.multiple_of((o * 4 + y) * 32 + depths.start, 8), 8), :] = value

    conv_rows(
        halo_reader(even_in, odd_in),
        HALO,
        lambda y, o, depths: partial[y, o, depths, :],
        taps,
        True,
        write,
    )

    def keep_first(z, value):
        first[z] = scale[z] * value

    def keep_out(z, value):
        row = (z % 4) * 16
        out[z // 4, row : row + 16, :] = depth_rows(chunks, z) + root[z] * value

    recurrence(
        lambda z: rows[pl.ds(z, 16, stride=32), :],
        lambda lag, z, before: table[before, lag - 1],
        keep_first,
        range(32),
    )
    recurrence(
        lambda z: first[z],
        lambda lag, z, before: table[before, lag - 1],
        keep_out,
        range(31, -1, -1),
    )
    for place, target in enumerate(targets):
        target[64:, :] = out[me ^ place]


def unpack_kernel(chips, number, *refs):
    count = len(chips)
    parts, (potential, gradient, planes, sent) = refs[:count], refs[-4:]
    me = lax.axis_index("depth")
    order = number[...].reshape(1, 32)
    lane = lane_index((1, 32))
    channels = []
    for slot in range(8 * count):
        place = 2 * chips[slot // 8] + slot // 4 % 2
        here = lane == (me ^ place) * 4 + slot % 4
        channels.append(jnp.sum(jnp.where(here, order, 0)))
    for half in range(2):
        for slot in range(8 * count):
            k, source, c = slot // 8, slot // 4 % 2, slot % 4
            rows = [64 * half + z * 16 + c * 4 for z in range(4)]
            pieces = [parts[k][source, row : row + 4, :] for row in rows]
            planes[half, slot] = jnp.concatenate(pieces, axis=0)
    for slot in range(8 * count):
        for half, out in enumerate((potential, gradient)):
            pltpu.make_async_copy(
                planes.at[half, slot], out.at[channels[slot]], sent.at[half]
            ).start()
    for half, out in enumerate((potential, gradient)):
        pltpu.make_async_copy(planes.at[half], out.at[: 8 * count], sent.at[half]).wait()


def swapped(even, odd):
    depths, slabs = lax.axis_size("depth"), lax.axis_size("inline")

    def swap(value, first):
        pairs = []
        for d in range(depths):
            for i in range(slabs):
                other = i + 1 if (i - first) % 2 == 0 else i - 1
                to = (d, other) if 0 <= other < slabs else (d ^ 1, i)
                pairs.append((d * slabs + i, to[0] * slabs + to[1]))
        return lax.ppermute(value, ("depth", "inline"), pairs)

    return swap(even, 0), swap(odd, 1)


def by_group(
    control,
    filter_coeffs,
    conv_kernels,
    channel_order,
    point_cells,
    point_values,
    point_weights,
    orient_cells,
    orient_normals,
    orient_weights,
):
    params = pltpu.CompilerParams(vmem_limit_bytes=48 << 20)
    in_vmem, in_hbm = (pl.BlockSpec(memory_space=space) for space in (pltpu.VMEM, pltpu.HBM))

    def call(kernel, outs, operands, scratch=(), ins=None, to=in_vmem, aliases=None):
        return pl.pallas_call(
            kernel,
            out_shape=outs,
            in_specs=ins or [in_vmem] * len(operands),
            out_specs=jax.tree.map(lambda _: to, outs),
            scratch_shapes=list(scratch),
            input_output_aliases=aliases or {},
            compiler_params=params,
        )(*operands)

    sources = (
        channel_order,
        jnp.transpose(filter_coeffs, (0, 2, 1)).reshape(16, 32),
        point_cells,
        point_weights,
        orient_cells,
        orient_weights,
        point_values.reshape(64, 128),
        orient_normals.reshape(96, 128),
        control.reshape(32, 16, 128),
    )
    sources = tuple(pltpu.with_memory_space_constraint(x, pltpu.HBM) for x in sources)
    held = [pltpu.VMEM(source.shape, source.dtype) for source in sources[1:6]]

    def exchange(rows, give, keep, chips):
        def swap(value, flip):
            return lax.ppermute(value, "depth", [(i, i ^ flip) for i in range(8)])

        both = f32(2, rows, 128)
        joined = call(join_kernel, (both,) * 4, (swap(give, 1), *keep))
        return [joined[k] if k == 0 else swap(joined[k], 2 * k) for k in chips]

    give, *held = call(
        pack_kernel,
        (
            f32(4, CHUNK, 128),
            f32(8, 128),
            f32(128, 128),
            jax.ShapeDtypeStruct((32,), jnp.int32),
            f32(32, 16, 128),
            f32(64, 128),
            f32(96, 128),
        ),
        sources,
        [pltpu.SMEM((32,), jnp.int32), *held, pltpu.SemaphoreType.DMA((10,))],
        [in_hbm] * 9,
    )
    keep = call(
        keep_kernel,
        (f32(CHUNK, 128),) * 4,
        held,
        [pltpu.SMEM((32,), jnp.int32), pltpu.SemaphoreType.DMA],
    )
    number = held[2]
    parts = exchange(CHUNK, give, keep, CHIPS)
    field, edge, plane = f32(4, 4, 32, 128), f32(2, 4, 32, 128), f32(4, 32, 128)
    by_depth = f32(32, 16, 128)
    rows = pltpu.VMEM((512, 128), jnp.float32)
    first = pltpu.VMEM((32, 16, 128), jnp.float32)
    chunks, smoothed, even, odd, table, scale, root = call(
        smooth_kernel,
        (f32(8, CHUNK, 128), field, edge, edge, f32(32, 4, 16, 128), by_depth, by_depth),
        parts,
        [pltpu.VMEM((8, 16, 128), jnp.float32), first, rows],
    )
    even, odd = swapped(even, odd)
    kernels = jnp.transpose(conv_kernels, (1, 3, 4, 2, 0)).reshape(400, 8)
    partial, constant, weight, oweight, taps = call(
        own_kernel, (field, field, plane, plane, f32(400, 128)), (chunks, smoothed, kernels)
    )
    partial = call(even_kernel, field, (partial, even, taps))
    potential, forcing, even, odd = call(
        forcing_kernel,
        (field, field, edge, edge),
        (partial, odd, taps, constant, weight, oweight),
    )
    even, odd = swapped(even, odd)
    partial, potential = call(
        spread_kernel, (field, f32(8, 64, 128)), (forcing, taps, potential), [rows]
    )
    give, *keep = call(
        gradient_kernel,
        (f32(4, 128, 128),) + (f32(128, 128),) * 4,
        (chunks, partial, even, odd, taps, table, scale, root, potential),
        [first, rows, pltpu.VMEM((8, 64, 128), jnp.float32)],
    )
    parts = exchange(128, give, keep, CHIPS)
    outs = ()
    for some in (slice(0, 1), slice(1, 2), slice(2, 4)):
        count = len(CHIPS[some])
        outs = call(
            functools.partial(unpack_kernel, CHIPS[some]),
            (by_depth, by_depth),
            (number, *parts[some], *outs),
            [
                pltpu.VMEM((2, 8 * count, 16, 128), jnp.float32),
                pltpu.SemaphoreType.DMA((2,)),
            ],
            [in_vmem] * (count + 1) + [in_hbm] * len(outs),
            in_hbm,
            {count + 1: 0, count + 2: 1} if outs else None,
        )
    potential, gradient = outs
    return potential.reshape(control.shape), gradient.reshape(control.shape)


def solution(mesh):
    placed = (
        P(None, "depth", "inline", None),
        P(None, None, "depth"),
        P(),
        P(),
        P(None, "depth", "inline", None),
        P(None, "depth", "inline", None),
        P("depth", "inline", None),
        P(None, "depth", "inline", None),
        P(None, None, "depth", "inline", None),
        P("depth", "inline", None),
    )

    def body(control, filter_coeffs, conv_kernels, *rest):
        groups, block = conv_kernels.shape, control.shape
        fits = groups[:3] == (mesh.shape["depth"], 4, 4) and groups[0] == 8
        if fits and block == (32, 4, 4, 128):
            return by_group(control, filter_coeffs, conv_kernels, *rest)
        return shards(control, filter_coeffs, conv_kernels, *rest)

    return jax.shard_map(
        body,
        mesh=mesh,
        in_specs=placed,
        out_specs=(P(None, "depth", "inline", None), P(None, "depth", "inline", None)),
        check_vma=False,
    )
```

```python
import functools

import jax
import jax.numpy as jnp
from jax import lax
from jax.experimental import pallas as pl
from jax.experimental.pallas import tpu as pltpu
from jax.sharding import PartitionSpec as P

HIGHEST = lax.Precision.HIGHEST


def entering(value, axis, join, neutral, backward):
    count, mine = (lax.axis_size(axis), lax.axis_index(axis))
    pieces = jax.tree.map(lambda part: lax.all_gather(part, axis), value)
    if backward:
        pieces = jax.tree.map(lambda part: part[::-1], pieces)
        mine = count - 1 - mine
    so_far = jax.tree.map(
        lambda part, zero: jnp.full_like(part, 0) + jnp.asarray(zero, part.dtype), value, neutral
    )

    def hop(position, so_far):
        longer = join(so_far, jax.tree.map(lambda part: part[position], pieces))
        return jax.tree.map(lambda new, old: jnp.where(position < mine, new, old), longer, so_far)

    return lax.fori_loop(0, count - 1, hop, so_far)


def extended_2(cells, sides, width):
    for axis, dim in sides:
        count = lax.axis_size(axis)
        ends = count - 1
        head = lax.slice_in_dim(cells, 0, width, axis=dim)
        tail = lax.slice_in_dim(cells, cells.shape[dim] - width, cells.shape[dim], axis=dim)
        cells = jnp.concatenate(
            [
                lax.ppermute(tail, axis, [(i, (i + 1) % count) for i in range(ends)]),
                cells,
                lax.ppermute(head, axis, [((i + 1) % count, i) for i in range(ends)]),
            ],
            axis=dim,
        )
    return cells


def mixing(kernels, channel_order):
    groups = kernels.shape[0]
    group_size = kernels.shape[1]
    channels = groups * group_size
    slots = jnp.arange(channels, dtype=jnp.int32)
    chooser = (channel_order[:, None] == slots[None, :]).astype(jnp.float32)
    in_group = (
        slots[:, None] // group_size == jnp.arange(groups, dtype=jnp.int32)[None, :]
    ).astype(jnp.float32)
    in_place = (
        slots[:, None] % group_size == jnp.arange(group_size, dtype=jnp.int32)[None, :]
    ).astype(jnp.float32)
    block_mix = jnp.einsum(
        "sg,sa,tg,tb,gabhw->sthw",
        in_group,
        in_place,
        in_group,
        in_place,
        kernels,
        precision=HIGHEST,
    )
    return jnp.einsum("sc,td,sthw->cdhw", chooser, chooser, block_mix, precision=HIGHEST)


def padded_conv(padded, weights):
    return lax.conv_general_dilated(
        padded,
        weights,
        (1, 1),
        ((0, 0), (2, 2)),
        dimension_numbers=("CNHW", "OIHW", "CNHW"),
        precision=HIGHEST,
    )


def compose(earlier, later):
    first_map, first_shift = earlier
    second_map, second_shift = later
    joined_map = jnp.einsum("cnij,cnjk->cnik", second_map, first_map, precision=HIGHEST)
    joined_shift = (
        jnp.einsum("cnij,cnjk->cnik", second_map, first_shift, precision=HIGHEST) + second_shift
    )
    return (joined_map, joined_shift)


def build_tiles(coeffs, by_column, block_len):
    lead = coeffs.shape[1:3]
    lag_steps = jnp.arange(1, 5, dtype=jnp.int32)[:, None, None]
    if by_column:
        row_ids = jnp.arange(block_len + 4, dtype=jnp.int32)[None, :, None]
        col_ids = jnp.arange(block_len, dtype=jnp.int32)[None, None, :]
        picker = (row_ids == col_ids + lag_steps).astype(jnp.float32)
        extended = jnp.einsum("lcnk,lzk->cnzk", coeffs, picker, precision=HIGHEST)
        lower_tile = extended[:, :, :block_len, :]
        exit_map = extended[:, :, block_len:, :]
        entry_base = (
            jnp.arange(block_len, dtype=jnp.int32)[:, None]
            == jnp.arange(4, dtype=jnp.int32)[None, :]
        ).astype(jnp.float32)
        entry_map = jnp.broadcast_to(entry_base, lead + (block_len, 4))
    else:
        row_ids = jnp.arange(block_len, dtype=jnp.int32)[None, :, None]
        col_ids = jnp.arange(block_len + 4, dtype=jnp.int32)[None, None, :]
        picker = (col_ids == row_ids - lag_steps + 4).astype(jnp.float32)
        extended = jnp.einsum("lcnz,lzk->cnzk", coeffs, picker, precision=HIGHEST)
        lower_tile = extended[:, :, :, 4:]
        entry_map = extended[:, :, :, :4]
        exit_base = (
            jnp.arange(block_len, dtype=jnp.int32)[None, :]
            == jnp.arange(4, dtype=jnp.int32)[:, None] + block_len - 4
        ).astype(jnp.float32)
        exit_map = jnp.broadcast_to(exit_base, lead + (4, block_len))
    return (lower_tile, entry_map, exit_map)


def sweep_blocks(field, coeffs, by_column, upward, prefix):
    if upward:
        field = field[:, ::-1, ::-1]
        coeffs = coeffs[:, :, ::-1, ::-1]
    block_len = coeffs.shape[3]
    lower_tile, entry_map, exit_map = build_tiles(coeffs, by_column, block_len)
    identity_tile = jnp.eye(block_len, dtype=jnp.float32)
    inverse = identity_tile + lower_tile
    power = lower_tile
    power = jnp.einsum("cnij,cnjk->cnik", power, power, precision=HIGHEST)
    inverse = inverse + jnp.einsum("cnij,cnjk->cnik", inverse, power, precision=HIGHEST)
    reach_map = jnp.einsum("cnzk,cnkj->cnzj", inverse, entry_map, precision=HIGHEST)
    carry_map = jnp.einsum("cniz,cnzj->cnij", exit_map, reach_map, precision=HIGHEST)
    local_part = jnp.einsum("cnzk,cnkm->cnzm", inverse, field, precision=HIGHEST)
    carry_out = jnp.einsum("cniz,cnzm->cnim", exit_map, local_part, precision=HIGHEST)
    incoming = prefix((carry_map, carry_out), upward)
    result = local_part + jnp.einsum("cnzj,cnjm->cnzm", reach_map, incoming, precision=HIGHEST)
    if upward:
        result = result[:, ::-1, ::-1]
    return result


def shards(
    control,
    filter_coeffs,
    conv_kernels,
    channel_order,
    point_cells,
    point_values,
    point_weights,
    orient_cells,
    orient_normals,
    orient_weights,
):
    channels, block_len, inline_rows, cross_cols = control.shape
    plane_cells = inline_rows * cross_cols
    source = control.reshape(channels, block_len, plane_cells)
    coeffs = filter_coeffs[:, :, None, :]

    def to_blocks(field):
        return field[:, None]

    def from_blocks(field):
        return field[:, 0]

    def scaled(field, factor):
        return factor[..., None] * field

    def prefix(maps, upward):
        start = (
            jnp.broadcast_to(jnp.eye(4, dtype=jnp.float32), maps[0].shape),
            jnp.zeros_like(maps[1]),
        )
        return entering(maps, "depth", compose, start, upward)[1]

    scaling = 1.0 - jnp.sum(coeffs, axis=0)
    root_scale = jnp.sqrt(scaling)
    filtered = sweep_blocks(scaled(to_blocks(source), root_scale), coeffs, False, False, prefix)
    smoothed = sweep_blocks(scaled(filtered, scaling), coeffs, False, True, prefix)
    smoothed_field = from_blocks(smoothed).reshape(control.shape)
    weights = mixing(conv_kernels, channel_order)
    smoothed_padded = extended_2(smoothed_field, (("inline", 2),), 2)
    potential = padded_conv(smoothed_padded, weights)
    flat_field = potential.reshape(channels, -1)
    depth_base = lax.axis_index("depth") * block_len
    inline_base = lax.axis_index("inline") * inline_rows
    cells = point_cells.reshape(3, -1)
    flat_index = (
        (cells[0] - depth_base) * inline_rows + cells[1] - inline_base
    ) * cross_cols + cells[2]
    misfit = (
        flat_field[:, flat_index] - point_values.reshape(channels, -1)
    ) * point_weights.reshape(-1)[None, :]
    ocells = orient_cells.reshape(3, -1)
    base_cell = (
        (ocells[0] - depth_base) * inline_rows + ocells[1] - inline_base
    ) * cross_cols + ocells[2]
    normals = orient_normals.reshape(3, channels, -1)
    oweight = orient_weights.reshape(-1)[None, :]
    update_values = [misfit]
    update_cells = [flat_index]
    for component, stride in enumerate((plane_cells, cross_cols, 1)):
        mismatch = flat_field[:, base_cell + stride] - flat_field[:, base_cell] - normals[component]
        weighted = mismatch * oweight
        update_values.append(weighted)
        update_cells.append(base_cell + stride)
        update_values.append(-weighted)
        update_cells.append(base_cell)
    all_values = jnp.concatenate(update_values, axis=1)
    all_cells = jnp.concatenate(update_cells, axis=0)
    adjoint_weights = jnp.transpose(weights, (1, 0, 2, 3))[:, :, ::-1, ::-1]
    forcing = jnp.zeros_like(flat_field).at[:, all_cells].add(all_values)
    forcing_padded = extended_2(forcing.reshape(control.shape), (("inline", 2),), 2)
    spread = padded_conv(forcing_padded, adjoint_weights).reshape(channels, block_len, plane_cells)
    adjoint_back = scaled(sweep_blocks(to_blocks(spread), coeffs, True, False, prefix), scaling)
    adjoint_fore = scaled(sweep_blocks(adjoint_back, coeffs, True, True, prefix), root_scale)
    gradient = control + from_blocks(adjoint_fore).reshape(control.shape)
    return (potential, gradient)


CHUNK = 96
CHIPS = (0, 3, 2, 1)
AT_VALUES, AT_NORMALS, AT_COEFFS, AT_MISC = 64, 72, 84, 88


def f32(*shape):
    return jax.ShapeDtypeStruct(shape, jnp.float32)


def lane_index(shape):
    return lax.broadcasted_iota(jnp.int32, shape, len(shape) - 1)


def place_points(target, channels, values, normals, misc, by_channel):
    target[AT_MISC:CHUNK, :] = misc
    for c, channel in enumerate(channels):
        row = AT_VALUES + 2 * c
        target[row : row + 2, :] = values[pl.ds(channel * 2, 2), :]
        for k in range(3):
            row = AT_NORMALS + 4 * k + c
            target[row : row + 1, :] = normals[pl.ds(k * 32 + channel, 1), :]
        row = AT_COEFFS + c
        target[row : row + 1, :] = by_channel[pl.ds(channel, 1), :]


def place_control(target, channels, control):
    for c, channel in enumerate(channels):
        plane = control[channel]
        for z in range(4):
            row = z * 16 + c * 4
            target[row : row + 4, :] = plane[z * 4 : z * 4 + 4]


def pack_kernel(*refs):
    sources, give, misc, by_channel, number = refs[:9], refs[9], refs[10], refs[11], refs[12]
    control, values, normals, order, coeffs, cells, weights, ocells, oweights, arrived = refs[13:]
    held = (order, number, coeffs, cells, weights, ocells, oweights, values, normals)
    copies = [
        pltpu.make_async_copy(source, target, arrived.at[k])
        for k, (source, target) in enumerate(zip(sources[:1] + sources, held + (control,)))
    ]
    for copy in copies:
        copy.start()

    def flat_cell(ref):
        z, y, x = (ref[k, 0] for k in range(3))
        return (((y & 3) * 4 + (z & 3)) * 128 + x).astype(jnp.float32)

    for copy in copies[:-1]:
        copy.wait()
    flat, oflat = flat_cell(cells), flat_cell(ocells)
    weight = weights[0]
    misc[...] = jnp.concatenate(
        [flat[:, :128], flat[:, 128:], oflat, weight[:, :128], weight[:, 128:], oweights[0]]
        + [jnp.zeros((2, 128), jnp.float32)],
        axis=0,
    )
    by_channel[:, :16] = jnp.transpose(
        jnp.concatenate([coeffs[...], jnp.zeros((16, 96), jnp.float32)], axis=1)
    )
    by_channel[:, 16:] = jnp.zeros((128, 112), jnp.float32)
    me = lax.axis_index("depth")
    places = [
        (give.at[k], [order[(me ^ (2 * k + 1)) * 4 + c] for c in range(4)]) for k in range(4)
    ]
    for target, channels in places:
        place_points(target, channels, values, normals, misc[...], by_channel)
    copies[-1].wait()
    for target, channels in places:
        place_control(target, channels, control)


def keep_kernel(misc, by_channel, number, control, values, normals, *refs):
    keep, order, arrived = refs[:4], refs[4], refs[5]
    numbers = pltpu.make_async_copy(number, order, arrived)
    numbers.start()
    numbers.wait()
    me = lax.axis_index("depth")
    for k in range(4):
        channels = [order[(me ^ (2 * k)) * 4 + c] for c in range(4)]
        place_points(keep[k], channels, values, normals, misc[...], by_channel)
        place_control(keep[k], channels, control)


def join_kernel(got, *refs):
    keep, joined = refs[:4], refs[4:]
    for k in range(4):
        joined[k][0] = keep[k][...]
        joined[k][1] = got[k]


def coefficient(expanded, lag, z):
    block, local = divmod(z, 4)
    k = (lag - 1) * 4 + local
    return jnp.broadcast_to(expanded[block, :, k : k + 1], (16, 128))


def repeat_coeffs(chunks, expanded):
    for block in range(8):
        for c in range(4):
            row = AT_COEFFS + c
            expanded[block, 4 * c : 4 * c + 4, :] = jnp.broadcast_to(
                chunks[block, row : row + 1, :], (4, 128)
            )


def recurrence(source, factor, emit, order):
    history = []
    for t in order:
        total = source(t)
        for lag in range(len(history), 0, -1):
            before, value = history[lag - 1]
            total = total + factor(lag, t, before) * value
        history = [(t, total)] + history[:3]
        emit(t, total)


def depth_rows(chunks, z):
    return chunks[z // 4, (z % 4) * 16 : (z % 4) * 16 + 16, :]


def smooth_kernel(*refs):
    parts, refs = refs[:4], refs[4:]
    chunks, smoothed, even, odd, table, scale, root, expanded, first, rows = refs
    me = lax.axis_index("depth")
    for k, part in zip(CHIPS, parts):
        for half in range(2):
            chunks[me ^ (2 * k + half)] = part[half]
    repeat_coeffs(chunks, expanded)
    lags = {}

    def start(z):
        lags.clear()
        lags.update({lag: coefficient(expanded, lag, z) for lag in range(1, 5)})
        for lag in range(1, 5):
            table[z, lag - 1] = lags[lag]
        lags[0] = 1.0 - ((lags[1] + lags[2]) + (lags[3] + lags[4]))
        scale[z] = lags[0]
        lags[-1] = jnp.sqrt(lags[0])
        root[z] = lags[-1]
        return lags[-1] * depth_rows(chunks, z)

    def keep_first(z, value):
        first[z] = lags[0] * value

    def keep_rows(z, value):
        rows[z * 16 : z * 16 + 16, :] = value

    recurrence(start, lambda lag, z, before: lags[lag], keep_first, range(32))
    recurrence(
        lambda z: first[z],
        lambda lag, z, before: table[z, lag - 1],
        keep_rows,
        range(31, -1, -1),
    )
    parity = lax.axis_index("inline") % 2
    for y in range(4):
        for c in range(4):
            smoothed[y, c] = rows[pl.ds(c * 4 + y, 32, stride=16), :]
    for y in range(2):
        even[y] = smoothed[2 - 2 * parity + y]
        odd[y] = smoothed[2 * parity + y]


def tap(table, a, b, h, w):
    row = ((a * 5 + h) * 5 + w) * 4 + b
    return jnp.broadcast_to(table[row : row + 1, :], (8, 128))


def conv_rows(read, rows_in, start, table, adjoint, write):
    lane = lane_index((8, 128))

    def moved(value, shift):
        if shift == 0:
            return value
        inside = lane >= -shift if shift < 0 else lane < 128 - shift
        return jnp.where(inside, pltpu.roll(value, -shift % 128, 1), 0.0)

    def some_depths(k, carry):
        pieces = [pl.ds(pl.multiple_of(k * 16 + 8 * n, 8), 8) for n in range(2)]
        total = [[[start(y, o, at) for at in pieces] for o in range(4)] for y in range(4)]
        for i in range(4):
            lines = {row: [read(row, i, at) for at in pieces] for row in rows_in}
            for w in range(5):
                shift = 2 - w if adjoint else w - 2
                shifted_lines = {
                    row: [moved(value, shift) for value in lines[row]] for row in rows_in
                }
                for h in range(5):
                    rows = [y - h + 2 if adjoint else y + h - 2 for y in range(4)]
                    for o in range(4):
                        weight = tap(table, i, o, h, w) if adjoint else tap(table, o, i, h, w)
                        for y, row in enumerate(rows):
                            if row in rows_in:
                                for n in range(2):
                                    line = shifted_lines[row][n]
                                    total[y][o][n] = total[y][o][n] + weight * line
        for y in range(4):
            for o in range(4):
                for n in range(2):
                    write(y, o, pieces[n], total[y][o][n])
        return carry

    lax.fori_loop(0, 2, some_depths, 0)


OWN = (0, 1, 2, 3)
HALO = (-2, -1, 4, 5)


def split(value):
    high = value.astype(jnp.bfloat16)
    return high, (value - high.astype(jnp.float32)).astype(jnp.bfloat16)


def point_fields(chunks, constant, weight, oweight):
    row = lax.broadcasted_iota(jnp.int32, (16, 256), 0)
    orow = lax.broadcasted_iota(jnp.int32, (16, 128), 0)
    column = lax.broadcasted_iota(jnp.int32, (128, 384), 0)
    for block in range(8):

        def line(k, block=block):
            return chunks[block, k : k + 1, :]

        def double(k, line=line):
            return jnp.concatenate([line(k), line(k + 1)], axis=1)

        flat = double(AT_MISC).astype(jnp.int32)
        oflat = line(AT_MISC + 2).astype(jnp.int32)
        w, ow = double(AT_MISC + 3), line(AT_MISC + 5)
        cell, ocell = flat >> 7, oflat >> 7
        at_cross = jnp.concatenate([flat & 127, oflat & 127], axis=1)
        columns = (column == at_cross).astype(jnp.float32).astype(jnp.bfloat16)
        here, ohere = row == cell, orow == ocell
        below, beside = orow == ocell + 1, orow == ocell + 4
        main, along = [], []
        for c in range(4):
            value = w * double(AT_VALUES + 2 * c)
            n0, n1, n2 = (ow * line(AT_NORMALS + 4 * k + c) for k in range(3))
            placed = (
                jnp.where(below, n0, 0.0)
                + jnp.where(beside, n1, 0.0)
                - jnp.where(ohere, n0 + n1 + n2, 0.0)
            )
            main.append(jnp.concatenate([jnp.where(here, value, 0.0), placed], axis=1))
            along.append(
                jnp.concatenate([jnp.zeros((16, 256), jnp.float32), jnp.where(ohere, n2, 0.0)], axis=1)
            )
        both = [
            jnp.concatenate([jnp.where(here, w, 0.0), jnp.zeros((16, 128), jnp.float32)], axis=1),
            jnp.concatenate([jnp.zeros((16, 256), jnp.float32), jnp.where(ohere, ow, 0.0)], axis=1),
        ]
        high, low = split(jnp.concatenate(main + both + along, axis=0))
        sums = lax.dot_general(
            jnp.concatenate([high, low], axis=0),
            columns,
            (((1,), (1,)), ((), ())),
            preferred_element_type=jnp.float32,
        )
        sums = sums[:160] + sums[160:]
        moved = pltpu.roll(sums[96:160], 1, 1)
        z = 4 * block
        for y in range(4):
            for c in range(4):
                k = 16 * c + 4 * y
                constant[y, c, z : z + 4, :] = sums[k : k + 4] + moved[k : k + 4]
            weight[y, z : z + 4, :] = sums[64 + 4 * y : 68 + 4 * y]
            oweight[y, z : z + 4, :] = sums[80 + 4 * y : 84 + 4 * y]


def own_kernel(chunks, smoothed, kernels, partial, constant, weight, oweight, table):
    group = lax.axis_index("depth")
    picked = jnp.where(lane_index((400, 8)) == group, kernels[...], 0.0)
    table[...] = jnp.broadcast_to(jnp.sum(picked, axis=1, keepdims=True), (400, 128))
    point_fields(chunks, constant, weight, oweight)

    def write(y, o, depths, value):
        partial[y, o, depths, :] = value

    conv_rows(
        lambda row, c, depths: smoothed[row, c, depths, :],
        OWN,
        lambda y, o, depths: jnp.zeros((8, 128), jnp.float32),
        table,
        False,
        write,
    )


def fold_rows(came, through, partial, table, adjoint, write):
    slab, last = lax.axis_index("inline"), lax.axis_size("inline") - 1

    def fold(rows, outside):
        def read(row, c, depths):
            line = came[row + 2 if row < 0 else row - 4, c, depths, :]
            return jnp.where(outside, 0.0, line)

        conv_rows(
            read, rows, lambda y, o, depths: partial[y, o, depths, :], table, adjoint, write
        )

    @pl.when(slab % 2 == through)
    def _():
        fold(HALO[2:], slab == last)

    @pl.when(slab % 2 != through)
    def _():
        fold(HALO[:2], slab == 0)


def even_kernel(adjoint, partial, even_in, table, out):
    def write(y, o, depths, value):
        out[y, o, depths, :] = value

    fold_rows(even_in, 0, partial, table, adjoint, write)


def forcing_kernel(
    partial, odd_in, table, constant, weight, oweight, potential, forcing, even, odd
):
    def write(y, o, depths, value):
        potential[y, o, depths, :] = value

    fold_rows(odd_in, 1, partial, table, False, write)
    parity = lax.axis_index("inline") % 2

    def some_depths(k, carry):
        depths = pl.ds(pl.multiple_of(k * 8, 8), 8)
        shares = [oweight[y, depths, :] for y in range(4)]
        weights = [weight[y, depths, :] for y in range(4)]
        for c in range(4):
            lines = [potential[y, c, depths, :] for y in range(4)]
            sums = [weights[y] * lines[y] - constant[y, c, depths, :] for y in range(4)]
            for y in range(4):
                deeper = shares[y] * (pltpu.roll(lines[y], 7, 0) - lines[y])
                across = shares[y] * (pltpu.roll(lines[y], 127, 1) - lines[y])
                sums[y] = sums[y] - deeper + pltpu.roll(deeper, 1, 0)
                sums[y] = sums[y] - across + pltpu.roll(across, 1, 1)
                if y < 3:
                    beside = shares[y] * (lines[y + 1] - lines[y])
                    sums[y] = sums[y] - beside
                    sums[y + 1] = sums[y + 1] + beside
            for y in range(4):
                forcing[y, c, depths, :] = sums[y]
            for y in range(2):
                even[y, c, depths, :] = jnp.where(parity == 0, sums[2 + y], sums[y])
                odd[y, c, depths, :] = jnp.where(parity == 0, sums[y], sums[2 + y])
        return carry

    lax.fori_loop(0, 4, some_depths, 0)


def spread_kernel(forcing, table, potential, partial, out, rows):
    def write(y, o, depths, value):
        partial[y, o, depths, :] = value

    conv_rows(
        lambda row, c, depths: forcing[row, c, depths, :],
        OWN,
        lambda y, o, depths: jnp.zeros((8, 128), jnp.float32),
        table,
        True,
        write,
    )
    for y in range(4):
        for c in range(4):
            rows[pl.ds((c * 4 + y) * 32, 32), :] = potential[y, c]
    for z in range(32):
        out[z // 4, (z % 4) * 16 : (z % 4) * 16 + 16, :] = rows[pl.ds(z, 16, stride=32), :]


def gradient_kernel(*refs):
    chunks, partial, odd_in, taps, table, scale, root, potential = refs[:8]
    give, keep, (first, rows, out) = refs[8], refs[9:13], refs[13:]
    me = lax.axis_index("depth")
    targets = [
        give.at[place // 2] if place % 2 else keep[place // 2] for place in range(8)
    ]
    for place, target in enumerate(targets):
        target[:64, :] = potential[me ^ place]

    def write(y, o, depths, value):
        rows[pl.ds(pl.multiple_of((o * 4 + y) * 32 + depths.start, 8), 8), :] = value

    fold_rows(odd_in, 1, partial, taps, True, write)

    def keep_first(z, value):
        first[z] = scale[z] * value

    def keep_out(z, value):
        row = (z % 4) * 16
        out[z // 4, row : row + 16, :] = depth_rows(chunks, z) + root[z] * value

    recurrence(
        lambda z: rows[pl.ds(z, 16, stride=32), :],
        lambda lag, z, before: table[before, lag - 1],
        keep_first,
        range(32),
    )
    recurrence(
        lambda z: first[z],
        lambda lag, z, before: table[before, lag - 1],
        keep_out,
        range(31, -1, -1),
    )
    for place, target in enumerate(targets):
        target[64:, :] = out[me ^ place]


def unpack_kernel(chips, number, *refs):
    count = len(chips)
    parts, (potential, gradient, planes, sent) = refs[:count], refs[-4:]
    me = lax.axis_index("depth")
    order = number[...].reshape(1, 32)
    lane = lane_index((1, 32))
    channels = []
    for slot in range(8 * count):
        place = 2 * chips[slot // 8] + slot // 4 % 2
        here = lane == (me ^ place) * 4 + slot % 4
        channels.append(jnp.sum(jnp.where(here, order, 0)))
    for half in range(2):
        for slot in range(8 * count):
            k, source, c = slot // 8, slot // 4 % 2, slot % 4
            rows = [64 * half + z * 16 + c * 4 for z in range(4)]
            pieces = [parts[k][source, row : row + 4, :] for row in rows]
            planes[half, slot] = jnp.concatenate(pieces, axis=0)
    for slot in range(8 * count):
        for half, out in enumerate((potential, gradient)):
            pltpu.make_async_copy(
                planes.at[half, slot], out.at[channels[slot]], sent.at[half]
            ).start()
    for half, out in enumerate((potential, gradient)):
        pltpu.make_async_copy(planes.at[half], out.at[: 8 * count], sent.at[half]).wait()


def swapped(even, odd):
    depths, slabs = lax.axis_size("depth"), lax.axis_size("inline")

    def swap(value, first):
        pairs = []
        for d in range(depths):
            for i in range(slabs):
                other = i + 1 if (i - first) % 2 == 0 else i - 1
                to = (d, other) if 0 <= other < slabs else (d ^ 1, i)
                pairs.append((d * slabs + i, to[0] * slabs + to[1]))
        return lax.ppermute(value, ("depth", "inline"), pairs)

    return swap(even, 0), swap(odd, 1)


def by_group(
    control,
    filter_coeffs,
    conv_kernels,
    channel_order,
    point_cells,
    point_values,
    point_weights,
    orient_cells,
    orient_normals,
    orient_weights,
):
    params = pltpu.CompilerParams(vmem_limit_bytes=48 << 20)
    in_vmem, in_hbm = (pl.BlockSpec(memory_space=space) for space in (pltpu.VMEM, pltpu.HBM))

    def call(kernel, outs, operands, scratch=(), ins=None, to=in_vmem, aliases=None):
        return pl.pallas_call(
            kernel,
            out_shape=outs,
            in_specs=ins or [in_vmem] * len(operands),
            out_specs=jax.tree.map(lambda _: to, outs),
            scratch_shapes=list(scratch),
            input_output_aliases=aliases or {},
            compiler_params=params,
        )(*operands)

    sources = (
        channel_order,
        jnp.transpose(filter_coeffs, (0, 2, 1)).reshape(16, 32),
        point_cells,
        point_weights,
        orient_cells,
        orient_weights,
        point_values.reshape(64, 128),
        orient_normals.reshape(96, 128),
        control.reshape(32, 16, 128),
    )
    sources = tuple(pltpu.with_memory_space_constraint(x, pltpu.HBM) for x in sources)
    held = [pltpu.VMEM(source.shape, source.dtype) for source in sources[1:6]]

    def exchange(rows, give, keep, chips):
        def swap(value, flip):
            return lax.ppermute(value, "depth", [(i, i ^ flip) for i in range(8)])

        both = f32(2, rows, 128)
        joined = call(join_kernel, (both,) * 4, (swap(give, 1), *keep))
        return [joined[k] if k == 0 else swap(joined[k], 2 * k) for k in chips]

    give, *held = call(
        pack_kernel,
        (
            f32(4, CHUNK, 128),
            f32(8, 128),
            f32(128, 128),
            jax.ShapeDtypeStruct((32,), jnp.int32),
            f32(32, 16, 128),
            f32(64, 128),
            f32(96, 128),
        ),
        sources,
        [pltpu.SMEM((32,), jnp.int32), *held, pltpu.SemaphoreType.DMA((10,))],
        [in_hbm] * 9,
    )
    keep = call(
        keep_kernel,
        (f32(CHUNK, 128),) * 4,
        held,
        [pltpu.SMEM((32,), jnp.int32), pltpu.SemaphoreType.DMA],
    )
    number = held[2]
    parts = exchange(CHUNK, give, keep, CHIPS)
    field, edge, plane = f32(4, 4, 32, 128), f32(2, 4, 32, 128), f32(4, 32, 128)
    by_depth = f32(32, 16, 128)
    rows = pltpu.VMEM((512, 128), jnp.float32)
    first = pltpu.VMEM((32, 16, 128), jnp.float32)
    chunks, smoothed, even, odd, table, scale, root = call(
        smooth_kernel,
        (f32(8, CHUNK, 128), field, edge, edge, f32(32, 4, 16, 128), by_depth, by_depth),
        parts,
        [pltpu.VMEM((8, 16, 128), jnp.float32), first, rows],
    )
    even, odd = swapped(even, odd)
    kernels = jnp.transpose(conv_kernels, (1, 3, 4, 2, 0)).reshape(400, 8)
    partial, constant, weight, oweight, taps = call(
        own_kernel, (field, field, plane, plane, f32(400, 128)), (chunks, smoothed, kernels)
    )
    partial = call(functools.partial(even_kernel, False), field, (partial, even, taps))
    potential, forcing, even, odd = call(
        forcing_kernel,
        (field, field, edge, edge),
        (partial, odd, taps, constant, weight, oweight),
    )
    even, odd = swapped(even, odd)
    partial, potential = call(
        spread_kernel, (field, f32(8, 64, 128)), (forcing, taps, potential), [rows]
    )
    partial = call(functools.partial(even_kernel, True), field, (partial, even, taps))
    give, *keep = call(
        gradient_kernel,
        (f32(4, 128, 128),) + (f32(128, 128),) * 4,
        (chunks, partial, odd, taps, table, scale, root, potential),
        [first, rows, pltpu.VMEM((8, 64, 128), jnp.float32)],
    )
    parts = exchange(128, give, keep, CHIPS)
    outs = ()
    for some in (slice(0, 1), slice(1, 2), slice(2, 4)):
        count = len(CHIPS[some])
        outs = call(
            functools.partial(unpack_kernel, CHIPS[some]),
            (by_depth, by_depth),
            (number, *parts[some], *outs),
            [
                pltpu.VMEM((2, 8 * count, 16, 128), jnp.float32),
                pltpu.SemaphoreType.DMA((2,)),
            ],
            [in_vmem] * (count + 1) + [in_hbm] * len(outs),
            in_hbm,
            {count + 1: 0, count + 2: 1} if outs else None,
        )
    potential, gradient = outs
    return potential.reshape(control.shape), gradient.reshape(control.shape)


def solution(mesh):
    placed = (
        P(None, "depth", "inline", None),
        P(None, None, "depth"),
        P(),
        P(),
        P(None, "depth", "inline", None),
        P(None, "depth", "inline", None),
        P("depth", "inline", None),
        P(None, "depth", "inline", None),
        P(None, None, "depth", "inline", None),
        P("depth", "inline", None),
    )

    def body(control, filter_coeffs, conv_kernels, *rest):
        groups, block = conv_kernels.shape, control.shape
        fits = groups[:3] == (mesh.shape["depth"], 4, 4) and groups[0] == 8
        if fits and block == (32, 4, 4, 128):
            return by_group(control, filter_coeffs, conv_kernels, *rest)
        return shards(control, filter_coeffs, conv_kernels, *rest)

    return jax.shard_map(
        body,
        mesh=mesh,
        in_specs=placed,
        out_specs=(P(None, "depth", "inline", None), P(None, "depth", "inline", None)),
        check_vma=False,
    )
```

```python
import functools

import jax
import jax.numpy as jnp
from jax import lax
from jax.experimental import pallas as pl
from jax.experimental.pallas import tpu as pltpu
from jax.sharding import PartitionSpec as P

HIGHEST = lax.Precision.HIGHEST


def entering(value, axis, join, neutral, backward):
    count, mine = (lax.axis_size(axis), lax.axis_index(axis))
    pieces = jax.tree.map(lambda part: lax.all_gather(part, axis), value)
    if backward:
        pieces = jax.tree.map(lambda part: part[::-1], pieces)
        mine = count - 1 - mine
    so_far = jax.tree.map(
        lambda part, zero: jnp.full_like(part, 0) + jnp.asarray(zero, part.dtype), value, neutral
    )

    def hop(position, so_far):
        longer = join(so_far, jax.tree.map(lambda part: part[position], pieces))
        return jax.tree.map(lambda new, old: jnp.where(position < mine, new, old), longer, so_far)

    return lax.fori_loop(0, count - 1, hop, so_far)


def extended_2(cells, sides, width):
    for axis, dim in sides:
        count = lax.axis_size(axis)
        ends = count - 1
        head = lax.slice_in_dim(cells, 0, width, axis=dim)
        tail = lax.slice_in_dim(cells, cells.shape[dim] - width, cells.shape[dim], axis=dim)
        cells = jnp.concatenate(
            [
                lax.ppermute(tail, axis, [(i, (i + 1) % count) for i in range(ends)]),
                cells,
                lax.ppermute(head, axis, [((i + 1) % count, i) for i in range(ends)]),
            ],
            axis=dim,
        )
    return cells


def mixing(kernels, channel_order):
    groups = kernels.shape[0]
    group_size = kernels.shape[1]
    channels = groups * group_size
    slots = jnp.arange(channels, dtype=jnp.int32)
    chooser = (channel_order[:, None] == slots[None, :]).astype(jnp.float32)
    in_group = (
        slots[:, None] // group_size == jnp.arange(groups, dtype=jnp.int32)[None, :]
    ).astype(jnp.float32)
    in_place = (
        slots[:, None] % group_size == jnp.arange(group_size, dtype=jnp.int32)[None, :]
    ).astype(jnp.float32)
    block_mix = jnp.einsum(
        "sg,sa,tg,tb,gabhw->sthw",
        in_group,
        in_place,
        in_group,
        in_place,
        kernels,
        precision=HIGHEST,
    )
    return jnp.einsum("sc,td,sthw->cdhw", chooser, chooser, block_mix, precision=HIGHEST)


def padded_conv(padded, weights):
    return lax.conv_general_dilated(
        padded,
        weights,
        (1, 1),
        ((0, 0), (2, 2)),
        dimension_numbers=("CNHW", "OIHW", "CNHW"),
        precision=HIGHEST,
    )


def compose(earlier, later):
    first_map, first_shift = earlier
    second_map, second_shift = later
    joined_map = jnp.einsum("cnij,cnjk->cnik", second_map, first_map, precision=HIGHEST)
    joined_shift = (
        jnp.einsum("cnij,cnjk->cnik", second_map, first_shift, precision=HIGHEST) + second_shift
    )
    return (joined_map, joined_shift)


def build_tiles(coeffs, by_column, block_len):
    lead = coeffs.shape[1:3]
    lag_steps = jnp.arange(1, 5, dtype=jnp.int32)[:, None, None]
    if by_column:
        row_ids = jnp.arange(block_len + 4, dtype=jnp.int32)[None, :, None]
        col_ids = jnp.arange(block_len, dtype=jnp.int32)[None, None, :]
        picker = (row_ids == col_ids + lag_steps).astype(jnp.float32)
        extended = jnp.einsum("lcnk,lzk->cnzk", coeffs, picker, precision=HIGHEST)
        lower_tile = extended[:, :, :block_len, :]
        exit_map = extended[:, :, block_len:, :]
        entry_base = (
            jnp.arange(block_len, dtype=jnp.int32)[:, None]
            == jnp.arange(4, dtype=jnp.int32)[None, :]
        ).astype(jnp.float32)
        entry_map = jnp.broadcast_to(entry_base, lead + (block_len, 4))
    else:
        row_ids = jnp.arange(block_len, dtype=jnp.int32)[None, :, None]
        col_ids = jnp.arange(block_len + 4, dtype=jnp.int32)[None, None, :]
        picker = (col_ids == row_ids - lag_steps + 4).astype(jnp.float32)
        extended = jnp.einsum("lcnz,lzk->cnzk", coeffs, picker, precision=HIGHEST)
        lower_tile = extended[:, :, :, 4:]
        entry_map = extended[:, :, :, :4]
        exit_base = (
            jnp.arange(block_len, dtype=jnp.int32)[None, :]
            == jnp.arange(4, dtype=jnp.int32)[:, None] + block_len - 4
        ).astype(jnp.float32)
        exit_map = jnp.broadcast_to(exit_base, lead + (4, block_len))
    return (lower_tile, entry_map, exit_map)


def sweep_blocks(field, coeffs, by_column, upward, prefix):
    if upward:
        field = field[:, ::-1, ::-1]
        coeffs = coeffs[:, :, ::-1, ::-1]
    block_len = coeffs.shape[3]
    lower_tile, entry_map, exit_map = build_tiles(coeffs, by_column, block_len)
    identity_tile = jnp.eye(block_len, dtype=jnp.float32)
    inverse = identity_tile + lower_tile
    power = lower_tile
    power = jnp.einsum("cnij,cnjk->cnik", power, power, precision=HIGHEST)
    inverse = inverse + jnp.einsum("cnij,cnjk->cnik", inverse, power, precision=HIGHEST)
    reach_map = jnp.einsum("cnzk,cnkj->cnzj", inverse, entry_map, precision=HIGHEST)
    carry_map = jnp.einsum("cniz,cnzj->cnij", exit_map, reach_map, precision=HIGHEST)
    local_part = jnp.einsum("cnzk,cnkm->cnzm", inverse, field, precision=HIGHEST)
    carry_out = jnp.einsum("cniz,cnzm->cnim", exit_map, local_part, precision=HIGHEST)
    incoming = prefix((carry_map, carry_out), upward)
    result = local_part + jnp.einsum("cnzj,cnjm->cnzm", reach_map, incoming, precision=HIGHEST)
    if upward:
        result = result[:, ::-1, ::-1]
    return result


def shards(
    control,
    filter_coeffs,
    conv_kernels,
    channel_order,
    point_cells,
    point_values,
    point_weights,
    orient_cells,
    orient_normals,
    orient_weights,
):
    channels, block_len, inline_rows, cross_cols = control.shape
    plane_cells = inline_rows * cross_cols
    source = control.reshape(channels, block_len, plane_cells)
    coeffs = filter_coeffs[:, :, None, :]

    def to_blocks(field):
        return field[:, None]

    def from_blocks(field):
        return field[:, 0]

    def scaled(field, factor):
        return factor[..., None] * field

    def prefix(maps, upward):
        start = (
            jnp.broadcast_to(jnp.eye(4, dtype=jnp.float32), maps[0].shape),
            jnp.zeros_like(maps[1]),
        )
        return entering(maps, "depth", compose, start, upward)[1]

    scaling = 1.0 - jnp.sum(coeffs, axis=0)
    root_scale = jnp.sqrt(scaling)
    filtered = sweep_blocks(scaled(to_blocks(source), root_scale), coeffs, False, False, prefix)
    smoothed = sweep_blocks(scaled(filtered, scaling), coeffs, False, True, prefix)
    smoothed_field = from_blocks(smoothed).reshape(control.shape)
    weights = mixing(conv_kernels, channel_order)
    smoothed_padded = extended_2(smoothed_field, (("inline", 2),), 2)
    potential = padded_conv(smoothed_padded, weights)
    flat_field = potential.reshape(channels, -1)
    depth_base = lax.axis_index("depth") * block_len
    inline_base = lax.axis_index("inline") * inline_rows
    cells = point_cells.reshape(3, -1)
    flat_index = (
        (cells[0] - depth_base) * inline_rows + cells[1] - inline_base
    ) * cross_cols + cells[2]
    misfit = (
        flat_field[:, flat_index] - point_values.reshape(channels, -1)
    ) * point_weights.reshape(-1)[None, :]
    ocells = orient_cells.reshape(3, -1)
    base_cell = (
        (ocells[0] - depth_base) * inline_rows + ocells[1] - inline_base
    ) * cross_cols + ocells[2]
    normals = orient_normals.reshape(3, channels, -1)
    oweight = orient_weights.reshape(-1)[None, :]
    update_values = [misfit]
    update_cells = [flat_index]
    for component, stride in enumerate((plane_cells, cross_cols, 1)):
        mismatch = flat_field[:, base_cell + stride] - flat_field[:, base_cell] - normals[component]
        weighted = mismatch * oweight
        update_values.append(weighted)
        update_cells.append(base_cell + stride)
        update_values.append(-weighted)
        update_cells.append(base_cell)
    all_values = jnp.concatenate(update_values, axis=1)
    all_cells = jnp.concatenate(update_cells, axis=0)
    adjoint_weights = jnp.transpose(weights, (1, 0, 2, 3))[:, :, ::-1, ::-1]
    forcing = jnp.zeros_like(flat_field).at[:, all_cells].add(all_values)
    forcing_padded = extended_2(forcing.reshape(control.shape), (("inline", 2),), 2)
    spread = padded_conv(forcing_padded, adjoint_weights).reshape(channels, block_len, plane_cells)
    adjoint_back = scaled(sweep_blocks(to_blocks(spread), coeffs, True, False, prefix), scaling)
    adjoint_fore = scaled(sweep_blocks(adjoint_back, coeffs, True, True, prefix), root_scale)
    gradient = control + from_blocks(adjoint_fore).reshape(control.shape)
    return (potential, gradient)


CHUNK = 96
CHIPS = (0, 3, 2, 1)
AT_VALUES, AT_NORMALS, AT_COEFFS, AT_MISC = 64, 72, 84, 88


def f32(*shape):
    return jax.ShapeDtypeStruct(shape, jnp.float32)


def lane_index(shape):
    return lax.broadcasted_iota(jnp.int32, shape, len(shape) - 1)


def place_points(target, channels, values, normals, misc, by_channel):
    target[AT_MISC:CHUNK, :] = misc
    for c, channel in enumerate(channels):
        row = AT_VALUES + 2 * c
        target[row : row + 2, :] = values[pl.ds(channel * 2, 2), :]
        for k in range(3):
            row = AT_NORMALS + 4 * k + c
            target[row : row + 1, :] = normals[pl.ds(k * 32 + channel, 1), :]
        row = AT_COEFFS + c
        target[row : row + 1, :] = by_channel[pl.ds(channel, 1), :]


def place_control(target, channels, control):
    for c, channel in enumerate(channels):
        plane = control[channel]
        for z in range(4):
            row = z * 16 + c * 4
            target[row : row + 4, :] = plane[z * 4 : z * 4 + 4]


def pack_kernel(*refs):
    sources, give, misc, by_channel, number = refs[:9], refs[9], refs[10], refs[11], refs[12]
    control, values, normals, order, coeffs, cells, weights, ocells, oweights, arrived = refs[13:]
    held = (order, number, coeffs, cells, weights, ocells, oweights, values, normals)
    copies = [
        pltpu.make_async_copy(source, target, arrived.at[k])
        for k, (source, target) in enumerate(zip(sources[:1] + sources, held + (control,)))
    ]
    for copy in copies:
        copy.start()

    def flat_cell(ref):
        z, y, x = (ref[k, 0] for k in range(3))
        return (((y & 3) * 4 + (z & 3)) * 128 + x).astype(jnp.float32)

    for copy in copies[:-1]:
        copy.wait()
    flat, oflat = flat_cell(cells), flat_cell(ocells)
    weight = weights[0]
    misc[...] = jnp.concatenate(
        [flat[:, :128], flat[:, 128:], oflat, weight[:, :128], weight[:, 128:], oweights[0]]
        + [jnp.zeros((2, 128), jnp.float32)],
        axis=0,
    )
    by_channel[:, :16] = jnp.transpose(
        jnp.concatenate([coeffs[...], jnp.zeros((16, 96), jnp.float32)], axis=1)
    )
    by_channel[:, 16:] = jnp.zeros((128, 112), jnp.float32)
    me = lax.axis_index("depth")
    places = [
        (give.at[k], [order[(me ^ (2 * k + 1)) * 4 + c] for c in range(4)]) for k in range(4)
    ]
    for target, channels in places:
        place_points(target, channels, values, normals, misc[...], by_channel)
    copies[-1].wait()
    for target, channels in places:
        place_control(target, channels, control)


def keep_kernel(misc, by_channel, number, control, values, normals, *refs):
    keep, order, arrived = refs[:4], refs[4], refs[5]
    numbers = pltpu.make_async_copy(number, order, arrived)
    numbers.start()
    numbers.wait()
    me = lax.axis_index("depth")
    for k in range(4):
        channels = [order[(me ^ (2 * k)) * 4 + c] for c in range(4)]
        place_points(keep[k], channels, values, normals, misc[...], by_channel)
        place_control(keep[k], channels, control)


def join_kernel(got, *refs):
    keep, joined = refs[:4], refs[4:]
    for k in range(4):
        joined[k][0] = keep[k][...]
        joined[k][1] = got[k]


def coefficient(expanded, lag, z):
    block, local = divmod(z, 4)
    k = (lag - 1) * 4 + local
    return jnp.broadcast_to(expanded[block, :, k : k + 1], (16, 128))


def repeat_coeffs(chunks, expanded):
    for block in range(8):
        for c in range(4):
            row = AT_COEFFS + c
            expanded[block, 4 * c : 4 * c + 4, :] = jnp.broadcast_to(
                chunks[block, row : row + 1, :], (4, 128)
            )


def recurrence(source, factor, emit, order):
    history = []
    for t in order:
        total = source(t)
        for lag in range(len(history), 0, -1):
            before, value = history[lag - 1]
            total = total + factor(lag, t, before) * value
        history = [(t, total)] + history[:3]
        emit(t, total)


def depth_rows(chunks, z):
    return chunks[z // 4, (z % 4) * 16 : (z % 4) * 16 + 16, :]


def smooth_kernel(*refs):
    parts, refs = refs[:4], refs[4:]
    chunks, smoothed, even, odd, table, scale, root, expanded, first, rows = refs
    me = lax.axis_index("depth")
    for k, part in zip(CHIPS, parts):
        for half in range(2):
            chunks[me ^ (2 * k + half)] = part[half]
    repeat_coeffs(chunks, expanded)
    lags = {}

    def start(z):
        lags.clear()
        lags.update({lag: coefficient(expanded, lag, z) for lag in range(1, 5)})
        for lag in range(1, 5):
            table[z, lag - 1] = lags[lag]
        lags[0] = 1.0 - ((lags[1] + lags[2]) + (lags[3] + lags[4]))
        scale[z] = lags[0]
        lags[-1] = jnp.sqrt(lags[0])
        root[z] = lags[-1]
        return lags[-1] * depth_rows(chunks, z)

    def keep_first(z, value):
        first[z] = lags[0] * value

    def keep_rows(z, value):
        rows[z * 16 : z * 16 + 16, :] = value

    recurrence(start, lambda lag, z, before: lags[lag], keep_first, range(32))
    recurrence(
        lambda z: first[z],
        lambda lag, z, before: table[z, lag - 1],
        keep_rows,
        range(31, -1, -1),
    )
    parity = lax.axis_index("inline") % 2
    for y in range(4):
        for c in range(4):
            smoothed[y, c] = rows[pl.ds(c * 4 + y, 32, stride=16), :]
    for y in range(2):
        even[y] = smoothed[2 - 2 * parity + y]
        odd[y] = smoothed[2 * parity + y]


def tap(table, a, b, h, w):
    row = ((a * 5 + h) * 5 + w) * 4 + b
    return jnp.broadcast_to(table[row : row + 1, :], (8, 128))


def conv_rows(read, rows_in, start, table, adjoint, write):
    lane = lane_index((8, 128))

    def moved(value, shift):
        if shift == 0:
            return value
        inside = lane >= -shift if shift < 0 else lane < 128 - shift
        return jnp.where(inside, pltpu.roll(value, -shift % 128, 1), 0.0)

    def some_depths(k, carry):
        pieces = [pl.ds(pl.multiple_of(k * 16 + 8 * n, 8), 8) for n in range(2)]
        total = [[[start(y, o, at) for at in pieces] for o in range(4)] for y in range(4)]
        for i in range(4):
            lines = {row: [read(row, i, at) for at in pieces] for row in rows_in}
            for w in range(5):
                shift = 2 - w if adjoint else w - 2
                shifted_lines = {
                    row: [moved(value, shift) for value in lines[row]] for row in rows_in
                }
                for h in range(5):
                    rows = [y - h + 2 if adjoint else y + h - 2 for y in range(4)]
                    for o in range(4):
                        weight = tap(table, i, o, h, w) if adjoint else tap(table, o, i, h, w)
                        for y, row in enumerate(rows):
                            if row in rows_in:
                                for n in range(2):
                                    line = shifted_lines[row][n]
                                    total[y][o][n] = total[y][o][n] + weight * line
        for y in range(4):
            for o in range(4):
                for n in range(2):
                    write(y, o, pieces[n], total[y][o][n])
        return carry

    lax.fori_loop(0, 2, some_depths, 0)


OWN = (0, 1, 2, 3)
HALO = (-2, -1, 4, 5)


def split(value):
    high = value.astype(jnp.bfloat16)
    return high, (value - high.astype(jnp.float32)).astype(jnp.bfloat16)


def point_fields(chunks, constant, weight, oweight):
    row = lax.broadcasted_iota(jnp.int32, (16, 256), 0)
    orow = lax.broadcasted_iota(jnp.int32, (16, 128), 0)
    column = lax.broadcasted_iota(jnp.int32, (128, 384), 0)
    for block in range(8):

        def line(k, block=block):
            return chunks[block, k : k + 1, :]

        def double(k, line=line):
            return jnp.concatenate([line(k), line(k + 1)], axis=1)

        flat = double(AT_MISC).astype(jnp.int32)
        oflat = line(AT_MISC + 2).astype(jnp.int32)
        w, ow = double(AT_MISC + 3), line(AT_MISC + 5)
        cell, ocell = flat >> 7, oflat >> 7
        at_cross = jnp.concatenate([flat & 127, oflat & 127], axis=1)
        columns = (column == at_cross).astype(jnp.float32).astype(jnp.bfloat16)
        here, ohere = row == cell, orow == ocell
        below, beside = orow == ocell + 1, orow == ocell + 4
        main, along = [], []
        for c in range(4):
            value = w * double(AT_VALUES + 2 * c)
            n0, n1, n2 = (ow * line(AT_NORMALS + 4 * k + c) for k in range(3))
            placed = (
                jnp.where(below, n0, 0.0)
                + jnp.where(beside, n1, 0.0)
                - jnp.where(ohere, n0 + n1 + n2, 0.0)
            )
            main.append(jnp.concatenate([jnp.where(here, value, 0.0), placed], axis=1))
            along.append(
                jnp.concatenate([jnp.zeros((16, 256), jnp.float32), jnp.where(ohere, n2, 0.0)], axis=1)
            )
        both = [
            jnp.concatenate([jnp.where(here, w, 0.0), jnp.zeros((16, 128), jnp.float32)], axis=1),
            jnp.concatenate([jnp.zeros((16, 256), jnp.float32), jnp.where(ohere, ow, 0.0)], axis=1),
        ]
        high, low = split(jnp.concatenate(main + both + along, axis=0))
        sums = lax.dot_general(
            jnp.concatenate([high, low], axis=0),
            columns,
            (((1,), (1,)), ((), ())),
            preferred_element_type=jnp.float32,
        )
        sums = sums[:160] + sums[160:]
        moved = pltpu.roll(sums[96:160], 1, 1)
        z = 4 * block
        for y in range(4):
            for c in range(4):
                k = 16 * c + 4 * y
                constant[y, c, z : z + 4, :] = sums[k : k + 4] + moved[k : k + 4]
            weight[y, z : z + 4, :] = sums[64 + 4 * y : 68 + 4 * y]
            oweight[y, z : z + 4, :] = sums[80 + 4 * y : 84 + 4 * y]


def own_kernel(chunks, smoothed, kernels, partial, constant, weight, oweight, table):
    group = lax.axis_index("depth")
    picked = jnp.where(lane_index((400, 8)) == group, kernels[...], 0.0)
    table[...] = jnp.broadcast_to(jnp.sum(picked, axis=1, keepdims=True), (400, 128))
    point_fields(chunks, constant, weight, oweight)

    def write(y, o, depths, value):
        partial[y, o, depths, :] = value

    conv_rows(
        lambda row, c, depths: smoothed[row, c, depths, :],
        OWN,
        lambda y, o, depths: jnp.zeros((8, 128), jnp.float32),
        table,
        False,
        write,
    )


def fold_rows(came, through, partial, table, adjoint, write):
    slab, last = lax.axis_index("inline"), lax.axis_size("inline") - 1

    upper = slab % 2 == through
    outside = slab == jnp.where(upper, last, 0)

    def start(y, o, depths):
        return partial[y, o, depths, :]

    def fold(rows):
        def read(row, c, depths):
            return came[row + 2 if row < 0 else row - 4, c, depths, :]

        conv_rows(read, rows, start, table, adjoint, write)

    @pl.when(upper & ~outside)
    def _():
        fold(HALO[2:])

    @pl.when(~upper & ~outside)
    def _():
        fold(HALO[:2])

    @pl.when(outside)
    def _():
        def some_depths(k, carry):
            depths = pl.ds(pl.multiple_of(k * 8, 8), 8)
            for y in range(4):
                for o in range(4):
                    write(y, o, depths, start(y, o, depths))
            return carry

        lax.fori_loop(0, 4, some_depths, 0)


def even_kernel(adjoint, partial, even_in, table, out):
    def write(y, o, depths, value):
        out[y, o, depths, :] = value

    fold_rows(even_in, 0, partial, table, adjoint, write)


def forcing_kernel(
    partial, odd_in, table, constant, weight, oweight, potential, forcing, even, odd
):
    def write(y, o, depths, value):
        potential[y, o, depths, :] = value

    fold_rows(odd_in, 1, partial, table, False, write)
    parity = lax.axis_index("inline") % 2

    def some_depths(k, carry):
        depths = pl.ds(pl.multiple_of(k * 8, 8), 8)
        shares = [oweight[y, depths, :] for y in range(4)]
        weights = [weight[y, depths, :] for y in range(4)]
        for c in range(4):
            lines = [potential[y, c, depths, :] for y in range(4)]
            sums = [weights[y] * lines[y] - constant[y, c, depths, :] for y in range(4)]
            for y in range(4):
                deeper = shares[y] * (pltpu.roll(lines[y], 7, 0) - lines[y])
                across = shares[y] * (pltpu.roll(lines[y], 127, 1) - lines[y])
                sums[y] = sums[y] - deeper + pltpu.roll(deeper, 1, 0)
                sums[y] = sums[y] - across + pltpu.roll(across, 1, 1)
                if y < 3:
                    beside = shares[y] * (lines[y + 1] - lines[y])
                    sums[y] = sums[y] - beside
                    sums[y + 1] = sums[y + 1] + beside
            for y in range(4):
                forcing[y, c, depths, :] = sums[y]
            for y in range(2):
                even[y, c, depths, :] = jnp.where(parity == 0, sums[2 + y], sums[y])
                odd[y, c, depths, :] = jnp.where(parity == 0, sums[y], sums[2 + y])
        return carry

    lax.fori_loop(0, 4, some_depths, 0)


def spread_kernel(forcing, table, potential, partial, out, rows):
    def write(y, o, depths, value):
        partial[y, o, depths, :] = value

    conv_rows(
        lambda row, c, depths: forcing[row, c, depths, :],
        OWN,
        lambda y, o, depths: jnp.zeros((8, 128), jnp.float32),
        table,
        True,
        write,
    )
    for y in range(4):
        for c in range(4):
            rows[pl.ds((c * 4 + y) * 32, 32), :] = potential[y, c]
    for z in range(32):
        out[z // 4, (z % 4) * 16 : (z % 4) * 16 + 16, :] = rows[pl.ds(z, 16, stride=32), :]


def gradient_kernel(*refs):
    chunks, partial, odd_in, taps, table, scale, root, potential = refs[:8]
    give, keep, (first, rows, out) = refs[8], refs[9:13], refs[13:]
    me = lax.axis_index("depth")
    targets = [
        give.at[place // 2] if place % 2 else keep[place // 2] for place in range(8)
    ]
    for place, target in enumerate(targets):
        target[:64, :] = potential[me ^ place]

    def write(y, o, depths, value):
        rows[pl.ds(pl.multiple_of((o * 4 + y) * 32 + depths.start, 8), 8), :] = value

    fold_rows(odd_in, 1, partial, taps, True, write)

    def keep_first(z, value):
        first[z] = scale[z] * value

    def keep_out(z, value):
        row = (z % 4) * 16
        out[z // 4, row : row + 16, :] = depth_rows(chunks, z) + root[z] * value

    recurrence(
        lambda z: rows[pl.ds(z, 16, stride=32), :],
        lambda lag, z, before: table[before, lag - 1],
        keep_first,
        range(32),
    )
    recurrence(
        lambda z: first[z],
        lambda lag, z, before: table[before, lag - 1],
        keep_out,
        range(31, -1, -1),
    )
    for place, target in enumerate(targets):
        target[64:, :] = out[me ^ place]


def unpack_kernel(chips, number, *refs):
    count = len(chips)
    parts, (potential, gradient, planes, sent) = refs[:count], refs[-4:]
    me = lax.axis_index("depth")
    order = number[...].reshape(1, 32)
    lane = lane_index((1, 32))
    channels = []
    for slot in range(8 * count):
        place = 2 * chips[slot // 8] + slot // 4 % 2
        here = lane == (me ^ place) * 4 + slot % 4
        channels.append(jnp.sum(jnp.where(here, order, 0)))
    for half in range(2):
        for slot in range(8 * count):
            k, source, c = slot // 8, slot // 4 % 2, slot % 4
            rows = [64 * half + z * 16 + c * 4 for z in range(4)]
            pieces = [parts[k][source, row : row + 4, :] for row in rows]
            planes[half, slot] = jnp.concatenate(pieces, axis=0)
    for slot in range(8 * count):
        for half, out in enumerate((potential, gradient)):
            pltpu.make_async_copy(
                planes.at[half, slot], out.at[channels[slot]], sent.at[half]
            ).start()
    for half, out in enumerate((potential, gradient)):
        pltpu.make_async_copy(planes.at[half], out.at[: 8 * count], sent.at[half]).wait()


def swapped(even, odd):
    depths, slabs = lax.axis_size("depth"), lax.axis_size("inline")

    def swap(value, first):
        pairs = []
        for d in range(depths):
            for i in range(slabs):
                other = i + 1 if (i - first) % 2 == 0 else i - 1
                to = (d, other) if 0 <= other < slabs else (d ^ 1, i)
                pairs.append((d * slabs + i, to[0] * slabs + to[1]))
        return lax.ppermute(value, ("depth", "inline"), pairs)

    return swap(even, 0), swap(odd, 1)


def by_group(
    control,
    filter_coeffs,
    conv_kernels,
    channel_order,
    point_cells,
    point_values,
    point_weights,
    orient_cells,
    orient_normals,
    orient_weights,
):
    params = pltpu.CompilerParams(vmem_limit_bytes=48 << 20)
    in_vmem, in_hbm = (pl.BlockSpec(memory_space=space) for space in (pltpu.VMEM, pltpu.HBM))

    def call(kernel, outs, operands, scratch=(), ins=None, to=in_vmem, aliases=None):
        return pl.pallas_call(
            kernel,
            out_shape=outs,
            in_specs=ins or [in_vmem] * len(operands),
            out_specs=jax.tree.map(lambda _: to, outs),
            scratch_shapes=list(scratch),
            input_output_aliases=aliases or {},
            compiler_params=params,
        )(*operands)

    sources = (
        channel_order,
        jnp.transpose(filter_coeffs, (0, 2, 1)).reshape(16, 32),
        point_cells,
        point_weights,
        orient_cells,
        orient_weights,
        point_values.reshape(64, 128),
        orient_normals.reshape(96, 128),
        control.reshape(32, 16, 128),
    )
    sources = tuple(pltpu.with_memory_space_constraint(x, pltpu.HBM) for x in sources)
    held = [pltpu.VMEM(source.shape, source.dtype) for source in sources[1:6]]

    def exchange(rows, give, keep, chips):
        def swap(value, flip):
            return lax.ppermute(value, "depth", [(i, i ^ flip) for i in range(8)])

        both = f32(2, rows, 128)
        joined = call(join_kernel, (both,) * 4, (swap(give, 1), *keep))
        return [joined[k] if k == 0 else swap(joined[k], 2 * k) for k in chips]

    give, *held = call(
        pack_kernel,
        (
            f32(4, CHUNK, 128),
            f32(8, 128),
            f32(128, 128),
            jax.ShapeDtypeStruct((32,), jnp.int32),
            f32(32, 16, 128),
            f32(64, 128),
            f32(96, 128),
        ),
        sources,
        [pltpu.SMEM((32,), jnp.int32), *held, pltpu.SemaphoreType.DMA((10,))],
        [in_hbm] * 9,
    )
    keep = call(
        keep_kernel,
        (f32(CHUNK, 128),) * 4,
        held,
        [pltpu.SMEM((32,), jnp.int32), pltpu.SemaphoreType.DMA],
    )
    number = held[2]
    parts = exchange(CHUNK, give, keep, CHIPS)
    field, edge, plane = f32(4, 4, 32, 128), f32(2, 4, 32, 128), f32(4, 32, 128)
    by_depth = f32(32, 16, 128)
    rows = pltpu.VMEM((512, 128), jnp.float32)
    first = pltpu.VMEM((32, 16, 128), jnp.float32)
    chunks, smoothed, even, odd, table, scale, root = call(
        smooth_kernel,
        (f32(8, CHUNK, 128), field, edge, edge, f32(32, 4, 16, 128), by_depth, by_depth),
        parts,
        [pltpu.VMEM((8, 16, 128), jnp.float32), first, rows],
    )
    even, odd = swapped(even, odd)
    kernels = jnp.transpose(conv_kernels, (1, 3, 4, 2, 0)).reshape(400, 8)
    partial, constant, weight, oweight, taps = call(
        own_kernel, (field, field, plane, plane, f32(400, 128)), (chunks, smoothed, kernels)
    )
    partial = call(functools.partial(even_kernel, False), field, (partial, even, taps))
    potential, forcing, even, odd = call(
        forcing_kernel,
        (field, field, edge, edge),
        (partial, odd, taps, constant, weight, oweight),
    )
    even, odd = swapped(even, odd)
    partial, potential = call(
        spread_kernel, (field, f32(8, 64, 128)), (forcing, taps, potential), [rows]
    )
    partial = call(functools.partial(even_kernel, True), field, (partial, even, taps))
    give, *keep = call(
        gradient_kernel,
        (f32(4, 128, 128),) + (f32(128, 128),) * 4,
        (chunks, partial, odd, taps, table, scale, root, potential),
        [first, rows, pltpu.VMEM((8, 64, 128), jnp.float32)],
    )
    parts = exchange(128, give, keep, CHIPS)
    outs = ()
    for some in (slice(0, 1), slice(1, 2), slice(2, 4)):
        count = len(CHIPS[some])
        outs = call(
            functools.partial(unpack_kernel, CHIPS[some]),
            (by_depth, by_depth),
            (number, *parts[some], *outs),
            [
                pltpu.VMEM((2, 8 * count, 16, 128), jnp.float32),
                pltpu.SemaphoreType.DMA((2,)),
            ],
            [in_vmem] * (count + 1) + [in_hbm] * len(outs),
            in_hbm,
            {count + 1: 0, count + 2: 1} if outs else None,
        )
    potential, gradient = outs
    return potential.reshape(control.shape), gradient.reshape(control.shape)


def solution(mesh):
    placed = (
        P(None, "depth", "inline", None),
        P(None, None, "depth"),
        P(),
        P(),
        P(None, "depth", "inline", None),
        P(None, "depth", "inline", None),
        P("depth", "inline", None),
        P(None, "depth", "inline", None),
        P(None, None, "depth", "inline", None),
        P("depth", "inline", None),
    )

    def body(control, filter_coeffs, conv_kernels, *rest):
        groups, block = conv_kernels.shape, control.shape
        fits = groups[:3] == (mesh.shape["depth"], 4, 4) and groups[0] == 8
        if fits and block == (32, 4, 4, 128):
            return by_group(control, filter_coeffs, conv_kernels, *rest)
        return shards(control, filter_coeffs, conv_kernels, *rest)

    return jax.shard_map(
        body,
        mesh=mesh,
        in_specs=placed,
        out_specs=(P(None, "depth", "inline", None), P(None, "depth", "inline", None)),
        check_vma=False,
    )
```
